32 devices in a mesh: dp: 8 (over y, x, core), expert: 4 (over z).
Axes of the slice: x: 2, y: 2, z: 4, core: 2. Of those that a mesh axis runs over, the one named last changes fastest.
Arguments:
- tokens: bfloat16 [12288, 1024], P(('dp', 'expert')), may hold values from -6 to 6
- cotangent: bfloat16 [12288, 1024], P(('dp', 'expert')), may hold values from -6 to 6
- routes: int32 [12288, 8], P(('dp', 'expert')), may hold values from 0 to 15, all different within a row; in each aligned block of 384 rows (0 to 383, 384 to 767, ...) at most 256 rows name the same one
- cont_ids: int32 [32, 128], P(('dp', 'expert')), may hold values from 0 to 1, never falling along the last dimension, each value on 1 to 96 neighbouring positions
- norm_gains: float32 [1024, 2], replicated, may hold values from 0.5 to 1.5
- gains_moment: float32 [1024, 2], P(('dp', 'expert')), may hold values from -192 to 192
- gains_average: float32 [1024, 2], P(('dp', 'expert')), may hold values from 0.5 to 1.5
- heads_in: bfloat16 [1024, 2048], replicated, may hold values from -0.5 to 0.5
- heads_in_master: float32 [1024, 2048], P(('dp', 'expert')), may hold values from -0.625 to 0.625
- heads_in_moment: float32 [1024, 2048], P(('dp', 'expert')), may hold values from -128 to 128
- heads_in_average: float32 [1024, 2048], P(('dp', 'expert')), may hold values from -0.625 to 0.625
- heads_out: bfloat16 [1024, 1024], replicated, may hold values from -1.5 to 1.5
- heads_out_master: float32 [1024, 1024], P(('dp', 'expert')), may hold values from -0.1875 to 0.1875
- heads_out_moment: float32 [1024, 1024], P(('dp', 'expert')), may hold values from -32 to 32
- heads_out_average: float32 [1024, 1024], P(('dp', 'expert')), may hold values from -0.1875 to 0.1875
- router: bfloat16 [1024, 16], replicated, may hold values from -0.09375 to 0.09375
- router_master: float32 [1024, 16], P(('dp', 'expert')), may hold values from -2.5 to 2.5
- router_moment: float32 [1024, 16], P(('dp', 'expert')), may hold values from -128 to 128
- router_average: float32 [1024, 16], P(('dp', 'expert')), may hold values from -2.5 to 2.5
- expert_in: bfloat16 [16, 1024, 1024], P('expert'), may hold values from -0.1875 to 0.1875
- expert_in_master: float32 [16, 1024, 1024], P('expert', 'dp'), may hold values from -0.25 to 0.25
- expert_in_moment: float32 [16, 1024, 1024], P('expert', 'dp'), may hold values from -16 to 16
- expert_in_average: float32 [16, 1024, 1024], P('expert', 'dp'), may hold values from -0.25 to 0.25
- expert_out: bfloat16 [16, 1024, 512], P('expert'), may hold values from -1 to 1
- expert_out_master: float32 [16, 1024, 512], P('expert', 'dp'), may hold values from -0.0546875 to 0.0546875
- expert_out_moment: float32 [16, 1024, 512], P('expert', 'dp'), may hold values from -3.5 to 3.5
- expert_out_average: float32 [16, 1024, 512], P('expert', 'dp'), may hold values from -0.0546875 to 0.0546875
Outputs:
- output: bfloat16 [12288, 1024], P(('dp', 'expert'))
- token_grad: float32 [12288, 1024], P(('dp', 'expert'))
- gains_next: float32 [1024, 2], P(('dp', 'expert'))
- gains_moment_next: float32 [1024, 2], P(('dp', 'expert'))
- gains_average_next: float32 [1024, 2], P(('dp', 'expert'))
- heads_in_next: float32 [1024, 2048], P(('dp', 'expert'))
- heads_in_moment_next: float32 [1024, 2048], P(('dp', 'expert'))
- heads_in_average_next: float32 [1024, 2048], P(('dp', 'expert'))
- heads_out_next: float32 [1024, 1024], P(('dp', 'expert'))
- heads_out_moment_next: float32 [1024, 1024], P(('dp', 'expert'))
- heads_out_average_next: float32 [1024, 1024], P(('dp', 'expert'))
- router_next: float32 [1024, 16], P(('dp', 'expert'))
- router_moment_next: float32 [1024, 16], P(('dp', 'expert'))
- router_average_next: float32 [1024, 16], P(('dp', 'expert'))
- expert_in_next: float32 [16, 1024, 1024], P('expert', 'dp')
- expert_in_moment_next: float32 [16, 1024, 1024], P('expert', 'dp')
- expert_in_average_next: float32 [16, 1024, 1024], P('expert', 'dp')
- expert_out_next: float32 [16, 1024, 512], P('expert', 'dp')
- expert_out_moment_next: float32 [16, 1024, 512], P('expert', 'dp')
- expert_out_average_next: float32 [16, 1024, 512], P('expert', 'dp')
The draws below stay inside these ranges and needn't reach their ends.
Inputs may be any that keep to these rules, and one draw needn't show every extreme that they name: `routes`: each row names 8 different experts. Among the tokens of one group no expert is named more than 256 times, a bound that some block reaches. `cont_ids`: in each row the numbers never fall; each of the 2 continuations has 1 to 96 tokens.
All inputs are finite; a program needn't handle non-finite values.
Results may differ from the reference program's by a relative error of at most 0.017.
Values may be sent and summed in bfloat16 or wider, within the bound.
A program may use at most 256 MiB of HBM per device.

```python
import math
import jax
import jax.numpy as jnp
import numpy as np
from jax import lax

D = 1024
HEADS = 16
KV_HEADS = 8
HEAD_DIM = 64
FF = 512
TOP = 8
EXP_DEV = 4
PROMPT = 256
CONT = 128
CONTS = 2
CONT_MOST = 96
TOK_DEV = 384
GROUPS = 32
TOKENS = 12288
EXPERTS = 16
CAP = 256
N_EXPERT = 4


def with_spikes(array, key, source, target, shards_of, factor):
    def block_of(axis_at):
        return (jnp.arange(array.shape[axis_at]) // (array.shape[axis_at] // shards_of)).reshape((-1,) + (1,) * (array.ndim - 1 - axis_at))

    first = jax.random.permutation(key, shards_of)[block_of(target)]
    other_side = (block_of(target) + shards_of // 2) % shards_of
    return jnp.where((block_of(source) == first) | (block_of(source) == other_side), factor * array, array)


def shard_levels(own_key, shape, cuts, low, largest):
    loudness = 1.0
    for axis_at, parts in cuts:
        heights = jax.random.uniform(jax.random.fold_in(jax.random.fold_in(own_key, 6), axis_at), (parts,), jnp.float32, low / len(cuts), largest / len(cuts))
        loudness = loudness * jnp.repeat(jnp.exp(heights), shape[axis_at] // parts).reshape((-1,) + (1,) * (len(shape) - 1 - axis_at))
    return loudness


def split_up(amount, total, bound, slope):
    portions = [(1 << 20) // math.isqrt(grade ** slope) + 1 for grade in range(2, amount + 1)]
    surplus, given = total - bound - (amount - 1), [1] * (amount - 1)
    while surplus > 0:
        candidates = [i for i in range(amount - 1) if given[i] < bound]
        pool, remaining = sum([portions[i] for i in candidates]), surplus
        for i in candidates:
            extra = min(bound - given[i], max(1, remaining * portions[i] // pool), surplus)
            given[i] = given[i] + extra
            surplus = surplus - extra
    return np.array([bound] + given)


def ragged(own_key, count, total, limit, skew):
    if count == 2:
        one = jax.random.randint(own_key, (), max(1, total - limit), min(limit, total - 1) + 1)
        return jnp.stack([one, total - one])
    tallies = jnp.asarray(split_up(count, total, limit, skew), jnp.int32)
    twos = (count - 1) // 2
    donor, receiver = tallies[1:1 + 2 * twos:2], tallies[2:2 + 2 * twos:2]
    margin = jnp.minimum(donor - 1, limit - receiver)
    moved = jax.random.randint(jax.random.fold_in(own_key, 1), (twos,), 0, 1 << 20) % (margin + 1)
    tallies = tallies.at[1:1 + 2 * twos:2].set(donor - moved).at[2:2 + 2 * twos:2].set(receiver + moved)
    return tallies[jax.random.permutation(jax.random.fold_in(own_key, 2), count)]


def shared_out(own_key, own, number, rows, number_of, top, bound, lean):
    sequence = jax.random.permutation(own_key, number_of)
    crowded, usual = shares(number_of, rows * top, bound, lean, True), shares(number_of, rows * top, bound, lean, False)
    places = jnp.arange(number_of)

    def named(sizes, offset_by):
        used = int((sizes > 0).sum())
        fixed = max(1, used // 4)
        moved = fixed + (places - fixed + offset_by * (used - fixed)) % max(1, number_of - fixed)
        return jnp.zeros((number_of,), jnp.int32).at[sequence[jnp.where(places < fixed, places, moved)]].set(jnp.asarray(sizes, jnp.int32))

    sizes = jnp.where(number % 4 == 0, named(crowded, number // 4), named(usual, number - number // 4 - 1))
    mixed = jax.random.permutation(jax.random.fold_in(own, 3), number_of)
    giver, receiver = mixed[0:number_of // 2 * 2:2], mixed[1:number_of // 2 * 2:2]
    slack = jnp.minimum(sizes[giver] - 1, bound - sizes[receiver]) // 2
    slack = jnp.where((giver == sequence[0]) | (receiver == sequence[0]) | (sizes[receiver] == 0), 0, jnp.maximum(slack, 0))
    moved = jax.random.randint(jax.random.fold_in(own, 4), (number_of // 2,), 0, 1 << 20) % (slack + 1)
    sizes = sizes.at[giver].add(-moved).at[receiver].add(moved)
    items = jnp.searchsorted(jnp.cumsum(sizes), jnp.arange(rows * top), side="right").astype(jnp.int32)
    grid = items.reshape(top, rows).T
    grid = grid[jax.random.permutation(jax.random.fold_in(own, 1), rows)]
    offset_by = jax.random.randint(jax.random.fold_in(own, 2), (rows, 1), 0, top)
    return jnp.take_along_axis(grid, (jnp.arange(top)[None, :] + offset_by) % top, axis=1)


def shares(count, total, most, slope, full):
    weights = [(1 << 20) // math.isqrt(standing ** slope) + 1 for standing in range(1, count + 1)]
    largest = most if full else min(most, max(-(-total // count), total * weights[0] // sum(weights)))
    least = 1 if total - largest >= count - 1 else 0
    given, surplus = [largest] + [least] * (count - 1), total - largest - least * (count - 1)
    while surplus > 0:
        candidates = [i for i in range(1, count) if given[i] < largest] or [i for i in range(1, count) if given[i] < most]
        whole, budget = sum([weights[i] for i in candidates]), surplus
        for i in candidates:
            addition = min(most - given[i], max(1, budget * weights[i] // whole), surplus)
            given[i] = given[i] + addition
            surplus = surplus - addition
    return np.array(given)


def centred(stream_key, dims, deviation, most, cuts=(), kind=jnp.bfloat16):
    values = jax.random.normal(stream_key, dims, jnp.float32) * deviation
    if len(cuts) > 0:
        values = shard_levels(stream_key, dims, cuts, -0.22, 0.18) * values
    return jnp.clip(values, min=-most, max=most).astype(kind)


def gaussian_with(rng, extent, spread, bound, pieces, heavy, held_as=jnp.bfloat16):
    array = spread * jax.random.normal(rng, extent, jnp.float32)
    if pieces:
        array = array * shard_levels(rng, extent, pieces, -0.22, 0.18)
    return jnp.clip(with_spikes(array, jax.random.fold_in(rng, 3), *heavy), -bound, bound).astype(held_as)


def setup_inputs(seed: int = 0) -> dict:
    streams_of = jax.random.split(jax.random.key(seed), 28)
    tokens = gaussian_with(streams_of[0], (TOKENS, D), 1.0, 6.0, ((0, 32),), (0, 1, 32, 2.75))
    cotangent = centred(streams_of[1], (TOKENS, D), 1.0, 6.0, ((0, 32),))
    routes_keys = jax.random.split(jax.random.fold_in(streams_of[2], 1), TOKENS // TOK_DEV)
    routes_turns = jax.random.permutation(jax.random.fold_in(streams_of[2], 3), TOKENS // TOK_DEV)
    routes = jax.vmap(lambda own, number: shared_out(jax.random.fold_in(streams_of[2], 2), own, number, TOK_DEV, EXPERTS, TOP, CAP, 1))(routes_keys, routes_turns).reshape((TOKENS, TOP))
    cont_ids = jax.vmap(lambda own: jnp.searchsorted(jnp.cumsum(ragged(own, CONTS, CONT, CONT_MOST, 1)), jnp.arange(CONT), side="right"))(jax.random.split(streams_of[3], GROUPS)).reshape((GROUPS, CONT)).astype(jnp.int32)
    norm_gains = jnp.clip(1.0 + 0.1 * jax.random.normal(streams_of[4], (D, 2), jnp.float32), 0.5, 1.5)
    gains_moment = centred(streams_of[5], (D, 2), (0.3 * TOKENS ** 0.5), 192.0, ((0, 32),), jnp.float32)
    gains_average = jnp.clip(1.0 + 0.1 * jax.random.normal(streams_of[6], (D, 2), jnp.float32), 0.5, 1.5)
    heads_in = centred(streams_of[7], (D, (HEADS + 2 * KV_HEADS) * HEAD_DIM), (D // 8) ** -0.5, 0.5)
    heads_in_master = centred(streams_of[8], (D, (HEADS + 2 * KV_HEADS) * HEAD_DIM), (0.001 * TOKENS ** 0.5), 0.625, ((0, 32),), jnp.float32)
    heads_in_moment = centred(streams_of[9], (D, (HEADS + 2 * KV_HEADS) * HEAD_DIM), (0.22 * TOKENS ** 0.5), 128.0, ((0, 32),), jnp.float32)
    heads_in_average = centred(streams_of[10], (D, (HEADS + 2 * KV_HEADS) * HEAD_DIM), (0.001 * TOKENS ** 0.5), 0.625, ((0, 32),), jnp.float32)
    heads_out = centred(streams_of[11], (D, HEADS * HEAD_DIM), (max(HEADS * HEAD_DIM // 64, 1)) ** -0.5, 1.5)
    heads_out_master = centred(streams_of[12], (D, HEADS * HEAD_DIM), (0.0003 * TOKENS ** 0.5), 0.1875, ((0, 32),), jnp.float32)
    heads_out_moment = centred(streams_of[13], (D, HEADS * HEAD_DIM), (0.055 * TOKENS ** 0.5), 32.0, ((0, 32),), jnp.float32)
    heads_out_average = centred(streams_of[14], (D, HEADS * HEAD_DIM), (0.0003 * TOKENS ** 0.5), 0.1875, ((0, 32),), jnp.float32)
    router = centred(streams_of[15], (D, EXPERTS), (4 * D) ** -0.5, 0.09375)
    router_master = centred(streams_of[16], (D, EXPERTS), (0.004 * TOKENS ** 0.5), 2.5, ((0, 32),), jnp.float32)
    router_moment = centred(streams_of[17], (D, EXPERTS), (0.2 * TOKENS ** 0.5), 128.0, ((0, 32),), jnp.float32)
    router_average = centred(streams_of[18], (D, EXPERTS), (0.004 * TOKENS ** 0.5), 2.5, ((0, 32),), jnp.float32)
    expert_in = centred(streams_of[19], (EXPERTS, D, 2 * FF), D ** -0.5, 0.1875, ((0, 4),))
    expert_in_master = centred(streams_of[20], (EXPERTS, D, 2 * FF), (0.0006 * (TOKENS * TOP / EXPERTS) ** 0.5), 0.25, ((0, 4), (1, 8)), jnp.float32)
    expert_in_moment = centred(streams_of[21], (EXPERTS, D, 2 * FF), (0.033 * (TOKENS * TOP / EXPERTS) ** 0.5), 16.0, ((0, 4), (1, 8)), jnp.float32)
    expert_in_average = centred(streams_of[22], (EXPERTS, D, 2 * FF), (0.0006 * (TOKENS * TOP / EXPERTS) ** 0.5), 0.25, ((0, 4), (1, 8)), jnp.float32)
    expert_out = centred(streams_of[23], (EXPERTS, D, FF), (FF // 16) ** -0.5, 1.0, ((0, 4),))
    expert_out_master = centred(streams_of[24], (EXPERTS, D, FF), (0.00012 * (TOKENS * TOP / EXPERTS) ** 0.5), 0.0546875, ((0, 4), (1, 8)), jnp.float32)
    expert_out_moment = centred(streams_of[25], (EXPERTS, D, FF), (0.007 * (TOKENS * TOP / EXPERTS) ** 0.5), 3.5, ((0, 4), (1, 8)), jnp.float32)
    expert_out_average = centred(streams_of[26], (EXPERTS, D, FF), (0.00012 * (TOKENS * TOP / EXPERTS) ** 0.5), 0.0546875, ((0, 4), (1, 8)), jnp.float32)
    return dict(tokens=tokens, cotangent=cotangent, routes=routes, cont_ids=cont_ids, norm_gains=norm_gains, gains_moment=gains_moment, gains_average=gains_average, heads_in=heads_in, heads_in_master=heads_in_master, heads_in_moment=heads_in_moment, heads_in_average=heads_in_average, heads_out=heads_out, heads_out_master=heads_out_master, heads_out_moment=heads_out_moment, heads_out_average=heads_out_average, router=router, router_master=router_master, router_moment=router_moment, router_average=router_average, expert_in=expert_in, expert_in_master=expert_in_master, expert_in_moment=expert_in_moment, expert_in_average=expert_in_average, expert_out=expert_out, expert_out_master=expert_out_master, expert_out_moment=expert_out_moment, expert_out_average=expert_out_average)


EPS = 1e-06
SCALE = 0.015625
THETA = 10000.0
MOMENTUM = 0.9
DECAY = 0.8
RATE = 0.001
HIGHEST = lax.Precision.HIGHEST

@jax.custom_vjp
def low(v):
    return lax.optimization_barrier(v.astype(jnp.bfloat16)).astype(jnp.float32)

@jax.custom_vjp
def low_back(v):
    return v

def low_keep(v):
    return (low(v), None)

def low_pass(kept, grad):
    return (grad,)

def back_keep(v):
    return (v, None)

def back_low(kept, grad):
    return (low(grad),)
low.defvjp(low_keep, low_pass)
low_back.defvjp(back_keep, back_low)

def layout(labels_row):
    places = jnp.arange(PROMPT + CONT, dtype=jnp.int32)
    earlier = lax.optimization_barrier(jnp.sum((labels_row[None, :] < labels_row[:, None]).astype(jnp.int32), axis=1))
    offset = places[PROMPT:] - PROMPT - earlier
    positions = jnp.concatenate([places[:PROMPT], PROMPT + offset]).astype(jnp.float32)
    labels = jnp.concatenate([jnp.full((PROMPT,), -1, jnp.int32), labels_row])
    allowed = (places[None, :] <= places[:, None]) & ((places[None, :] < PROMPT) | (labels[None, :] == labels[:, None]))
    return (positions, allowed)

def rope_tables(positions):
    middle = HEAD_DIM // 2
    frequency = THETA ** (-2.0 * jnp.arange(middle, dtype=jnp.float32) / HEAD_DIM)
    angles = positions[:, None] * frequency[None, :]
    angles = jnp.concatenate([angles, angles], axis=1)
    return (jnp.cos(angles)[:, None, :], jnp.sin(angles)[:, None, :])

def rotate(values, cosine, sine_table):
    middle = values.shape[-1] // 2
    turned = jnp.concatenate([-values[..., middle:], values[..., :middle]], axis=-1)
    return values * cosine + turned * sine_table

def attend(qkv_rows, labels_row):
    positions, allowed = layout(labels_row)
    cosine, sine_table = rope_tables(positions)
    row_count = qkv_rows.shape[0]
    query_end = HEADS * HEAD_DIM
    key_end = query_end + KV_HEADS * HEAD_DIM
    queries = low(rotate(qkv_rows[:, :query_end].reshape(row_count, HEADS, HEAD_DIM), cosine, sine_table))
    key_rows = low(rotate(qkv_rows[:, query_end:key_end].reshape(row_count, KV_HEADS, HEAD_DIM), cosine, sine_table))
    values = low(qkv_rows[:, key_end:].reshape(row_count, KV_HEADS, HEAD_DIM))
    queries = queries.reshape(row_count, KV_HEADS, HEADS // KV_HEADS, HEAD_DIM)
    scores = low_back(jnp.einsum('qkgd,pkd->kgqp', queries, key_rows, precision=HIGHEST) * SCALE)
    scores = jnp.where(allowed[None, None], scores, -1e+30)
    weights = low(jax.nn.softmax(scores, axis=-1))
    attended = jnp.einsum('kgqp,pkd->qkgd', weights, values, precision=HIGHEST)
    return attended.reshape(row_count, HEADS * HEAD_DIM)

def rms_norm(values, gain):
    return values * lax.rsqrt(lax.optimization_barrier(jnp.mean(values * values, axis=-1, keepdims=True)) + EPS) * gain

def slot_tables(routes):
    matches = (routes[:, :, None] == jnp.arange(EXPERTS, dtype=jnp.int32)[None, None, :]).astype(jnp.int32)
    counts = lax.optimization_barrier(jnp.sum(matches, axis=1)).reshape(GROUPS, TOK_DEV, EXPERTS)
    before = (jnp.cumsum(counts, axis=1) - counts).reshape(TOKENS, EXPERTS)
    slots = jnp.take_along_axis(before, routes, axis=1)
    group_ids = (jnp.arange(TOKENS, dtype=jnp.int32) // TOK_DEV)[:, None]
    row_ids = group_ids * CAP + slots
    token_ids = jnp.broadcast_to(jnp.arange(TOKENS, dtype=jnp.int32)[:, None], routes.shape)
    pick_ids = jnp.arange(TOKENS * TOP, dtype=jnp.int32).reshape(TOKENS, TOP)
    slot_tokens = jnp.full((EXPERTS, GROUPS * CAP), TOKENS, jnp.int32).at[routes, row_ids].set(token_ids)
    slot_picks = jnp.full((EXPERTS, GROUPS * CAP), TOKENS * TOP, jnp.int32).at[routes, row_ids].set(pick_ids)
    return (slot_tokens, slot_picks)

def forward(token_rows, gain_cols, in_weight, out_weight, router_weight, expert_up, expert_down, routes, cont_ids, slot_tokens, slot_picks):
    normed_one = low(rms_norm(token_rows, gain_cols[:, 0]))
    projected = low_back(jnp.dot(normed_one, in_weight, precision=HIGHEST))

    def one_group(group_item):
        return attend(group_item[0], group_item[1])
    attended = lax.map(jax.checkpoint(one_group), (projected.reshape(GROUPS, TOK_DEV, -1), cont_ids))
    attended = low(low_back(attended.reshape(TOKENS, HEADS * HEAD_DIM)))
    branch = low_back(jnp.dot(attended, out_weight.T, precision=HIGHEST))
    hidden = token_rows + branch
    normed_two = low(rms_norm(hidden, gain_cols[:, 1]))
    logits = jnp.dot(normed_two, router_weight, precision=HIGHEST)
    gate_probs = jax.nn.softmax(jnp.take_along_axis(logits, routes, axis=1), axis=-1).reshape(-1)
    bank_tokens = slot_tokens.reshape(N_EXPERT, EXP_DEV, GROUPS * CAP)
    bank_picks = slot_picks.reshape(N_EXPERT, EXP_DEV, GROUPS * CAP)
    bank_up = expert_up.reshape(N_EXPERT, EXP_DEV, D, 2 * FF)
    bank_down = expert_down.reshape(N_EXPERT, EXP_DEV, D, FF)

    def one_bank(running, bank_item):
        row_sets, pick_sets, up_sets, down_sets = bank_item
        view = low_back(normed_two)
        partial_value = jnp.zeros_like(running)
        for inner in range(EXP_DEV):
            row_ids = row_sets[inner]
            inputs = low_back(jnp.take(view, row_ids, axis=0, mode='fill', fill_value=0.0))
            gate_up = low_back(jnp.dot(inputs, up_sets[inner], precision=HIGHEST))
            activated = low(jax.nn.silu(gate_up[:, :FF]) * gate_up[:, FF:])
            result = low(low_back(jnp.dot(activated, down_sets[inner].T, precision=HIGHEST)))
            scaled = jnp.take(gate_probs, pick_sets[inner], axis=0, mode='fill', fill_value=0.0)[:, None] * result
            partial_value = partial_value.at[row_ids].add(scaled, mode='drop')
        return (running + low(partial_value), None)
    mixture, unused = lax.scan(jax.checkpoint(one_bank), jnp.zeros_like(hidden), (bank_tokens, bank_picks, bank_up, bank_down))
    return hidden + mixture

def update(gradient, master, moment, average):
    moment_next = MOMENTUM * moment + gradient
    master_next = master - RATE * (gradient + MOMENTUM * moment_next)
    return (master_next, moment_next, DECAY * average + (1.0 - DECAY) * master_next)

def reference(tokens, cotangent, routes, cont_ids, norm_gains, gains_moment, gains_average, heads_in, heads_in_master, heads_in_moment, heads_in_average, heads_out, heads_out_master, heads_out_moment, heads_out_average, router, router_master, router_moment, router_average, expert_in, expert_in_master, expert_in_moment, expert_in_average, expert_out, expert_out_master, expert_out_moment, expert_out_average):
    slot_tokens, slot_picks = slot_tables(routes)

    def run(token_rows, gain_cols, in_weight, out_weight, router_weight, expert_up, expert_down):
        return forward(token_rows, gain_cols, in_weight, out_weight, router_weight, expert_up, expert_down, routes, cont_ids, slot_tokens, slot_picks)
    result, pullback = jax.vjp(run, tokens.astype(jnp.float32), norm_gains, heads_in.astype(jnp.float32), heads_out.astype(jnp.float32), router.astype(jnp.float32), expert_in.astype(jnp.float32), expert_out.astype(jnp.float32))
    gradients = pullback(cotangent.astype(jnp.float32))
    gains_new = update(gradients[1], norm_gains, gains_moment, gains_average)
    inproj_new = update(gradients[2], heads_in_master, heads_in_moment, heads_in_average)
    outproj_new = update(gradients[3], heads_out_master, heads_out_moment, heads_out_average)
    router_new = update(gradients[4], router_master, router_moment, router_average)
    upper_new = update(gradients[5], expert_in_master, expert_in_moment, expert_in_average)
    lower_new = update(gradients[6], expert_out_master, expert_out_moment, expert_out_average)
    return (result.astype(jnp.bfloat16), gradients[0], gains_new[0], gains_new[1], gains_new[2], inproj_new[0], inproj_new[1], inproj_new[2], outproj_new[0], outproj_new[1], outproj_new[2], router_new[0], router_new[1], router_new[2], upper_new[0], upper_new[1], upper_new[2], lower_new[0], lower_new[1], lower_new[2])
```

```python
import jax
import jax.numpy as jnp
from jax import lax
from jax.sharding import PartitionSpec as P

HEADS = 16
KV_HEADS = 8
HEAD_DIM = 64


EPS = 1e-06
SCALE = 0.015625
THETA = 10000.0
MOMENTUM = 0.9
DECAY = 0.8
RATE = 0.001
HIGHEST = lax.Precision.HIGHEST


def layout(labels_row, prompt_len):
    places = jnp.arange(prompt_len + labels_row.shape[0], dtype=jnp.int32)
    earlier = jnp.sum((labels_row[None, :] < labels_row[:, None]).astype(jnp.int32), axis=1)
    offset = places[prompt_len:] - prompt_len - earlier
    positions = jnp.concatenate([places[:prompt_len], prompt_len + offset]).astype(jnp.float32)
    labels = jnp.concatenate([jnp.full((prompt_len,), -1, jnp.int32), labels_row])
    allowed = (places[None, :] <= places[:, None]) & (
        (places[None, :] < prompt_len) | (labels[None, :] == labels[:, None])
    )
    return (positions, allowed)


def rope_tables(positions):
    middle = HEAD_DIM // 2
    frequency = THETA ** (-2.0 * jnp.arange(middle, dtype=jnp.float32) / HEAD_DIM)
    angles = positions[:, None] * frequency[None, :]
    angles = jnp.concatenate([angles, angles], axis=1)
    return (jnp.cos(angles)[:, None, :], jnp.sin(angles)[:, None, :])


def rotate(values, cosine, sine_table):
    middle = values.shape[-1] // 2
    turned = jnp.concatenate([-values[..., middle:], values[..., :middle]], axis=-1)
    return values * cosine + turned * sine_table


def unrotate(gradient, cosine, sine_table):
    middle = gradient.shape[-1] // 2
    shifted = gradient * sine_table
    return gradient * cosine + jnp.concatenate(
        [shifted[..., middle:], -shifted[..., :middle]], axis=-1
    )


def masked_scores(queries, key_rows, allowed):
    products = (
        jnp.einsum("qkgd,pkd->kgqp", queries, key_rows, preferred_element_type=jnp.float32) * SCALE
    )
    return jnp.where(allowed[None, None], products, -1e30)


def rms_parts(values, gain):
    factor = lax.rsqrt(jnp.mean(values * values, axis=-1, keepdims=True) + EPS)
    return (values * factor * gain, factor)


def rms_back(incoming, values, factor, gain):
    normed = values * factor
    gain_grad = jnp.sum(incoming * normed, axis=0)
    weighted = incoming * gain
    input_grad = factor * (weighted - normed * jnp.mean(weighted * normed, axis=-1, keepdims=True))
    return (input_grad, gain_grad)


def update(gradient, master, moment, average):
    moment_next = MOMENTUM * moment + gradient
    master_next = master - RATE * (gradient + MOMENTUM * moment_next)
    return (master_next, moment_next, DECAY * average + (1.0 - DECAY) * master_next)


def body(
    tokens,
    cotangent,
    routes,
    cont_ids,
    norm_gains,
    gains_moment,
    gains_average,
    heads_in,
    heads_in_master,
    heads_in_moment,
    heads_in_average,
    heads_out,
    heads_out_master,
    heads_out_moment,
    heads_out_average,
    router,
    router_master,
    router_moment,
    router_average,
    expert_in,
    expert_in_master,
    expert_in_moment,
    expert_in_average,
    expert_out,
    expert_out_master,
    expert_out_moment,
    expert_out_average,
):
    token_count, model_width = tokens.shape
    local_experts = expert_in.shape[0]
    peer_count = lax.axis_size("expert")
    experts = local_experts * peer_count
    ff_width = expert_out.shape[2]
    group_size = HEADS // KV_HEADS
    query_end = HEADS * HEAD_DIM
    key_end = query_end + KV_HEADS * HEAD_DIM
    token_rows = tokens.astype(jnp.float32)
    normed_one, factor_one = rms_parts(token_rows, norm_gains[:, 0])
    first_in = normed_one.astype(jnp.bfloat16)
    projected = jnp.dot(first_in, heads_in, preferred_element_type=jnp.float32)
    positions, allowed = layout(cont_ids[0], token_count - cont_ids.shape[1])
    cosine, sine_table = rope_tables(positions)
    queries = rotate(
        projected[:, :query_end].reshape(token_count, HEADS, HEAD_DIM), cosine, sine_table
    )
    queries = queries.astype(jnp.bfloat16).reshape(token_count, KV_HEADS, group_size, HEAD_DIM)
    key_rows = rotate(
        projected[:, query_end:key_end].reshape(token_count, KV_HEADS, HEAD_DIM), cosine, sine_table
    ).astype(jnp.bfloat16)
    value_rows = (
        projected[:, key_end:].reshape(token_count, KV_HEADS, HEAD_DIM).astype(jnp.bfloat16)
    )
    scores = masked_scores(queries, key_rows, allowed)
    row_peak = jnp.max(scores, axis=-1, keepdims=True)
    log_total = row_peak + jnp.log(jnp.sum(jnp.exp(scores - row_peak), axis=-1, keepdims=True))
    weights = jnp.exp(scores - log_total).astype(jnp.bfloat16)
    attended = jnp.einsum("kgqp,pkd->qkgd", weights, value_rows, preferred_element_type=jnp.float32)
    attended = attended.reshape(token_count, query_end).astype(jnp.bfloat16)
    branch = jnp.einsum("th,dh->td", attended, heads_out, preferred_element_type=jnp.float32)
    hidden = token_rows + branch
    normed_two, factor_two = rms_parts(hidden, norm_gains[:, 1])
    second_in = normed_two.astype(jnp.bfloat16)
    logits = jnp.dot(second_in, router, preferred_element_type=jnp.float32)
    named = jnp.any(
        routes[:, :, None] == jnp.arange(experts, dtype=jnp.int32)[None, None, :], axis=1
    )
    peak = jnp.max(jnp.where(named, logits, -jnp.inf), axis=1, keepdims=True)
    powers = jnp.where(named, jnp.exp(logits - peak), 0.0)
    gates = powers / jnp.sum(powers, axis=1, keepdims=True)
    incoming = cotangent.astype(jnp.float32)
    slots = lax.axis_index("expert") * local_experts
    rows_all = lax.all_gather(second_in, "expert", axis=0, tiled=True)
    cots_all = lax.all_gather(cotangent, "expert", axis=0, tiled=True)
    gates_all = lax.all_gather(gates, "expert", axis=0, tiled=True)
    gates_here = lax.dynamic_slice_in_dim(gates_all, slots, local_experts, 1)
    gate_col = gates_here.T[:, :, None]
    gate_up = jnp.einsum("td,edf->etf", rows_all, expert_in, preferred_element_type=jnp.float32)
    gate_part = gate_up[..., :ff_width]
    up_part = gate_up[..., ff_width:]
    sigmoid_gate = jax.nn.sigmoid(gate_part)
    silu_gate = gate_part * sigmoid_gate
    active = silu_gate * up_part
    gated = (active * gate_col).astype(jnp.bfloat16)
    mix_part = jnp.einsum("etf,edf->td", gated, expert_out, preferred_element_type=jnp.float32)
    back = jnp.einsum("td,edf->etf", cots_all, expert_out, preferred_element_type=jnp.float32)
    gate_grads_here = jnp.sum(active * back, axis=-1).T
    grad_activated = back * gate_col
    grad_gate_part = (
        grad_activated * up_part * sigmoid_gate * (1.0 + gate_part * (1.0 - sigmoid_gate))
    )
    grad_up_part = grad_activated * silu_gate
    grad_gate_up = jnp.concatenate([grad_gate_part, grad_up_part], axis=-1).astype(jnp.bfloat16)
    grad_part = jnp.einsum("etf,edf->td", grad_gate_up, expert_in, preferred_element_type=jnp.float32)
    grad_second = lax.psum_scatter(
        grad_part.astype(jnp.bfloat16), "expert", scatter_dimension=0, tiled=True
    ).astype(jnp.float32)
    mixture = lax.psum_scatter(
        mix_part.astype(jnp.bfloat16), "expert", scatter_dimension=0, tiled=True
    ).astype(jnp.float32)
    grad_expert_out = jnp.einsum("td,etf->edf", cots_all, gated, preferred_element_type=jnp.float32)
    grad_expert_in = jnp.einsum(
        "td,etf->edf", rows_all, grad_gate_up, preferred_element_type=jnp.float32
    )
    output = (hidden + mixture).astype(jnp.bfloat16)
    grad_gates = lax.all_to_all(
        gate_grads_here.reshape(peer_count, token_count, local_experts),
        "expert",
        split_axis=0,
        concat_axis=0,
    )
    grad_gates = jnp.transpose(grad_gates, (1, 0, 2)).reshape(token_count, experts)
    grad_logits = gates * (grad_gates - jnp.sum(gates * grad_gates, axis=1, keepdims=True))
    grad_router = jnp.dot(second_in.astype(jnp.float32).T, grad_logits, precision=HIGHEST)
    grad_second = grad_second + jnp.dot(
        grad_logits, router.astype(jnp.float32).T, precision=HIGHEST
    )
    grad_hidden_norm, grad_gain_two = rms_back(grad_second, hidden, factor_two, norm_gains[:, 1])
    grad_hidden = incoming + grad_hidden_norm
    grad_branch = grad_hidden.astype(jnp.bfloat16)
    grad_heads_out = jnp.einsum(
        "td,th->dh", grad_branch, attended, preferred_element_type=jnp.float32
    )
    grad_attended = jnp.dot(grad_branch, heads_out, preferred_element_type=jnp.float32).astype(
        jnp.bfloat16
    )
    grad_attended = grad_attended.reshape(token_count, KV_HEADS, group_size, HEAD_DIM)
    weight_full = jnp.exp(masked_scores(queries, key_rows, allowed) - log_total)
    grad_weights = jnp.einsum(
        "qkgd,pkd->kgqp", grad_attended, value_rows, preferred_element_type=jnp.float32
    )
    spread = jnp.sum(weight_full * grad_weights, axis=-1, keepdims=True)
    grad_scores = (weight_full * (grad_weights - spread)).astype(jnp.bfloat16)
    grad_queries = (
        jnp.einsum("kgqp,pkd->qkgd", grad_scores, key_rows, preferred_element_type=jnp.float32)
        * SCALE
    )
    grad_keys = (
        jnp.einsum("kgqp,qkgd->pkd", grad_scores, queries, preferred_element_type=jnp.float32)
        * SCALE
    )
    grad_values = jnp.einsum(
        "kgqp,qkgd->pkd",
        weight_full.astype(jnp.bfloat16),
        grad_attended,
        preferred_element_type=jnp.float32,
    )
    grad_projected = jnp.concatenate(
        [
            unrotate(
                grad_queries.reshape(token_count, HEADS, HEAD_DIM), cosine, sine_table
            ).reshape(token_count, query_end),
            unrotate(grad_keys, cosine, sine_table).reshape(token_count, KV_HEADS * HEAD_DIM),
            grad_values.reshape(token_count, KV_HEADS * HEAD_DIM),
        ],
        axis=1,
    ).astype(jnp.bfloat16)
    grad_heads_in = jnp.einsum(
        "td,tc->dc", first_in, grad_projected, preferred_element_type=jnp.float32
    )
    grad_first = jnp.einsum(
        "tc,dc->td", grad_projected, heads_in, preferred_element_type=jnp.float32
    )
    grad_tokens_norm, grad_gain_one = rms_back(grad_first, token_rows, factor_one, norm_gains[:, 0])
    token_grad = grad_hidden + grad_tokens_norm
    head_grads = jnp.concatenate(
        [
            grad_heads_in,
            grad_heads_out,
            grad_router,
            grad_gain_one[:, None],
            grad_gain_two[:, None],
        ],
        axis=1,
    ).astype(jnp.bfloat16)
    head_sums = lax.psum_scatter(
        head_grads, ("dp", "expert"), scatter_dimension=0, tiled=True
    ).astype(jnp.float32)
    cut_in = grad_heads_in.shape[1]
    cut_out = cut_in + grad_heads_out.shape[1]
    summed = (
        head_sums[:, :cut_in],
        head_sums[:, cut_in:cut_out],
        head_sums[:, cut_out : cut_out + experts],
        head_sums[:, cut_out + experts :],
    )
    expert_sums = (
        lax.psum_scatter(
            grad_expert_in.astype(jnp.bfloat16), "dp", scatter_dimension=1, tiled=True
        ).astype(jnp.float32),
        lax.psum_scatter(
            grad_expert_out.astype(jnp.bfloat16), "dp", scatter_dimension=1, tiled=True
        ).astype(jnp.float32),
    )
    shard_rows = model_width // lax.axis_size(("dp", "expert"))
    gains_share = lax.dynamic_slice_in_dim(
        norm_gains, lax.axis_index(("dp", "expert")) * shard_rows, shard_rows, 0
    )
    gains_new = update(summed[3], gains_share, gains_moment, gains_average)
    inproj_new = update(summed[0], heads_in_master, heads_in_moment, heads_in_average)
    outproj_new = update(summed[1], heads_out_master, heads_out_moment, heads_out_average)
    router_new = update(summed[2], router_master, router_moment, router_average)
    upper_new = update(expert_sums[0], expert_in_master, expert_in_moment, expert_in_average)
    lower_new = update(expert_sums[1], expert_out_master, expert_out_moment, expert_out_average)
    return (
        output,
        token_grad,
        gains_new[0],
        gains_new[1],
        gains_new[2],
        inproj_new[0],
        inproj_new[1],
        inproj_new[2],
        outproj_new[0],
        outproj_new[1],
        outproj_new[2],
        router_new[0],
        router_new[1],
        router_new[2],
        upper_new[0],
        upper_new[1],
        upper_new[2],
        lower_new[0],
        lower_new[1],
        lower_new[2],
    )


def solution(mesh):
    return jax.shard_map(
        body,
        mesh=mesh,
        in_specs=(
            P(("dp", "expert"), None),
            P(("dp", "expert"), None),
            P(("dp", "expert"), None),
            P(("dp", "expert"), None),
            P(),
            P(("dp", "expert"), None),
            P(("dp", "expert"), None),
            P(),
            P(("dp", "expert"), None),
            P(("dp", "expert"), None),
            P(("dp", "expert"), None),
            P(),
            P(("dp", "expert"), None),
            P(("dp", "expert"), None),
            P(("dp", "expert"), None),
            P(),
            P(("dp", "expert"), None),
            P(("dp", "expert"), None),
            P(("dp", "expert"), None),
            P("expert", None, None),
            P("expert", "dp", None),
            P("expert", "dp", None),
            P("expert", "dp", None),
            P("expert", None, None),
            P("expert", "dp", None),
            P("expert", "dp", None),
            P("expert", "dp", None),
        ),
        out_specs=(
            P(("dp", "expert"), None),
            P(("dp", "expert"), None),
            P(("dp", "expert"), None),
            P(("dp", "expert"), None),
            P(("dp", "expert"), None),
            P(("dp", "expert"), None),
            P(("dp", "expert"), None),
            P(("dp", "expert"), None),
            P(("dp", "expert"), None),
            P(("dp", "expert"), None),
            P(("dp", "expert"), None),
            P(("dp", "expert"), None),
            P(("dp", "expert"), None),
            P(("dp", "expert"), None),
            P("expert", "dp", None),
            P("expert", "dp", None),
            P("expert", "dp", None),
            P("expert", "dp", None),
            P("expert", "dp", None),
            P("expert", "dp", None),
        ),
        check_vma=False,
    )
```

```python
import functools

import jax
import jax.numpy as jnp
from jax import lax
from jax.experimental import pallas as pl
from jax.experimental.pallas import tpu as pltpu
from jax.sharding import PartitionSpec as P

HEADS = 16
KV_HEADS = 8
HEAD_DIM = 64


EPS = 1e-06
SCALE = 0.015625
THETA = 10000.0
MOMENTUM = 0.9
DECAY = 0.8
RATE = 0.001
HIGHEST = lax.Precision.HIGHEST


def layout(labels_row, prompt_len):
    places = jnp.arange(prompt_len + labels_row.shape[0], dtype=jnp.int32)
    earlier = jnp.sum((labels_row[None, :] < labels_row[:, None]).astype(jnp.int32), axis=1)
    offset = places[prompt_len:] - prompt_len - earlier
    positions = jnp.concatenate([places[:prompt_len], prompt_len + offset]).astype(jnp.float32)
    labels = jnp.concatenate([jnp.full((prompt_len,), -1, jnp.int32), labels_row])
    allowed = (places[None, :] <= places[:, None]) & (
        (places[None, :] < prompt_len) | (labels[None, :] == labels[:, None])
    )
    return (positions, allowed)


def rope_tables(positions):
    middle = HEAD_DIM // 2
    frequency = THETA ** (-2.0 * jnp.arange(middle, dtype=jnp.float32) / HEAD_DIM)
    angles = positions[:, None] * frequency[None, :]
    angles = jnp.concatenate([angles, angles], axis=1)
    return (jnp.cos(angles)[:, None, :], jnp.sin(angles)[:, None, :])


def rotate(values, cosine, sine_table):
    middle = values.shape[-1] // 2
    turned = jnp.concatenate([-values[..., middle:], values[..., :middle]], axis=-1)
    return values * cosine + turned * sine_table


def unrotate(gradient, cosine, sine_table):
    middle = gradient.shape[-1] // 2
    shifted = gradient * sine_table
    return gradient * cosine + jnp.concatenate(
        [shifted[..., middle:], -shifted[..., :middle]], axis=-1
    )


def masked_scores(queries, key_rows, allowed):
    products = (
        jnp.einsum("qkgd,pkd->kgqp", queries, key_rows, preferred_element_type=jnp.float32) * SCALE
    )
    return jnp.where(allowed[None, None], products, -1e30)


def rms_parts(values, gain):
    factor = lax.rsqrt(jnp.mean(values * values, axis=-1, keepdims=True) + EPS)
    return (values * factor * gain, factor)


def rms_back(incoming, values, factor, gain):
    normed = values * factor
    gain_grad = jnp.sum(incoming * normed, axis=0)
    weighted = incoming * gain
    input_grad = factor * (weighted - normed * jnp.mean(weighted * normed, axis=-1, keepdims=True))
    return (input_grad, gain_grad)


def update(gradient, master, moment, average):
    moment_next = MOMENTUM * moment + gradient
    master_next = master - RATE * (gradient + MOMENTUM * moment_next)
    return (master_next, moment_next, DECAY * average + (1.0 - DECAY) * master_next)


F32 = jnp.float32
BF16 = jnp.bfloat16
MESH = pl.DeviceIdType.MESH
VMEM_MOST = 60 * 2**20


def contract(left, right, left_axis, right_axis):
    return lax.dot_general(
        left, right, (((left_axis,), (right_axis,)), ((), ())), preferred_element_type=F32
    )


def visit_order(line):
    return [sorted(range(line), key=lambda s: (abs(s - z), s)) for z in range(line)]


def pick(table, row, column):
    value = jnp.int32(table[0][0])
    for r in range(len(table)):
        for c in range(len(table[0])):
            value = jnp.where((row == r) & (column == c), jnp.int32(table[r][c]), value)
    return value


def bank_kernel(
    line,
    rows_hbm,
    cots_hbm,
    gates_hbm,
    up_hbm,
    down_hbm,
    mix_hbm,
    back_hbm,
    gate_grads_hbm,
    gated_hbm,
    inner_hbm,
    rows_all_hbm,
    rows,
    cots,
    gates,
    gate_grads,
    gate_grads_sent,
    up,
    down,
    mix_sum,
    back_sum,
    stage,
    gated,
    inner,
    columns,
    row_send,
    row_recv,
    gate_send,
    gate_recv,
    weight_sem,
    local_sem,
    out_sem,
    grad_send,
    grad_recv,
):
    dp = lax.axis_index("dp")
    z = lax.axis_index("expert")
    experts, width, ff_width = down.shape

    def weight_copies(e):
        return (
            pltpu.make_async_copy(up_hbm.at[e], up.at[e], weight_sem.at[0, e]),
            pltpu.make_async_copy(down_hbm.at[e], down.at[e], weight_sem.at[1, e]),
        )

    for e in range(experts):
        for copy in weight_copies(e):
            copy.start()
    own_rows = pltpu.make_async_copy(rows_hbm, rows.at[z], local_sem.at[0])
    own_rows.start()
    all_cots = pltpu.make_async_copy(cots_hbm, cots, local_sem.at[1])
    all_cots.start()
    own_gates = pltpu.make_async_copy(gates_hbm.at[z], gates.at[z], local_sem.at[2])
    own_gates.start()

    barrier = pltpu.get_barrier_semaphore()
    for step in range(1, line):
        pl.semaphore_signal(
            barrier, inc=1, device_id=(dp, lax.rem(z + step, line)), device_id_type=MESH
        )
    pl.semaphore_wait(barrier, line - 1)

    def row_copy(source, block, sem, target):
        return pltpu.make_async_remote_copy(
            src_ref=source,
            dst_ref=rows.at[block],
            send_sem=row_send.at[sem],
            recv_sem=row_recv.at[block],
            device_id=(dp, target),
            device_id_type=MESH,
        )

    @pl.when(z < line - 1)
    def _():
        row_copy(rows_hbm, z, line, z + 1).start()

    @pl.when(z > 0)
    def _():
        row_copy(rows_hbm, z, line + 1, z - 1).start()

    def gate_copy(step):
        peer = lax.rem(z + step, line)
        return pltpu.make_async_remote_copy(
            src_ref=gates_hbm.at[peer],
            dst_ref=gates.at[z],
            send_sem=gate_send.at[step],
            recv_sem=gate_recv.at[step],
            device_id=(dp, peer),
            device_id_type=MESH,
        )

    for step in range(1, line):
        gate_copy(step).start()
    own_rows.wait()
    all_cots.wait()
    own_gates.wait()
    for step in range(1, line):
        gate_copy(step).wait()

    order = visit_order(line)

    def out_copies(slot, block):
        return (
            pltpu.make_async_copy(stage.at[slot, 0], mix_hbm.at[block], out_sem.at[slot, 0]),
            pltpu.make_async_copy(stage.at[slot, 1], back_hbm.at[block], out_sem.at[slot, 1]),
            pltpu.make_async_copy(gated.at[slot], gated_hbm.at[block], out_sem.at[slot, 2]),
            pltpu.make_async_copy(inner.at[slot], inner_hbm.at[block], out_sem.at[slot, 3]),
        )

    def grad_copy(block, step):
        return pltpu.make_async_remote_copy(
            src_ref=gate_grads_sent.at[block],
            dst_ref=gate_grads.at[z],
            send_sem=grad_send.at[block],
            recv_sem=grad_recv.at[z],
            device_id=(dp, block),
            device_id_type=MESH,
        )

    def visit(k, _):
        block = pick(order, z, k)
        slot = lax.rem(k, 2)
        apart = jnp.abs(block - z)
        previous = pick(order, z, jnp.maximum(k - 1, 0))
        first = (k > 0) & (apart != jnp.abs(previous - z))
        below = z - apart
        above = z + apart

        @pl.when(first & (below >= 0))
        def _():
            low = jnp.maximum(below, 0)
            row_copy(rows_hbm, low, low, z).wait_recv()

            @pl.when(z < line - 1)
            def _():
                row_copy(rows.at[low], low, low, z + 1).start()

        @pl.when(first & (above < line))
        def _():
            high = jnp.minimum(above, line - 1)
            row_copy(rows_hbm, high, high, z).wait_recv()

            @pl.when(z > 0)
            def _():
                row_copy(rows.at[high], high, high, z - 1).start()

        @pl.when(k >= 2)
        def _():
            for copy in out_copies(slot, pick(order, z, jnp.maximum(k - 2, 0))):
                copy.wait()

        mix_sum[...] = jnp.zeros_like(mix_sum)
        back_sum[...] = jnp.zeros_like(back_sum)
        columns[...] = jnp.zeros_like(columns)
        gate_columns = gates[block].T
        lane = lax.broadcasted_iota(jnp.int32, gate_columns.shape, 1)
        wide_lane = lax.broadcasted_iota(jnp.int32, columns.shape, 1)

        def expert(e, _):
            @pl.when(k == 0)
            def _():
                for copy in weight_copies(e):
                    copy.wait()

            gate_col = jnp.sum(jnp.where(lane == e, gate_columns, 0.0), axis=1, keepdims=True)
            both = contract(rows[block], up[e], 1, 0)
            returned = contract(cots[block], down[e], 1, 0)
            gate_part = both[:, :ff_width]
            up_part = both[:, ff_width:]
            sigmoid_gate = jax.nn.sigmoid(gate_part)
            silu_gate = gate_part * sigmoid_gate
            active = silu_gate * up_part
            gated_part = (active * gate_col).astype(BF16)
            gated[slot, :, pl.ds(pl.multiple_of(e * ff_width, ff_width), ff_width)] = gated_part
            mix_sum[...] += contract(gated_part, down[e], 1, 1)
            gate_grad = jnp.sum(active * returned, axis=1, keepdims=True)
            columns[...] = jnp.where(wide_lane == e, gate_grad, columns[...])
            scaled = returned * gate_col
            grad_gate = scaled * up_part * (sigmoid_gate * (1.0 + gate_part * (1.0 - sigmoid_gate)))
            grad_up = scaled * silu_gate
            grads = jnp.concatenate([grad_gate, grad_up], axis=1).astype(BF16)
            inner[slot, :, pl.ds(pl.multiple_of(e * 2 * ff_width, ff_width), 2 * ff_width)] = grads
            back_sum[...] += contract(grads, up[e], 1, 1)
            return 0

        lax.fori_loop(0, experts, expert, 0)
        stage[slot, 0] = mix_sum[...].astype(BF16)
        stage[slot, 1] = back_sum[...].astype(BF16)
        for copy in out_copies(slot, block):
            copy.start()
        gate_grads_sent[block] = columns[...].T[: gate_grads.shape[1]]

        @pl.when(block == z)
        def _():
            gate_grads[z] = gate_grads_sent[z]

        @pl.when(block != z)
        def _():
            grad_copy(block, 0).start()

        return 0

    lax.fori_loop(0, line, visit, 0)
    for k in (line - 2, line - 1):
        for copy in out_copies(k % 2, pick(order, z, k)):
            copy.wait()

    @pl.when(z < line - 1)
    def _():
        row_copy(rows_hbm, z, line, z + 1).wait_send()

    @pl.when(z > 0)
    def _():
        row_copy(rows_hbm, z, line + 1, z - 1).wait_send()

    for s in range(line):

        @pl.when(((s < z) & (z < line - 1)) | ((s > z) & (z > 0)))
        def _(s=s):
            row_copy(rows_hbm, s, s, z).wait_send()

        @pl.when(s != z)
        def _(s=s):
            grad_copy(s, 0).wait_send()
            pltpu.make_async_remote_copy(
                src_ref=gate_grads_sent.at[s],
                dst_ref=gate_grads.at[s],
                send_sem=grad_send.at[s],
                recv_sem=grad_recv.at[s],
                device_id=(dp, z),
                device_id_type=MESH,
            ).wait_recv()

    last = (
        pltpu.make_async_copy(rows, rows_all_hbm, local_sem.at[0]),
        pltpu.make_async_copy(gate_grads, gate_grads_hbm, local_sem.at[1]),
    )
    for copy in last:
        copy.start()
    for copy in last:
        copy.wait()


def bank(rows, cots, gates, up, down, line):
    tokens, width = rows.shape
    experts, _, ff_width = down.shape
    shape = jax.ShapeDtypeStruct
    held = gates.shape[1:]
    anywhere = pl.BlockSpec(memory_space=pl.ANY)
    work = 10 * line * tokens * experts * width * ff_width
    return pl.pallas_call(
        functools.partial(bank_kernel, line),
        out_shape=(
            shape((line, tokens, width), BF16),
            shape((line, tokens, width), BF16),
            shape((line,) + held, F32),
            shape((line, tokens, experts * ff_width), BF16),
            shape((line, tokens, experts * 2 * ff_width), BF16),
            shape((line, tokens, width), BF16),
        ),
        in_specs=[anywhere] * 5,
        out_specs=(anywhere,) * 6,
        scratch_shapes=[
            pltpu.VMEM((line, tokens, width), BF16),
            pltpu.VMEM((line, tokens, width), BF16),
            pltpu.VMEM((line,) + held, F32),
            pltpu.VMEM((line,) + held, F32),
            pltpu.VMEM((line,) + held, F32),
            pltpu.VMEM(up.shape, BF16),
            pltpu.VMEM(down.shape, BF16),
            pltpu.VMEM((tokens, width), F32),
            pltpu.VMEM((tokens, width), F32),
            pltpu.VMEM((2, 2, tokens, width), BF16),
            pltpu.VMEM((2, tokens, experts * ff_width), BF16),
            pltpu.VMEM((2, tokens, experts * 2 * ff_width), BF16),
            pltpu.VMEM((tokens, 128), F32),
            pltpu.SemaphoreType.DMA((line + 2,)),
            pltpu.SemaphoreType.DMA((line,)),
            pltpu.SemaphoreType.DMA((line,)),
            pltpu.SemaphoreType.DMA((line,)),
            pltpu.SemaphoreType.DMA((2, experts)),
            pltpu.SemaphoreType.DMA((3,)),
            pltpu.SemaphoreType.DMA((2, 4)),
            pltpu.SemaphoreType.DMA((line,)),
            pltpu.SemaphoreType.DMA((line,)),
        ],
        compiler_params=pltpu.CompilerParams(
            collective_id=1, has_side_effects=True, vmem_limit_bytes=VMEM_MOST
        ),
        cost_estimate=pl.CostEstimate(flops=work, bytes_accessed=2**26, transcendentals=0),
    )(rows, cots, gates, up, down)


def weight_grads_kernel(rows, cots, gated, inner, up_grad, down_grad):
    step = 256
    for at in range(0, rows.shape[1], step):
        up_grad[0, at : at + step] = contract(rows[:, at : at + step], inner[...], 0, 0).astype(BF16)
        down_grad[0, at : at + step] = contract(cots[:, at : at + step], gated[...], 0, 0).astype(
            BF16
        )


def weight_grads(rows, cots, gated, inner, experts):
    tokens, width = rows.shape
    ff_width = gated.shape[1] // experts
    whole = pl.BlockSpec((tokens, width), lambda e: (0, 0))
    return pl.pallas_call(
        weight_grads_kernel,
        grid=(experts,),
        out_shape=(
            jax.ShapeDtypeStruct((experts, width, 2 * ff_width), BF16),
            jax.ShapeDtypeStruct((experts, width, ff_width), BF16),
        ),
        in_specs=[
            whole,
            whole,
            pl.BlockSpec((tokens, ff_width), lambda e: (0, e)),
            pl.BlockSpec((tokens, 2 * ff_width), lambda e: (0, e)),
        ],
        out_specs=(
            pl.BlockSpec((1, width, 2 * ff_width), lambda e: (e, 0, 0)),
            pl.BlockSpec((1, width, ff_width), lambda e: (e, 0, 0)),
        ),
        compiler_params=pltpu.CompilerParams(vmem_limit_bytes=VMEM_MOST),
        cost_estimate=pl.CostEstimate(
            flops=6 * tokens * width * experts * ff_width,
            bytes_accessed=2 * tokens * (2 * width + 3 * experts * ff_width)
            + 6 * experts * width * ff_width,
            transcendentals=0,
        ),
    )(rows, cots, gated, inner)


def body(
    tokens,
    cotangent,
    routes,
    cont_ids,
    norm_gains,
    gains_moment,
    gains_average,
    heads_in,
    heads_in_master,
    heads_in_moment,
    heads_in_average,
    heads_out,
    heads_out_master,
    heads_out_moment,
    heads_out_average,
    router,
    router_master,
    router_moment,
    router_average,
    expert_in,
    expert_in_master,
    expert_in_moment,
    expert_in_average,
    expert_out,
    expert_out_master,
    expert_out_moment,
    expert_out_average,
):
    token_count, model_width = tokens.shape
    local_experts = expert_in.shape[0]
    peer_count = lax.axis_size("expert")
    experts = local_experts * peer_count
    group_size = HEADS // KV_HEADS
    query_end = HEADS * HEAD_DIM
    key_end = query_end + KV_HEADS * HEAD_DIM
    token_rows = tokens.astype(jnp.float32)
    normed_one, factor_one = rms_parts(token_rows, norm_gains[:, 0])
    first_in = normed_one.astype(jnp.bfloat16)
    projected = jnp.dot(first_in, heads_in, preferred_element_type=jnp.float32)
    positions, allowed = layout(cont_ids[0], token_count - cont_ids.shape[1])
    cosine, sine_table = rope_tables(positions)
    queries = rotate(
        projected[:, :query_end].reshape(token_count, HEADS, HEAD_DIM), cosine, sine_table
    )
    queries = queries.astype(jnp.bfloat16).reshape(token_count, KV_HEADS, group_size, HEAD_DIM)
    key_rows = rotate(
        projected[:, query_end:key_end].reshape(token_count, KV_HEADS, HEAD_DIM), cosine, sine_table
    ).astype(jnp.bfloat16)
    value_rows = (
        projected[:, key_end:].reshape(token_count, KV_HEADS, HEAD_DIM).astype(jnp.bfloat16)
    )
    scores = masked_scores(queries, key_rows, allowed)
    row_peak = jnp.max(scores, axis=-1, keepdims=True)
    log_total = row_peak + jnp.log(jnp.sum(jnp.exp(scores - row_peak), axis=-1, keepdims=True))
    weights = jnp.exp(scores - log_total).astype(jnp.bfloat16)
    attended = jnp.einsum("kgqp,pkd->qkgd", weights, value_rows, preferred_element_type=jnp.float32)
    attended = attended.reshape(token_count, query_end).astype(jnp.bfloat16)
    branch = jnp.einsum("th,dh->td", attended, heads_out, preferred_element_type=jnp.float32)
    hidden = token_rows + branch
    normed_two, factor_two = rms_parts(hidden, norm_gains[:, 1])
    second_in = normed_two.astype(jnp.bfloat16)
    logits = jnp.dot(second_in, router, preferred_element_type=jnp.float32)
    named = jnp.any(
        routes[:, :, None] == jnp.arange(experts, dtype=jnp.int32)[None, None, :], axis=1
    )
    peak = jnp.max(jnp.where(named, logits, -jnp.inf), axis=1, keepdims=True)
    powers = jnp.where(named, jnp.exp(logits - peak), 0.0)
    gates = powers / jnp.sum(powers, axis=1, keepdims=True)
    incoming = cotangent.astype(jnp.float32)
    cots_all = lax.all_gather(cotangent, "expert", axis=0, tiled=False)
    padded = -local_experts % 8
    gate_rows = jnp.pad(
        gates.T.reshape(peer_count, local_experts, token_count), ((0, 0), (0, padded), (0, 0))
    )
    mix_part, grad_part, gate_grads, gated, grad_gate_up, rows_all = bank(
        second_in, cots_all, gate_rows, expert_in, expert_out, peer_count
    )
    grad_second = lax.psum_scatter(
        grad_part.reshape(peer_count * token_count, model_width),
        "expert",
        scatter_dimension=0,
        tiled=True,
    ).astype(jnp.float32)
    mixture = lax.psum_scatter(
        mix_part.reshape(peer_count * token_count, model_width),
        "expert",
        scatter_dimension=0,
        tiled=True,
    ).astype(jnp.float32)
    grad_expert_in, grad_expert_out = weight_grads(
        rows_all.reshape(peer_count * token_count, model_width),
        cots_all.reshape(peer_count * token_count, model_width),
        gated.reshape(peer_count * token_count, -1),
        grad_gate_up.reshape(peer_count * token_count, -1),
        local_experts,
    )
    output = (hidden + mixture).astype(jnp.bfloat16)
    grad_gates = gate_grads[:, :local_experts].reshape(experts, token_count).T
    grad_logits = gates * (grad_gates - jnp.sum(gates * grad_gates, axis=1, keepdims=True))
    grad_router = jnp.dot(second_in.astype(jnp.float32).T, grad_logits, precision=HIGHEST)
    grad_second = grad_second + jnp.dot(
        grad_logits, router.astype(jnp.float32).T, precision=HIGHEST
    )
    grad_hidden_norm, grad_gain_two = rms_back(grad_second, hidden, factor_two, norm_gains[:, 1])
    grad_hidden = incoming + grad_hidden_norm
    grad_branch = grad_hidden.astype(jnp.bfloat16)
    grad_heads_out = jnp.einsum(
        "td,th->dh", grad_branch, attended, preferred_element_type=jnp.float32
    )
    grad_attended = jnp.dot(grad_branch, heads_out, preferred_element_type=jnp.float32).astype(
        jnp.bfloat16
    )
    grad_attended = grad_attended.reshape(token_count, KV_HEADS, group_size, HEAD_DIM)
    weight_full = jnp.exp(masked_scores(queries, key_rows, allowed) - log_total)
    grad_weights = jnp.einsum(
        "qkgd,pkd->kgqp", grad_attended, value_rows, preferred_element_type=jnp.float32
    )
    spread = jnp.sum(weight_full * grad_weights, axis=-1, keepdims=True)
    grad_scores = (weight_full * (grad_weights - spread)).astype(jnp.bfloat16)
    grad_queries = (
        jnp.einsum("kgqp,pkd->qkgd", grad_scores, key_rows, preferred_element_type=jnp.float32)
        * SCALE
    )
    grad_keys = (
        jnp.einsum("kgqp,qkgd->pkd", grad_scores, queries, preferred_element_type=jnp.float32)
        * SCALE
    )
    grad_values = jnp.einsum(
        "kgqp,qkgd->pkd",
        weight_full.astype(jnp.bfloat16),
        grad_attended,
        preferred_element_type=jnp.float32,
    )
    grad_projected = jnp.concatenate(
        [
            unrotate(
                grad_queries.reshape(token_count, HEADS, HEAD_DIM), cosine, sine_table
            ).reshape(token_count, query_end),
            unrotate(grad_keys, cosine, sine_table).reshape(token_count, KV_HEADS * HEAD_DIM),
            grad_values.reshape(token_count, KV_HEADS * HEAD_DIM),
        ],
        axis=1,
    ).astype(jnp.bfloat16)
    grad_heads_in = jnp.einsum(
        "td,tc->dc", first_in, grad_projected, preferred_element_type=jnp.float32
    )
    grad_first = jnp.einsum(
        "tc,dc->td", grad_projected, heads_in, preferred_element_type=jnp.float32
    )
    grad_tokens_norm, grad_gain_one = rms_back(grad_first, token_rows, factor_one, norm_gains[:, 0])
    token_grad = grad_hidden + grad_tokens_norm
    head_grads = jnp.concatenate(
        [
            grad_heads_in,
            grad_heads_out,
            grad_router,
            grad_gain_one[:, None],
            grad_gain_two[:, None],
        ],
        axis=1,
    ).astype(jnp.bfloat16)
    head_sums = lax.psum_scatter(
        head_grads, ("dp", "expert"), scatter_dimension=0, tiled=True
    ).astype(jnp.float32)
    cut_in = grad_heads_in.shape[1]
    cut_out = cut_in + grad_heads_out.shape[1]
    summed = (
        head_sums[:, :cut_in],
        head_sums[:, cut_in:cut_out],
        head_sums[:, cut_out : cut_out + experts],
        head_sums[:, cut_out + experts :],
    )
    expert_sums = (
        lax.psum_scatter(
            grad_expert_in.astype(jnp.bfloat16), "dp", scatter_dimension=1, tiled=True
        ).astype(jnp.float32),
        lax.psum_scatter(
            grad_expert_out.astype(jnp.bfloat16), "dp", scatter_dimension=1, tiled=True
        ).astype(jnp.float32),
    )
    shard_rows = model_width // lax.axis_size(("dp", "expert"))
    gains_share = lax.dynamic_slice_in_dim(
        norm_gains, lax.axis_index(("dp", "expert")) * shard_rows, shard_rows, 0
    )
    gains_new = update(summed[3], gains_share, gains_moment, gains_average)
    inproj_new = update(summed[0], heads_in_master, heads_in_moment, heads_in_average)
    outproj_new = update(summed[1], heads_out_master, heads_out_moment, heads_out_average)
    router_new = update(summed[2], router_master, router_moment, router_average)
    upper_new = update(expert_sums[0], expert_in_master, expert_in_moment, expert_in_average)
    lower_new = update(expert_sums[1], expert_out_master, expert_out_moment, expert_out_average)
    return (
        output,
        token_grad,
        gains_new[0],
        gains_new[1],
        gains_new[2],
        inproj_new[0],
        inproj_new[1],
        inproj_new[2],
        outproj_new[0],
        outproj_new[1],
        outproj_new[2],
        router_new[0],
        router_new[1],
        router_new[2],
        upper_new[0],
        upper_new[1],
        upper_new[2],
        lower_new[0],
        lower_new[1],
        lower_new[2],
    )


def solution(mesh):
    return jax.shard_map(
        body,
        mesh=mesh,
        in_specs=(
            P(("dp", "expert"), None),
            P(("dp", "expert"), None),
            P(("dp", "expert"), None),
            P(("dp", "expert"), None),
            P(),
            P(("dp", "expert"), None),
            P(("dp", "expert"), None),
            P(),
            P(("dp", "expert"), None),
            P(("dp", "expert"), None),
            P(("dp", "expert"), None),
            P(),
            P(("dp", "expert"), None),
            P(("dp", "expert"), None),
            P(("dp", "expert"), None),
            P(),
            P(("dp", "expert"), None),
            P(("dp", "expert"), None),
            P(("dp", "expert"), None),
            P("expert", None, None),
            P("expert", "dp", None),
            P("expert", "dp", None),
            P("expert", "dp", None),
            P("expert", None, None),
            P("expert", "dp", None),
            P("expert", "dp", None),
            P("expert", "dp", None),
        ),
        out_specs=(
            P(("dp", "expert"), None),
            P(("dp", "expert"), None),
            P(("dp", "expert"), None),
            P(("dp", "expert"), None),
            P(("dp", "expert"), None),
            P(("dp", "expert"), None),
            P(("dp", "expert"), None),
            P(("dp", "expert"), None),
            P(("dp", "expert"), None),
            P(("dp", "expert"), None),
            P(("dp", "expert"), None),
            P(("dp", "expert"), None),
            P(("dp", "expert"), None),
            P(("dp", "expert"), None),
            P("expert", "dp", None),
            P("expert", "dp", None),
            P("expert", "dp", None),
            P("expert", "dp", None),
            P("expert", "dp", None),
            P("expert", "dp", None),
        ),
        check_vma=False,
    )
```

```python
import functools

import jax
import jax.numpy as jnp
from jax import lax
from jax.experimental import pallas as pl
from jax.experimental.pallas import tpu as pltpu
from jax.sharding import PartitionSpec as P

HEADS = 16
KV_HEADS = 8
HEAD_DIM = 64


EPS = 1e-06
SCALE = 0.015625
THETA = 10000.0
MOMENTUM = 0.9
DECAY = 0.8
RATE = 0.001
HIGHEST = lax.Precision.HIGHEST


def layout(labels_row, prompt_len):
    places = jnp.arange(prompt_len + labels_row.shape[0], dtype=jnp.int32)
    earlier = jnp.sum((labels_row[None, :] < labels_row[:, None]).astype(jnp.int32), axis=1)
    offset = places[prompt_len:] - prompt_len - earlier
    positions = jnp.concatenate([places[:prompt_len], prompt_len + offset]).astype(jnp.float32)
    labels = jnp.concatenate([jnp.full((prompt_len,), -1, jnp.int32), labels_row])
    allowed = (places[None, :] <= places[:, None]) & (
        (places[None, :] < prompt_len) | (labels[None, :] == labels[:, None])
    )
    return (positions, allowed)


def rope_tables(positions):
    middle = HEAD_DIM // 2
    frequency = THETA ** (-2.0 * jnp.arange(middle, dtype=jnp.float32) / HEAD_DIM)
    angles = positions[:, None] * frequency[None, :]
    angles = jnp.concatenate([angles, angles], axis=1)
    return (jnp.cos(angles)[:, None, :], jnp.sin(angles)[:, None, :])


def rotate(values, cosine, sine_table):
    middle = values.shape[-1] // 2
    turned = jnp.concatenate([-values[..., middle:], values[..., :middle]], axis=-1)
    return values * cosine + turned * sine_table


def unrotate(gradient, cosine, sine_table):
    middle = gradient.shape[-1] // 2
    shifted = gradient * sine_table
    return gradient * cosine + jnp.concatenate(
        [shifted[..., middle:], -shifted[..., :middle]], axis=-1
    )


def masked_scores(queries, key_rows, allowed):
    products = (
        jnp.einsum("qkgd,pkd->kgqp", queries, key_rows, preferred_element_type=jnp.float32) * SCALE
    )
    return jnp.where(allowed[None, None], products, -1e30)


def rms_parts(values, gain):
    factor = lax.rsqrt(jnp.mean(values * values, axis=-1, keepdims=True) + EPS)
    return (values * factor * gain, factor)


def rms_back(incoming, values, factor, gain):
    normed = values * factor
    gain_grad = jnp.sum(incoming * normed, axis=0)
    weighted = incoming * gain
    input_grad = factor * (weighted - normed * jnp.mean(weighted * normed, axis=-1, keepdims=True))
    return (input_grad, gain_grad)


def update(gradient, master, moment, average):
    moment_next = MOMENTUM * moment + gradient
    master_next = master - RATE * (gradient + MOMENTUM * moment_next)
    return (master_next, moment_next, DECAY * average + (1.0 - DECAY) * master_next)


F32 = jnp.float32
BF16 = jnp.bfloat16
MESH = pl.DeviceIdType.MESH
VMEM_MOST = 60 * 2**20


def contract(left, right, left_axis, right_axis):
    return lax.dot_general(
        left, right, (((left_axis,), (right_axis,)), ((), ())), preferred_element_type=F32
    )


def visit_order(line):
    return [sorted(range(line), key=lambda s: (abs(s - z), s)) for z in range(line)]


def pick(table, row, column):
    value = jnp.int32(table[0][0])
    for r in range(len(table)):
        for c in range(len(table[0])):
            value = jnp.where((row == r) & (column == c), jnp.int32(table[r][c]), value)
    return value


def bank_kernel(
    line,
    rows_hbm,
    cots_hbm,
    gates_hbm,
    up_hbm,
    down_hbm,
    mix_hbm,
    back_hbm,
    gate_grads_hbm,
    gated_hbm,
    inner_hbm,
    rows_all_hbm,
    rows,
    cots,
    gates,
    gate_grads,
    gate_grads_sent,
    up,
    down,
    mix_sum,
    back_sum,
    stage,
    gated,
    inner,
    columns,
    row_send,
    row_recv,
    gate_send,
    gate_recv,
    weight_sem,
    local_sem,
    out_sem,
    grad_send,
    grad_recv,
):
    dp = lax.axis_index("dp")
    z = lax.axis_index("expert")
    experts, width, ff_width = down.shape

    def weight_copies(e):
        return (
            pltpu.make_async_copy(up_hbm.at[e], up.at[e], weight_sem.at[0, e]),
            pltpu.make_async_copy(down_hbm.at[e], down.at[e], weight_sem.at[1, e]),
        )

    for e in range(experts):
        for copy in weight_copies(e):
            copy.start()
    own_rows = pltpu.make_async_copy(rows_hbm, rows.at[z], local_sem.at[0])
    own_rows.start()
    all_cots = pltpu.make_async_copy(cots_hbm, cots, local_sem.at[1])
    all_cots.start()
    own_gates = pltpu.make_async_copy(gates_hbm.at[z], gates.at[z], local_sem.at[2])
    own_gates.start()

    barrier = pltpu.get_barrier_semaphore()
    for step in range(1, line):
        pl.semaphore_signal(
            barrier, inc=1, device_id=(dp, lax.rem(z + step, line)), device_id_type=MESH
        )
    pl.semaphore_wait(barrier, line - 1)

    def row_copy(source, block, sem, target):
        return pltpu.make_async_remote_copy(
            src_ref=source,
            dst_ref=rows.at[block],
            send_sem=row_send.at[sem],
            recv_sem=row_recv.at[block],
            device_id=(dp, target),
            device_id_type=MESH,
        )

    @pl.when(z < line - 1)
    def _():
        row_copy(rows_hbm, z, line, z + 1).start()

    @pl.when(z > 0)
    def _():
        row_copy(rows_hbm, z, line + 1, z - 1).start()

    def gate_copy(step):
        peer = lax.rem(z + step, line)
        return pltpu.make_async_remote_copy(
            src_ref=gates_hbm.at[peer],
            dst_ref=gates.at[z],
            send_sem=gate_send.at[step],
            recv_sem=gate_recv.at[step],
            device_id=(dp, peer),
            device_id_type=MESH,
        )

    for step in range(1, line):
        gate_copy(step).start()
    own_rows.wait()
    all_cots.wait()
    own_gates.wait()
    for step in range(1, line):
        gate_copy(step).wait()

    order = visit_order(line)

    def out_copies(slot, block):
        return (
            pltpu.make_async_copy(stage.at[slot, 0], mix_hbm.at[block], out_sem.at[slot, 0]),
            pltpu.make_async_copy(stage.at[slot, 1], back_hbm.at[block], out_sem.at[slot, 1]),
            pltpu.make_async_copy(gated.at[slot], gated_hbm.at[block], out_sem.at[slot, 2]),
            pltpu.make_async_copy(inner.at[slot], inner_hbm.at[block], out_sem.at[slot, 3]),
        )

    def grad_copy(block, step):
        return pltpu.make_async_remote_copy(
            src_ref=gate_grads_sent.at[block],
            dst_ref=gate_grads.at[z],
            send_sem=grad_send.at[block],
            recv_sem=grad_recv.at[z],
            device_id=(dp, block),
            device_id_type=MESH,
        )

    def visit(k, _):
        block = pick(order, z, k)
        slot = lax.rem(k, 2)
        apart = jnp.abs(block - z)
        previous = pick(order, z, jnp.maximum(k - 1, 0))
        first = (k > 0) & (apart != jnp.abs(previous - z))
        below = z - apart
        above = z + apart

        @pl.when(first & (below >= 0))
        def _():
            low = jnp.maximum(below, 0)
            row_copy(rows_hbm, low, low, z).wait_recv()

            @pl.when(z < line - 1)
            def _():
                row_copy(rows.at[low], low, low, z + 1).start()

        @pl.when(first & (above < line))
        def _():
            high = jnp.minimum(above, line - 1)
            row_copy(rows_hbm, high, high, z).wait_recv()

            @pl.when(z > 0)
            def _():
                row_copy(rows.at[high], high, high, z - 1).start()

        @pl.when(k >= 2)
        def _():
            for copy in out_copies(slot, pick(order, z, jnp.maximum(k - 2, 0))):
                copy.wait()

        mix_sum[...] = jnp.zeros_like(mix_sum)
        back_sum[...] = jnp.zeros_like(back_sum)
        columns[...] = jnp.zeros_like(columns)
        gate_columns = gates[block].T
        lane = lax.broadcasted_iota(jnp.int32, gate_columns.shape, 1)
        wide_lane = lax.broadcasted_iota(jnp.int32, columns.shape, 1)

        def expert(e, _):
            @pl.when(k == 0)
            def _():
                for copy in weight_copies(e):
                    copy.wait()

            gate_col = jnp.sum(jnp.where(lane == e, gate_columns, 0.0), axis=1, keepdims=True)
            both = contract(rows[block], up[e], 1, 0)
            returned = contract(cots[block], down[e], 1, 0)
            gate_part = both[:, :ff_width]
            up_part = both[:, ff_width:]
            sigmoid_gate = jax.nn.sigmoid(gate_part)
            silu_gate = gate_part * sigmoid_gate
            active = silu_gate * up_part
            gated_part = (active * gate_col).astype(BF16)
            gated[slot, :, pl.ds(pl.multiple_of(e * ff_width, ff_width), ff_width)] = gated_part
            mix_sum[...] += contract(gated_part, down[e], 1, 1)
            gate_grad = jnp.sum(active * returned, axis=1, keepdims=True)
            columns[...] = jnp.where(wide_lane == e, gate_grad, columns[...])
            scaled = returned * gate_col
            grad_gate = scaled * up_part * (sigmoid_gate * (1.0 + gate_part * (1.0 - sigmoid_gate)))
            grad_up = scaled * silu_gate
            grads = jnp.concatenate([grad_gate, grad_up], axis=1).astype(BF16)
            inner[slot, :, pl.ds(pl.multiple_of(e * 2 * ff_width, ff_width), 2 * ff_width)] = grads
            back_sum[...] += contract(grads, up[e], 1, 1)
            return 0

        lax.fori_loop(0, experts, expert, 0)
        stage[slot, 0] = mix_sum[...].astype(BF16)
        stage[slot, 1] = back_sum[...].astype(BF16)
        for copy in out_copies(slot, block):
            copy.start()
        gate_grads_sent[block] = columns[...].T[: gate_grads.shape[1]]

        @pl.when(block == z)
        def _():
            gate_grads[z] = gate_grads_sent[z]

        @pl.when(block != z)
        def _():
            grad_copy(block, 0).start()

        return 0

    lax.fori_loop(0, line, visit, 0)
    for k in (line - 2, line - 1):
        for copy in out_copies(k % 2, pick(order, z, k)):
            copy.wait()

    @pl.when(z < line - 1)
    def _():
        row_copy(rows_hbm, z, line, z + 1).wait_send()

    @pl.when(z > 0)
    def _():
        row_copy(rows_hbm, z, line + 1, z - 1).wait_send()

    for s in range(line):

        @pl.when(((s < z) & (z < line - 1)) | ((s > z) & (z > 0)))
        def _(s=s):
            row_copy(rows_hbm, s, s, z).wait_send()

        @pl.when(s != z)
        def _(s=s):
            grad_copy(s, 0).wait_send()
            pltpu.make_async_remote_copy(
                src_ref=gate_grads_sent.at[s],
                dst_ref=gate_grads.at[s],
                send_sem=grad_send.at[s],
                recv_sem=grad_recv.at[s],
                device_id=(dp, z),
                device_id_type=MESH,
            ).wait_recv()

    last = (
        pltpu.make_async_copy(rows, rows_all_hbm, local_sem.at[0]),
        pltpu.make_async_copy(gate_grads, gate_grads_hbm, local_sem.at[1]),
    )
    for copy in last:
        copy.start()
    for copy in last:
        copy.wait()


def bank(rows, cots, gates, up, down, line):
    tokens, width = rows.shape
    experts, _, ff_width = down.shape
    shape = jax.ShapeDtypeStruct
    held = gates.shape[1:]
    anywhere = pl.BlockSpec(memory_space=pl.ANY)
    work = 10 * line * tokens * experts * width * ff_width
    return pl.pallas_call(
        functools.partial(bank_kernel, line),
        out_shape=(
            shape((line, tokens, width), BF16),
            shape((line, tokens, width), BF16),
            shape((line,) + held, F32),
            shape((line, tokens, experts * ff_width), BF16),
            shape((line, tokens, experts * 2 * ff_width), BF16),
            shape((line, tokens, width), BF16),
        ),
        in_specs=[anywhere] * 5,
        out_specs=(anywhere,) * 6,
        scratch_shapes=[
            pltpu.VMEM((line, tokens, width), BF16),
            pltpu.VMEM((line, tokens, width), BF16),
            pltpu.VMEM((line,) + held, F32),
            pltpu.VMEM((line,) + held, F32),
            pltpu.VMEM((line,) + held, F32),
            pltpu.VMEM(up.shape, BF16),
            pltpu.VMEM(down.shape, BF16),
            pltpu.VMEM((tokens, width), F32),
            pltpu.VMEM((tokens, width), F32),
            pltpu.VMEM((2, 2, tokens, width), BF16),
            pltpu.VMEM((2, tokens, experts * ff_width), BF16),
            pltpu.VMEM((2, tokens, experts * 2 * ff_width), BF16),
            pltpu.VMEM((tokens, 128), F32),
            pltpu.SemaphoreType.DMA((line + 2,)),
            pltpu.SemaphoreType.DMA((line,)),
            pltpu.SemaphoreType.DMA((line,)),
            pltpu.SemaphoreType.DMA((line,)),
            pltpu.SemaphoreType.DMA((2, experts)),
            pltpu.SemaphoreType.DMA((3,)),
            pltpu.SemaphoreType.DMA((2, 4)),
            pltpu.SemaphoreType.DMA((line,)),
            pltpu.SemaphoreType.DMA((line,)),
        ],
        compiler_params=pltpu.CompilerParams(
            collective_id=1, has_side_effects=True, vmem_limit_bytes=VMEM_MOST
        ),
        cost_estimate=pl.CostEstimate(flops=work, bytes_accessed=2**26, transcendentals=0),
    )(rows, cots, gates, up, down)


def weight_grads_kernel(rows, cots, gated, inner, up_grad, down_grad):
    step = 256
    for at in range(0, rows.shape[1], step):
        up_grad[0, at : at + step] = contract(rows[:, at : at + step], inner[...], 0, 0).astype(BF16)
        down_grad[0, at : at + step] = contract(cots[:, at : at + step], gated[...], 0, 0).astype(
            BF16
        )


def weight_grads(rows, cots, gated, inner, experts):
    tokens, width = rows.shape
    ff_width = gated.shape[1] // experts
    whole = pl.BlockSpec((tokens, width), lambda e: (0, 0))
    return pl.pallas_call(
        weight_grads_kernel,
        grid=(experts,),
        out_shape=(
            jax.ShapeDtypeStruct((experts, width, 2 * ff_width), BF16),
            jax.ShapeDtypeStruct((experts, width, ff_width), BF16),
        ),
        in_specs=[
            whole,
            whole,
            pl.BlockSpec((tokens, ff_width), lambda e: (0, e)),
            pl.BlockSpec((tokens, 2 * ff_width), lambda e: (0, e)),
        ],
        out_specs=(
            pl.BlockSpec((1, width, 2 * ff_width), lambda e: (e, 0, 0)),
            pl.BlockSpec((1, width, ff_width), lambda e: (e, 0, 0)),
        ),
        compiler_params=pltpu.CompilerParams(vmem_limit_bytes=VMEM_MOST),
        cost_estimate=pl.CostEstimate(
            flops=6 * tokens * width * experts * ff_width,
            bytes_accessed=2 * tokens * (2 * width + 3 * experts * ff_width)
            + 6 * experts * width * ff_width,
            transcendentals=0,
        ),
    )(rows, cots, gated, inner)


def bank_grads_kernel(
    rows_hbm,
    cots_hbm,
    gated_hbm,
    inner_hbm,
    sum_hbm,
    rows,
    cots,
    gated,
    inner,
    grads,
    core_sum,
    first_sum,
    last_sum,
    total,
    load_sem,
    send_sem,
    recv_sem,
    out_sem,
):
    experts = grads.shape[0]
    ff_width = gated.shape[2]
    block_rows = grads.shape[4]
    dp = lax.axis_index("dp")
    z = lax.axis_index("expert")
    y, x, core = dp // 4, lax.rem(dp // 2, 2), lax.rem(dp, 2)
    core_peer, x_peer, y_peer = dp + 1 - 2 * core, dp + 2 - 4 * x, dp + 4 - 8 * y

    def loads(e, slot):
        return (
            pltpu.make_async_copy(
                gated_hbm.at[:, pl.ds(pl.multiple_of(e * ff_width, ff_width), ff_width)],
                gated.at[slot],
                load_sem.at[slot, 0],
            ),
            pltpu.make_async_copy(
                inner_hbm.at[:, pl.ds(pl.multiple_of(2 * e * ff_width, ff_width), 2 * ff_width)],
                inner.at[slot],
                load_sem.at[slot, 1],
            ),
        )

    row_load = pltpu.make_async_copy(rows_hbm, rows, load_sem.at[0, 2])
    cot_load = pltpu.make_async_copy(cots_hbm, cots, load_sem.at[1, 2])
    row_load.start()
    for copy in loads(0, 0):
        copy.start()
    cot_load.start()
    barrier = pltpu.get_barrier_semaphore()
    for peer in (core_peer, x_peer, y_peer):
        pl.semaphore_signal(barrier, inc=1, device_id=(peer, z), device_id_type=MESH)
    pl.semaphore_wait(barrier, 3)
    row_load.wait()
    cot_load.wait()

    def send(stage, e, source, target, peer):
        return pltpu.make_async_remote_copy(
            src_ref=source,
            dst_ref=target,
            send_sem=send_sem.at[stage, e],
            recv_sem=recv_sem.at[stage, e],
            device_id=(peer, z),
            device_id_type=MESH,
        )

    def core_send(e):
        return send(0, e, grads.at[e, :, :, 1 - core], core_sum.at[e], core_peer)

    def first_send(e, along_x):
        if along_x:
            return send(1, e, core_sum.at[e, :, 1 - x], first_sum.at[e], x_peer)
        return send(1, e, core_sum.at[e, 1 - y], first_sum.at[e], y_peer)

    def last_send(e, along_x):
        if along_x:
            return send(2, e, first_sum.at[e, 1 - x], last_sum.at[e], x_peer)
        return send(2, e, first_sum.at[e, 1 - y], last_sum.at[e], y_peer)

    def by_parity(e, act):
        even = lax.rem(e, 2) == 0

        @pl.when(even)
        def _():
            act(True)

        @pl.when(jnp.logical_not(even))
        def _():
            act(False)

    def after_core(e):
        core_send(e).wait_recv()
        for yy in range(2):
            for xx in range(2):
                core_sum[e, yy, xx] = (
                    grads[e, yy, xx, core].astype(F32) + core_sum[e, yy, xx].astype(F32)
                ).astype(BF16)
        by_parity(e, lambda even: first_send(e, even).start())

    def after_first(e):
        def act(even):
            first_send(e, even).wait_recv()
            for other in range(2):
                kept = core_sum[e, other, x] if even else core_sum[e, y, other]
                first_sum[e, other] = (
                    kept.astype(F32) + first_sum[e, other].astype(F32)
                ).astype(BF16)
            last_send(e, not even).start()

        by_parity(e, act)

    def after_last(e):
        def act(even):
            last_send(e, not even).wait_recv()
            kept = first_sum[e, y] if even else first_sum[e, x]
            total[e] = kept.astype(F32) + last_sum[e].astype(F32)

        by_parity(e, act)
        pltpu.make_async_copy(total.at[e], sum_hbm.at[e], out_sem.at[e]).start()

    def step(e, _):
        slot = lax.rem(e, 2)
        for copy in loads(e, slot):
            copy.wait()

        @pl.when(e + 1 < experts)
        def _():
            for copy in loads(e + 1, 1 - slot):
                copy.start()

        def tile(at, _):
            columns = pl.ds(pl.multiple_of(at * 2 * block_rows, 2 * block_rows), 2 * block_rows)
            up_grad = contract(rows[:, columns], inner[slot], 0, 0).astype(BF16)
            down_grad = contract(cots[:, columns], gated[slot], 0, 0).astype(BF16)
            for side in range(2):
                part = slice(side * block_rows, (side + 1) * block_rows)
                grads[e, at // 2, lax.rem(at, 2), side, :, : 2 * ff_width] = up_grad[part]
                grads[e, at // 2, lax.rem(at, 2), side, :, 2 * ff_width :] = down_grad[part]
            return 0

        lax.fori_loop(0, 4, tile, 0)
        core_send(e).start()

        @pl.when(e >= 1)
        def _():
            after_core(e - 1)

        @pl.when(e >= 3)
        def _():
            after_first(e - 3)

        return 0

    lax.fori_loop(0, experts, step, 0)
    after_core(experts - 1)

    for e in range(max(experts - 3, 0), experts):
        after_first(e)
        if e - 2 >= 0:
            after_last(e - 2)
    for e in range(max(experts - 2, 0), experts):
        after_last(e)
    for e in range(experts):
        core_send(e).wait_send()
        first_send(e, e % 2 == 0).wait_send()
        last_send(e, e % 2 == 1).wait_send()
        pltpu.make_async_copy(total.at[e], sum_hbm.at[e], out_sem.at[e]).wait()


def bank_grads(rows, cots, gated, inner, experts):
    tokens, width = rows.shape
    ff_width = gated.shape[1] // experts
    lanes = 3 * ff_width
    block_rows = width // 8
    anywhere = pl.BlockSpec(memory_space=pl.ANY)
    return pl.pallas_call(
        bank_grads_kernel,
        out_shape=jax.ShapeDtypeStruct((experts, block_rows, lanes), F32),
        in_specs=[anywhere] * 4,
        out_specs=anywhere,
        scratch_shapes=[
            pltpu.VMEM((tokens, width), BF16),
            pltpu.VMEM((tokens, width), BF16),
            pltpu.VMEM((2, tokens, ff_width), BF16),
            pltpu.VMEM((2, tokens, 2 * ff_width), BF16),
            pltpu.VMEM((experts, 2, 2, 2, block_rows, lanes), BF16),
            pltpu.VMEM((experts, 2, 2, block_rows, lanes), BF16),
            pltpu.VMEM((experts, 2, block_rows, lanes), BF16),
            pltpu.VMEM((experts, block_rows, lanes), BF16),
            pltpu.VMEM((experts, block_rows, lanes), F32),
            pltpu.SemaphoreType.DMA((2, 3)),
            pltpu.SemaphoreType.DMA((3, experts)),
            pltpu.SemaphoreType.DMA((3, experts)),
            pltpu.SemaphoreType.DMA((experts,)),
        ],
        compiler_params=pltpu.CompilerParams(
            collective_id=2, has_side_effects=True, vmem_limit_bytes=VMEM_MOST
        ),
        cost_estimate=pl.CostEstimate(
            flops=6 * tokens * width * experts * ff_width,
            bytes_accessed=2**27,
            transcendentals=0,
        ),
    )(rows, cots, gated, inner)


def head_sums_kernel(
    units,
    in_hbm,
    out_hbm,
    small_hbm,
    in_sum_hbm,
    out_sum_hbm,
    small_sum_hbm,
    *scratch,
):
    count = len(units)
    owns, cores, firsts, lasts, sums, lines, totals = (
        scratch[i * count : (i + 1) * count] for i in range(7)
    )
    load_sem, send_sem, recv_sem, line_send, line_recv, out_sem = scratch[7 * count :]
    dp = lax.axis_index("dp")
    z = lax.axis_index("expert")
    line = lines[0].shape[0]
    y, x, core = dp // 4, lax.rem(dp // 2, 2), lax.rem(dp, 2)
    core_peer, x_peer, y_peer = dp + 1 - 2 * core, dp + 2 - 4 * x, dp + 4 - 8 * y
    sources = (in_hbm, out_hbm, small_hbm)
    targets = (in_sum_hbm, out_sum_hbm, small_sum_hbm)

    def own_load(u):
        return pltpu.make_async_copy(
            sources[units[u][0]].at[:, :, core, :, :, pl.ds(units[u][1], units[u][2])],
            owns[u],
            load_sem.at[u],
        )

    def send(stage, u, source, target, peer):
        return pltpu.make_async_remote_copy(
            src_ref=source,
            dst_ref=target,
            send_sem=send_sem.at[stage, u],
            recv_sem=recv_sem.at[stage, u],
            device_id=(peer, z),
            device_id_type=MESH,
        )

    def core_send(u):
        return send(
            0,
            u,
            sources[units[u][0]].at[:, :, 1 - core, :, :, pl.ds(units[u][1], units[u][2])],
            cores[u],
            core_peer,
        )

    def first_send(u):
        if u % 2 == 0:
            return send(1, u, cores[u].at[:, 1 - x], firsts[u], x_peer)
        return send(1, u, cores[u].at[1 - y], firsts[u], y_peer)

    def last_send(u):
        if u % 2 == 0:
            return send(2, u, firsts[u].at[1 - y], lasts[u], y_peer)
        return send(2, u, firsts[u].at[1 - x], lasts[u], x_peer)

    def line_send_copy(u, step):
        peer = lax.rem(z + step, line)
        return pltpu.make_async_remote_copy(
            src_ref=sums[u].at[peer],
            dst_ref=lines[u].at[step],
            send_sem=line_send.at[u, step],
            recv_sem=line_recv.at[u, step],
            device_id=(dp, peer),
            device_id_type=MESH,
        )

    def out_copy(u):
        return pltpu.make_async_copy(
            totals[u],
            targets[units[u][0]].at[:, pl.ds(units[u][1], units[u][2])],
            out_sem.at[u],
        )

    for u in range(count):
        own_load(u).start()
    barrier = pltpu.get_barrier_semaphore()
    for peer in (core_peer, x_peer, y_peer):
        pl.semaphore_signal(barrier, inc=1, device_id=(peer, z), device_id_type=MESH)
    for step in range(1, line):
        pl.semaphore_signal(
            barrier, inc=1, device_id=(dp, lax.rem(z + step, line)), device_id_type=MESH
        )
    pl.semaphore_wait(barrier, 3 + line - 1)
    for u in range(count):
        core_send(u).start()
    for u in range(count):
        own_load(u).wait()
        core_send(u).wait_recv()
        cores[u][...] = (owns[u][...].astype(F32) + cores[u][...].astype(F32)).astype(BF16)
        first_send(u).start()

    def after_first(u):
        first_send(u).wait_recv()
        for other in range(2):
            kept = cores[u][other, x] if u % 2 == 0 else cores[u][y, other]
            firsts[u][other] = (kept.astype(F32) + firsts[u][other].astype(F32)).astype(BF16)
        last_send(u).start()

    def after_last(u):
        last_send(u).wait_recv()
        kept = firsts[u][y] if u % 2 == 0 else firsts[u][x]
        sums[u][...] = (kept.astype(F32) + lasts[u][...].astype(F32)).astype(BF16)
        for step in range(1, line):
            line_send_copy(u, step).start()

    def after_line(u):
        value = sums[u][z].astype(F32)
        for step in range(1, line):
            line_send_copy(u, step).wait_recv()
            value = value + lines[u][step].astype(F32)
        totals[u][...] = value
        out_copy(u).start()

    for u in range(count + 4):
        if u < count:
            after_first(u)
        if 2 <= u < count + 2:
            after_last(u - 2)
        if u >= 4:
            after_line(u - 4)
    for u in range(count):
        core_send(u).wait_send()
        first_send(u).wait_send()
        last_send(u).wait_send()
        for step in range(1, line):
            line_send_copy(u, step).wait_send()
        out_copy(u).wait()


def head_sums(in_grad, out_grad, small_grad, line):
    width = in_grad.shape[0]
    rows = width // (8 * line)
    units = []
    for which, grad in enumerate((in_grad, out_grad, small_grad)):
        for at in range(0, grad.shape[1], 512):
            units.append((which, at, min(512, grad.shape[1] - at)))

    def blocks(grad):
        return grad.reshape(2, 2, 2, line, rows, grad.shape[1])

    def buffers(shape, kind):
        return [pltpu.VMEM(shape + (lanes,), kind) for _, _, lanes in units]

    anywhere = pl.BlockSpec(memory_space=pl.ANY)
    count = len(units)
    return pl.pallas_call(
        functools.partial(head_sums_kernel, units),
        out_shape=tuple(
            jax.ShapeDtypeStruct((rows, grad.shape[1]), F32)
            for grad in (in_grad, out_grad, small_grad)
        ),
        in_specs=[anywhere] * 3,
        out_specs=(anywhere,) * 3,
        scratch_shapes=[
            *buffers((2, 2, line, rows), BF16),
            *buffers((2, 2, line, rows), BF16),
            *buffers((2, line, rows), BF16),
            *buffers((line, rows), BF16),
            *buffers((line, rows), BF16),
            *buffers((line, rows), BF16),
            *buffers((rows,), F32),
            pltpu.SemaphoreType.DMA((count,)),
            pltpu.SemaphoreType.DMA((3, count)),
            pltpu.SemaphoreType.DMA((3, count)),
            pltpu.SemaphoreType.DMA((count, line)),
            pltpu.SemaphoreType.DMA((count, line)),
            pltpu.SemaphoreType.DMA((count,)),
        ],
        compiler_params=pltpu.CompilerParams(
            collective_id=3, has_side_effects=True, vmem_limit_bytes=VMEM_MOST
        ),
        cost_estimate=pl.CostEstimate(flops=2**22, bytes_accessed=2**26, transcendentals=0),
    )(blocks(in_grad), blocks(out_grad), blocks(small_grad))


def body(
    tokens,
    cotangent,
    routes,
    cont_ids,
    norm_gains,
    gains_moment,
    gains_average,
    heads_in,
    heads_in_master,
    heads_in_moment,
    heads_in_average,
    heads_out,
    heads_out_master,
    heads_out_moment,
    heads_out_average,
    router,
    router_master,
    router_moment,
    router_average,
    expert_in,
    expert_in_master,
    expert_in_moment,
    expert_in_average,
    expert_out,
    expert_out_master,
    expert_out_moment,
    expert_out_average,
):
    token_count, model_width = tokens.shape
    local_experts = expert_in.shape[0]
    peer_count = lax.axis_size("expert")
    experts = local_experts * peer_count
    group_size = HEADS // KV_HEADS
    query_end = HEADS * HEAD_DIM
    key_end = query_end + KV_HEADS * HEAD_DIM
    token_rows = tokens.astype(jnp.float32)
    normed_one, factor_one = rms_parts(token_rows, norm_gains[:, 0])
    first_in = normed_one.astype(jnp.bfloat16)
    projected = jnp.dot(first_in, heads_in, preferred_element_type=jnp.float32)
    positions, allowed = layout(cont_ids[0], token_count - cont_ids.shape[1])
    cosine, sine_table = rope_tables(positions)
    queries = rotate(
        projected[:, :query_end].reshape(token_count, HEADS, HEAD_DIM), cosine, sine_table
    )
    queries = queries.astype(jnp.bfloat16).reshape(token_count, KV_HEADS, group_size, HEAD_DIM)
    key_rows = rotate(
        projected[:, query_end:key_end].reshape(token_count, KV_HEADS, HEAD_DIM), cosine, sine_table
    ).astype(jnp.bfloat16)
    value_rows = (
        projected[:, key_end:].reshape(token_count, KV_HEADS, HEAD_DIM).astype(jnp.bfloat16)
    )
    scores = masked_scores(queries, key_rows, allowed)
    row_peak = jnp.max(scores, axis=-1, keepdims=True)
    log_total = row_peak + jnp.log(jnp.sum(jnp.exp(scores - row_peak), axis=-1, keepdims=True))
    weights = jnp.exp(scores - log_total).astype(jnp.bfloat16)
    attended = jnp.einsum("kgqp,pkd->qkgd", weights, value_rows, preferred_element_type=jnp.float32)
    attended = attended.reshape(token_count, query_end).astype(jnp.bfloat16)
    branch = jnp.einsum("th,dh->td", attended, heads_out, preferred_element_type=jnp.float32)
    hidden = token_rows + branch
    normed_two, factor_two = rms_parts(hidden, norm_gains[:, 1])
    second_in = normed_two.astype(jnp.bfloat16)
    logits = jnp.dot(second_in, router, preferred_element_type=jnp.float32)
    named = jnp.any(
        routes[:, :, None] == jnp.arange(experts, dtype=jnp.int32)[None, None, :], axis=1
    )
    peak = jnp.max(jnp.where(named, logits, -jnp.inf), axis=1, keepdims=True)
    powers = jnp.where(named, jnp.exp(logits - peak), 0.0)
    gates = powers / jnp.sum(powers, axis=1, keepdims=True)
    incoming = cotangent.astype(jnp.float32)
    cots_all = lax.all_gather(cotangent, "expert", axis=0, tiled=False)
    padded = -local_experts % 8
    gate_rows = jnp.pad(
        gates.T.reshape(peer_count, local_experts, token_count), ((0, 0), (0, padded), (0, 0))
    )
    mix_part, grad_part, gate_grads, gated, grad_gate_up, rows_all = bank(
        second_in, cots_all, gate_rows, expert_in, expert_out, peer_count
    )
    grad_second = lax.psum_scatter(
        grad_part.reshape(peer_count * token_count, model_width),
        "expert",
        scatter_dimension=0,
        tiled=True,
    ).astype(jnp.float32)
    mixture = lax.psum_scatter(
        mix_part.reshape(peer_count * token_count, model_width),
        "expert",
        scatter_dimension=0,
        tiled=True,
    ).astype(jnp.float32)
    grad_sources = (
        rows_all.reshape(peer_count * token_count, model_width),
        cots_all.reshape(peer_count * token_count, model_width),
        gated.reshape(peer_count * token_count, -1),
        grad_gate_up.reshape(peer_count * token_count, -1),
    )
    paired = lax.axis_size("dp") == 8
    if paired:
        bank_sums = bank_grads(*grad_sources, local_experts)
        expert_sums = (bank_sums[:, :, : expert_in.shape[2]], bank_sums[:, :, expert_in.shape[2] :])
    else:
        expert_sums = tuple(
            lax.psum_scatter(part, "dp", scatter_dimension=1, tiled=True).astype(jnp.float32)
            for part in weight_grads(*grad_sources, local_experts)
        )
    output = (hidden + mixture).astype(jnp.bfloat16)
    grad_gates = gate_grads[:, :local_experts].reshape(experts, token_count).T
    grad_logits = gates * (grad_gates - jnp.sum(gates * grad_gates, axis=1, keepdims=True))
    grad_router = jnp.dot(second_in.astype(jnp.float32).T, grad_logits, precision=HIGHEST)
    grad_second = grad_second + jnp.dot(
        grad_logits, router.astype(jnp.float32).T, precision=HIGHEST
    )
    grad_hidden_norm, grad_gain_two = rms_back(grad_second, hidden, factor_two, norm_gains[:, 1])
    grad_hidden = incoming + grad_hidden_norm
    grad_branch = grad_hidden.astype(jnp.bfloat16)
    grad_heads_out = jnp.einsum(
        "td,th->dh", grad_branch, attended, preferred_element_type=jnp.float32
    )
    grad_attended = jnp.dot(grad_branch, heads_out, preferred_element_type=jnp.float32).astype(
        jnp.bfloat16
    )
    grad_attended = grad_attended.reshape(token_count, KV_HEADS, group_size, HEAD_DIM)
    weight_full = jnp.exp(masked_scores(queries, key_rows, allowed) - log_total)
    grad_weights = jnp.einsum(
        "qkgd,pkd->kgqp", grad_attended, value_rows, preferred_element_type=jnp.float32
    )
    spread = jnp.sum(weight_full * grad_weights, axis=-1, keepdims=True)
    grad_scores = (weight_full * (grad_weights - spread)).astype(jnp.bfloat16)
    grad_queries = (
        jnp.einsum("kgqp,pkd->qkgd", grad_scores, key_rows, preferred_element_type=jnp.float32)
        * SCALE
    )
    grad_keys = (
        jnp.einsum("kgqp,qkgd->pkd", grad_scores, queries, preferred_element_type=jnp.float32)
        * SCALE
    )
    grad_values = jnp.einsum(
        "kgqp,qkgd->pkd",
        weight_full.astype(jnp.bfloat16),
        grad_attended,
        preferred_element_type=jnp.float32,
    )
    grad_projected = jnp.concatenate(
        [
            unrotate(
                grad_queries.reshape(token_count, HEADS, HEAD_DIM), cosine, sine_table
            ).reshape(token_count, query_end),
            unrotate(grad_keys, cosine, sine_table).reshape(token_count, KV_HEADS * HEAD_DIM),
            grad_values.reshape(token_count, KV_HEADS * HEAD_DIM),
        ],
        axis=1,
    ).astype(jnp.bfloat16)
    grad_heads_in = jnp.einsum(
        "td,tc->dc", first_in, grad_projected, preferred_element_type=jnp.float32
    )
    grad_first = jnp.einsum(
        "tc,dc->td", grad_projected, heads_in, preferred_element_type=jnp.float32
    )
    grad_tokens_norm, grad_gain_one = rms_back(grad_first, token_rows, factor_one, norm_gains[:, 0])
    token_grad = grad_hidden + grad_tokens_norm
    grad_gains = jnp.stack([grad_gain_one, grad_gain_two], axis=1)
    cut_in = grad_heads_in.shape[1]
    cut_out = cut_in + grad_heads_out.shape[1]
    small_grads = jnp.concatenate([grad_router, grad_gains], axis=1)
    if paired:
        padded = -small_grads.shape[1] % 128
        head_in_sum, head_out_sum, small_sum = head_sums(
            grad_heads_in.astype(jnp.bfloat16),
            grad_heads_out.astype(jnp.bfloat16),
            jnp.pad(small_grads, ((0, 0), (0, padded))).astype(jnp.bfloat16),
            peer_count,
        )
    else:
        packed = jnp.concatenate([grad_heads_in, grad_heads_out, small_grads], axis=1)
        head_total = lax.psum_scatter(
            packed.astype(jnp.bfloat16), ("dp", "expert"), scatter_dimension=0, tiled=True
        ).astype(jnp.float32)
        head_in_sum = head_total[:, :cut_in]
        head_out_sum = head_total[:, cut_in:cut_out]
        small_sum = head_total[:, cut_out:]
    summed = (
        head_in_sum,
        head_out_sum,
        small_sum[:, :experts],
        small_sum[:, experts : experts + 2],
    )
    shard_rows = model_width // lax.axis_size(("dp", "expert"))
    gains_share = lax.dynamic_slice_in_dim(
        norm_gains, lax.axis_index(("dp", "expert")) * shard_rows, shard_rows, 0
    )
    gains_new = update(summed[3], gains_share, gains_moment, gains_average)
    inproj_new = update(summed[0], heads_in_master, heads_in_moment, heads_in_average)
    outproj_new = update(summed[1], heads_out_master, heads_out_moment, heads_out_average)
    router_new = update(summed[2], router_master, router_moment, router_average)
    upper_new = update(expert_sums[0], expert_in_master, expert_in_moment, expert_in_average)
    lower_new = update(expert_sums[1], expert_out_master, expert_out_moment, expert_out_average)
    return (
        output,
        token_grad,
        gains_new[0],
        gains_new[1],
        gains_new[2],
        inproj_new[0],
        inproj_new[1],
        inproj_new[2],
        outproj_new[0],
        outproj_new[1],
        outproj_new[2],
        router_new[0],
        router_new[1],
        router_new[2],
        upper_new[0],
        upper_new[1],
        upper_new[2],
        lower_new[0],
        lower_new[1],
        lower_new[2],
    )


def solution(mesh):
    return jax.shard_map(
        body,
        mesh=mesh,
        in_specs=(
            P(("dp", "expert"), None),
            P(("dp", "expert"), None),
            P(("dp", "expert"), None),
            P(("dp", "expert"), None),
            P(),
            P(("dp", "expert"), None),
            P(("dp", "expert"), None),
            P(),
            P(("dp", "expert"), None),
            P(("dp", "expert"), None),
            P(("dp", "expert"), None),
            P(),
            P(("dp", "expert"), None),
            P(("dp", "expert"), None),
            P(("dp", "expert"), None),
            P(),
            P(("dp", "expert"), None),
            P(("dp", "expert"), None),
            P(("dp", "expert"), None),
            P("expert", None, None),
            P("expert", "dp", None),
            P("expert", "dp", None),
            P("expert", "dp", None),
            P("expert", None, None),
            P("expert", "dp", None),
            P("expert", "dp", None),
            P("expert", "dp", None),
        ),
        out_specs=(
            P(("dp", "expert"), None),
            P(("dp", "expert"), None),
            P(("dp", "expert"), None),
            P(("dp", "expert"), None),
            P(("dp", "expert"), None),
            P(("dp", "expert"), None),
            P(("dp", "expert"), None),
            P(("dp", "expert"), None),
            P(("dp", "expert"), None),
            P(("dp", "expert"), None),
            P(("dp", "expert"), None),
            P(("dp", "expert"), None),
            P(("dp", "expert"), None),
            P(("dp", "expert"), None),
            P("expert", "dp", None),
            P("expert", "dp", None),
            P("expert", "dp", None),
            P("expert", "dp", None),
            P("expert", "dp", None),
            P("expert", "dp", None),
        ),
        check_vma=False,
    )
```

```python
import functools

import jax
import jax.numpy as jnp
from jax import lax
from jax.experimental import pallas as pl
from jax.experimental.pallas import tpu as pltpu
from jax.sharding import PartitionSpec as P

HEADS = 16
KV_HEADS = 8
HEAD_DIM = 64


EPS = 1e-06
SCALE = 0.015625
THETA = 10000.0
MOMENTUM = 0.9
DECAY = 0.8
RATE = 0.001
HIGHEST = lax.Precision.HIGHEST


def layout(labels_row, prompt_len):
    places = jnp.arange(prompt_len + labels_row.shape[0], dtype=jnp.int32)
    earlier = jnp.sum((labels_row[None, :] < labels_row[:, None]).astype(jnp.int32), axis=1)
    offset = places[prompt_len:] - prompt_len - earlier
    positions = jnp.concatenate([places[:prompt_len], prompt_len + offset]).astype(jnp.float32)
    labels = jnp.concatenate([jnp.full((prompt_len,), -1, jnp.int32), labels_row])
    allowed = (places[None, :] <= places[:, None]) & (
        (places[None, :] < prompt_len) | (labels[None, :] == labels[:, None])
    )
    return (positions, allowed)


def rope_tables(positions):
    middle = HEAD_DIM // 2
    frequency = THETA ** (-2.0 * jnp.arange(middle, dtype=jnp.float32) / HEAD_DIM)
    angles = positions[:, None] * frequency[None, :]
    cosine, sine = jnp.cos(angles), jnp.sin(angles)
    return (
        jnp.concatenate([cosine] * 4, axis=1),
        jnp.concatenate([-sine, sine, -sine, sine], axis=1),
    )


def update(gradient, master, moment, average):
    moment_next = MOMENTUM * moment + gradient
    master_next = master - RATE * (gradient + MOMENTUM * moment_next)
    return (master_next, moment_next, DECAY * average + (1.0 - DECAY) * master_next)


F32 = jnp.float32
BF16 = jnp.bfloat16
MESH = pl.DeviceIdType.MESH
VMEM_MOST = 60 * 2**20


def contract(left, right, left_axis, right_axis):
    return lax.dot_general(
        left, right, (((left_axis,), (right_axis,)), ((), ())), preferred_element_type=F32
    )


def visit_order(line):
    return [sorted(range(line), key=lambda s: (abs(s - z), s)) for z in range(line)]


def pick(table, row, column):
    value = jnp.int32(table[0][0])
    for r in range(len(table)):
        for c in range(len(table[0])):
            value = jnp.where((row == r) & (column == c), jnp.int32(table[r][c]), value)
    return value


def bank_kernel(
    line,
    rows_hbm,
    cots_hbm,
    gates_hbm,
    up_hbm,
    down_hbm,
    mix_hbm,
    back_hbm,
    gate_grads_hbm,
    gated_hbm,
    inner_hbm,
    rows_all_hbm,
    rows,
    cots,
    gates,
    gate_grads,
    gate_grads_sent,
    up,
    down,
    mix_sum,
    back_sum,
    stage,
    gated,
    inner,
    columns,
    row_send,
    row_recv,
    gate_send,
    gate_recv,
    weight_sem,
    local_sem,
    out_sem,
    grad_send,
    grad_recv,
):
    dp = lax.axis_index("dp")
    z = lax.axis_index("expert")
    experts, width, ff_width = down.shape

    def weight_copies(e):
        return (
            pltpu.make_async_copy(up_hbm.at[e], up.at[e], weight_sem.at[0, e]),
            pltpu.make_async_copy(down_hbm.at[e], down.at[e], weight_sem.at[1, e]),
        )

    for e in range(experts):
        for copy in weight_copies(e):
            copy.start()
    own_rows = pltpu.make_async_copy(rows_hbm, rows.at[z], local_sem.at[0])
    own_rows.start()
    all_cots = pltpu.make_async_copy(cots_hbm, cots, local_sem.at[1])
    all_cots.start()
    own_gates = pltpu.make_async_copy(gates_hbm.at[z], gates.at[z], local_sem.at[2])
    own_gates.start()

    barrier = pltpu.get_barrier_semaphore()
    for step in range(1, line):
        pl.semaphore_signal(
            barrier, inc=1, device_id=(dp, lax.rem(z + step, line)), device_id_type=MESH
        )
    pl.semaphore_wait(barrier, line - 1)

    def row_copy(source, block, sem, target):
        return pltpu.make_async_remote_copy(
            src_ref=source,
            dst_ref=rows.at[block],
            send_sem=row_send.at[sem],
            recv_sem=row_recv.at[block],
            device_id=(dp, target),
            device_id_type=MESH,
        )

    @pl.when(z < line - 1)
    def _():
        row_copy(rows_hbm, z, line, z + 1).start()

    @pl.when(z > 0)
    def _():
        row_copy(rows_hbm, z, line + 1, z - 1).start()

    def gate_copy(step):
        peer = lax.rem(z + step, line)
        return pltpu.make_async_remote_copy(
            src_ref=gates_hbm.at[peer],
            dst_ref=gates.at[z],
            send_sem=gate_send.at[step],
            recv_sem=gate_recv.at[step],
            device_id=(dp, peer),
            device_id_type=MESH,
        )

    for step in range(1, line):
        gate_copy(step).start()
    own_rows.wait()
    all_cots.wait()
    own_gates.wait()
    for step in range(1, line):
        gate_copy(step).wait()

    order = visit_order(line)

    def out_copies(slot, block):
        return (
            pltpu.make_async_copy(stage.at[slot, 0], mix_hbm.at[block], out_sem.at[slot, 0]),
            pltpu.make_async_copy(stage.at[slot, 1], back_hbm.at[block], out_sem.at[slot, 1]),
            pltpu.make_async_copy(gated.at[slot], gated_hbm.at[block], out_sem.at[slot, 2]),
            pltpu.make_async_copy(inner.at[slot], inner_hbm.at[block], out_sem.at[slot, 3]),
        )

    def grad_copy(block, step):
        return pltpu.make_async_remote_copy(
            src_ref=gate_grads_sent.at[block],
            dst_ref=gate_grads.at[z],
            send_sem=grad_send.at[block],
            recv_sem=grad_recv.at[z],
            device_id=(dp, block),
            device_id_type=MESH,
        )

    def visit(k, _):
        block = pick(order, z, k)
        slot = lax.rem(k, 2)
        apart = jnp.abs(block - z)
        previous = pick(order, z, jnp.maximum(k - 1, 0))
        first = (k > 0) & (apart != jnp.abs(previous - z))
        below = z - apart
        above = z + apart

        @pl.when(first & (below >= 0))
        def _():
            low = jnp.maximum(below, 0)
            row_copy(rows_hbm, low, low, z).wait_recv()

            @pl.when(z < line - 1)
            def _():
                row_copy(rows.at[low], low, low, z + 1).start()

        @pl.when(first & (above < line))
        def _():
            high = jnp.minimum(above, line - 1)
            row_copy(rows_hbm, high, high, z).wait_recv()

            @pl.when(z > 0)
            def _():
                row_copy(rows.at[high], high, high, z - 1).start()

        @pl.when(k >= 2)
        def _():
            for copy in out_copies(slot, pick(order, z, jnp.maximum(k - 2, 0))):
                copy.wait()

        mix_sum[...] = jnp.zeros_like(mix_sum)
        back_sum[...] = jnp.zeros_like(back_sum)
        columns[...] = jnp.zeros_like(columns)
        gate_columns = gates[block].T
        lane = lax.broadcasted_iota(jnp.int32, gate_columns.shape, 1)
        wide_lane = lax.broadcasted_iota(jnp.int32, columns.shape, 1)

        def expert(e, _):
            @pl.when(k == 0)
            def _():
                for copy in weight_copies(e):
                    copy.wait()

            gate_col = jnp.sum(jnp.where(lane == e, gate_columns, 0.0), axis=1, keepdims=True)
            both = contract(rows[block], up[e], 1, 0)
            returned = contract(cots[block], down[e], 1, 0)
            gate_part = both[:, :ff_width]
            up_part = both[:, ff_width:]
            sigmoid_gate = jax.nn.sigmoid(gate_part)
            silu_gate = gate_part * sigmoid_gate
            active = silu_gate * up_part
            gated_part = (active * gate_col).astype(BF16)
            gated[slot, :, pl.ds(pl.multiple_of(e * ff_width, ff_width), ff_width)] = gated_part
            mix_sum[...] += contract(gated_part, down[e], 1, 1)
            gate_grad = jnp.sum(active * returned, axis=1, keepdims=True)
            columns[...] = jnp.where(wide_lane == e, gate_grad, columns[...])
            scaled = returned * gate_col
            grad_gate = scaled * up_part * (sigmoid_gate * (1.0 + gate_part * (1.0 - sigmoid_gate)))
            grad_up = scaled * silu_gate
            grads = jnp.concatenate([grad_gate, grad_up], axis=1).astype(BF16)
            inner[slot, :, pl.ds(pl.multiple_of(e * 2 * ff_width, ff_width), 2 * ff_width)] = grads
            back_sum[...] += contract(grads, up[e], 1, 1)
            return 0

        lax.fori_loop(0, experts, expert, 0)
        stage[slot, 0] = mix_sum[...].astype(BF16)
        stage[slot, 1] = back_sum[...].astype(BF16)
        for copy in out_copies(slot, block):
            copy.start()
        gate_grads_sent[block] = columns[...].T[: gate_grads.shape[1]]

        @pl.when(block == z)
        def _():
            gate_grads[z] = gate_grads_sent[z]

        @pl.when(block != z)
        def _():
            grad_copy(block, 0).start()

        return 0

    lax.fori_loop(0, line, visit, 0)
    for k in (line - 2, line - 1):
        for copy in out_copies(k % 2, pick(order, z, k)):
            copy.wait()

    @pl.when(z < line - 1)
    def _():
        row_copy(rows_hbm, z, line, z + 1).wait_send()

    @pl.when(z > 0)
    def _():
        row_copy(rows_hbm, z, line + 1, z - 1).wait_send()

    for s in range(line):

        @pl.when(((s < z) & (z < line - 1)) | ((s > z) & (z > 0)))
        def _(s=s):
            row_copy(rows_hbm, s, s, z).wait_send()

        @pl.when(s != z)
        def _(s=s):
            grad_copy(s, 0).wait_send()
            pltpu.make_async_remote_copy(
                src_ref=gate_grads_sent.at[s],
                dst_ref=gate_grads.at[s],
                send_sem=grad_send.at[s],
                recv_sem=grad_recv.at[s],
                device_id=(dp, z),
                device_id_type=MESH,
            ).wait_recv()

    last = (
        pltpu.make_async_copy(rows, rows_all_hbm, local_sem.at[0]),
        pltpu.make_async_copy(gate_grads, gate_grads_hbm, local_sem.at[1]),
    )
    for copy in last:
        copy.start()
    for copy in last:
        copy.wait()


def bank(rows, cots, gates, up, down, line):
    tokens, width = rows.shape
    experts, _, ff_width = down.shape
    shape = jax.ShapeDtypeStruct
    held = gates.shape[1:]
    anywhere = pl.BlockSpec(memory_space=pl.ANY)
    work = 10 * line * tokens * experts * width * ff_width
    return pl.pallas_call(
        functools.partial(bank_kernel, line),
        out_shape=(
            shape((line, tokens, width), BF16),
            shape((line, tokens, width), BF16),
            shape((line,) + held, F32),
            shape((line, tokens, experts * ff_width), BF16),
            shape((line, tokens, experts * 2 * ff_width), BF16),
            shape((line, tokens, width), BF16),
        ),
        in_specs=[anywhere] * 5,
        out_specs=(anywhere,) * 6,
        scratch_shapes=[
            pltpu.VMEM((line, tokens, width), BF16),
            pltpu.VMEM((line, tokens, width), BF16),
            pltpu.VMEM((line,) + held, F32),
            pltpu.VMEM((line,) + held, F32),
            pltpu.VMEM((line,) + held, F32),
            pltpu.VMEM(up.shape, BF16),
            pltpu.VMEM(down.shape, BF16),
            pltpu.VMEM((tokens, width), F32),
            pltpu.VMEM((tokens, width), F32),
            pltpu.VMEM((2, 2, tokens, width), BF16),
            pltpu.VMEM((2, tokens, experts * ff_width), BF16),
            pltpu.VMEM((2, tokens, experts * 2 * ff_width), BF16),
            pltpu.VMEM((tokens, 128), F32),
            pltpu.SemaphoreType.DMA((line + 2,)),
            pltpu.SemaphoreType.DMA((line,)),
            pltpu.SemaphoreType.DMA((line,)),
            pltpu.SemaphoreType.DMA((line,)),
            pltpu.SemaphoreType.DMA((2, experts)),
            pltpu.SemaphoreType.DMA((3,)),
            pltpu.SemaphoreType.DMA((2, 4)),
            pltpu.SemaphoreType.DMA((line,)),
            pltpu.SemaphoreType.DMA((line,)),
        ],
        compiler_params=pltpu.CompilerParams(
            collective_id=1, has_side_effects=True, vmem_limit_bytes=VMEM_MOST
        ),
        cost_estimate=pl.CostEstimate(flops=work, bytes_accessed=2**26, transcendentals=0),
    )(rows, cots, gates, up, down)


def weight_grads_kernel(rows, cots, gated, inner, up_grad, down_grad):
    step = 256
    for at in range(0, rows.shape[1], step):
        up_grad[0, at : at + step] = contract(rows[:, at : at + step], inner[...], 0, 0).astype(BF16)
        down_grad[0, at : at + step] = contract(cots[:, at : at + step], gated[...], 0, 0).astype(
            BF16
        )


def weight_grads(rows, cots, gated, inner, experts):
    tokens, width = rows.shape
    ff_width = gated.shape[1] // experts
    whole = pl.BlockSpec((tokens, width), lambda e: (0, 0))
    return pl.pallas_call(
        weight_grads_kernel,
        grid=(experts,),
        out_shape=(
            jax.ShapeDtypeStruct((experts, width, 2 * ff_width), BF16),
            jax.ShapeDtypeStruct((experts, width, ff_width), BF16),
        ),
        in_specs=[
            whole,
            whole,
            pl.BlockSpec((tokens, ff_width), lambda e: (0, e)),
            pl.BlockSpec((tokens, 2 * ff_width), lambda e: (0, e)),
        ],
        out_specs=(
            pl.BlockSpec((1, width, 2 * ff_width), lambda e: (e, 0, 0)),
            pl.BlockSpec((1, width, ff_width), lambda e: (e, 0, 0)),
        ),
        compiler_params=pltpu.CompilerParams(vmem_limit_bytes=VMEM_MOST),
        cost_estimate=pl.CostEstimate(
            flops=6 * tokens * width * experts * ff_width,
            bytes_accessed=2 * tokens * (2 * width + 3 * experts * ff_width)
            + 6 * experts * width * ff_width,
            transcendentals=0,
        ),
    )(rows, cots, gated, inner)


def bank_grads_kernel(
    rows_hbm,
    cots_hbm,
    gated_hbm,
    inner_hbm,
    sum_hbm,
    rows,
    cots,
    gated,
    inner,
    grads,
    core_sum,
    first_sum,
    last_sum,
    total,
    load_sem,
    send_sem,
    recv_sem,
    out_sem,
):
    experts = grads.shape[0]
    ff_width = gated.shape[2]
    block_rows = grads.shape[4]
    dp = lax.axis_index("dp")
    z = lax.axis_index("expert")
    y, x, core = dp // 4, lax.rem(dp // 2, 2), lax.rem(dp, 2)
    core_peer, x_peer, y_peer = dp + 1 - 2 * core, dp + 2 - 4 * x, dp + 4 - 8 * y

    def loads(e, slot):
        return (
            pltpu.make_async_copy(
                gated_hbm.at[:, pl.ds(pl.multiple_of(e * ff_width, ff_width), ff_width)],
                gated.at[slot],
                load_sem.at[slot, 0],
            ),
            pltpu.make_async_copy(
                inner_hbm.at[:, pl.ds(pl.multiple_of(2 * e * ff_width, ff_width), 2 * ff_width)],
                inner.at[slot],
                load_sem.at[slot, 1],
            ),
        )

    row_load = pltpu.make_async_copy(rows_hbm, rows, load_sem.at[0, 2])
    cot_load = pltpu.make_async_copy(cots_hbm, cots, load_sem.at[1, 2])
    row_load.start()
    for copy in loads(0, 0):
        copy.start()
    cot_load.start()
    barrier = pltpu.get_barrier_semaphore()
    for peer in (core_peer, x_peer, y_peer):
        pl.semaphore_signal(barrier, inc=1, device_id=(peer, z), device_id_type=MESH)
    pl.semaphore_wait(barrier, 3)
    row_load.wait()
    cot_load.wait()

    def send(stage, e, source, target, peer):
        return pltpu.make_async_remote_copy(
            src_ref=source,
            dst_ref=target,
            send_sem=send_sem.at[stage, e],
            recv_sem=recv_sem.at[stage, e],
            device_id=(peer, z),
            device_id_type=MESH,
        )

    def core_send(e):
        return send(0, e, grads.at[e, :, :, 1 - core], core_sum.at[e], core_peer)

    def first_send(e, along_x):
        if along_x:
            return send(1, e, core_sum.at[e, :, 1 - x], first_sum.at[e], x_peer)
        return send(1, e, core_sum.at[e, 1 - y], first_sum.at[e], y_peer)

    def last_send(e, along_x):
        if along_x:
            return send(2, e, first_sum.at[e, 1 - x], last_sum.at[e], x_peer)
        return send(2, e, first_sum.at[e, 1 - y], last_sum.at[e], y_peer)

    def by_parity(e, act):
        even = lax.rem(e, 2) == 0

        @pl.when(even)
        def _():
            act(True)

        @pl.when(jnp.logical_not(even))
        def _():
            act(False)

    def after_core(e):
        core_send(e).wait_recv()
        for yy in range(2):
            for xx in range(2):
                core_sum[e, yy, xx] = (
                    grads[e, yy, xx, core].astype(F32) + core_sum[e, yy, xx].astype(F32)
                ).astype(BF16)
        by_parity(e, lambda even: first_send(e, even).start())

    def after_first(e):
        def act(even):
            first_send(e, even).wait_recv()
            for other in range(2):
                kept = core_sum[e, other, x] if even else core_sum[e, y, other]
                first_sum[e, other] = (
                    kept.astype(F32) + first_sum[e, other].astype(F32)
                ).astype(BF16)
            last_send(e, not even).start()

        by_parity(e, act)

    def after_last(e):
        def act(even):
            last_send(e, not even).wait_recv()
            kept = first_sum[e, y] if even else first_sum[e, x]
            total[e] = kept.astype(F32) + last_sum[e].astype(F32)

        by_parity(e, act)
        pltpu.make_async_copy(total.at[e], sum_hbm.at[e], out_sem.at[e]).start()

    def step(e, _):
        slot = lax.rem(e, 2)
        for copy in loads(e, slot):
            copy.wait()

        @pl.when(e + 1 < experts)
        def _():
            for copy in loads(e + 1, 1 - slot):
                copy.start()

        def tile(at, _):
            columns = pl.ds(pl.multiple_of(at * 2 * block_rows, 2 * block_rows), 2 * block_rows)
            up_grad = contract(rows[:, columns], inner[slot], 0, 0).astype(BF16)
            down_grad = contract(cots[:, columns], gated[slot], 0, 0).astype(BF16)
            for side in range(2):
                part = slice(side * block_rows, (side + 1) * block_rows)
                grads[e, at // 2, lax.rem(at, 2), side, :, : 2 * ff_width] = up_grad[part]
                grads[e, at // 2, lax.rem(at, 2), side, :, 2 * ff_width :] = down_grad[part]
            return 0

        lax.fori_loop(0, 4, tile, 0)
        core_send(e).start()

        @pl.when(e >= 1)
        def _():
            after_core(e - 1)

        @pl.when(e >= 3)
        def _():
            after_first(e - 3)

        return 0

    lax.fori_loop(0, experts, step, 0)
    after_core(experts - 1)

    for e in range(max(experts - 3, 0), experts):
        after_first(e)
        if e - 2 >= 0:
            after_last(e - 2)
    for e in range(max(experts - 2, 0), experts):
        after_last(e)
    for e in range(experts):
        core_send(e).wait_send()
        first_send(e, e % 2 == 0).wait_send()
        last_send(e, e % 2 == 1).wait_send()
        pltpu.make_async_copy(total.at[e], sum_hbm.at[e], out_sem.at[e]).wait()


def bank_grads(rows, cots, gated, inner, experts):
    tokens, width = rows.shape
    ff_width = gated.shape[1] // experts
    lanes = 3 * ff_width
    block_rows = width // 8
    anywhere = pl.BlockSpec(memory_space=pl.ANY)
    return pl.pallas_call(
        bank_grads_kernel,
        out_shape=jax.ShapeDtypeStruct((experts, block_rows, lanes), F32),
        in_specs=[anywhere] * 4,
        out_specs=anywhere,
        scratch_shapes=[
            pltpu.VMEM((tokens, width), BF16),
            pltpu.VMEM((tokens, width), BF16),
            pltpu.VMEM((2, tokens, ff_width), BF16),
            pltpu.VMEM((2, tokens, 2 * ff_width), BF16),
            pltpu.VMEM((experts, 2, 2, 2, block_rows, lanes), BF16),
            pltpu.VMEM((experts, 2, 2, block_rows, lanes), BF16),
            pltpu.VMEM((experts, 2, block_rows, lanes), BF16),
            pltpu.VMEM((experts, block_rows, lanes), BF16),
            pltpu.VMEM((experts, block_rows, lanes), F32),
            pltpu.SemaphoreType.DMA((2, 3)),
            pltpu.SemaphoreType.DMA((3, experts)),
            pltpu.SemaphoreType.DMA((3, experts)),
            pltpu.SemaphoreType.DMA((experts,)),
        ],
        compiler_params=pltpu.CompilerParams(
            collective_id=2, has_side_effects=True, vmem_limit_bytes=VMEM_MOST
        ),
        cost_estimate=pl.CostEstimate(
            flops=6 * tokens * width * experts * ff_width,
            bytes_accessed=2**27,
            transcendentals=0,
        ),
    )(rows, cots, gated, inner)


PAIR = 2 * HEAD_DIM
UNIT = 512


def line_gather(line, z, dp, source, landing, send_sem, recv_sem):
    def copy(origin, block, sem, target):
        return pltpu.make_async_remote_copy(
            src_ref=origin,
            dst_ref=landing.at[block],
            send_sem=send_sem.at[sem],
            recv_sem=recv_sem.at[block],
            device_id=(dp, target),
            device_id_type=MESH,
        )

    def start():
        @pl.when(z < line - 1)
        def _():
            copy(source, z, line, z + 1).start()

        @pl.when(z > 0)
        def _():
            copy(source, z, line + 1, z - 1).start()

    def pass_on(apart):
        low = jnp.maximum(z - apart, 0)
        high = jnp.minimum(z + apart, line - 1)

        @pl.when(z - apart >= 0)
        def _():
            copy(source, low, low, z).wait_recv()

            @pl.when(z < line - 1)
            def _():
                copy(landing.at[low], low, low, z + 1).start()

        @pl.when(z + apart < line)
        def _():
            copy(source, high, high, z).wait_recv()

            @pl.when(z > 0)
            def _():
                copy(landing.at[high], high, high, z - 1).start()

    def finish():
        @pl.when(z < line - 1)
        def _():
            copy(source, z, line, z + 1).wait_send()

        @pl.when(z > 0)
        def _():
            copy(source, z, line + 1, z - 1).wait_send()

        for s in range(line):

            @pl.when(((s < z) & (z < line - 1)) | ((s > z) & (z > 0)))
            def _(s=s):
                copy(source, s, s, z).wait_send()

    return start, pass_on, finish


def swap_halves(value):
    lane = lax.broadcasted_iota(jnp.int32, value.shape, 1)
    half = HEAD_DIM // 2
    return jnp.where(
        lax.rem(lane, HEAD_DIM) < half,
        pltpu.roll(value, value.shape[1] - half, 1),
        pltpu.roll(value, half, 1),
    )


def sides(pair, side, scale):
    value = pair.astype(F32)
    if scale is not None:
        value = value * scale
    turned = pltpu.roll(value, HEAD_DIM, 1)
    lane = lax.broadcasted_iota(jnp.int32, value.shape, 1)
    left, right = (value, turned) if side == 0 else (turned, value)
    return (
        jnp.where(lane < HEAD_DIM, left, 0.0).astype(BF16),
        jnp.where(lane < HEAD_DIM, 0.0, right).astype(BF16),
    )


def lanes_at(start, size):
    return pl.ds(pl.multiple_of(start, 128), size)


def attend_kernel(
    line,
    tokens,
    cots_hbm,
    gain_rows,
    heads_in,
    heads_out,
    router_rows,
    route_rows,
    cosine,
    sine,
    bias,
    first_in,
    queries,
    keys,
    values,
    attended,
    hidden,
    second_in,
    gate_rows,
    log_totals,
    cots_all,
    send_sem,
    recv_sem,
    own_sem,
):
    dp = lax.axis_index("dp")
    z = lax.axis_index("expert")
    start, pass_on, finish = line_gather(line, z, dp, cots_hbm, cots_all, send_sem, recv_sem)
    barrier = pltpu.get_barrier_semaphore()
    for step in range(1, line):
        pl.semaphore_signal(
            barrier, inc=1, device_id=(dp, lax.rem(z + step, line)), device_id_type=MESH
        )
    pl.semaphore_wait(barrier, line - 1)
    start()
    own = pltpu.make_async_copy(cots_hbm, cots_all.at[z], own_sem)
    own.start()

    query_end = HEADS * HEAD_DIM
    key_end = query_end + KV_HEADS * HEAD_DIM
    token_rows = tokens[...].astype(F32)
    factor = lax.rsqrt(jnp.mean(token_rows * token_rows, axis=1, keepdims=True) + EPS)
    first_in[...] = (token_rows * factor * gain_rows[0:1]).astype(BF16)
    log_totals[...] = jnp.zeros_like(log_totals)

    def pair(j, _):
        for side in range(2):
            wide = contract(
                first_in[...], heads_in[:, lanes_at((2 * j + side) * PAIR, PAIR)], 1, 0
            )
            queries[:, lanes_at((2 * j + side) * PAIR, PAIR)] = (
                wide * cosine[...] + swap_halves(wide) * sine[...]
            ).astype(BF16)
        wide = contract(first_in[...], heads_in[:, lanes_at(query_end + j * PAIR, PAIR)], 1, 0)
        keys[:, lanes_at(j * PAIR, PAIR)] = (
            wide * cosine[...] + swap_halves(wide) * sine[...]
        ).astype(BF16)
        values[:, lanes_at(j * PAIR, PAIR)] = contract(
            first_in[...], heads_in[:, lanes_at(key_end + j * PAIR, PAIR)], 1, 0
        ).astype(BF16)
        for side in range(2):
            group = queries[:, lanes_at((2 * j + side) * PAIR, PAIR)]
            key_sides = sides(keys[:, lanes_at(j * PAIR, PAIR)], side, SCALE)
            value_sides = sides(values[:, lanes_at(j * PAIR, PAIR)], side, None)
            total = jnp.zeros(group.shape, F32)
            for member in range(2):
                scores = contract(group, key_sides[member], 1, 1) + bias[...]
                peak = jnp.max(scores, axis=1, keepdims=True)
                powers = jnp.exp(scores - peak)
                amount = jnp.sum(powers, axis=1, keepdims=True)
                lane = lax.broadcasted_iota(jnp.int32, log_totals.shape, 1)
                log_totals[...] = jnp.where(
                    lane == 4 * j + 2 * side + member, peak + jnp.log(amount), log_totals[...]
                )
                weights = (powers * (1.0 / amount)).astype(BF16)
                total = total + contract(weights, value_sides[member], 1, 0)
            attended[:, lanes_at((2 * j + side) * PAIR, PAIR)] = total.astype(BF16)
        return 0

    lax.fori_loop(0, KV_HEADS // 2, pair, 0)
    pass_on(1)
    hidden_rows = token_rows + contract(attended[...], heads_out[...], 1, 1)
    hidden[...] = hidden_rows
    factor = lax.rsqrt(jnp.mean(hidden_rows * hidden_rows, axis=1, keepdims=True) + EPS)
    second = (hidden_rows * factor * gain_rows[1:2]).astype(BF16)
    second_in[...] = second
    logits = contract(router_rows[...], second, 1, 1)
    expert = lax.broadcasted_iota(jnp.int32, logits.shape, 0)
    named = expert == route_rows[0:1]
    for k in range(1, route_rows.shape[0]):
        named = named | (expert == route_rows[k : k + 1])
    peak = jnp.max(jnp.where(named, logits, -1e30), axis=0, keepdims=True)
    powers = jnp.where(named, jnp.exp(jnp.where(named, logits, peak) - peak), 0.0)
    gate_rows[...] = powers / jnp.sum(powers, axis=0, keepdims=True)
    for apart in range(2, line):
        pass_on(apart)
    finish()
    own.wait()


def attend(tokens, cots, gain_rows, heads_in, heads_out, router_rows, route_rows, tables, line):
    count, width = tokens.shape
    experts = router_rows.shape[0]
    kv_width = KV_HEADS * HEAD_DIM
    shape = jax.ShapeDtypeStruct
    held = pl.BlockSpec(memory_space=pltpu.VMEM)
    anywhere = pl.BlockSpec(memory_space=pl.ANY)
    return pl.pallas_call(
        functools.partial(attend_kernel, line),
        out_shape=(
            shape((count, width), BF16),
            shape((count, HEADS * HEAD_DIM), BF16),
            shape((count, kv_width), BF16),
            shape((count, kv_width), BF16),
            shape((count, HEADS * HEAD_DIM), BF16),
            shape((count, width), F32),
            shape((count, width), BF16),
            shape((experts, count), F32),
            shape((count, 128), F32),
            shape((line, count, width), BF16),
        ),
        in_specs=[held, anywhere] + [held] * 8,
        out_specs=(held,) * 9 + (anywhere,),
        scratch_shapes=[
            pltpu.SemaphoreType.DMA((line + 2,)),
            pltpu.SemaphoreType.DMA((line,)),
            pltpu.SemaphoreType.DMA,
        ],
        compiler_params=pltpu.CompilerParams(
            collective_id=4, has_side_effects=True, vmem_limit_bytes=VMEM_MOST
        ),
        cost_estimate=pl.CostEstimate(flops=2**33, bytes_accessed=2**24, transcendentals=2**21),
    )(tokens, cots, gain_rows, heads_in, heads_out, router_rows, route_rows, *tables)


def attend_back_kernel(
    paired,
    line,
    back_rows,
    hidden,
    cots,
    second_in,
    gate_rows,
    gate_grads,
    router_rows,
    gain_rows,
    heads_out,
    queries,
    keys,
    values,
    attended,
    log_totals,
    cosine,
    sine,
    bias,
    tokens_hbm,
    first_hbm,
    in_hbm,
    token_grad,
    sum_hbm,
    small_hbm,
    tokens,
    first_in,
    heads_in,
    grad_hidden,
    grad_attended,
    grad_projected,
    small_rows,
    own,
    own_small,
    *scratch,
):
    dp = lax.axis_index("dp")
    z = lax.axis_index("expert")
    units = own.shape[0]
    block_rows = own.shape[4]
    load_sem = scratch[0]
    loads = (
        pltpu.make_async_copy(first_hbm, first_in, load_sem.at[0]),
        pltpu.make_async_copy(tokens_hbm, tokens, load_sem.at[1]),
        pltpu.make_async_copy(in_hbm, heads_in, load_sem.at[2]),
    )
    for copy in loads:
        copy.start()
    if paired:
        (
            cores,
            firsts,
            lasts,
            sums,
            lines,
            totals,
            small_cores,
            small_firsts,
            small_lasts,
            small_sums,
            small_lines,
            small_totals,
            send_sem,
            recv_sem,
            line_send,
            line_recv,
            out_sem,
        ) = scratch[1:]
        rows = totals.shape[1]
        y, x, core = dp // 4, lax.rem(dp // 2, 2), lax.rem(dp, 2)
        core_peer, x_peer, y_peer = dp + 1 - 2 * core, dp + 2 - 4 * x, dp + 4 - 8 * y
        barrier = pltpu.get_barrier_semaphore()
        for peer in (core_peer, x_peer, y_peer):
            pl.semaphore_signal(barrier, inc=1, device_id=(peer, z), device_id_type=MESH)
        for step in range(1, line):
            pl.semaphore_signal(
                barrier, inc=1, device_id=(dp, lax.rem(z + step, line)), device_id_type=MESH
            )
        pl.semaphore_wait(barrier, 3 + line - 1)
        buffers = (own, cores, firsts, lasts, sums, lines, totals)
        small_buffers = (
            own_small,
            small_cores,
            small_firsts,
            small_lasts,
            small_sums,
            small_lines,
            small_totals,
        )

        def send(stage, u, source, target, peer):
            return pltpu.make_async_remote_copy(
                src_ref=source,
                dst_ref=target,
                send_sem=send_sem.at[stage, u],
                recv_sem=recv_sem.at[stage, u],
                device_id=(peer, z),
                device_id_type=MESH,
            )

        class Sums:
            def __init__(self, held, shift):
                self.own, self.cores, self.firsts, self.lasts = held[:4]
                self.sums, self.lines, self.totals = held[4:]
                self.shift = shift

            def core_send(self, u):
                return send(
                    0,
                    u + self.shift,
                    self.own.at[u, :, :, 1 - core],
                    self.cores.at[u],
                    core_peer,
                )

            def first_send(self, u, along_x):
                if along_x:
                    source, peer = self.cores.at[u, :, 1 - x], x_peer
                else:
                    source, peer = self.cores.at[u, 1 - y], y_peer
                return send(1, u + self.shift, source, self.firsts.at[u], peer)

            def last_send(self, u, along_x):
                if along_x:
                    source, peer = self.firsts.at[u, 1 - x], x_peer
                else:
                    source, peer = self.firsts.at[u, 1 - y], y_peer
                return send(2, u + self.shift, source, self.lasts.at[u], peer)

            def line_copy(self, u, step):
                peer = lax.rem(z + step, line)
                return pltpu.make_async_remote_copy(
                    src_ref=self.sums.at[u, pl.ds(pl.multiple_of(peer * rows, rows), rows)],
                    dst_ref=self.lines.at[u, step],
                    send_sem=line_send.at[u + self.shift, step],
                    recv_sem=line_recv.at[u + self.shift, step],
                    device_id=(dp, peer),
                    device_id_type=MESH,
                )

            def by_parity(self, u, act):
                even = lax.rem(jnp.int32(u), 2) == 0

                @pl.when(even)
                def _():
                    act(True)

                @pl.when(jnp.logical_not(even))
                def _():
                    act(False)

            def after_core(self, u):
                self.core_send(u).wait_recv()
                for yy in range(2):
                    for xx in range(2):
                        self.cores[u, yy, xx] = (
                            self.own[u, yy, xx, core].astype(F32)
                            + self.cores[u, yy, xx].astype(F32)
                        ).astype(BF16)
                self.by_parity(u, lambda even: self.first_send(u, even).start())

            def after_first(self, u):
                def act(even):
                    self.first_send(u, even).wait_recv()
                    for other in range(2):
                        kept = self.cores[u, other, x] if even else self.cores[u, y, other]
                        self.firsts[u, other] = (
                            kept.astype(F32) + self.firsts[u, other].astype(F32)
                        ).astype(BF16)
                    self.last_send(u, not even).start()

                self.by_parity(u, act)

            def after_last(self, u):
                def act(even):
                    self.last_send(u, not even).wait_recv()
                    kept = self.firsts[u, y] if even else self.firsts[u, x]
                    self.sums[u] = (kept.astype(F32) + self.lasts[u].astype(F32)).astype(BF16)

                self.by_parity(u, act)
                for step in range(1, line):
                    self.line_copy(u, step).start()

            def after_line(self, u):
                value = self.sums[u, pl.ds(pl.multiple_of(z * rows, rows), rows)].astype(F32)
                for step in range(1, line):
                    self.line_copy(u, step).wait_recv()
                    value = value + self.lines[u, step].astype(F32)
                self.totals[u] = value

            def finish(self, u):
                self.core_send(u).wait_send()
                self.first_send(u, u % 2 == 0).wait_send()
                self.last_send(u, u % 2 == 1).wait_send()
                for step in range(1, line):
                    self.line_copy(u, step).wait_send()

        wide_sums = Sums(buffers, 0)
        small_sum = Sums(small_buffers, units)

    def keep(target, u, value):
        for block in range(8):
            target[u, block // 4, block // 2 % 2, block % 2] = value[
                block * block_rows : (block + 1) * block_rows
            ]

    gates = gate_rows[...]
    gate_grad = gate_grads[...]
    logit_grad = gates * (gate_grad - jnp.sum(gates * gate_grad, axis=0, keepdims=True))
    high = logit_grad.astype(BF16)
    low = (logit_grad - high.astype(F32)).astype(BF16)
    grad_second = (
        back_rows[...].astype(F32)
        + contract(high, router_rows[...], 0, 0)
        + contract(low, router_rows[...], 0, 0)
    )
    small_rows[...] = jnp.zeros_like(small_rows)
    experts = high.shape[0]
    small_rows[:experts] = contract(high, second_in[...], 1, 0) + contract(low, second_in[...], 1, 0)

    def norm_back(incoming, rows, gain):
        factor = lax.rsqrt(jnp.mean(rows * rows, axis=1, keepdims=True) + EPS)
        normed = rows * factor
        gain_grad = jnp.sum(incoming * normed, axis=0, keepdims=True)
        weighted = incoming * gain
        mean = jnp.mean(weighted * normed, axis=1, keepdims=True)
        return factor * (weighted - normed * mean), gain_grad

    norm_grad, gain_grad = norm_back(grad_second, hidden[...], gain_rows[1:2])
    small_rows[experts + 1 : experts + 2] = gain_grad
    grad_hidden[...] = cots[...].astype(F32) + norm_grad
    branch = grad_hidden[...].astype(BF16)
    for u in range(2):
        keep(
            own,
            u,
            contract(branch, attended[:, u * UNIT : (u + 1) * UNIT], 0, 0).astype(BF16),
        )
        if paired:
            wide_sums.core_send(u).start()
    grad_attended[...] = contract(branch, heads_out[...], 1, 0).astype(BF16)
    loads[0].wait()
    if paired:
        wide_sums.after_core(0)

    def pair(j, _):
        key_pair = keys[:, lanes_at(j * PAIR, PAIR)]
        value_pair = values[:, lanes_at(j * PAIR, PAIR)]
        key_grads = []
        value_grads = []
        for side in range(2):
            at = lanes_at((2 * j + side) * PAIR, PAIR)
            group = queries[:, at]
            group_grad = grad_attended[:, at]
            key_sides = sides(key_pair, side, SCALE)
            value_sides = sides(value_pair, side, None)
            product = group_grad.astype(F32) * attended[:, at].astype(F32)
            lane = lax.broadcasted_iota(jnp.int32, product.shape, 1)
            grad = jnp.zeros(group.shape, F32)
            key_grad = []
            value_grad = []
            for member in range(2):
                head = 4 * j + 2 * side + member
                log_total = jnp.sum(
                    jnp.where(lane == head, log_totals[...], 0.0), axis=1, keepdims=True
                )
                mine = (lane < HEAD_DIM) if member == 0 else (lane >= HEAD_DIM)
                spread = jnp.sum(jnp.where(mine, product, 0.0), axis=1, keepdims=True)
                scores = contract(group, key_sides[member], 1, 1) + bias[...]
                weights = jnp.exp(scores - log_total)
                weight_grads = contract(group_grad, value_sides[member], 1, 1)
                score_grads = (weights * (weight_grads - spread)).astype(BF16)
                grad = grad + contract(score_grads, key_sides[member], 1, 0)
                rows_of = slice(member * HEAD_DIM, (member + 1) * HEAD_DIM)
                key_grad.append(contract(group, score_grads, 0, 0)[rows_of])
                value_grad.append(contract(group_grad, weights.astype(BF16), 0, 0)[rows_of])
            grad_projected[j, :, side * PAIR : (side + 1) * PAIR] = (
                grad * cosine[...] - swap_halves(grad) * sine[...]
            ).astype(BF16)
            key_grads.append(key_grad[0] + key_grad[1])
            value_grads.append(value_grad[0] + value_grad[1])
        key_rows = jnp.concatenate(key_grads, axis=0).T * SCALE
        grad_projected[j, :, 2 * PAIR : 3 * PAIR] = (
            key_rows * cosine[...] - swap_halves(key_rows) * sine[...]
        ).astype(BF16)
        grad_projected[j, :, 3 * PAIR :] = jnp.concatenate(value_grads, axis=0).T.astype(BF16)
        keep(own, 2 + j, contract(first_in[...], grad_projected[j], 0, 0).astype(BF16))
        if paired:
            wide_sums.core_send(2 + j).start()
            wide_sums.after_core(1 + j)
            wide_sums.after_first(j)

            @pl.when(j >= 1)
            def _():
                wide_sums.after_last(j - 1)

            @pl.when(j >= 2)
            def _():
                wide_sums.after_line(j - 2)

        return 0

    pairs = KV_HEADS // 2
    lax.fori_loop(0, pairs, pair, 0)
    last = units - 1
    if paired:
        wide_sums.after_core(last)
        wide_sums.after_first(last - 1)
        wide_sums.after_last(last - 2)
    loads[1].wait()
    loads[2].wait()
    grad_first = jnp.zeros(grad_hidden.shape, F32)
    query_end = HEADS * HEAD_DIM
    key_end = query_end + KV_HEADS * HEAD_DIM
    for j in range(pairs):
        for at, begin, size in (
            (0, 2 * j * PAIR, 2 * PAIR),
            (2 * PAIR, query_end + j * PAIR, PAIR),
            (3 * PAIR, key_end + j * PAIR, PAIR),
        ):
            grad_first = grad_first + contract(
                grad_projected[j, :, at : at + size], heads_in[:, begin : begin + size], 1, 1
            )
    norm_grad, gain_grad = norm_back(grad_first, tokens[...].astype(F32), gain_rows[0:1])
    small_rows[experts : experts + 1] = gain_grad
    keep(own_small, 0, small_rows[...].T.astype(BF16))
    if paired:
        small_sum.core_send(0).start()
    token_grad[...] = grad_hidden[...] + norm_grad
    if paired:
        wide_sums.after_line(last - 3)
        small_sum.after_core(0)
        wide_sums.after_first(last)
        wide_sums.after_last(last - 1)
        wide_sums.after_line(last - 2)
        small_sum.after_first(0)
        wide_sums.after_last(last)
        small_sum.after_last(0)
        wide_sums.after_line(last - 1)
        wide_sums.after_line(last)
        small_sum.after_line(0)
        outs = (
            pltpu.make_async_copy(totals, sum_hbm, out_sem.at[0]),
            pltpu.make_async_copy(small_totals, small_hbm, out_sem.at[1]),
        )
    else:
        outs = (
            pltpu.make_async_copy(own, sum_hbm, load_sem.at[3]),
            pltpu.make_async_copy(own_small, small_hbm, load_sem.at[4]),
        )
    for copy in outs:
        copy.start()
    if paired:
        for u in range(units):
            wide_sums.finish(u)
        small_sum.finish(0)
    for copy in outs:
        copy.wait()


def attend_back(held_args, far_args, paired, line):
    tokens, first_in, heads_in = far_args
    count, width = tokens.shape
    pairs = KV_HEADS // 2
    units = 2 + pairs
    block_rows = width // 8
    rows = block_rows // line
    shape = jax.ShapeDtypeStruct
    held = pl.BlockSpec(memory_space=pltpu.VMEM)
    anywhere = pl.BlockSpec(memory_space=pl.ANY)
    if paired:
        sum_shapes = (shape((units, rows, UNIT), F32), shape((1, rows, 128), F32))
    else:
        sum_shapes = (
            shape((units, 2, 2, 2, block_rows, UNIT), BF16),
            shape((1, 2, 2, 2, block_rows, 128), BF16),
        )
    exchange = []
    if paired:
        for number, lanes in ((units, UNIT), (1, 128)):
            exchange += [
                pltpu.VMEM((number, 2, 2, block_rows, lanes), BF16),
                pltpu.VMEM((number, 2, block_rows, lanes), BF16),
                pltpu.VMEM((number, block_rows, lanes), BF16),
                pltpu.VMEM((number, block_rows, lanes), BF16),
                pltpu.VMEM((number, line, rows, lanes), BF16),
                pltpu.VMEM((number, rows, lanes), F32),
            ]
        exchange += [
            pltpu.SemaphoreType.DMA((3, units + 1)),
            pltpu.SemaphoreType.DMA((3, units + 1)),
            pltpu.SemaphoreType.DMA((units + 1, line)),
            pltpu.SemaphoreType.DMA((units + 1, line)),
            pltpu.SemaphoreType.DMA((2,)),
        ]
    settings = dict(vmem_limit_bytes=VMEM_MOST)
    if paired:
        settings.update(collective_id=3, has_side_effects=True)
    return pl.pallas_call(
        functools.partial(attend_back_kernel, paired, line),
        out_shape=(shape((count, width), F32),) + sum_shapes,
        in_specs=[held] * len(held_args) + [anywhere] * 3,
        out_specs=(held, anywhere, anywhere),
        scratch_shapes=[
            pltpu.VMEM((count, width), BF16),
            pltpu.VMEM((count, width), BF16),
            pltpu.VMEM(heads_in.shape, BF16),
            pltpu.VMEM((count, width), F32),
            pltpu.VMEM((count, HEADS * HEAD_DIM), BF16),
            pltpu.VMEM((pairs, count, 4 * PAIR), BF16),
            pltpu.VMEM((128, width), F32),
            pltpu.VMEM((units, 2, 2, 2, block_rows, UNIT), BF16),
            pltpu.VMEM((1, 2, 2, 2, block_rows, 128), BF16),
            pltpu.SemaphoreType.DMA((5,)),
            *exchange,
        ],
        compiler_params=pltpu.CompilerParams(**settings),
        cost_estimate=pl.CostEstimate(flops=2**34, bytes_accessed=2**25, transcendentals=2**21),
    )(*held_args, *far_args)


def unit_columns(sums):
    pairs = KV_HEADS // 2
    parts = sums[2 : 2 + pairs]
    rows = sums.shape[1]

    def side_by_side(value):
        return jnp.transpose(value, (1, 0, 2)).reshape(rows, -1)

    return (
        jnp.concatenate(
            [
                side_by_side(parts[:, :, : 2 * PAIR]),
                side_by_side(parts[:, :, 2 * PAIR : 3 * PAIR]),
                side_by_side(parts[:, :, 3 * PAIR :]),
            ],
            axis=1,
        ),
        side_by_side(sums[:2]),
    )


def body(
    tokens,
    cotangent,
    routes,
    cont_ids,
    norm_gains,
    gains_moment,
    gains_average,
    heads_in,
    heads_in_master,
    heads_in_moment,
    heads_in_average,
    heads_out,
    heads_out_master,
    heads_out_moment,
    heads_out_average,
    router,
    router_master,
    router_moment,
    router_average,
    expert_in,
    expert_in_master,
    expert_in_moment,
    expert_in_average,
    expert_out,
    expert_out_master,
    expert_out_moment,
    expert_out_average,
):
    token_count, model_width = tokens.shape
    local_experts = expert_in.shape[0]
    peer_count = lax.axis_size("expert")
    experts = local_experts * peer_count
    paired = lax.axis_size("dp") == 8 and peer_count == 4
    positions, allowed = layout(cont_ids[0], token_count - cont_ids.shape[1])
    tables = (*rope_tables(positions), jnp.where(allowed, 0.0, -1e30))
    gain_rows = norm_gains.T
    router_rows = router.T
    (
        first_in,
        queries,
        key_rows,
        value_rows,
        attended,
        hidden,
        second_in,
        gates,
        log_totals,
        cots_all,
    ) = attend(
        tokens,
        cotangent,
        gain_rows,
        heads_in,
        heads_out,
        router_rows,
        routes.T,
        tables,
        peer_count,
    )
    padded = -local_experts % 8
    gate_rows = jnp.pad(
        gates.reshape(peer_count, local_experts, token_count), ((0, 0), (0, padded), (0, 0))
    )
    mix_part, grad_part, gate_grads, gated, grad_gate_up, rows_all = bank(
        second_in, cots_all, gate_rows, expert_in, expert_out, peer_count
    )
    back_rows = lax.psum_scatter(
        grad_part.reshape(peer_count * token_count, model_width),
        "expert",
        scatter_dimension=0,
        tiled=True,
    )
    grad_sources = (
        rows_all.reshape(peer_count * token_count, model_width),
        cots_all.reshape(peer_count * token_count, model_width),
        gated.reshape(peer_count * token_count, -1),
        grad_gate_up.reshape(peer_count * token_count, -1),
    )
    if paired:
        bank_sums = bank_grads(*grad_sources, local_experts)
        expert_sums = (bank_sums[:, :, : expert_in.shape[2]], bank_sums[:, :, expert_in.shape[2] :])
    else:
        expert_sums = tuple(
            lax.psum_scatter(part, "dp", scatter_dimension=1, tiled=True).astype(jnp.float32)
            for part in weight_grads(*grad_sources, local_experts)
        )
    mix_part, back_rows, expert_sums = lax.optimization_barrier(
        (mix_part, back_rows, expert_sums)
    )
    mixture = lax.psum_scatter(
        mix_part.reshape(peer_count * token_count, model_width),
        "expert",
        scatter_dimension=0,
        tiled=True,
    ).astype(jnp.float32)
    output = (hidden + mixture).astype(jnp.bfloat16)
    token_grad, unit_sums, small_sum = attend_back(
        (
            back_rows,
            hidden,
            cotangent,
            second_in,
            gates,
            gate_grads[:, :local_experts].reshape(experts, token_count),
            router_rows,
            gain_rows,
            heads_out,
            queries,
            key_rows,
            value_rows,
            attended,
            log_totals,
            *tables,
        ),
        (tokens, first_in, heads_in),
        paired,
        peer_count,
    )
    if paired:
        small_sum = small_sum[0]
    else:
        head_parts = unit_columns(unit_sums.reshape(unit_sums.shape[0], model_width, UNIT))
        packed = jnp.concatenate([*head_parts, small_sum.reshape(model_width, 128)], axis=1)
        head_total = lax.psum_scatter(
            packed, ("dp", "expert"), scatter_dimension=0, tiled=True
        ).astype(jnp.float32)
        cut_in = head_parts[0].shape[1]
        cut_out = cut_in + head_parts[1].shape[1]
        head_parts = (head_total[:, :cut_in], head_total[:, cut_in:cut_out])
        small_sum = head_total[:, cut_out:]
    if paired:
        head_parts = unit_columns(unit_sums)
    head_in_sum, head_out_sum = head_parts
    summed = (
        head_in_sum,
        head_out_sum,
        small_sum[:, :experts],
        small_sum[:, experts : experts + 2],
    )
    shard_rows = model_width // lax.axis_size(("dp", "expert"))
    gains_share = lax.dynamic_slice_in_dim(
        norm_gains, lax.axis_index(("dp", "expert")) * shard_rows, shard_rows, 0
    )
    gains_new = update(summed[3], gains_share, gains_moment, gains_average)
    inproj_new = update(summed[0], heads_in_master, heads_in_moment, heads_in_average)
    outproj_new = update(summed[1], heads_out_master, heads_out_moment, heads_out_average)
    router_new = update(summed[2], router_master, router_moment, router_average)
    upper_new = update(expert_sums[0], expert_in_master, expert_in_moment, expert_in_average)
    lower_new = update(expert_sums[1], expert_out_master, expert_out_moment, expert_out_average)
    return (
        output,
        token_grad,
        gains_new[0],
        gains_new[1],
        gains_new[2],
        inproj_new[0],
        inproj_new[1],
        inproj_new[2],
        outproj_new[0],
        outproj_new[1],
        outproj_new[2],
        router_new[0],
        router_new[1],
        router_new[2],
        upper_new[0],
        upper_new[1],
        upper_new[2],
        lower_new[0],
        lower_new[1],
        lower_new[2],
    )


def solution(mesh):
    return jax.shard_map(
        body,
        mesh=mesh,
        in_specs=(
            P(("dp", "expert"), None),
            P(("dp", "expert"), None),
            P(("dp", "expert"), None),
            P(("dp", "expert"), None),
            P(),
            P(("dp", "expert"), None),
            P(("dp", "expert"), None),
            P(),
            P(("dp", "expert"), None),
            P(("dp", "expert"), None),
            P(("dp", "expert"), None),
            P(),
            P(("dp", "expert"), None),
            P(("dp", "expert"), None),
            P(("dp", "expert"), None),
            P(),
            P(("dp", "expert"), None),
            P(("dp", "expert"), None),
            P(("dp", "expert"), None),
            P("expert", None, None),
            P("expert", "dp", None),
            P("expert", "dp", None),
            P("expert", "dp", None),
            P("expert", None, None),
            P("expert", "dp", None),
            P("expert", "dp", None),
            P("expert", "dp", None),
        ),
        out_specs=(
            P(("dp", "expert"), None),
            P(("dp", "expert"), None),
            P(("dp", "expert"), None),
            P(("dp", "expert"), None),
            P(("dp", "expert"), None),
            P(("dp", "expert"), None),
            P(("dp", "expert"), None),
            P(("dp", "expert"), None),
            P(("dp", "expert"), None),
            P(("dp", "expert"), None),
            P(("dp", "expert"), None),
            P(("dp", "expert"), None),
            P(("dp", "expert"), None),
            P(("dp", "expert"), None),
            P("expert", "dp", None),
            P("expert", "dp", None),
            P("expert", "dp", None),
            P("expert", "dp", None),
            P("expert", "dp", None),
            P("expert", "dp", None),
        ),
        check_vma=False,
    )
```

```python
import functools

import jax
import jax.numpy as jnp
from jax import lax
from jax.experimental import pallas as pl
from jax.experimental.pallas import tpu as pltpu
from jax.sharding import PartitionSpec as P

HEADS = 16
KV_HEADS = 8
HEAD_DIM = 64


EPS = 1e-06
SCALE = 0.015625
THETA = 10000.0
MOMENTUM = 0.9
DECAY = 0.8
RATE = 0.001
HIGHEST = lax.Precision.HIGHEST


def layout(labels_row, prompt_len):
    places = jnp.arange(prompt_len + labels_row.shape[0], dtype=jnp.int32)
    earlier = jnp.sum((labels_row[None, :] < labels_row[:, None]).astype(jnp.int32), axis=1)
    offset = places[prompt_len:] - prompt_len - earlier
    positions = jnp.concatenate([places[:prompt_len], prompt_len + offset]).astype(jnp.float32)
    labels = jnp.concatenate([jnp.full((prompt_len,), -1, jnp.int32), labels_row])
    allowed = (places[None, :] <= places[:, None]) & (
        (places[None, :] < prompt_len) | (labels[None, :] == labels[:, None])
    )
    return (positions, allowed)


def rope_tables(positions):
    middle = HEAD_DIM // 2
    frequency = THETA ** (-2.0 * jnp.arange(middle, dtype=jnp.float32) / HEAD_DIM)
    angles = positions[:, None] * frequency[None, :]
    cosine, sine = jnp.cos(angles), jnp.sin(angles)
    return (
        jnp.concatenate([cosine] * 4, axis=1),
        jnp.concatenate([-sine, sine, -sine, sine], axis=1),
    )


def update(gradient, master, moment, average):
    moment_next = MOMENTUM * moment + gradient
    master_next = master - RATE * (gradient + MOMENTUM * moment_next)
    return (master_next, moment_next, DECAY * average + (1.0 - DECAY) * master_next)


F32 = jnp.float32
BF16 = jnp.bfloat16
MESH = pl.DeviceIdType.MESH
VMEM_MOST = 61 * 2**20


def contract(left, right, left_axis, right_axis):
    return lax.dot_general(
        left, right, (((left_axis,), (right_axis,)), ((), ())), preferred_element_type=F32
    )


def visit_order(line):
    return [sorted(range(line), key=lambda s: (abs(s - z), s)) for z in range(line)]


def line_gather(line, z, dp, source, landing, send_sem, recv_sem):
    def copy(origin, block, sem, target):
        return pltpu.make_async_remote_copy(
            src_ref=origin,
            dst_ref=landing.at[block],
            send_sem=send_sem.at[sem],
            recv_sem=recv_sem.at[block],
            device_id=(dp, target),
            device_id_type=MESH,
        )

    def start():
        @pl.when(z < line - 1)
        def _():
            copy(source, z, line, z + 1).start()

        @pl.when(z > 0)
        def _():
            copy(source, z, line + 1, z - 1).start()

    def pass_on(apart):
        low = jnp.maximum(z - apart, 0)
        high = jnp.minimum(z + apart, line - 1)

        @pl.when(z - apart >= 0)
        def _():
            copy(source, low, low, z).wait_recv()

            @pl.when(z < line - 1)
            def _():
                copy(landing.at[low], low, low, z + 1).start()

        @pl.when(z + apart < line)
        def _():
            copy(source, high, high, z).wait_recv()

            @pl.when(z > 0)
            def _():
                copy(landing.at[high], high, high, z - 1).start()

    def finish():
        @pl.when(z < line - 1)
        def _():
            copy(source, z, line, z + 1).wait_send()

        @pl.when(z > 0)
        def _():
            copy(source, z, line + 1, z - 1).wait_send()

        for s in range(line):

            @pl.when(((s < z) & (z < line - 1)) | ((s > z) & (z > 0)))
            def _(s=s):
                copy(source, s, s, z).wait_send()

    return start, pass_on, finish


def pass_steps(line, experts):
    steps = []
    for z in range(line):
        order = visit_order(line)[z]
        for apart in range(1, line):
            met = [k for k in range(line) if abs(order[k] - z) == apart]
            if not met:
                continue
            forwards = (z - apart >= 0 and z < line - 1) or (z + apart < line and z > 0)
            early = experts // 2 if forwards and apart > 1 else 0
            steps.append((z, met[0] * experts - early, apart))
    return steps


def pick(table, row, column):
    value = jnp.int32(table[0][0])
    for r in range(len(table)):
        for c in range(len(table[0])):
            value = jnp.where((row == r) & (column == c), jnp.int32(table[r][c]), value)
    return value


def weight_grads_kernel(rows, cots, gated, inner, up_grad, down_grad):
    step = 256
    for at in range(0, rows.shape[1], step):
        up_grad[0, at : at + step] = contract(rows[:, at : at + step], inner[...], 0, 0).astype(BF16)
        down_grad[0, at : at + step] = contract(cots[:, at : at + step], gated[...], 0, 0).astype(
            BF16
        )


def weight_grads(rows, cots, gated, inner, experts):
    tokens, width = rows.shape
    ff_width = gated.shape[1] // experts
    whole = pl.BlockSpec((tokens, width), lambda e: (0, 0))
    return pl.pallas_call(
        weight_grads_kernel,
        grid=(experts,),
        out_shape=(
            jax.ShapeDtypeStruct((experts, width, 2 * ff_width), BF16),
            jax.ShapeDtypeStruct((experts, width, ff_width), BF16),
        ),
        in_specs=[
            whole,
            whole,
            pl.BlockSpec((tokens, ff_width), lambda e: (0, e)),
            pl.BlockSpec((tokens, 2 * ff_width), lambda e: (0, e)),
        ],
        out_specs=(
            pl.BlockSpec((1, width, 2 * ff_width), lambda e: (e, 0, 0)),
            pl.BlockSpec((1, width, ff_width), lambda e: (e, 0, 0)),
        ),
        compiler_params=pltpu.CompilerParams(vmem_limit_bytes=VMEM_MOST),
        cost_estimate=pl.CostEstimate(
            flops=6 * tokens * width * experts * ff_width,
            bytes_accessed=2 * tokens * (2 * width + 3 * experts * ff_width)
            + 6 * experts * width * ff_width,
            transcendentals=0,
        ),
    )(rows, cots, gated, inner)


def bank_grads_kernel(
    rows_hbm,
    cots_hbm,
    gated_hbm,
    inner_hbm,
    sum_hbm,
    rows,
    cots,
    gated,
    inner,
    grads,
    core_sum,
    first_sum,
    load_sem,
    send_sem,
    recv_sem,
    out_sem,
):
    experts = grads.shape[0]
    ff_width = gated.shape[2]
    block_rows = grads.shape[4]
    dp = lax.axis_index("dp")
    z = lax.axis_index("expert")
    y, x, core = dp // 4, lax.rem(dp // 2, 2), lax.rem(dp, 2)
    core_peer, x_peer, y_peer = dp + 1 - 2 * core, dp + 2 - 4 * x, dp + 4 - 8 * y

    def loads(e, slot):
        return (
            pltpu.make_async_copy(
                gated_hbm.at[:, pl.ds(pl.multiple_of(e * ff_width, ff_width), ff_width)],
                gated.at[slot],
                load_sem.at[slot, 0],
            ),
            pltpu.make_async_copy(
                inner_hbm.at[:, pl.ds(pl.multiple_of(2 * e * ff_width, ff_width), 2 * ff_width)],
                inner.at[slot],
                load_sem.at[slot, 1],
            ),
        )

    row_load = pltpu.make_async_copy(rows_hbm, rows, load_sem.at[0, 2])
    cot_load = pltpu.make_async_copy(cots_hbm, cots, load_sem.at[1, 2])
    row_load.start()
    for copy in loads(0, 0):
        copy.start()
    cot_load.start()
    barrier = pltpu.get_barrier_semaphore()
    for peer in (core_peer, x_peer, y_peer):
        pl.semaphore_signal(barrier, inc=1, device_id=(peer, z), device_id_type=MESH)
    pl.semaphore_wait(barrier, 3)
    row_load.wait()
    cot_load.wait()

    def send(stage, e, source, target, peer):
        return pltpu.make_async_remote_copy(
            src_ref=source,
            dst_ref=target,
            send_sem=send_sem.at[stage, e],
            recv_sem=recv_sem.at[stage, e],
            device_id=(peer, z),
            device_id_type=MESH,
        )

    def core_send(e):
        return send(0, e, grads.at[e, :, :, 1 - core], core_sum.at[e], core_peer)

    def first_send(e, along_x):
        if along_x:
            return send(1, e, core_sum.at[e, :, 1 - x], first_sum.at[e], x_peer)
        return send(1, e, core_sum.at[e, 1 - y], first_sum.at[e], y_peer)

    def by_parity(e, act):
        even = lax.rem(e, 2) == 0

        @pl.when(even)
        def _():
            act(True)

        @pl.when(jnp.logical_not(even))
        def _():
            act(False)

    def after_core(e):
        core_send(e).wait_recv()
        for yy in range(2):
            for xx in range(2):
                core_sum[e, yy, xx] = (
                    grads[e, yy, xx, core].astype(F32) + core_sum[e, yy, xx].astype(F32)
                ).astype(BF16)
        by_parity(e, lambda even: first_send(e, even).start())

    def after_first(e):
        def act(even):
            first_send(e, even).wait_recv()
            for other in range(2):
                kept = core_sum[e, other, x] if even else core_sum[e, y, other]
                first_sum[e, other] = (
                    kept.astype(F32) + first_sum[e, other].astype(F32)
                ).astype(BF16)

        by_parity(e, act)
        pltpu.make_async_copy(first_sum.at[e], sum_hbm.at[e], out_sem.at[e]).start()

    def step(e, _):
        slot = lax.rem(e, 2)
        for copy in loads(e, slot):
            copy.wait()

        @pl.when(e + 1 < experts)
        def _():
            for copy in loads(e + 1, 1 - slot):
                copy.start()

        def tile(at, _):
            columns = pl.ds(pl.multiple_of(at * 2 * block_rows, 2 * block_rows), 2 * block_rows)
            up_grad = contract(rows[:, columns], inner[slot], 0, 0).astype(BF16)
            down_grad = contract(cots[:, columns], gated[slot], 0, 0).astype(BF16)
            for side in range(2):
                part = slice(side * block_rows, (side + 1) * block_rows)
                grads[e, at // 2, lax.rem(at, 2), side, :, : 2 * ff_width] = up_grad[part]
                grads[e, at // 2, lax.rem(at, 2), side, :, 2 * ff_width :] = down_grad[part]
            return 0

        lax.fori_loop(0, 4, tile, 0)
        core_send(e).start()

        @pl.when(e >= 1)
        def _():
            after_core(e - 1)

        @pl.when(e >= 3)
        def _():
            after_first(e - 3)

        return 0

    lax.fori_loop(0, experts, step, 0)
    after_core(experts - 1)

    for e in range(max(experts - 3, 0), experts):
        after_first(e)
    for e in range(experts):
        core_send(e).wait_send()
        first_send(e, e % 2 == 0).wait_send()
        pltpu.make_async_copy(first_sum.at[e], sum_hbm.at[e], out_sem.at[e]).wait()


def bank_grads(rows, cots, gated, inner, experts):
    tokens, width = rows.shape
    ff_width = gated.shape[1] // experts
    lanes = 3 * ff_width
    block_rows = width // 8
    anywhere = pl.BlockSpec(memory_space=pl.ANY)
    return pl.pallas_call(
        bank_grads_kernel,
        out_shape=jax.ShapeDtypeStruct((experts, 2, block_rows, lanes), BF16),
        in_specs=[anywhere] * 4,
        out_specs=anywhere,
        scratch_shapes=[
            pltpu.VMEM((tokens, width), BF16),
            pltpu.VMEM((tokens, width), BF16),
            pltpu.VMEM((2, tokens, ff_width), BF16),
            pltpu.VMEM((2, tokens, 2 * ff_width), BF16),
            pltpu.VMEM((experts, 2, 2, 2, block_rows, lanes), BF16),
            pltpu.VMEM((experts, 2, 2, block_rows, lanes), BF16),
            pltpu.VMEM((experts, 2, block_rows, lanes), BF16),
            pltpu.SemaphoreType.DMA((2, 3)),
            pltpu.SemaphoreType.DMA((2, experts)),
            pltpu.SemaphoreType.DMA((2, experts)),
            pltpu.SemaphoreType.DMA((experts,)),
        ],
        compiler_params=pltpu.CompilerParams(
            collective_id=2, has_side_effects=True, vmem_limit_bytes=VMEM_MOST
        ),
        cost_estimate=pl.CostEstimate(
            flops=6 * tokens * width * experts * ff_width,
            bytes_accessed=2**27,
            transcendentals=0,
        ),
    )(rows, cots, gated, inner)


PAIR = 2 * HEAD_DIM
UNIT = 512


def swap_halves(value):
    lane = lax.broadcasted_iota(jnp.int32, value.shape, 1)
    half = HEAD_DIM // 2
    return jnp.where(
        lax.rem(lane, HEAD_DIM) < half,
        pltpu.roll(value, value.shape[1] - half, 1),
        pltpu.roll(value, half, 1),
    )


def sides(pair, side, scale):
    value = pair.astype(F32)
    if scale is not None:
        value = value * scale
    turned = pltpu.roll(value, HEAD_DIM, 1)
    lane = lax.broadcasted_iota(jnp.int32, value.shape, 1)
    left, right = (value, turned) if side == 0 else (turned, value)
    return (
        jnp.where(lane < HEAD_DIM, left, 0.0).astype(BF16),
        jnp.where(lane < HEAD_DIM, 0.0, right).astype(BF16),
    )


def lanes_at(start, size):
    return pl.ds(pl.multiple_of(start, 128), size)


def front_kernel(
    line,
    prompt,
    late,
    tokens,
    cots_hbm,
    gain_rows,
    heads_in,
    heads_out,
    router_rows,
    route_rows,
    cosine,
    sine,
    bias,
    up_hbm,
    down_hbm,
    first_in,
    queries,
    keys,
    values,
    attended,
    hidden,
    second_in,
    gate_rows,
    log_totals,
    cots_all,
    mix_all,
    mix_late,
    back_hbm,
    gate_grads_hbm,
    gated_hbm,
    inner_hbm,
    rows_all_hbm,
    cots,
    rows,
    gates_own,
    gates,
    gate_grads,
    gate_grads_sent,
    up,
    down,
    projected,
    stage,
    mix_stage,
    gated,
    inner,
    columns,
    cot_send,
    cot_recv,
    row_send,
    row_recv,
    gate_send,
    gate_recv,
    weight_sem,
    local_sem,
    out_sem,
    grad_send,
    grad_recv,
    mix_send,
    mix_recv,
):
    dp = lax.axis_index("dp")
    z = lax.axis_index("expert")
    experts, _, ff_width = down_hbm.shape
    start_cots, pass_cots, finish_cots = line_gather(
        line, z, dp, cots_hbm, cots_all, cot_send, cot_recv
    )
    start_rows, pass_rows, finish_rows = line_gather(
        line, z, dp, second_in, rows, row_send, row_recv
    )

    def weight_copies(e):
        return (
            pltpu.make_async_copy(
                up_hbm.at[e],
                up.at[:, pl.ds(pl.multiple_of(e * 2 * ff_width, ff_width), 2 * ff_width)],
                weight_sem.at[0, e],
            ),
            pltpu.make_async_copy(
                down_hbm.at[e],
                down.at[:, pl.ds(pl.multiple_of(e * ff_width, ff_width), ff_width)],
                weight_sem.at[1, e],
            ),
        )

    barrier = pltpu.get_barrier_semaphore()
    for step in range(1, line):
        pl.semaphore_signal(
            barrier, inc=1, device_id=(dp, lax.rem(z + step, line)), device_id_type=MESH
        )
    pl.semaphore_wait(barrier, line - 1)
    start_cots()
    cots_in = pltpu.make_async_copy(cots_hbm, cots, local_sem.at[2])
    cots_in.start()
    for e in range(experts):
        for copy in weight_copies(e):
            copy.start()

    query_end = HEADS * HEAD_DIM
    key_end = query_end + KV_HEADS * HEAD_DIM
    token_rows = tokens[...].astype(F32)
    factor = lax.rsqrt(jnp.mean(token_rows * token_rows, axis=1, keepdims=True) + EPS)
    first_in[...] = (token_rows * factor * gain_rows[0:1]).astype(BF16)
    log_totals[...] = jnp.zeros_like(log_totals)
    cots_in.wait()
    own_cots = pltpu.make_async_copy(cots, cots_all.at[z], local_sem.at[0])
    own_cots.start()

    def project(i, _):
        at = lanes_at(i * UNIT, UNIT)
        projected[:, at] = contract(first_in[...], heads_in[:, at], 1, 0)
        return 0

    lax.fori_loop(0, heads_in.shape[1] // UNIT, project, 0)

    def pair(j, _):
        for side in range(2):
            at = lanes_at((2 * j + side) * PAIR, PAIR)
            wide = projected[:, at]
            queries[:, at] = (wide * cosine[...] + swap_halves(wide) * sine[...]).astype(BF16)
        wide = projected[:, lanes_at(query_end + j * PAIR, PAIR)]
        keys[:, lanes_at(j * PAIR, PAIR)] = (
            wide * cosine[...] + swap_halves(wide) * sine[...]
        ).astype(BF16)
        values[:, lanes_at(j * PAIR, PAIR)] = projected[
            :, lanes_at(key_end + j * PAIR, PAIR)
        ].astype(BF16)
        heads = [(side, member) for side in range(2) for member in range(2)]
        groups = [queries[:, lanes_at((2 * j + side) * PAIR, PAIR)] for side in range(2)]
        key_sides = [sides(keys[:, lanes_at(j * PAIR, PAIR)], side, SCALE) for side in range(2)]
        value_sides = [sides(values[:, lanes_at(j * PAIR, PAIR)], side, None) for side in range(2)]
        parts = ((0, prompt, prompt), (prompt, groups[0].shape[0], groups[0].shape[0]))

        def scores_of(side, member):
            return [
                contract(groups[side][begin:end], key_sides[side][member][:seen], 1, 1)
                + bias[begin:end, :seen]
                for begin, end, seen in parts
            ]

        lane = lax.broadcasted_iota(jnp.int32, log_totals.shape, 1)
        added = jnp.zeros(log_totals.shape, F32)
        sums = [0.0, 0.0]
        scores = scores_of(*heads[0])
        for number, (side, member) in enumerate(heads):
            following = scores_of(*heads[number + 1]) if number + 1 < len(heads) else None
            mixed = []
            totals = []
            for part, (_, _, seen) in zip(scores, parts):
                peak = jnp.max(part, axis=1, keepdims=True)
                powers = jnp.exp(part - peak)
                amount = jnp.sum(powers, axis=1, keepdims=True)
                weights = (powers * (1.0 / amount)).astype(BF16)
                totals.append(peak + jnp.log(amount))
                mixed.append(contract(weights, value_sides[side][member][:seen], 1, 0))
            sums[side] = sums[side] + jnp.concatenate(mixed, axis=0)
            added = jnp.where(lane == 4 * j + number, jnp.concatenate(totals, axis=0), added)
            scores = following
        log_totals[...] += added
        for side in range(2):
            attended[:, lanes_at((2 * j + side) * PAIR, PAIR)] = sums[side].astype(BF16)
        return 0

    lax.fori_loop(0, KV_HEADS // 2, pair, 0)
    hidden_rows = token_rows + contract(attended[...], heads_out[...], 1, 1)
    hidden[...] = hidden_rows
    factor = lax.rsqrt(jnp.mean(hidden_rows * hidden_rows, axis=1, keepdims=True) + EPS)
    second = (hidden_rows * factor * gain_rows[1:2]).astype(BF16)
    second_in[...] = second
    start_rows()
    own_rows = pltpu.make_async_copy(second_in, rows.at[z], local_sem.at[1])
    own_rows.start()
    logits = contract(router_rows[...], second, 1, 1)
    expert = lax.broadcasted_iota(jnp.int32, logits.shape, 0)
    named = expert == route_rows[0:1]
    for k in range(1, route_rows.shape[0]):
        named = named | (expert == route_rows[k : k + 1])
    peak = jnp.max(jnp.where(named, logits, -1e30), axis=0, keepdims=True)
    powers = jnp.where(named, jnp.exp(jnp.where(named, logits, peak) - peak), 0.0)
    gate_values = powers / jnp.sum(powers, axis=0, keepdims=True)
    gate_rows[...] = gate_values
    gates_own[...] = jnp.zeros_like(gates_own)
    for peer in range(line):
        gates_own[peer, :experts] = gate_values[peer * experts : (peer + 1) * experts]
    gates[z] = gates_own[z]
    def gate_copy(step):
        peer = lax.rem(z + step, line)
        return pltpu.make_async_remote_copy(
            src_ref=gates_own.at[peer],
            dst_ref=gates.at[z],
            send_sem=gate_send.at[step],
            recv_sem=gate_recv.at[step],
            device_id=(dp, peer),
            device_id_type=MESH,
        )

    for step in range(1, line):
        gate_copy(step).start()
    own_rows.wait()
    own_cots.wait()
    pass_cots(1)
    for step in range(1, line):
        gate_copy(step).wait()

    order = visit_order(line)

    def out_copies(slot, block):
        return (
            pltpu.make_async_copy(stage.at[slot], back_hbm.at[block], out_sem.at[slot, 0]),
            pltpu.make_async_copy(gated.at[slot], gated_hbm.at[block], out_sem.at[slot, 1]),
            pltpu.make_async_copy(inner.at[slot], inner_hbm.at[block], out_sem.at[slot, 2]),
        )

    def mix_copy(block, source, target):
        return pltpu.make_async_remote_copy(
            src_ref=mix_stage.at[block],
            dst_ref=mix_all.at[source],
            send_sem=mix_send.at[block],
            recv_sem=mix_recv.at[source],
            device_id=(dp, target),
            device_id_type=MESH,
        )

    def own_mix():
        return pltpu.make_async_copy(mix_stage.at[z], mix_all.at[z], local_sem.at[3])

    def late_mix(side):
        return pltpu.make_async_copy(
            mix_stage.at[side * (line - 1)], mix_late.at[side], local_sem.at[4 + side]
        )

    def at_end(block):
        return (block == 0) | (block == line - 1)

    def grad_copy(block, step):
        return pltpu.make_async_remote_copy(
            src_ref=gate_grads_sent.at[block],
            dst_ref=gate_grads.at[z],
            send_sem=grad_send.at[block],
            recv_sem=grad_recv.at[z],
            device_id=(dp, block),
            device_id_type=MESH,
        )

    def visit(k, _):
        block = pick(order, z, k)
        slot = lax.rem(k, 2)
        @pl.when(k >= 2)
        def _():
            for copy in out_copies(slot, pick(order, z, jnp.maximum(k - 2, 0))):
                copy.wait()

        cot_load = pltpu.make_async_copy(cots_all.at[block], cots, local_sem.at[2])
        gate_columns = gates[block].T
        tile = min(ff_width, 256)
        def arrive(e):
            step = k * experts + e
            apart = jnp.int32(0)
            for at_z, at_step, distance in pass_steps(line, experts):
                apart = jnp.where((z == at_z) & (step == at_step), distance, apart)

            @pl.when(apart > 0)
            def _():
                pass_rows(apart)

            if line > 2:

                @pl.when(apart == 1)
                def _():
                    pass_cots(2)

            @pl.when(apart > 2)
            def _():
                pass_cots(apart)

            @pl.when((k > 0) & (e == 0))
            def _():
                cot_load.start()
                cot_load.wait()

        def products(e, at):
            gate_at = pl.multiple_of(2 * e * ff_width + at, tile)
            up_at = pl.multiple_of((2 * e + 1) * ff_width + at, tile)
            down_at = pl.multiple_of(e * ff_width + at, tile)
            return (
                contract(rows[block], up[:, pl.ds(gate_at, tile)], 1, 0),
                contract(rows[block], up[:, pl.ds(up_at, tile)], 1, 0),
                contract(cots[...], down[:, pl.ds(down_at, tile)], 1, 0),
            )

        narrow_lane = lax.broadcasted_iota(jnp.int32, gate_columns.shape, 1)
        wide_lane = lax.broadcasted_iota(jnp.int32, columns.shape, 1)
        several = experts // 2
        columns[...] = jnp.zeros_like(columns)

        def half(part, _):
            begin = part * several
            arrive(begin)

            @pl.when(k == 0)
            def _():
                for e in range(several):
                    for copy in weight_copies(begin + e):
                        copy.wait()

            tiles = [(e, at) for e in range(several) for at in range(0, ff_width, tile)]
            ready = products(begin + tiles[0][0], tiles[0][1])
            sums = [0.0] * several
            for number, (near, at) in enumerate(tiles):
                following = None
                if number + 1 < len(tiles):
                    following = products(begin + tiles[number + 1][0], tiles[number + 1][1])
                e = begin + near
                gate_part, up_part, returned = ready
                gate_col = jnp.sum(
                    jnp.where(narrow_lane == e, gate_columns, 0.0), axis=1, keepdims=True
                )
                sigmoid_gate = jax.nn.sigmoid(gate_part)
                silu_gate = gate_part * sigmoid_gate
                active = silu_gate * up_part
                sums[near] = sums[near] + jnp.sum(active * returned, axis=1, keepdims=True)
                scaled = returned * gate_col
                grad_gate = scaled * up_part * (sigmoid_gate + silu_gate * (1.0 - sigmoid_gate))
                gate_at = pl.multiple_of(2 * e * ff_width + at, tile)
                up_at = pl.multiple_of((2 * e + 1) * ff_width + at, tile)
                down_at = pl.multiple_of(e * ff_width + at, tile)
                gated[slot, :, pl.ds(down_at, tile)] = (active * gate_col).astype(BF16)
                inner[slot, :, pl.ds(gate_at, tile)] = grad_gate.astype(BF16)
                inner[slot, :, pl.ds(up_at, tile)] = (scaled * silu_gate).astype(BF16)
                ready = following
            value = columns[...]
            for near in range(several):
                value = jnp.where(wide_lane == begin + near, sums[near], value)
            columns[...] = value
            return 0

        lax.fori_loop(0, 2, half, 0)
        mix_stage[block] = contract(gated[slot], down[...], 1, 1).astype(BF16)

        @pl.when(block == z)
        def _():
            own_mix().start()

        if late:
            for side in range(2):

                @pl.when((block != z) & (block == side * (line - 1)))
                def _(side=side):
                    late_mix(side).start()

            @pl.when((block != z) & jnp.logical_not(at_end(block)))
            def _():
                mix_copy(block, z, block).start()

        else:

            @pl.when(block != z)
            def _():
                mix_copy(block, z, block).start()

        stage[slot] = contract(inner[slot], up[...], 1, 1).astype(BF16)
        for copy in out_copies(slot, block):
            copy.start()
        gate_grads_sent[block] = columns[...].T[: gate_grads.shape[1]]

        @pl.when(block == z)
        def _():
            gate_grads[z] = gate_grads_sent[z]

        @pl.when(block != z)
        def _():
            grad_copy(block, 0).start()

        return 0

    lax.fori_loop(0, line, visit, 0)
    for k in range(max(line - 2, 0), line):
        for copy in out_copies(k % 2, pick(order, z, k)):
            copy.wait()

    finish_rows()
    finish_cots()
    own_mix().wait()
    if late:
        for side in range(2):

            @pl.when(z != side * (line - 1))
            def _(side=side):
                late_mix(side).wait()

    for s in range(line):
        send_ends = late and s in (0, line - 1)

        @pl.when(z != s)
        def _(s=s, send_ends=send_ends):
            if not send_ends:
                mix_copy(s, s, z).wait_send()
            if late:

                @pl.when(jnp.logical_not(at_end(z)))
                def _():
                    mix_copy(s, s, z).wait_recv()

            else:
                mix_copy(s, s, z).wait_recv()

    for s in range(line):

        @pl.when(s != z)
        def _(s=s):
            grad_copy(s, 0).wait_send()
            pltpu.make_async_remote_copy(
                src_ref=gate_grads_sent.at[s],
                dst_ref=gate_grads.at[s],
                send_sem=grad_send.at[s],
                recv_sem=grad_recv.at[s],
                device_id=(dp, z),
                device_id_type=MESH,
            ).wait_recv()

    last = (
        pltpu.make_async_copy(rows, rows_all_hbm, local_sem.at[0]),
        pltpu.make_async_copy(gate_grads, gate_grads_hbm, local_sem.at[1]),
    )
    for copy in last:
        copy.start()
    for copy in last:
        copy.wait()


def front(
    late,
    tokens,
    cots,
    gain_rows,
    heads_in,
    heads_out,
    router_rows,
    route_rows,
    tables,
    up,
    down,
    line,
    prompt,
):
    count, width = tokens.shape
    named = router_rows.shape[0]
    experts, _, ff_width = down.shape
    kv_width = KV_HEADS * HEAD_DIM
    shape = jax.ShapeDtypeStruct
    padded = experts + -experts % 8
    held = pl.BlockSpec(memory_space=pltpu.VMEM)
    anywhere = pl.BlockSpec(memory_space=pl.ANY)
    small = pltpu.VMEM((line, padded, count), F32)
    return pl.pallas_call(
        functools.partial(front_kernel, line, prompt, late),
        out_shape=(
            shape((count, width), BF16),
            shape((count, HEADS * HEAD_DIM), BF16),
            shape((count, kv_width), BF16),
            shape((count, kv_width), BF16),
            shape((count, HEADS * HEAD_DIM), BF16),
            shape((count, width), F32),
            shape((count, width), BF16),
            shape((named, count), F32),
            shape((count, 128), F32),
            shape((line, count, width), BF16),
            shape((line, count, width), BF16),
            shape((2, count, width), BF16),
            shape((line, count, width), BF16),
            shape((line, padded, count), F32),
            shape((line, count, experts * ff_width), BF16),
            shape((line, count, experts * 2 * ff_width), BF16),
            shape((line, count, width), BF16),
        ),
        in_specs=[held, anywhere] + [held] * 8 + [anywhere] * 2,
        out_specs=(held,) * 9 + (anywhere,) * 8,
        scratch_shapes=[
            pltpu.VMEM((count, width), BF16),
            pltpu.VMEM((line, count, width), BF16),
            small,
            small,
            small,
            small,
            pltpu.VMEM((width, experts * 2 * ff_width), BF16),
            pltpu.VMEM((width, experts * ff_width), BF16),
            pltpu.VMEM((count, heads_in.shape[1]), F32),
            pltpu.VMEM((2, count, width), BF16),
            pltpu.VMEM((line, count, width), BF16),
            pltpu.VMEM((2, count, experts * ff_width), BF16),
            pltpu.VMEM((2, count, experts * 2 * ff_width), BF16),
            pltpu.VMEM((count, 128), F32),
            pltpu.SemaphoreType.DMA((line + 2,)),
            pltpu.SemaphoreType.DMA((line,)),
            pltpu.SemaphoreType.DMA((line + 2,)),
            pltpu.SemaphoreType.DMA((line,)),
            pltpu.SemaphoreType.DMA((line,)),
            pltpu.SemaphoreType.DMA((line,)),
            pltpu.SemaphoreType.DMA((2, experts)),
            pltpu.SemaphoreType.DMA((6,)),
            pltpu.SemaphoreType.DMA((2, 3)),
            pltpu.SemaphoreType.DMA((line,)),
            pltpu.SemaphoreType.DMA((line,)),
            pltpu.SemaphoreType.DMA((line,)),
            pltpu.SemaphoreType.DMA((line,)),
        ],
        compiler_params=pltpu.CompilerParams(
            collective_id=4, has_side_effects=True, vmem_limit_bytes=VMEM_MOST
        ),
        cost_estimate=pl.CostEstimate(flops=2**35, bytes_accessed=2**26, transcendentals=2**22),
    )(
        tokens,
        cots,
        gain_rows,
        heads_in,
        heads_out,
        router_rows,
        route_rows,
        *tables,
        up,
        down,
    )


def attend_back_kernel(
    paired,
    line,
    back_rows,
    hidden,
    cots,
    second_in,
    gate_rows,
    gate_grads,
    router_rows,
    gain_rows,
    heads_out,
    queries,
    keys,
    values,
    attended,
    log_totals,
    cosine,
    sine,
    bias,
    tokens_hbm,
    first_hbm,
    in_hbm,
    mix_hbm,
    late_hbm,
    *others,
):
    bank_hbm, others = (others[0], others[1:]) if paired else (None, others)
    output, token_grad, sum_hbm, small_hbm, *others = others
    bank_sum_hbm, others = (others[0], others[1:]) if paired else (None, others)
    (
        tokens,
        first_in,
        heads_in,
        mixes,
        grad_hidden,
        grad_attended,
        grad_projected,
        small_rows,
        own,
        own_small,
        *scratch,
    ) = others
    dp = lax.axis_index("dp")
    z = lax.axis_index("expert")
    units = own.shape[0]
    block_rows = own.shape[4]
    load_sem = scratch[0]
    loads = (
        pltpu.make_async_copy(first_hbm, first_in, load_sem.at[0]),
        pltpu.make_async_copy(tokens_hbm, tokens, load_sem.at[1]),
        pltpu.make_async_copy(in_hbm, heads_in, load_sem.at[2]),
    )
    for copy in loads:
        copy.start()

    def mix_load(b):
        return pltpu.make_async_copy(mix_hbm.at[b], mixes.at[b], load_sem.at[5 + b])

    def direct(b):
        ends = (z == 0) | (z == line - 1)
        return jnp.logical_not(ends) | (z == b) if paired else z == z

    for b in range(line):

        @pl.when(direct(b))
        def _(b=b):
            mix_load(b).start()

    if paired:
        (
            cores,
            firsts,
            lasts,
            sums,
            lines,
            totals,
            small_cores,
            small_firsts,
            small_lasts,
            small_sums,
            small_lines,
            small_totals,
            send_sem,
            recv_sem,
            line_send,
            line_recv,
            out_sem,
            bank_kept,
            bank_last,
            bank_total,
            bank_sem,
            late_send_sem,
            late_recv_sem,
        ) = scratch[1:]
        rows = totals.shape[1]
        y, x, core = dp // 4, lax.rem(dp // 2, 2), lax.rem(dp, 2)
        core_peer, x_peer, y_peer = dp + 1 - 2 * core, dp + 2 - 4 * x, dp + 4 - 8 * y
        barrier = pltpu.get_barrier_semaphore()
        for peer in (core_peer, x_peer, y_peer):
            pl.semaphore_signal(barrier, inc=1, device_id=(peer, z), device_id_type=MESH)
        for step in range(1, line):
            pl.semaphore_signal(
                barrier, inc=1, device_id=(dp, lax.rem(z + step, line)), device_id_type=MESH
            )
        pl.semaphore_wait(barrier, 3 + line - 1)

        def bank_kept_copy(e):
            kept = y if e % 2 == 0 else x
            return pltpu.make_async_copy(
                bank_hbm.at[e, kept], bank_kept.at[e], bank_sem.at[0, e]
            )

        def bank_last_copy(e):
            sent, peer = (1 - y, y_peer) if e % 2 == 0 else (1 - x, x_peer)
            return pltpu.make_async_remote_copy(
                src_ref=bank_hbm.at[e, sent],
                dst_ref=bank_last.at[e],
                send_sem=bank_sem.at[1, e],
                recv_sem=bank_sem.at[2, e],
                device_id=(peer, z),
                device_id_type=MESH,
            )

        def bank_total_copy(e):
            return pltpu.make_async_copy(
                bank_total.at[e], bank_sum_hbm.at[e], bank_sem.at[3, e]
            )

        for e in range(bank_hbm.shape[0]):
            bank_kept_copy(e).start()
            bank_last_copy(e).start()

        def late_send(side, source):
            return pltpu.make_async_remote_copy(
                src_ref=late_hbm.at[side],
                dst_ref=mixes.at[source],
                send_sem=late_send_sem.at[side],
                recv_sem=late_recv_sem.at[source],
                device_id=(dp, side * (line - 1)),
                device_id_type=MESH,
            )

        for side in range(2):

            @pl.when(z != side * (line - 1))
            def _(side=side):
                late_send(side, z).start()

        buffers = (own, cores, firsts, lasts, sums, lines, totals)
        small_buffers = (
            own_small,
            small_cores,
            small_firsts,
            small_lasts,
            small_sums,
            small_lines,
            small_totals,
        )

        def send(stage, u, source, target, peer):
            return pltpu.make_async_remote_copy(
                src_ref=source,
                dst_ref=target,
                send_sem=send_sem.at[stage, u],
                recv_sem=recv_sem.at[stage, u],
                device_id=(peer, z),
                device_id_type=MESH,
            )

        class Sums:
            def __init__(self, held, shift):
                self.own, self.cores, self.firsts, self.lasts = held[:4]
                self.sums, self.lines, self.totals = held[4:]
                self.shift = shift

            def core_send(self, u):
                return send(
                    0,
                    u + self.shift,
                    self.own.at[u, :, :, 1 - core],
                    self.cores.at[u],
                    core_peer,
                )

            def first_send(self, u, along_x):
                if along_x:
                    source, peer = self.cores.at[u, :, 1 - x], x_peer
                else:
                    source, peer = self.cores.at[u, 1 - y], y_peer
                return send(1, u + self.shift, source, self.firsts.at[u], peer)

            def last_send(self, u, along_x):
                if along_x:
                    source, peer = self.firsts.at[u, 1 - x], x_peer
                else:
                    source, peer = self.firsts.at[u, 1 - y], y_peer
                return send(2, u + self.shift, source, self.lasts.at[u], peer)

            def line_copy(self, u, step):
                peer = lax.rem(z + step, line)
                return pltpu.make_async_remote_copy(
                    src_ref=self.sums.at[u, pl.ds(pl.multiple_of(peer * rows, rows), rows)],
                    dst_ref=self.lines.at[u, step],
                    send_sem=line_send.at[u + self.shift, step],
                    recv_sem=line_recv.at[u + self.shift, step],
                    device_id=(dp, peer),
                    device_id_type=MESH,
                )

            def by_parity(self, u, act):
                even = lax.rem(jnp.int32(u), 2) == 0

                @pl.when(even)
                def _():
                    act(True)

                @pl.when(jnp.logical_not(even))
                def _():
                    act(False)

            def after_core(self, u):
                self.core_send(u).wait_recv()
                for yy in range(2):
                    for xx in range(2):
                        self.cores[u, yy, xx] = (
                            self.own[u, yy, xx, core].astype(F32)
                            + self.cores[u, yy, xx].astype(F32)
                        ).astype(BF16)
                self.by_parity(u, lambda even: self.first_send(u, even).start())

            def after_first(self, u):
                def act(even):
                    self.first_send(u, even).wait_recv()
                    for other in range(2):
                        kept = self.cores[u, other, x] if even else self.cores[u, y, other]
                        self.firsts[u, other] = (
                            kept.astype(F32) + self.firsts[u, other].astype(F32)
                        ).astype(BF16)
                    self.last_send(u, not even).start()

                self.by_parity(u, act)

            def after_last(self, u):
                def act(even):
                    self.last_send(u, not even).wait_recv()
                    kept = self.firsts[u, y] if even else self.firsts[u, x]
                    self.sums[u] = (kept.astype(F32) + self.lasts[u].astype(F32)).astype(BF16)

                self.by_parity(u, act)
                for step in range(1, line):
                    self.line_copy(u, step).start()

            def after_line(self, u):
                value = self.sums[u, pl.ds(pl.multiple_of(z * rows, rows), rows)].astype(F32)
                for step in range(1, line):
                    self.line_copy(u, step).wait_recv()
                    value = value + self.lines[u, step].astype(F32)
                self.totals[u] = value

            def finish(self, u):
                self.core_send(u).wait_send()
                self.first_send(u, u % 2 == 0).wait_send()
                self.last_send(u, u % 2 == 1).wait_send()
                for step in range(1, line):
                    self.line_copy(u, step).wait_send()

        wide_sums = Sums(buffers, 0)
        small_sum = Sums(small_buffers, units)

    def keep(target, u, value):
        for block in range(8):
            target[u, block // 4, block // 2 % 2, block % 2] = value[
                block * block_rows : (block + 1) * block_rows
            ]

    gates = gate_rows[...]
    gate_grad = gate_grads[...]
    logit_grad = gates * (gate_grad - jnp.sum(gates * gate_grad, axis=0, keepdims=True))
    high = logit_grad.astype(BF16)
    low = (logit_grad - high.astype(F32)).astype(BF16)
    grad_second = (
        back_rows[...].astype(F32)
        + contract(high, router_rows[...], 0, 0)
        + contract(low, router_rows[...], 0, 0)
    )
    small_rows[...] = jnp.zeros_like(small_rows)
    experts = high.shape[0]
    small_rows[:experts] = contract(high, second_in[...], 1, 0) + contract(low, second_in[...], 1, 0)

    def norm_back(incoming, rows, gain):
        factor = lax.rsqrt(jnp.mean(rows * rows, axis=1, keepdims=True) + EPS)
        normed = rows * factor
        gain_grad = jnp.sum(incoming * normed, axis=0, keepdims=True)
        weighted = incoming * gain
        mean = jnp.mean(weighted * normed, axis=1, keepdims=True)
        return factor * (weighted - normed * mean), gain_grad

    norm_grad, gain_grad = norm_back(grad_second, hidden[...], gain_rows[1:2])
    small_rows[experts + 1 : experts + 2] = gain_grad
    grad_hidden[...] = cots[...].astype(F32) + norm_grad
    branch = grad_hidden[...].astype(BF16)
    for u in range(2):
        keep(
            own,
            u,
            contract(branch, attended[:, u * UNIT : (u + 1) * UNIT], 0, 0).astype(BF16),
        )
        if paired:
            wide_sums.core_send(u).start()
    grad_attended[...] = contract(branch, heads_out[...], 1, 0).astype(BF16)
    loads[0].wait()
    if paired:
        wide_sums.after_core(0)

    def pair(j, _):
        key_pair = keys[:, lanes_at(j * PAIR, PAIR)]
        value_pair = values[:, lanes_at(j * PAIR, PAIR)]
        key_grads = []
        value_grads = []
        for side in range(2):
            at = lanes_at((2 * j + side) * PAIR, PAIR)
            group = queries[:, at]
            group_grad = grad_attended[:, at]
            key_sides = sides(key_pair, side, SCALE)
            value_sides = sides(value_pair, side, None)
            product = group_grad.astype(F32) * attended[:, at].astype(F32)
            lane = lax.broadcasted_iota(jnp.int32, product.shape, 1)
            grad = jnp.zeros(group.shape, F32)
            key_grad = []
            value_grad = []
            for member in range(2):
                head = 4 * j + 2 * side + member
                log_total = jnp.sum(
                    jnp.where(lane == head, log_totals[...], 0.0), axis=1, keepdims=True
                )
                mine = (lane < HEAD_DIM) if member == 0 else (lane >= HEAD_DIM)
                spread = jnp.sum(jnp.where(mine, product, 0.0), axis=1, keepdims=True)
                scores = contract(group, key_sides[member], 1, 1) + bias[...]
                weights = jnp.exp(scores - log_total)
                weight_grads = contract(group_grad, value_sides[member], 1, 1)
                score_grads = (weights * (weight_grads - spread)).astype(BF16)
                grad = grad + contract(score_grads, key_sides[member], 1, 0)
                rows_of = slice(member * HEAD_DIM, (member + 1) * HEAD_DIM)
                key_grad.append(contract(group, score_grads, 0, 0)[rows_of])
                value_grad.append(contract(group_grad, weights.astype(BF16), 0, 0)[rows_of])
            grad_projected[j, :, side * PAIR : (side + 1) * PAIR] = (
                grad * cosine[...] - swap_halves(grad) * sine[...]
            ).astype(BF16)
            key_grads.append(key_grad[0] + key_grad[1])
            value_grads.append(value_grad[0] + value_grad[1])
        key_rows = jnp.concatenate(key_grads, axis=0).T * SCALE
        grad_projected[j, :, 2 * PAIR : 3 * PAIR] = (
            key_rows * cosine[...] - swap_halves(key_rows) * sine[...]
        ).astype(BF16)
        grad_projected[j, :, 3 * PAIR :] = jnp.concatenate(value_grads, axis=0).T.astype(BF16)
        keep(own, 2 + j, contract(first_in[...], grad_projected[j], 0, 0).astype(BF16))
        if paired:
            wide_sums.core_send(2 + j).start()
            wide_sums.after_core(1 + j)

            @pl.when(j >= 2)
            def _():
                wide_sums.after_first(j - 2)

        return 0

    pairs = KV_HEADS // 2
    lax.fori_loop(0, pairs, pair, 0)
    last = units - 1
    if paired:
        wide_sums.after_core(last)
        wide_sums.after_first(2)
        wide_sums.after_last(0)
    loads[1].wait()
    loads[2].wait()
    grad_first = jnp.zeros(grad_hidden.shape, F32)
    query_end = HEADS * HEAD_DIM
    key_end = query_end + KV_HEADS * HEAD_DIM
    for j in range(pairs):
        for at, begin, size in (
            (0, 2 * j * PAIR, 2 * PAIR),
            (2 * PAIR, query_end + j * PAIR, PAIR),
            (3 * PAIR, key_end + j * PAIR, PAIR),
        ):
            grad_first = grad_first + contract(
                grad_projected[j, :, at : at + size], heads_in[:, begin : begin + size], 1, 1
            )
    norm_grad, gain_grad = norm_back(grad_first, tokens[...].astype(F32), gain_rows[0:1])
    small_rows[experts : experts + 1] = gain_grad
    keep(own_small, 0, small_rows[...].T.astype(BF16))
    if paired:
        small_sum.core_send(0).start()
    token_grad[...] = grad_hidden[...] + norm_grad
    if paired:
        for e in range(bank_hbm.shape[0]):
            bank_kept_copy(e).wait()
            bank_last_copy(e).wait()
            bank_total[e] = bank_kept[e].astype(F32) + bank_last[e].astype(F32)
            bank_total_copy(e).start()

    @pl.when(direct(-1))
    def _():
        total = hidden[...]
        for b in range(line):
            mix_load(b).wait()
            total = total + mixes[b].astype(F32)
        output[...] = total.astype(BF16)

    if paired:
        small_sum.after_core(0)
        wide_sums.after_first(3)
        wide_sums.after_last(1)
        wide_sums.after_first(4)
        wide_sums.after_last(2)
        small_sum.after_first(0)
        wide_sums.after_first(5)
        wide_sums.after_last(3)
        small_sum.after_last(0)
        wide_sums.after_line(0)
        wide_sums.after_last(4)
        wide_sums.after_line(1)
        wide_sums.after_last(5)
        for u in range(2, units):
            wide_sums.after_line(u)
        small_sum.after_line(0)
        outs = (
            pltpu.make_async_copy(totals, sum_hbm, out_sem.at[0]),
            pltpu.make_async_copy(small_totals, small_hbm, out_sem.at[1]),
        )
    else:
        outs = (
            pltpu.make_async_copy(own, sum_hbm, load_sem.at[3]),
            pltpu.make_async_copy(own_small, small_hbm, load_sem.at[4]),
        )
    for copy in outs:
        copy.start()
    if paired:
        for u in range(units):
            wide_sums.finish(u)
        small_sum.finish(0)
        for e in range(bank_hbm.shape[0]):
            bank_total_copy(e).wait()
        for side in range(2):

            @pl.when(z != side * (line - 1))
            def _(side=side):
                late_send(side, z).wait_send()

            @pl.when(z == side * (line - 1))
            def _():
                mix_load(z).wait()
                total = hidden[...] + mixes[z].astype(F32)
                for step in range(1, line):
                    source = lax.rem(z + step, line)
                    late_send(0, source).wait_recv()
                    total = total + mixes[source].astype(F32)
                output[...] = total.astype(BF16)

    for copy in outs:
        copy.wait()


def attend_back(held_args, far_args, paired, line):
    tokens, first_in, heads_in = far_args[:3]
    count, width = tokens.shape
    pairs = KV_HEADS // 2
    units = 2 + pairs
    block_rows = width // 8
    rows = block_rows // line
    shape = jax.ShapeDtypeStruct
    held = pl.BlockSpec(memory_space=pltpu.VMEM)
    anywhere = pl.BlockSpec(memory_space=pl.ANY)
    if paired:
        sum_shapes = (shape((units, rows, UNIT), F32), shape((1, rows, 128), F32))
    else:
        sum_shapes = (
            shape((units, 2, 2, 2, block_rows, UNIT), BF16),
            shape((1, 2, 2, 2, block_rows, 128), BF16),
        )
    exchange = []
    if paired:
        for number, lanes in ((units, UNIT), (1, 128)):
            exchange += [
                pltpu.VMEM((number, 2, 2, block_rows, lanes), BF16),
                pltpu.VMEM((number, 2, block_rows, lanes), BF16),
                pltpu.VMEM((number, block_rows, lanes), BF16),
                pltpu.VMEM((number, block_rows, lanes), BF16),
                pltpu.VMEM((number, line, rows, lanes), BF16),
                pltpu.VMEM((number, rows, lanes), F32),
            ]
        exchange += [
            pltpu.SemaphoreType.DMA((3, units + 1)),
            pltpu.SemaphoreType.DMA((3, units + 1)),
            pltpu.SemaphoreType.DMA((units + 1, line)),
            pltpu.SemaphoreType.DMA((units + 1, line)),
            pltpu.SemaphoreType.DMA((2,)),
        ]
        bank_shape = (far_args[5].shape[0],) + far_args[5].shape[2:]
        sum_shapes += (shape(bank_shape, F32),)
        exchange += [
            pltpu.VMEM(bank_shape, BF16),
            pltpu.VMEM(bank_shape, BF16),
            pltpu.VMEM(bank_shape, F32),
            pltpu.SemaphoreType.DMA((4, bank_shape[0])),
            pltpu.SemaphoreType.DMA((2,)),
            pltpu.SemaphoreType.DMA((line,)),
        ]
    settings = dict(vmem_limit_bytes=VMEM_MOST)
    if paired:
        settings.update(collective_id=3, has_side_effects=True)
    return pl.pallas_call(
        functools.partial(attend_back_kernel, paired, line),
        out_shape=(shape((count, width), BF16), shape((count, width), F32)) + sum_shapes,
        in_specs=[held] * len(held_args) + [anywhere] * len(far_args),
        out_specs=(held, held) + (anywhere,) * len(sum_shapes),
        scratch_shapes=[
            pltpu.VMEM((count, width), BF16),
            pltpu.VMEM((count, width), BF16),
            pltpu.VMEM(heads_in.shape, BF16),
            pltpu.VMEM((line, count, width), BF16),
            pltpu.VMEM((count, width), F32),
            pltpu.VMEM((count, HEADS * HEAD_DIM), BF16),
            pltpu.VMEM((pairs, count, 4 * PAIR), BF16),
            pltpu.VMEM((128, width), F32),
            pltpu.VMEM((units, 2, 2, 2, block_rows, UNIT), BF16),
            pltpu.VMEM((1, 2, 2, 2, block_rows, 128), BF16),
            pltpu.SemaphoreType.DMA((5 + line,)),
            *exchange,
        ],
        compiler_params=pltpu.CompilerParams(**settings),
        cost_estimate=pl.CostEstimate(flops=2**34, bytes_accessed=2**25, transcendentals=2**21),
    )(*held_args, *far_args)


def unit_columns(sums):
    pairs = KV_HEADS // 2
    parts = sums[2 : 2 + pairs]
    rows = sums.shape[1]

    def side_by_side(value):
        return jnp.transpose(value, (1, 0, 2)).reshape(rows, -1)

    return (
        jnp.concatenate(
            [
                side_by_side(parts[:, :, : 2 * PAIR]),
                side_by_side(parts[:, :, 2 * PAIR : 3 * PAIR]),
                side_by_side(parts[:, :, 3 * PAIR :]),
            ],
            axis=1,
        ),
        side_by_side(sums[:2]),
    )


def body(
    tokens,
    cotangent,
    routes,
    cont_ids,
    norm_gains,
    gains_moment,
    gains_average,
    heads_in,
    heads_in_master,
    heads_in_moment,
    heads_in_average,
    heads_out,
    heads_out_master,
    heads_out_moment,
    heads_out_average,
    router,
    router_master,
    router_moment,
    router_average,
    expert_in,
    expert_in_master,
    expert_in_moment,
    expert_in_average,
    expert_out,
    expert_out_master,
    expert_out_moment,
    expert_out_average,
):
    token_count, model_width = tokens.shape
    local_experts = expert_in.shape[0]
    peer_count = lax.axis_size("expert")
    experts = local_experts * peer_count
    paired = lax.axis_size("dp") == 8 and peer_count == 4
    positions, allowed = layout(cont_ids[0], token_count - cont_ids.shape[1])
    tables = (*rope_tables(positions), jnp.where(allowed, 0.0, -1e30))
    gain_rows = norm_gains.T
    router_rows = router.T
    (
        first_in,
        queries,
        key_rows,
        value_rows,
        attended,
        hidden,
        second_in,
        gates,
        log_totals,
        cots_all,
        mix_all,
        mix_late,
        grad_part,
        gate_grads,
        gated,
        grad_gate_up,
        rows_all,
    ) = front(
        paired,
        tokens,
        cotangent,
        gain_rows,
        heads_in,
        heads_out,
        router_rows,
        routes.T,
        tables,
        expert_in,
        expert_out,
        peer_count,
        token_count - cont_ids.shape[1],
    )
    back_rows = lax.psum_scatter(
        grad_part.reshape(peer_count * token_count, model_width),
        "expert",
        scatter_dimension=0,
        tiled=True,
    )
    grad_sources = (
        rows_all.reshape(peer_count * token_count, model_width),
        cots_all.reshape(peer_count * token_count, model_width),
        gated.reshape(peer_count * token_count, -1),
        grad_gate_up.reshape(peer_count * token_count, -1),
    )
    if paired:
        expert_sums = (bank_grads(*grad_sources, local_experts),)
    else:
        expert_sums = tuple(
            lax.psum_scatter(part, "dp", scatter_dimension=1, tiled=True).astype(jnp.float32)
            for part in weight_grads(*grad_sources, local_experts)
        )
    output, token_grad, unit_sums, small_sum, *bank_sums = attend_back(
        (
            back_rows,
            hidden,
            cotangent,
            second_in,
            gates,
            gate_grads[:, :local_experts].reshape(experts, token_count),
            router_rows,
            gain_rows,
            heads_out,
            queries,
            key_rows,
            value_rows,
            attended,
            log_totals,
            *tables,
        ),
        (tokens, first_in, heads_in, mix_all, mix_late, *(expert_sums if paired else ())),
        paired,
        peer_count,
    )
    if paired:
        small_sum = small_sum[0]
        cut = expert_in.shape[2]
        expert_sums = (bank_sums[0][:, :, :cut], bank_sums[0][:, :, cut:])
    else:
        head_parts = unit_columns(unit_sums.reshape(unit_sums.shape[0], model_width, UNIT))
        packed = jnp.concatenate([*head_parts, small_sum.reshape(model_width, 128)], axis=1)
        head_total = lax.psum_scatter(
            packed, ("dp", "expert"), scatter_dimension=0, tiled=True
        ).astype(jnp.float32)
        cut_in = head_parts[0].shape[1]
        cut_out = cut_in + head_parts[1].shape[1]
        head_parts = (head_total[:, :cut_in], head_total[:, cut_in:cut_out])
        small_sum = head_total[:, cut_out:]
    if paired:
        head_parts = unit_columns(unit_sums)
    head_in_sum, head_out_sum = head_parts
    summed = (
        head_in_sum,
        head_out_sum,
    )
    shard_rows = model_width // lax.axis_size(("dp", "expert"))
    small_rows = small_sum.T
    gains_share = lax.dynamic_slice_in_dim(
        gain_rows, lax.axis_index(("dp", "expert")) * shard_rows, shard_rows, 1
    )
    gains_new = update(
        small_rows[experts : experts + 2], gains_share, gains_moment.T, gains_average.T
    )
    gains_new = tuple(value.T for value in gains_new)
    inproj_new = update(summed[0], heads_in_master, heads_in_moment, heads_in_average)
    outproj_new = update(summed[1], heads_out_master, heads_out_moment, heads_out_average)
    router_new = update(
        small_rows[:experts], router_master.T, router_moment.T, router_average.T
    )
    router_new = tuple(value.T for value in router_new)
    upper_new = update(expert_sums[0], expert_in_master, expert_in_moment, expert_in_average)
    lower_new = update(expert_sums[1], expert_out_master, expert_out_moment, expert_out_average)
    return (
        output,
        token_grad,
        gains_new[0],
        gains_new[1],
        gains_new[2],
        inproj_new[0],
        inproj_new[1],
        inproj_new[2],
        outproj_new[0],
        outproj_new[1],
        outproj_new[2],
        router_new[0],
        router_new[1],
        router_new[2],
        upper_new[0],
        upper_new[1],
        upper_new[2],
        lower_new[0],
        lower_new[1],
        lower_new[2],
    )


def solution(mesh):
    return jax.shard_map(
        body,
        mesh=mesh,
        in_specs=(
            P(("dp", "expert"), None),
            P(("dp", "expert"), None),
            P(("dp", "expert"), None),
            P(("dp", "expert"), None),
            P(),
            P(("dp", "expert"), None),
            P(("dp", "expert"), None),
            P(),
            P(("dp", "expert"), None),
            P(("dp", "expert"), None),
            P(("dp", "expert"), None),
            P(),
            P(("dp", "expert"), None),
            P(("dp", "expert"), None),
            P(("dp", "expert"), None),
            P(),
            P(("dp", "expert"), None),
            P(("dp", "expert"), None),
            P(("dp", "expert"), None),
            P("expert", None, None),
            P("expert", "dp", None),
            P("expert", "dp", None),
            P("expert", "dp", None),
            P("expert", None, None),
            P("expert", "dp", None),
            P("expert", "dp", None),
            P("expert", "dp", None),
        ),
        out_specs=(
            P(("dp", "expert"), None),
            P(("dp", "expert"), None),
            P(("dp", "expert"), None),
            P(("dp", "expert"), None),
            P(("dp", "expert"), None),
            P(("dp", "expert"), None),
            P(("dp", "expert"), None),
            P(("dp", "expert"), None),
            P(("dp", "expert"), None),
            P(("dp", "expert"), None),
            P(("dp", "expert"), None),
            P(("dp", "expert"), None),
            P(("dp", "expert"), None),
            P(("dp", "expert"), None),
            P("expert", "dp", None),
            P("expert", "dp", None),
            P("expert", "dp", None),
            P("expert", "dp", None),
            P("expert", "dp", None),
            P("expert", "dp", None),
        ),
        check_vma=False,
    )
```

```python
import functools

import jax
import jax.numpy as jnp
from jax import lax
from jax.experimental import pallas as pl
from jax.experimental.pallas import tpu as pltpu
from jax.sharding import PartitionSpec as P

HEADS = 16
KV_HEADS = 8
HEAD_DIM = 64


EPS = 1e-06
SCALE = 0.015625
THETA = 10000.0
MOMENTUM = 0.9
DECAY = 0.8
RATE = 0.001
HIGHEST = lax.Precision.HIGHEST


def layout(labels_row, prompt_len):
    places = jnp.arange(prompt_len + labels_row.shape[0], dtype=jnp.int32)
    earlier = jnp.sum((labels_row[None, :] < labels_row[:, None]).astype(jnp.int32), axis=1)
    offset = places[prompt_len:] - prompt_len - earlier
    positions = jnp.concatenate([places[:prompt_len], prompt_len + offset]).astype(jnp.float32)
    labels = jnp.concatenate([jnp.full((prompt_len,), -1, jnp.int32), labels_row])
    allowed = (places[None, :] <= places[:, None]) & (
        (places[None, :] < prompt_len) | (labels[None, :] == labels[:, None])
    )
    return (positions, allowed)


def rope_tables(positions):
    middle = HEAD_DIM // 2
    frequency = THETA ** (-2.0 * jnp.arange(middle, dtype=jnp.float32) / HEAD_DIM)
    angles = positions[:, None] * frequency[None, :]
    cosine, sine = jnp.cos(angles), jnp.sin(angles)
    return (
        jnp.concatenate([cosine] * 4, axis=1),
        jnp.concatenate([-sine, sine, -sine, sine], axis=1),
    )


def update(gradient, master, moment, average):
    moment_next = MOMENTUM * moment + gradient
    master_next = master - RATE * (gradient + MOMENTUM * moment_next)
    return (master_next, moment_next, DECAY * average + (1.0 - DECAY) * master_next)


F32 = jnp.float32
BF16 = jnp.bfloat16
MESH = pl.DeviceIdType.MESH
VMEM_MOST = 61 * 2**20


def contract(left, right, left_axis, right_axis):
    return lax.dot_general(
        left, right, (((left_axis,), (right_axis,)), ((), ())), preferred_element_type=F32
    )


def visit_order(line):
    return [sorted(range(line), key=lambda s: (abs(s - z), s)) for z in range(line)]


def line_gather(line, z, dp, source, landing, send_sem, recv_sem):
    def copy(origin, block, sem, target):
        return pltpu.make_async_remote_copy(
            src_ref=origin,
            dst_ref=landing.at[block],
            send_sem=send_sem.at[sem],
            recv_sem=recv_sem.at[block],
            device_id=(dp, target),
            device_id_type=MESH,
        )

    def start():
        @pl.when(z < line - 1)
        def _():
            copy(source, z, line, z + 1).start()

        @pl.when(z > 0)
        def _():
            copy(source, z, line + 1, z - 1).start()

    def pass_on(apart):
        low = jnp.maximum(z - apart, 0)
        high = jnp.minimum(z + apart, line - 1)

        @pl.when(z - apart >= 0)
        def _():
            copy(source, low, low, z).wait_recv()

            @pl.when(z < line - 1)
            def _():
                copy(landing.at[low], low, low, z + 1).start()

        @pl.when(z + apart < line)
        def _():
            copy(source, high, high, z).wait_recv()

            @pl.when(z > 0)
            def _():
                copy(landing.at[high], high, high, z - 1).start()

    def finish():
        @pl.when(z < line - 1)
        def _():
            copy(source, z, line, z + 1).wait_send()

        @pl.when(z > 0)
        def _():
            copy(source, z, line + 1, z - 1).wait_send()

        for s in range(line):

            @pl.when(((s < z) & (z < line - 1)) | ((s > z) & (z > 0)))
            def _(s=s):
                copy(source, s, s, z).wait_send()

    return start, pass_on, finish


def pass_steps(line, experts):
    steps = []
    for z in range(line):
        order = visit_order(line)[z]
        for apart in range(1, line):
            met = [k for k in range(line) if abs(order[k] - z) == apart]
            if not met:
                continue
            forwards = (z - apart >= 0 and z < line - 1) or (z + apart < line and z > 0)
            early = experts // 2 if forwards and apart > 1 else 0
            steps.append((z, met[0] * experts - early, apart))
    return steps


def pick(table, row, column):
    value = jnp.int32(table[0][0])
    for r in range(len(table)):
        for c in range(len(table[0])):
            value = jnp.where((row == r) & (column == c), jnp.int32(table[r][c]), value)
    return value


def weight_grads_kernel(rows, cots, gated, inner, up_grad, down_grad):
    step = 256
    for at in range(0, rows.shape[1], step):
        up_grad[0, at : at + step] = contract(rows[:, at : at + step], inner[...], 0, 0).astype(BF16)
        down_grad[0, at : at + step] = contract(cots[:, at : at + step], gated[...], 0, 0).astype(
            BF16
        )


def weight_grads(rows, cots, gated, inner, experts):
    tokens, width = rows.shape
    ff_width = gated.shape[1] // experts
    whole = pl.BlockSpec((tokens, width), lambda e: (0, 0))
    return pl.pallas_call(
        weight_grads_kernel,
        grid=(experts,),
        out_shape=(
            jax.ShapeDtypeStruct((experts, width, 2 * ff_width), BF16),
            jax.ShapeDtypeStruct((experts, width, ff_width), BF16),
        ),
        in_specs=[
            whole,
            whole,
            pl.BlockSpec((tokens, ff_width), lambda e: (0, e)),
            pl.BlockSpec((tokens, 2 * ff_width), lambda e: (0, e)),
        ],
        out_specs=(
            pl.BlockSpec((1, width, 2 * ff_width), lambda e: (e, 0, 0)),
            pl.BlockSpec((1, width, ff_width), lambda e: (e, 0, 0)),
        ),
        compiler_params=pltpu.CompilerParams(vmem_limit_bytes=VMEM_MOST),
        cost_estimate=pl.CostEstimate(
            flops=6 * tokens * width * experts * ff_width,
            bytes_accessed=2 * tokens * (2 * width + 3 * experts * ff_width)
            + 6 * experts * width * ff_width,
            transcendentals=0,
        ),
    )(rows, cots, gated, inner)


def bank_grads_kernel(
    rows_hbm,
    cots_hbm,
    gated_hbm,
    inner_hbm,
    sum_hbm,
    rows,
    cots,
    gated,
    inner,
    grads,
    core_sum,
    first_sum,
    load_sem,
    send_sem,
    recv_sem,
    out_sem,
):
    experts = grads.shape[0]
    ff_width = gated.shape[2]
    block_rows = grads.shape[4]
    dp = lax.axis_index("dp")
    z = lax.axis_index("expert")
    y, x, core = dp // 4, lax.rem(dp // 2, 2), lax.rem(dp, 2)
    core_peer, x_peer, y_peer = dp + 1 - 2 * core, dp + 2 - 4 * x, dp + 4 - 8 * y

    def loads(e, slot):
        return (
            pltpu.make_async_copy(
                gated_hbm.at[:, pl.ds(pl.multiple_of(e * ff_width, ff_width), ff_width)],
                gated.at[slot],
                load_sem.at[slot, 0],
            ),
            pltpu.make_async_copy(
                inner_hbm.at[:, pl.ds(pl.multiple_of(2 * e * ff_width, ff_width), 2 * ff_width)],
                inner.at[slot],
                load_sem.at[slot, 1],
            ),
        )

    row_load = pltpu.make_async_copy(rows_hbm, rows, load_sem.at[0, 2])
    cot_load = pltpu.make_async_copy(cots_hbm, cots, load_sem.at[1, 2])
    row_load.start()
    for copy in loads(0, 0):
        copy.start()
    cot_load.start()
    barrier = pltpu.get_barrier_semaphore()
    for peer in (core_peer, x_peer, y_peer):
        pl.semaphore_signal(barrier, inc=1, device_id=(peer, z), device_id_type=MESH)
    pl.semaphore_wait(barrier, 3)
    row_load.wait()
    cot_load.wait()

    def send(stage, e, source, target, peer):
        return pltpu.make_async_remote_copy(
            src_ref=source,
            dst_ref=target,
            send_sem=send_sem.at[stage, e],
            recv_sem=recv_sem.at[stage, e],
            device_id=(peer, z),
            device_id_type=MESH,
        )

    def core_send(e):
        return send(0, e, grads.at[e, :, :, 1 - core], core_sum.at[e], core_peer)

    def first_send(e, along_x):
        if along_x:
            return send(1, e, core_sum.at[e, :, 1 - x], first_sum.at[e], x_peer)
        return send(1, e, core_sum.at[e, 1 - y], first_sum.at[e], y_peer)

    def by_parity(e, act):
        even = lax.rem(e, 2) == 0

        @pl.when(even)
        def _():
            act(True)

        @pl.when(jnp.logical_not(even))
        def _():
            act(False)

    def after_core(e):
        core_send(e).wait_recv()
        for yy in range(2):
            for xx in range(2):
                core_sum[e, yy, xx] = (
                    grads[e, yy, xx, core].astype(F32) + core_sum[e, yy, xx].astype(F32)
                ).astype(BF16)
        by_parity(e, lambda even: first_send(e, even).start())

    def after_first(e):
        def act(even):
            first_send(e, even).wait_recv()
            for other in range(2):
                kept = core_sum[e, other, x] if even else core_sum[e, y, other]
                first_sum[e, other] = (
                    kept.astype(F32) + first_sum[e, other].astype(F32)
                ).astype(BF16)

        by_parity(e, act)
        pltpu.make_async_copy(first_sum.at[e], sum_hbm.at[e], out_sem.at[e]).start()

    def step(e, _):
        slot = lax.rem(e, 2)
        for copy in loads(e, slot):
            copy.wait()

        @pl.when(e + 1 < experts)
        def _():
            for copy in loads(e + 1, 1 - slot):
                copy.start()

        def tile(at, _):
            columns = pl.ds(pl.multiple_of(at * 2 * block_rows, 2 * block_rows), 2 * block_rows)
            up_grad = contract(rows[:, columns], inner[slot], 0, 0).astype(BF16)
            down_grad = contract(cots[:, columns], gated[slot], 0, 0).astype(BF16)
            for side in range(2):
                part = slice(side * block_rows, (side + 1) * block_rows)
                grads[e, at // 2, lax.rem(at, 2), side, :, : 2 * ff_width] = up_grad[part]
                grads[e, at // 2, lax.rem(at, 2), side, :, 2 * ff_width :] = down_grad[part]
            return 0

        lax.fori_loop(0, 4, tile, 0)
        core_send(e).start()

        @pl.when(e >= 1)
        def _():
            after_core(e - 1)

        @pl.when(e >= 3)
        def _():
            after_first(e - 3)

        return 0

    lax.fori_loop(0, experts, step, 0)
    after_core(experts - 1)

    for e in range(max(experts - 3, 0), experts):
        after_first(e)
    for e in range(experts):
        core_send(e).wait_send()
        first_send(e, e % 2 == 0).wait_send()
        pltpu.make_async_copy(first_sum.at[e], sum_hbm.at[e], out_sem.at[e]).wait()


def bank_grads(rows, cots, gated, inner, experts):
    tokens, width = rows.shape
    ff_width = gated.shape[1] // experts
    lanes = 3 * ff_width
    block_rows = width // 8
    anywhere = pl.BlockSpec(memory_space=pl.ANY)
    return pl.pallas_call(
        bank_grads_kernel,
        out_shape=jax.ShapeDtypeStruct((experts, 2, block_rows, lanes), BF16),
        in_specs=[anywhere] * 4,
        out_specs=anywhere,
        scratch_shapes=[
            pltpu.VMEM((tokens, width), BF16),
            pltpu.VMEM((tokens, width), BF16),
            pltpu.VMEM((2, tokens, ff_width), BF16),
            pltpu.VMEM((2, tokens, 2 * ff_width), BF16),
            pltpu.VMEM((experts, 2, 2, 2, block_rows, lanes), BF16),
            pltpu.VMEM((experts, 2, 2, block_rows, lanes), BF16),
            pltpu.VMEM((experts, 2, block_rows, lanes), BF16),
            pltpu.SemaphoreType.DMA((2, 3)),
            pltpu.SemaphoreType.DMA((2, experts)),
            pltpu.SemaphoreType.DMA((2, experts)),
            pltpu.SemaphoreType.DMA((experts,)),
        ],
        compiler_params=pltpu.CompilerParams(
            collective_id=2, has_side_effects=True, vmem_limit_bytes=VMEM_MOST
        ),
        cost_estimate=pl.CostEstimate(
            flops=6 * tokens * width * experts * ff_width,
            bytes_accessed=2**27,
            transcendentals=0,
        ),
    )(rows, cots, gated, inner)


PAIR = 2 * HEAD_DIM
UNIT = 512
PIECES = 3


def swap_halves(value):
    lane = lax.broadcasted_iota(jnp.int32, value.shape, 1)
    half = HEAD_DIM // 2
    return jnp.where(
        lax.rem(lane, HEAD_DIM) < half,
        pltpu.roll(value, value.shape[1] - half, 1),
        pltpu.roll(value, half, 1),
    )


def sides(pair, side, scale):
    value = pair.astype(F32)
    if scale is not None:
        value = value * scale
    turned = pltpu.roll(value, HEAD_DIM, 1)
    lane = lax.broadcasted_iota(jnp.int32, value.shape, 1)
    left, right = (value, turned) if side == 0 else (turned, value)
    return (
        jnp.where(lane < HEAD_DIM, left, 0.0).astype(BF16),
        jnp.where(lane < HEAD_DIM, 0.0, right).astype(BF16),
    )


def lanes_at(start, size):
    return pl.ds(pl.multiple_of(start, 128), size)


def front_kernel(
    line,
    prompt,
    late,
    tokens,
    cots_hbm,
    gain_rows,
    heads_in_hbm,
    heads_out_hbm,
    router_rows,
    route_rows,
    cosine,
    sine,
    bias,
    up_hbm,
    down_hbm,
    first_in_hbm,
    queries_hbm,
    keys_hbm,
    values_hbm,
    attended_hbm,
    hidden_hbm,
    second_in_hbm,
    gate_rows,
    log_totals,
    cots_all,
    mix_all,
    mix_late,
    back_hbm,
    gate_grads_hbm,
    gated_hbm,
    inner_hbm,
    rows_all_hbm,
    cots,
    rows,
    gates_own,
    gates,
    gate_grads,
    gate_grads_sent,
    up,
    down,
    projected,
    stage,
    mix_stage,
    gated,
    inner,
    columns,
    cot_send,
    cot_recv,
    row_send,
    row_recv,
    gate_send,
    gate_recv,
    weight_sem,
    local_sem,
    out_sem,
    grad_send,
    grad_recv,
    mix_send,
    mix_recv,
    heads_in,
    heads_out,
    first_in,
    queries,
    keys,
    values,
    attended,
    hidden,
    second_in,
    held_sem,
):
    dp = lax.axis_index("dp")
    z = lax.axis_index("expert")
    experts, _, ff_width = down_hbm.shape
    start_cots, pass_cots, finish_cots = line_gather(
        line, z, dp, cots_hbm, cots_all, cot_send, cot_recv
    )
    start_rows, pass_rows, finish_rows = line_gather(
        line, z, dp, second_in, rows, row_send, row_recv
    )

    heads_in_load = pltpu.make_async_copy(heads_in_hbm, heads_in, held_sem.at[0])
    heads_out_load = pltpu.make_async_copy(heads_out_hbm, heads_out, held_sem.at[1])
    held_out = [
        pltpu.make_async_copy(source, target, held_sem.at[2 + number])
        for number, (source, target) in enumerate(
            (
                (first_in, first_in_hbm),
                (queries, queries_hbm),
                (keys, keys_hbm),
                (values, values_hbm),
                (attended, attended_hbm),
                (hidden, hidden_hbm),
                (second_in, second_in_hbm),
            )
        )
    ]

    def weight_copies(e):
        return (
            pltpu.make_async_copy(
                up_hbm.at[e],
                up.at[:, pl.ds(pl.multiple_of(e * 2 * ff_width, ff_width), 2 * ff_width)],
                weight_sem.at[0, e],
            ),
            pltpu.make_async_copy(
                down_hbm.at[e],
                down.at[:, pl.ds(pl.multiple_of(e * ff_width, ff_width), ff_width)],
                weight_sem.at[1, e],
            ),
        )

    barrier = pltpu.get_barrier_semaphore()
    for step in range(1, line):
        pl.semaphore_signal(
            barrier, inc=1, device_id=(dp, lax.rem(z + step, line)), device_id_type=MESH
        )
    pl.semaphore_wait(barrier, line - 1)
    start_cots()
    cots_in = pltpu.make_async_copy(cots_hbm, cots, local_sem.at[2])
    cots_in.start()
    heads_in_load.start()
    heads_out_load.start()
    for e in range(experts):
        for copy in weight_copies(e):
            copy.start()

    query_end = HEADS * HEAD_DIM
    key_end = query_end + KV_HEADS * HEAD_DIM
    token_rows = tokens[...].astype(F32)
    factor = lax.rsqrt(jnp.mean(token_rows * token_rows, axis=1, keepdims=True) + EPS)
    first_in[...] = (token_rows * factor * gain_rows[0:1]).astype(BF16)
    log_totals[...] = jnp.zeros_like(log_totals)
    cots_in.wait()
    own_cots = pltpu.make_async_copy(cots, cots_all.at[z], local_sem.at[0])
    own_cots.start()

    heads_in_load.wait()

    def project(i, _):
        at = lanes_at(i * UNIT, UNIT)
        projected[:, at] = contract(first_in[...], heads_in[:, at], 1, 0)
        return 0

    lax.fori_loop(0, heads_in.shape[1] // UNIT, project, 0)

    def pair(j, _):
        for side in range(2):
            at = lanes_at((2 * j + side) * PAIR, PAIR)
            wide = projected[:, at]
            queries[:, at] = (wide * cosine[...] + swap_halves(wide) * sine[...]).astype(BF16)
        wide = projected[:, lanes_at(query_end + j * PAIR, PAIR)]
        keys[:, lanes_at(j * PAIR, PAIR)] = (
            wide * cosine[...] + swap_halves(wide) * sine[...]
        ).astype(BF16)
        values[:, lanes_at(j * PAIR, PAIR)] = projected[
            :, lanes_at(key_end + j * PAIR, PAIR)
        ].astype(BF16)
        heads = [(side, member) for side in range(2) for member in range(2)]
        groups = [queries[:, lanes_at((2 * j + side) * PAIR, PAIR)] for side in range(2)]
        key_sides = [sides(keys[:, lanes_at(j * PAIR, PAIR)], side, SCALE) for side in range(2)]
        value_sides = [sides(values[:, lanes_at(j * PAIR, PAIR)], side, None) for side in range(2)]
        parts = ((0, prompt, prompt), (prompt, groups[0].shape[0], groups[0].shape[0]))

        def scores_of(side, member):
            return [
                contract(groups[side][begin:end], key_sides[side][member][:seen], 1, 1)
                + bias[begin:end, :seen]
                for begin, end, seen in parts
            ]

        lane = lax.broadcasted_iota(jnp.int32, log_totals.shape, 1)
        added = jnp.zeros(log_totals.shape, F32)
        sums = [0.0, 0.0]
        scores = scores_of(*heads[0])
        for number, (side, member) in enumerate(heads):
            following = scores_of(*heads[number + 1]) if number + 1 < len(heads) else None
            mixed = []
            totals = []
            for part, (_, _, seen) in zip(scores, parts):
                peak = jnp.max(part, axis=1, keepdims=True)
                powers = jnp.exp(part - peak)
                amount = jnp.sum(powers, axis=1, keepdims=True)
                weights = (powers * (1.0 / amount)).astype(BF16)
                totals.append(peak + jnp.log(amount))
                mixed.append(contract(weights, value_sides[side][member][:seen], 1, 0))
            sums[side] = sums[side] + jnp.concatenate(mixed, axis=0)
            added = jnp.where(lane == 4 * j + number, jnp.concatenate(totals, axis=0), added)
            scores = following
        log_totals[...] += added
        for side in range(2):
            attended[:, lanes_at((2 * j + side) * PAIR, PAIR)] = sums[side].astype(BF16)
        return 0

    lax.fori_loop(0, KV_HEADS // 2, pair, 0)
    heads_out_load.wait()
    hidden_rows = token_rows + contract(attended[...], heads_out[...], 1, 1)
    hidden[...] = hidden_rows
    factor = lax.rsqrt(jnp.mean(hidden_rows * hidden_rows, axis=1, keepdims=True) + EPS)
    second = (hidden_rows * factor * gain_rows[1:2]).astype(BF16)
    second_in[...] = second
    start_rows()
    for copy in held_out:
        copy.start()
    own_rows = pltpu.make_async_copy(second_in, rows.at[z], local_sem.at[1])
    own_rows.start()
    logits = contract(router_rows[...], second, 1, 1)
    expert = lax.broadcasted_iota(jnp.int32, logits.shape, 0)
    named = expert == route_rows[0:1]
    for k in range(1, route_rows.shape[0]):
        named = named | (expert == route_rows[k : k + 1])
    peak = jnp.max(jnp.where(named, logits, -1e30), axis=0, keepdims=True)
    powers = jnp.where(named, jnp.exp(jnp.where(named, logits, peak) - peak), 0.0)
    gate_values = powers / jnp.sum(powers, axis=0, keepdims=True)
    gate_rows[...] = gate_values
    gates_own[...] = jnp.zeros_like(gates_own)
    for peer in range(line):
        gates_own[peer, :experts] = gate_values[peer * experts : (peer + 1) * experts]
    gates[z] = gates_own[z]
    def gate_copy(step):
        peer = lax.rem(z + step, line)
        return pltpu.make_async_remote_copy(
            src_ref=gates_own.at[peer],
            dst_ref=gates.at[z],
            send_sem=gate_send.at[step],
            recv_sem=gate_recv.at[step],
            device_id=(dp, peer),
            device_id_type=MESH,
        )

    for step in range(1, line):
        gate_copy(step).start()
    own_rows.wait()
    own_cots.wait()
    pass_cots(1)
    for step in range(1, line):
        gate_copy(step).wait()

    order = visit_order(line)

    def out_copies(slot, block):
        return (
            pltpu.make_async_copy(stage.at[slot], back_hbm.at[block], out_sem.at[slot, 0]),
            pltpu.make_async_copy(gated.at[slot], gated_hbm.at[block], out_sem.at[slot, 1]),
            pltpu.make_async_copy(inner.at[slot], inner_hbm.at[block], out_sem.at[slot, 2]),
        )

    def mix_copy(block, source, target):
        return pltpu.make_async_remote_copy(
            src_ref=mix_stage.at[block],
            dst_ref=mix_all.at[source],
            send_sem=mix_send.at[block],
            recv_sem=mix_recv.at[source],
            device_id=(dp, target),
            device_id_type=MESH,
        )

    def own_mix():
        return pltpu.make_async_copy(mix_stage.at[z], mix_all.at[z], local_sem.at[3])

    def late_mix(side):
        return pltpu.make_async_copy(
            mix_stage.at[side * (line - 1)], mix_late.at[side], local_sem.at[4 + side]
        )

    def at_end(block):
        return (block == 0) | (block == line - 1)

    def grad_copy(block, step):
        return pltpu.make_async_remote_copy(
            src_ref=gate_grads_sent.at[block],
            dst_ref=gate_grads.at[z],
            send_sem=grad_send.at[block],
            recv_sem=grad_recv.at[z],
            device_id=(dp, block),
            device_id_type=MESH,
        )

    def visit(k, _):
        block = pick(order, z, k)
        slot = lax.rem(k, 2)
        @pl.when(k >= 2)
        def _():
            for copy in out_copies(slot, pick(order, z, jnp.maximum(k - 2, 0))):
                copy.wait()

        cot_load = pltpu.make_async_copy(cots_all.at[block], cots, local_sem.at[2])
        gate_columns = gates[block].T
        tile = min(ff_width, 256)
        def arrive(e):
            step = k * experts + e
            apart = jnp.int32(0)
            for at_z, at_step, distance in pass_steps(line, experts):
                apart = jnp.where((z == at_z) & (step == at_step), distance, apart)

            @pl.when(apart > 0)
            def _():
                pass_rows(apart)

            if line > 2:

                @pl.when(apart == 1)
                def _():
                    pass_cots(2)

            @pl.when(apart > 2)
            def _():
                pass_cots(apart)

            @pl.when((k > 0) & (e == 0))
            def _():
                cot_load.start()
                cot_load.wait()

        def products(e, at):
            gate_at = pl.multiple_of(2 * e * ff_width + at, tile)
            up_at = pl.multiple_of((2 * e + 1) * ff_width + at, tile)
            down_at = pl.multiple_of(e * ff_width + at, tile)
            return (
                contract(rows[block], up[:, pl.ds(gate_at, tile)], 1, 0),
                contract(rows[block], up[:, pl.ds(up_at, tile)], 1, 0),
                contract(cots[...], down[:, pl.ds(down_at, tile)], 1, 0),
            )

        narrow_lane = lax.broadcasted_iota(jnp.int32, gate_columns.shape, 1)
        wide_lane = lax.broadcasted_iota(jnp.int32, columns.shape, 1)
        several = experts // 2
        columns[...] = jnp.zeros_like(columns)

        def half(part, _):
            begin = part * several
            arrive(begin)

            @pl.when(k == 0)
            def _():
                for e in range(several):
                    for copy in weight_copies(begin + e):
                        copy.wait()

            tiles = [(e, at) for e in range(several) for at in range(0, ff_width, tile)]
            ready = products(begin + tiles[0][0], tiles[0][1])
            sums = [0.0] * several
            for number, (near, at) in enumerate(tiles):
                following = None
                if number + 1 < len(tiles):
                    following = products(begin + tiles[number + 1][0], tiles[number + 1][1])
                e = begin + near
                gate_part, up_part, returned = ready
                gate_col = jnp.sum(
                    jnp.where(narrow_lane == e, gate_columns, 0.0), axis=1, keepdims=True
                )
                sigmoid_gate = jax.nn.sigmoid(gate_part)
                silu_gate = gate_part * sigmoid_gate
                active = silu_gate * up_part
                sums[near] = sums[near] + jnp.sum(active * returned, axis=1, keepdims=True)
                scaled = returned * gate_col
                grad_gate = scaled * up_part * (sigmoid_gate + silu_gate * (1.0 - sigmoid_gate))
                gate_at = pl.multiple_of(2 * e * ff_width + at, tile)
                up_at = pl.multiple_of((2 * e + 1) * ff_width + at, tile)
                down_at = pl.multiple_of(e * ff_width + at, tile)
                gated[slot, :, pl.ds(down_at, tile)] = (active * gate_col).astype(BF16)
                inner[slot, :, pl.ds(gate_at, tile)] = grad_gate.astype(BF16)
                inner[slot, :, pl.ds(up_at, tile)] = (scaled * silu_gate).astype(BF16)
                ready = following
            value = columns[...]
            for near in range(several):
                value = jnp.where(wide_lane == begin + near, sums[near], value)
            columns[...] = value
            return 0

        lax.fori_loop(0, 2, half, 0)
        mix_stage[block] = contract(gated[slot], down[...], 1, 1).astype(BF16)

        @pl.when(block == z)
        def _():
            own_mix().start()

        if late:
            for side in range(2):

                @pl.when((block != z) & (block == side * (line - 1)))
                def _(side=side):
                    late_mix(side).start()

            @pl.when((block != z) & jnp.logical_not(at_end(block)))
            def _():
                mix_copy(block, z, block).start()

        else:

            @pl.when(block != z)
            def _():
                mix_copy(block, z, block).start()

        stage[slot] = contract(inner[slot], up[...], 1, 1).astype(BF16)
        for copy in out_copies(slot, block):
            copy.start()
        gate_grads_sent[block] = columns[...].T[: gate_grads.shape[1]]

        @pl.when(block == z)
        def _():
            gate_grads[z] = gate_grads_sent[z]

        @pl.when(block != z)
        def _():
            grad_copy(block, 0).start()

        return 0

    lax.fori_loop(0, line, visit, 0)
    for k in range(max(line - 2, 0), line):
        for copy in out_copies(k % 2, pick(order, z, k)):
            copy.wait()

    finish_rows()
    finish_cots()
    for copy in held_out:
        copy.wait()
    own_mix().wait()
    if late:
        for side in range(2):

            @pl.when(z != side * (line - 1))
            def _(side=side):
                late_mix(side).wait()

    for s in range(line):
        send_ends = late and s in (0, line - 1)

        @pl.when(z != s)
        def _(s=s, send_ends=send_ends):
            if not send_ends:
                mix_copy(s, s, z).wait_send()
            if late:

                @pl.when(jnp.logical_not(at_end(z)))
                def _():
                    mix_copy(s, s, z).wait_recv()

            else:
                mix_copy(s, s, z).wait_recv()

    for s in range(line):

        @pl.when(s != z)
        def _(s=s):
            grad_copy(s, 0).wait_send()
            pltpu.make_async_remote_copy(
                src_ref=gate_grads_sent.at[s],
                dst_ref=gate_grads.at[s],
                send_sem=grad_send.at[s],
                recv_sem=grad_recv.at[s],
                device_id=(dp, z),
                device_id_type=MESH,
            ).wait_recv()

    last = (
        pltpu.make_async_copy(rows, rows_all_hbm, local_sem.at[0]),
        pltpu.make_async_copy(gate_grads, gate_grads_hbm, local_sem.at[1]),
    )
    for copy in last:
        copy.start()
    for copy in last:
        copy.wait()


def front(
    late,
    tokens,
    cots,
    gain_rows,
    heads_in,
    heads_out,
    router_rows,
    route_rows,
    tables,
    up,
    down,
    line,
    prompt,
):
    count, width = tokens.shape
    named = router_rows.shape[0]
    experts, _, ff_width = down.shape
    kv_width = KV_HEADS * HEAD_DIM
    shape = jax.ShapeDtypeStruct
    padded = experts + -experts % 8
    held = pl.BlockSpec(memory_space=pltpu.VMEM)
    anywhere = pl.BlockSpec(memory_space=pl.ANY)
    small = pltpu.VMEM((line, padded, count), F32)
    return pl.pallas_call(
        functools.partial(front_kernel, line, prompt, late),
        out_shape=(
            shape((count, width), BF16),
            shape((count, HEADS * HEAD_DIM), BF16),
            shape((count, kv_width), BF16),
            shape((count, kv_width), BF16),
            shape((count, HEADS * HEAD_DIM), BF16),
            shape((count, width), F32),
            shape((count, width), BF16),
            shape((named, count), F32),
            shape((count, 128), F32),
            shape((line, count, width), BF16),
            shape((line, count, width), BF16),
            shape((2, count, width), BF16),
            shape((line, count, width), BF16),
            shape((line, padded, count), F32),
            shape((line, count, experts * ff_width), BF16),
            shape((line, count, experts * 2 * ff_width), BF16),
            shape((line, count, width), BF16),
        ),
        in_specs=[held, anywhere, held, anywhere, anywhere] + [held] * 5 + [anywhere] * 2,
        out_specs=(anywhere,) * 7 + (held,) * 2 + (anywhere,) * 8,
        scratch_shapes=[
            pltpu.VMEM((count, width), BF16),
            pltpu.VMEM((line, count, width), BF16),
            small,
            small,
            small,
            small,
            pltpu.VMEM((width, experts * 2 * ff_width), BF16),
            pltpu.VMEM((width, experts * ff_width), BF16),
            pltpu.VMEM((count, heads_in.shape[1]), F32),
            pltpu.VMEM((2, count, width), BF16),
            pltpu.VMEM((line, count, width), BF16),
            pltpu.VMEM((2, count, experts * ff_width), BF16),
            pltpu.VMEM((2, count, experts * 2 * ff_width), BF16),
            pltpu.VMEM((count, 128), F32),
            pltpu.SemaphoreType.DMA((line + 2,)),
            pltpu.SemaphoreType.DMA((line,)),
            pltpu.SemaphoreType.DMA((line + 2,)),
            pltpu.SemaphoreType.DMA((line,)),
            pltpu.SemaphoreType.DMA((line,)),
            pltpu.SemaphoreType.DMA((line,)),
            pltpu.SemaphoreType.DMA((2, experts)),
            pltpu.SemaphoreType.DMA((6,)),
            pltpu.SemaphoreType.DMA((2, 3)),
            pltpu.SemaphoreType.DMA((line,)),
            pltpu.SemaphoreType.DMA((line,)),
            pltpu.SemaphoreType.DMA((line,)),
            pltpu.SemaphoreType.DMA((line,)),
            pltpu.VMEM(heads_in.shape, BF16),
            pltpu.VMEM(heads_out.shape, BF16),
            pltpu.VMEM((count, width), BF16),
            pltpu.VMEM((count, HEADS * HEAD_DIM), BF16),
            pltpu.VMEM((count, kv_width), BF16),
            pltpu.VMEM((count, kv_width), BF16),
            pltpu.VMEM((count, HEADS * HEAD_DIM), BF16),
            pltpu.VMEM((count, width), F32),
            pltpu.VMEM((count, width), BF16),
            pltpu.SemaphoreType.DMA((9,)),
        ],
        compiler_params=pltpu.CompilerParams(
            collective_id=4, has_side_effects=True, vmem_limit_bytes=VMEM_MOST
        ),
        cost_estimate=pl.CostEstimate(flops=2**35, bytes_accessed=2**26, transcendentals=2**22),
    )(
        tokens,
        cots,
        gain_rows,
        heads_in,
        heads_out,
        router_rows,
        route_rows,
        *tables,
        up,
        down,
    )


def attend_back_kernel(
    paired,
    line,
    back_rows,
    hidden,
    cots,
    second_in,
    gate_rows,
    gate_grads,
    router_rows,
    gain_rows,
    heads_out,
    queries,
    keys,
    values,
    attended,
    log_totals,
    cosine,
    sine,
    bias,
    tokens_hbm,
    first_hbm,
    in_hbm,
    mix_hbm,
    late_hbm,
    *others,
):
    bank_hbm, others = (others[0], others[1:]) if paired else (None, others)
    output, token_grad, sum_hbm, small_hbm, *others = others
    bank_sum_hbm, others = (others[0], others[1:]) if paired else (None, others)
    (
        tokens,
        first_in,
        heads_in,
        mixes,
        grad_hidden,
        grad_attended,
        grad_projected,
        small_rows,
        own,
        own_small,
        *scratch,
    ) = others
    dp = lax.axis_index("dp")
    z = lax.axis_index("expert")
    units = own.shape[0]
    block_rows = own.shape[4]
    load_sem = scratch[0]
    loads = (
        pltpu.make_async_copy(first_hbm, first_in, load_sem.at[0]),
        pltpu.make_async_copy(tokens_hbm, tokens, load_sem.at[1]),
        pltpu.make_async_copy(in_hbm, heads_in, load_sem.at[2]),
    )
    for copy in loads:
        copy.start()

    def mix_load(b):
        return pltpu.make_async_copy(mix_hbm.at[b], mixes.at[b], load_sem.at[5 + b])

    def direct(b):
        ends = (z == 0) | (z == line - 1)
        return jnp.logical_not(ends) | (z == b) if paired else z == z

    for b in range(line):

        @pl.when(direct(b))
        def _(b=b):
            mix_load(b).start()

    if paired:
        (
            cores,
            firsts,
            lasts,
            sums,
            lines,
            totals,
            small_cores,
            small_firsts,
            small_lasts,
            small_sums,
            small_lines,
            small_totals,
            send_sem,
            recv_sem,
            line_send,
            line_recv,
            out_sem,
            bank_kept,
            bank_last,
            bank_total,
            bank_sem,
            small_columns,
            chain_own,
            chain_in,
            chain_out,
            chain_load_sem,
            chain_sem,
        ) = scratch[1:]
        rows = totals.shape[1]
        y, x, core = dp // 4, lax.rem(dp // 2, 2), lax.rem(dp, 2)
        core_peer, x_peer, y_peer = dp + 1 - 2 * core, dp + 2 - 4 * x, dp + 4 - 8 * y
        barrier = pltpu.get_barrier_semaphore()
        for peer in (core_peer, x_peer, y_peer):
            pl.semaphore_signal(barrier, inc=1, device_id=(peer, z), device_id_type=MESH)
        for step in range(1, line):
            pl.semaphore_signal(
                barrier, inc=1, device_id=(dp, lax.rem(z + step, line)), device_id_type=MESH
            )
        pl.semaphore_wait(barrier, 3 + line - 1)

        def bank_kept_copy(e):
            kept = y if e % 2 == 0 else x
            return pltpu.make_async_copy(
                bank_hbm.at[e, kept], bank_kept.at[e], bank_sem.at[0, e]
            )

        def bank_last_copy(e):
            sent, peer = (1 - y, y_peer) if e % 2 == 0 else (1 - x, x_peer)
            return pltpu.make_async_remote_copy(
                src_ref=bank_hbm.at[e, sent],
                dst_ref=bank_last.at[e],
                send_sem=bank_sem.at[1, e],
                recv_sem=bank_sem.at[2, e],
                device_id=(peer, z),
                device_id_type=MESH,
            )

        def bank_total_copy(e):
            return pltpu.make_async_copy(
                bank_total.at[e], bank_sum_hbm.at[e], bank_sem.at[3, e]
            )

        for e in range(bank_hbm.shape[0]):
            bank_kept_copy(e).start()
            bank_last_copy(e).start()

        piece = hidden.shape[0] // PIECES

        def part(p):
            return pl.ds(p * piece, piece)

        def chain_load(side):
            return pltpu.make_async_copy(
                late_hbm.at[side], chain_own.at[side], chain_load_sem.at[side]
            )

        def chain_send(side, p, source):
            return pltpu.make_async_remote_copy(
                src_ref=source.at[side, part(p)],
                dst_ref=chain_in.at[side, part(p)],
                send_sem=chain_sem.at[0, side, p],
                recv_sem=chain_sem.at[1, side, p],
                device_id=(dp, jnp.clip(z + 2 * side - 1, 0, line - 1)),
                device_id_type=MESH,
            )

        inside = (z > 0) & (z < line - 1)
        starts = (z == line - 1, z == 0)
        for side in range(2):

            @pl.when(inside)
            def _(side=side):
                chain_load(side).start()

            @pl.when(starts[side])
            def _(side=side):
                for p in range(PIECES):
                    chain_send(side, p, late_hbm).start()

        def relay(side, p):
            if p == 0:
                chain_load(side).wait()
            chain_send(side, p, chain_out).wait_recv()
            chain_out[side, part(p)] = (
                chain_own[side, part(p)].astype(F32) + chain_in[side, part(p)].astype(F32)
            ).astype(BF16)
            chain_send(side, p, chain_out).start()

        def relay_on(near, p):
            low_half = 2 * z < line - 1

            @pl.when(inside & low_half)
            def _():
                relay(1 if near else 0, p)

            @pl.when(inside & jnp.logical_not(low_half))
            def _():
                relay(0 if near else 1, p)

        buffers = (own, cores, firsts, lasts, sums, lines, totals)
        small_buffers = (
            own_small,
            small_cores,
            small_firsts,
            small_lasts,
            small_sums,
            small_lines,
            small_totals,
        )

        def send(stage, u, source, target, peer):
            return pltpu.make_async_remote_copy(
                src_ref=source,
                dst_ref=target,
                send_sem=send_sem.at[stage, u],
                recv_sem=recv_sem.at[stage, u],
                device_id=(peer, z),
                device_id_type=MESH,
            )

        class Sums:
            def __init__(self, held, shift):
                self.own, self.cores, self.firsts, self.lasts = held[:4]
                self.sums, self.lines, self.totals = held[4:]
                self.shift = shift

            def core_send(self, u):
                return send(
                    0,
                    u + self.shift,
                    self.own.at[u, :, :, 1 - core],
                    self.cores.at[u],
                    core_peer,
                )

            def first_send(self, u, along_x):
                if along_x:
                    source, peer = self.cores.at[u, :, 1 - x], x_peer
                else:
                    source, peer = self.cores.at[u, 1 - y], y_peer
                return send(1, u + self.shift, source, self.firsts.at[u], peer)

            def last_send(self, u, along_x):
                if along_x:
                    source, peer = self.firsts.at[u, 1 - x], x_peer
                else:
                    source, peer = self.firsts.at[u, 1 - y], y_peer
                return send(2, u + self.shift, source, self.lasts.at[u], peer)

            def line_copy(self, u, step):
                peer = lax.rem(z + step, line)
                return pltpu.make_async_remote_copy(
                    src_ref=self.sums.at[u, pl.ds(pl.multiple_of(peer * rows, rows), rows)],
                    dst_ref=self.lines.at[u, step],
                    send_sem=line_send.at[u + self.shift, step],
                    recv_sem=line_recv.at[u + self.shift, step],
                    device_id=(dp, peer),
                    device_id_type=MESH,
                )

            def by_parity(self, u, act):
                even = lax.rem(jnp.int32(u), 2) == 0

                @pl.when(even)
                def _():
                    act(True)

                @pl.when(jnp.logical_not(even))
                def _():
                    act(False)

            def after_core(self, u):
                self.core_send(u).wait_recv()
                for yy in range(2):
                    for xx in range(2):
                        self.cores[u, yy, xx] = (
                            self.own[u, yy, xx, core].astype(F32)
                            + self.cores[u, yy, xx].astype(F32)
                        ).astype(BF16)
                self.by_parity(u, lambda even: self.first_send(u, even).start())

            def after_first(self, u):
                def act(even):
                    self.first_send(u, even).wait_recv()
                    for other in range(2):
                        kept = self.cores[u, other, x] if even else self.cores[u, y, other]
                        self.firsts[u, other] = (
                            kept.astype(F32) + self.firsts[u, other].astype(F32)
                        ).astype(BF16)
                    self.last_send(u, not even).start()

                self.by_parity(u, act)

            def after_last(self, u):
                def act(even):
                    self.last_send(u, not even).wait_recv()
                    kept = self.firsts[u, y] if even else self.firsts[u, x]
                    self.sums[u] = (kept.astype(F32) + self.lasts[u].astype(F32)).astype(BF16)

                self.by_parity(u, act)
                for step in range(1, line):
                    self.line_copy(u, step).start()

            def after_line(self, u):
                value = self.sums[u, pl.ds(pl.multiple_of(z * rows, rows), rows)].astype(F32)
                for step in range(1, line):
                    self.line_copy(u, step).wait_recv()
                    value = value + self.lines[u, step].astype(F32)
                self.totals[u] = value

            def finish(self, u):
                self.core_send(u).wait_send()
                self.first_send(u, u % 2 == 0).wait_send()
                self.last_send(u, u % 2 == 1).wait_send()
                for step in range(1, line):
                    self.line_copy(u, step).wait_send()

        wide_sums = Sums(buffers, 0)
        small_sum = Sums(small_buffers, units)

    def keep(target, u, value):
        for block in range(8):
            target[u, block // 4, block // 2 % 2, block % 2] = value[
                block * block_rows : (block + 1) * block_rows
            ]

    gates = gate_rows[...]
    gate_grad = gate_grads[...]
    logit_grad = gates * (gate_grad - jnp.sum(gates * gate_grad, axis=0, keepdims=True))
    high = logit_grad.astype(BF16)
    low = (logit_grad - high.astype(F32)).astype(BF16)
    grad_second = (
        back_rows[...].astype(F32)
        + contract(high, router_rows[...], 0, 0)
        + contract(low, router_rows[...], 0, 0)
    )
    small_rows[...] = jnp.zeros_like(small_rows)
    experts = high.shape[0]
    small_rows[:experts] = contract(high, second_in[...], 1, 0) + contract(low, second_in[...], 1, 0)

    def norm_back(incoming, rows, gain):
        factor = lax.rsqrt(jnp.mean(rows * rows, axis=1, keepdims=True) + EPS)
        normed = rows * factor
        gain_grad = jnp.sum(incoming * normed, axis=0, keepdims=True)
        weighted = incoming * gain
        mean = jnp.mean(weighted * normed, axis=1, keepdims=True)
        return factor * (weighted - normed * mean), gain_grad

    norm_grad, gain_grad = norm_back(grad_second, hidden[...], gain_rows[1:2])
    small_rows[experts + 1 : experts + 2] = gain_grad
    grad_hidden[...] = cots[...].astype(F32) + norm_grad
    branch = grad_hidden[...].astype(BF16)
    for u in range(2):
        keep(
            own,
            u,
            contract(branch, attended[:, u * UNIT : (u + 1) * UNIT], 0, 0).astype(BF16),
        )
        if paired:
            wide_sums.core_send(u).start()
    grad_attended[...] = contract(branch, heads_out[...], 1, 0).astype(BF16)
    loads[0].wait()
    if paired:
        wide_sums.after_core(0)
        relay_on(True, 0)

    def pair(j, _):
        key_pair = keys[:, lanes_at(j * PAIR, PAIR)]
        value_pair = values[:, lanes_at(j * PAIR, PAIR)]
        key_grads = []
        value_grads = []
        for side in range(2):
            at = lanes_at((2 * j + side) * PAIR, PAIR)
            group = queries[:, at]
            group_grad = grad_attended[:, at]
            key_sides = sides(key_pair, side, SCALE)
            value_sides = sides(value_pair, side, None)
            product = group_grad.astype(F32) * attended[:, at].astype(F32)
            lane = lax.broadcasted_iota(jnp.int32, product.shape, 1)
            grad = jnp.zeros(group.shape, F32)
            key_grad = []
            value_grad = []
            for member in range(2):
                head = 4 * j + 2 * side + member
                log_total = jnp.sum(
                    jnp.where(lane == head, log_totals[...], 0.0), axis=1, keepdims=True
                )
                mine = (lane < HEAD_DIM) if member == 0 else (lane >= HEAD_DIM)
                spread = jnp.sum(jnp.where(mine, product, 0.0), axis=1, keepdims=True)
                scores = contract(group, key_sides[member], 1, 1) + bias[...]
                weights = jnp.exp(scores - log_total)
                weight_grads = contract(group_grad, value_sides[member], 1, 1)
                score_grads = (weights * (weight_grads - spread)).astype(BF16)
                grad = grad + contract(score_grads, key_sides[member], 1, 0)
                rows_of = slice(member * HEAD_DIM, (member + 1) * HEAD_DIM)
                key_grad.append(contract(group, score_grads, 0, 0)[rows_of])
                value_grad.append(contract(group_grad, weights.astype(BF16), 0, 0)[rows_of])
            grad_projected[j, :, side * PAIR : (side + 1) * PAIR] = (
                grad * cosine[...] - swap_halves(grad) * sine[...]
            ).astype(BF16)
            key_grads.append(key_grad[0] + key_grad[1])
            value_grads.append(value_grad[0] + value_grad[1])
        key_rows = jnp.concatenate(key_grads, axis=0).T * SCALE
        grad_projected[j, :, 2 * PAIR : 3 * PAIR] = (
            key_rows * cosine[...] - swap_halves(key_rows) * sine[...]
        ).astype(BF16)
        grad_projected[j, :, 3 * PAIR :] = jnp.concatenate(value_grads, axis=0).T.astype(BF16)
        keep(own, 2 + j, contract(first_in[...], grad_projected[j], 0, 0).astype(BF16))
        if paired:
            wide_sums.core_send(2 + j).start()
            wide_sums.after_core(1 + j)

            @pl.when(j >= 2)
            def _():
                wide_sums.after_first(j - 2)

            for at, near, p in ((0, True, 1), (1, True, 2), (2, False, 0), (3, False, 1)):

                @pl.when(j == at)
                def _(near=near, p=p):
                    relay_on(near, p)

        return 0

    pairs = KV_HEADS // 2
    lax.fori_loop(0, pairs, pair, 0)
    last = units - 1
    if paired:
        wide_sums.after_core(last)
        relay_on(False, 2)
        wide_sums.after_first(2)
        wide_sums.after_last(0)
    loads[1].wait()
    loads[2].wait()
    grad_first = jnp.zeros(grad_hidden.shape, F32)
    query_end = HEADS * HEAD_DIM
    key_end = query_end + KV_HEADS * HEAD_DIM
    for j in range(pairs):
        for at, begin, size in (
            (0, 2 * j * PAIR, 2 * PAIR),
            (2 * PAIR, query_end + j * PAIR, PAIR),
            (3 * PAIR, key_end + j * PAIR, PAIR),
        ):
            grad_first = grad_first + contract(
                grad_projected[j, :, at : at + size], heads_in[:, begin : begin + size], 1, 1
            )
    norm_grad, gain_grad = norm_back(grad_first, tokens[...].astype(F32), gain_rows[0:1])
    small_rows[experts : experts + 1] = gain_grad
    keep(own_small, 0, small_rows[...].T.astype(BF16))
    if paired:
        small_sum.core_send(0).start()
    token_grad[...] = grad_hidden[...] + norm_grad
    if paired:
        for e in range(bank_hbm.shape[0]):
            bank_kept_copy(e).wait()
            bank_last_copy(e).wait()
            bank_total[e] = bank_kept[e].astype(F32) + bank_last[e].astype(F32)
            bank_total_copy(e).start()

    @pl.when(direct(-1))
    def _():
        total = hidden[...]
        for b in range(line):
            mix_load(b).wait()
            total = total + mixes[b].astype(F32)
        output[...] = total.astype(BF16)

    if paired:
        small_sum.after_core(0)
        wide_sums.after_first(3)
        wide_sums.after_last(1)
        wide_sums.after_first(4)
        wide_sums.after_last(2)
        small_sum.after_first(0)
        wide_sums.after_first(5)
        wide_sums.after_last(3)
        small_sum.after_last(0)
        wide_sums.after_line(0)
        wide_sums.after_last(4)
        wide_sums.after_line(1)
        wide_sums.after_last(5)
        for u in range(2, units):
            wide_sums.after_line(u)
        small_sum.after_line(0)
        places = [(u, 0, UNIT, key_end + KV_HEADS * HEAD_DIM + u * UNIT) for u in range(2)]
        for j in range(pairs):
            places.append((2 + j, 0, 2 * PAIR, 2 * j * PAIR))
            places.append((2 + j, 2 * PAIR, PAIR, query_end + j * PAIR))
            places.append((2 + j, 3 * PAIR, PAIR, key_end + j * PAIR))
        small_columns[...] = small_totals[0].T
        outs = [pltpu.make_async_copy(small_columns, small_hbm, out_sem.at[len(places)])]
        for number, (u, at, size, column) in enumerate(places):
            outs.append(
                pltpu.make_async_copy(
                    totals.at[u, :, at : at + size],
                    sum_hbm.at[:, column : column + size],
                    out_sem.at[number],
                )
            )
    else:
        outs = (
            pltpu.make_async_copy(own, sum_hbm, load_sem.at[3]),
            pltpu.make_async_copy(own_small, small_hbm, load_sem.at[4]),
        )
    for copy in outs:
        copy.start()
    if paired:
        for u in range(units):
            wide_sums.finish(u)
        small_sum.finish(0)
        for e in range(bank_hbm.shape[0]):
            bank_total_copy(e).wait()
        for side in range(2):

            @pl.when(starts[1 - side])
            def _(side=side):
                mix_load(z).wait()
                for p in range(PIECES):
                    chain_send(side, p, late_hbm).wait_recv()
                output[...] = (
                    hidden[...] + mixes[z].astype(F32) + chain_in[side].astype(F32)
                ).astype(BF16)

            @pl.when(jnp.logical_not(starts[1 - side]))
            def _(side=side):
                for p in range(PIECES):
                    chain_send(side, p, late_hbm).wait_send()

    for copy in outs:
        copy.wait()


def attend_back(held_args, far_args, paired, line):
    tokens, first_in, heads_in = far_args[:3]
    count, width = tokens.shape
    pairs = KV_HEADS // 2
    units = 2 + pairs
    block_rows = width // 8
    rows = block_rows // line
    shape = jax.ShapeDtypeStruct
    held = pl.BlockSpec(memory_space=pltpu.VMEM)
    anywhere = pl.BlockSpec(memory_space=pl.ANY)
    if paired:
        sum_shapes = (shape((rows, units * UNIT), F32), shape((128, rows), F32))
    else:
        sum_shapes = (
            shape((units, 2, 2, 2, block_rows, UNIT), BF16),
            shape((1, 2, 2, 2, block_rows, 128), BF16),
        )
    exchange = []
    if paired:
        for number, lanes in ((units, UNIT), (1, 128)):
            exchange += [
                pltpu.VMEM((number, 2, 2, block_rows, lanes), BF16),
                pltpu.VMEM((number, 2, block_rows, lanes), BF16),
                pltpu.VMEM((number, block_rows, lanes), BF16),
                pltpu.VMEM((number, block_rows, lanes), BF16),
                pltpu.VMEM((number, line, rows, lanes), BF16),
                pltpu.VMEM((number, rows, lanes), F32),
            ]
        exchange += [
            pltpu.SemaphoreType.DMA((3, units + 1)),
            pltpu.SemaphoreType.DMA((3, units + 1)),
            pltpu.SemaphoreType.DMA((units + 1, line)),
            pltpu.SemaphoreType.DMA((units + 1, line)),
            pltpu.SemaphoreType.DMA((3 + 3 * pairs,)),
        ]
        bank_shape = (far_args[5].shape[0],) + far_args[5].shape[2:]
        sum_shapes += (shape(bank_shape, F32),)
        exchange += [
            pltpu.VMEM(bank_shape, BF16),
            pltpu.VMEM(bank_shape, BF16),
            pltpu.VMEM(bank_shape, F32),
            pltpu.SemaphoreType.DMA((4, bank_shape[0])),
            pltpu.VMEM((128, rows), F32),
            pltpu.VMEM((2, count, width), BF16),
            pltpu.VMEM((2, count, width), BF16),
            pltpu.VMEM((2, count, width), BF16),
            pltpu.SemaphoreType.DMA((2,)),
            pltpu.SemaphoreType.DMA((2, 2, PIECES)),
        ]
    settings = dict(vmem_limit_bytes=VMEM_MOST)
    if paired:
        settings.update(collective_id=3, has_side_effects=True)
    return pl.pallas_call(
        functools.partial(attend_back_kernel, paired, line),
        out_shape=(shape((count, width), BF16), shape((count, width), F32)) + sum_shapes,
        in_specs=[held] * len(held_args) + [anywhere] * len(far_args),
        out_specs=(held, held) + (anywhere,) * len(sum_shapes),
        scratch_shapes=[
            pltpu.VMEM((count, width), BF16),
            pltpu.VMEM((count, width), BF16),
            pltpu.VMEM(heads_in.shape, BF16),
            pltpu.VMEM((line, count, width), BF16),
            pltpu.VMEM((count, width), F32),
            pltpu.VMEM((count, HEADS * HEAD_DIM), BF16),
            pltpu.VMEM((pairs, count, 4 * PAIR), BF16),
            pltpu.VMEM((128, width), F32),
            pltpu.VMEM((units, 2, 2, 2, block_rows, UNIT), BF16),
            pltpu.VMEM((1, 2, 2, 2, block_rows, 128), BF16),
            pltpu.SemaphoreType.DMA((5 + line,)),
            *exchange,
        ],
        compiler_params=pltpu.CompilerParams(**settings),
        cost_estimate=pl.CostEstimate(flops=2**34, bytes_accessed=2**25, transcendentals=2**21),
    )(*held_args, *far_args)


def unit_columns(sums):
    pairs = KV_HEADS // 2
    parts = sums[2 : 2 + pairs]
    rows = sums.shape[1]

    def side_by_side(value):
        return jnp.transpose(value, (1, 0, 2)).reshape(rows, -1)

    return (
        jnp.concatenate(
            [
                side_by_side(parts[:, :, : 2 * PAIR]),
                side_by_side(parts[:, :, 2 * PAIR : 3 * PAIR]),
                side_by_side(parts[:, :, 3 * PAIR :]),
            ],
            axis=1,
        ),
        side_by_side(sums[:2]),
    )


def update_kernel(width, experts, bank_sum, head_sum, small_rows, *refs):
    lanes = refs[0].shape[2]
    gradients = (
        bank_sum[0, :, :lanes],
        bank_sum[0, :, lanes:],
        head_sum[:, :width],
        head_sum[:, width:],
        small_rows[:experts],
        small_rows[experts : experts + 2],
    )
    count = len(gradients)
    for number, gradient in enumerate(gradients):
        held = refs[3 * number : 3 * number + 3]
        results = refs[3 * (count + number) : 3 * (count + number) + 3]
        at = (0,) if held[0].ndim == 3 else (Ellipsis,)
        values = update(gradient, *(ref[at] for ref in held))
        for ref, value in zip(results, values):
            ref[at] = value


def update_all(bank_sum, head_sum, small_rows, states):
    experts, block_rows, _ = bank_sum.shape
    half = block_rows // 2
    rows = head_sum.shape[0] // experts

    def spec(value):
        if value.ndim == 3:
            return pl.BlockSpec((1, half, value.shape[2]), lambda i: (i // 2, i % 2, 0))
        if value.shape[0] == head_sum.shape[0] and value.shape[1] > 128:
            return pl.BlockSpec((rows, value.shape[1]), lambda i: (i // 2, 0))
        return pl.BlockSpec(value.shape, lambda i: (0, 0))

    flat = [value for state in states for value in state]
    results = pl.pallas_call(
        functools.partial(update_kernel, states[2][0].shape[1], states[4][0].shape[0]),
        grid=(2 * experts,),
        out_shape=tuple(jax.ShapeDtypeStruct(value.shape, F32) for value in flat),
        in_specs=[spec(value) for value in (bank_sum, head_sum, small_rows, *flat)],
        out_specs=tuple(spec(value) for value in flat),
        compiler_params=pltpu.CompilerParams(vmem_limit_bytes=VMEM_MOST),
        cost_estimate=pl.CostEstimate(flops=2**23, bytes_accessed=25 * 2**20, transcendentals=0),
    )(bank_sum, head_sum, small_rows, *flat)
    return [tuple(results[i : i + 3]) for i in range(0, len(flat), 3)]


def body(
    tokens,
    cotangent,
    routes,
    cont_ids,
    norm_gains,
    gains_moment,
    gains_average,
    heads_in,
    heads_in_master,
    heads_in_moment,
    heads_in_average,
    heads_out,
    heads_out_master,
    heads_out_moment,
    heads_out_average,
    router,
    router_master,
    router_moment,
    router_average,
    expert_in,
    expert_in_master,
    expert_in_moment,
    expert_in_average,
    expert_out,
    expert_out_master,
    expert_out_moment,
    expert_out_average,
):
    token_count, model_width = tokens.shape
    local_experts = expert_in.shape[0]
    peer_count = lax.axis_size("expert")
    experts = local_experts * peer_count
    paired = lax.axis_size("dp") == 8 and peer_count == 4
    positions, allowed = layout(cont_ids[0], token_count - cont_ids.shape[1])
    tables = (*rope_tables(positions), jnp.where(allowed, 0.0, -1e30))
    gain_rows = norm_gains.T
    router_rows = router.T
    (
        first_in,
        queries,
        key_rows,
        value_rows,
        attended,
        hidden,
        second_in,
        gates,
        log_totals,
        cots_all,
        mix_all,
        mix_late,
        grad_part,
        gate_grads,
        gated,
        grad_gate_up,
        rows_all,
    ) = front(
        paired,
        tokens,
        cotangent,
        gain_rows,
        heads_in,
        heads_out,
        router_rows,
        routes.T,
        tables,
        expert_in,
        expert_out,
        peer_count,
        token_count - cont_ids.shape[1],
    )
    back_rows = lax.psum_scatter(
        grad_part.reshape(peer_count * token_count, model_width),
        "expert",
        scatter_dimension=0,
        tiled=True,
    )
    grad_sources = (
        rows_all.reshape(peer_count * token_count, model_width),
        cots_all.reshape(peer_count * token_count, model_width),
        gated.reshape(peer_count * token_count, -1),
        grad_gate_up.reshape(peer_count * token_count, -1),
    )
    if paired:
        expert_sums = (bank_grads(*grad_sources, local_experts),)
    else:
        expert_sums = tuple(
            lax.psum_scatter(part, "dp", scatter_dimension=1, tiled=True).astype(jnp.float32)
            for part in weight_grads(*grad_sources, local_experts)
        )
    output, token_grad, unit_sums, small_sum, *bank_sums = attend_back(
        (
            back_rows,
            hidden,
            cotangent,
            second_in,
            gates,
            gate_grads[:, :local_experts].reshape(experts, token_count),
            router_rows,
            gain_rows,
            heads_out,
            queries,
            key_rows,
            value_rows,
            attended,
            log_totals,
            *tables,
        ),
        (tokens, first_in, heads_in, mix_all, mix_late, *(expert_sums if paired else ())),
        paired,
        peer_count,
    )
    shard_rows = model_width // lax.axis_size(("dp", "expert"))
    gains_share = lax.dynamic_slice_in_dim(
        gain_rows, lax.axis_index(("dp", "expert")) * shard_rows, shard_rows, 1
    )
    states = (
        (expert_in_master, expert_in_moment, expert_in_average),
        (expert_out_master, expert_out_moment, expert_out_average),
        (heads_in_master, heads_in_moment, heads_in_average),
        (heads_out_master, heads_out_moment, heads_out_average),
        (router_master.T, router_moment.T, router_average.T),
        (gains_share, gains_moment.T, gains_average.T),
    )
    if paired:
        news = update_all(bank_sums[0], unit_sums, small_sum, states)
    else:
        head_parts = unit_columns(unit_sums.reshape(unit_sums.shape[0], model_width, UNIT))
        packed = jnp.concatenate([*head_parts, small_sum.reshape(model_width, 128)], axis=1)
        head_total = lax.psum_scatter(
            packed, ("dp", "expert"), scatter_dimension=0, tiled=True
        ).astype(jnp.float32)
        cut_in = head_parts[0].shape[1]
        cut_out = cut_in + head_parts[1].shape[1]
        small_rows = head_total[:, cut_out:].T
        sums = (
            *expert_sums,
            head_total[:, :cut_in],
            head_total[:, cut_in:cut_out],
            small_rows[:experts],
            small_rows[experts : experts + 2],
        )
        news = [update(gradient, *state) for gradient, state in zip(sums, states)]
    upper_new, lower_new, inproj_new, outproj_new, router_new, gains_new = news
    router_new = tuple(value.T for value in router_new)
    gains_new = tuple(value.T for value in gains_new)
    return (
        output,
        token_grad,
        gains_new[0],
        gains_new[1],
        gains_new[2],
        inproj_new[0],
        inproj_new[1],
        inproj_new[2],
        outproj_new[0],
        outproj_new[1],
        outproj_new[2],
        router_new[0],
        router_new[1],
        router_new[2],
        upper_new[0],
        upper_new[1],
        upper_new[2],
        lower_new[0],
        lower_new[1],
        lower_new[2],
    )


def solution(mesh):
    return jax.shard_map(
        body,
        mesh=mesh,
        in_specs=(
            P(("dp", "expert"), None),
            P(("dp", "expert"), None),
            P(("dp", "expert"), None),
            P(("dp", "expert"), None),
            P(),
            P(("dp", "expert"), None),
            P(("dp", "expert"), None),
            P(),
            P(("dp", "expert"), None),
            P(("dp", "expert"), None),
            P(("dp", "expert"), None),
            P(),
            P(("dp", "expert"), None),
            P(("dp", "expert"), None),
            P(("dp", "expert"), None),
            P(),
            P(("dp", "expert"), None),
            P(("dp", "expert"), None),
            P(("dp", "expert"), None),
            P("expert", None, None),
            P("expert", "dp", None),
            P("expert", "dp", None),
            P("expert", "dp", None),
            P("expert", None, None),
            P("expert", "dp", None),
            P("expert", "dp", None),
            P("expert", "dp", None),
        ),
        out_specs=(
            P(("dp", "expert"), None),
            P(("dp", "expert"), None),
            P(("dp", "expert"), None),
            P(("dp", "expert"), None),
            P(("dp", "expert"), None),
            P(("dp", "expert"), None),
            P(("dp", "expert"), None),
            P(("dp", "expert"), None),
            P(("dp", "expert"), None),
            P(("dp", "expert"), None),
            P(("dp", "expert"), None),
            P(("dp", "expert"), None),
            P(("dp", "expert"), None),
            P(("dp", "expert"), None),
            P("expert", "dp", None),
            P("expert", "dp", None),
            P("expert", "dp", None),
            P("expert", "dp", None),
            P("expert", "dp", None),
            P("expert", "dp", None),
        ),
        check_vma=False,
    )
```

```python
import functools

import jax
import jax.numpy as jnp
import numpy as np
from jax import lax
from jax.experimental import pallas as pl
from jax.experimental.pallas import tpu as pltpu
from jax.sharding import PartitionSpec as P

HEADS = 16
KV_HEADS = 8
HEAD_DIM = 64


EPS = 1e-06
SCALE = 0.015625
THETA = 10000.0
MOMENTUM = 0.9
DECAY = 0.8
RATE = 0.001
HIGHEST = lax.Precision.HIGHEST


def update(gradient, master, moment, average):
    moment_next = MOMENTUM * moment + gradient
    master_next = master - RATE * (gradient + MOMENTUM * moment_next)
    return (master_next, moment_next, DECAY * average + (1.0 - DECAY) * master_next)


F32 = jnp.float32
BF16 = jnp.bfloat16
MESH = pl.DeviceIdType.MESH
VMEM_MOST = 61 * 2**20


def contract(left, right, left_axis, right_axis):
    return lax.dot_general(
        left, right, (((left_axis,), (right_axis,)), ((), ())), preferred_element_type=F32
    )


def visit_order(line):
    return [sorted(range(line), key=lambda s: (abs(s - z), s)) for z in range(line)]


def line_gather(line, z, dp, source, landing, send_sem, recv_sem):
    def copy(origin, block, sem, target):
        return pltpu.make_async_remote_copy(
            src_ref=origin,
            dst_ref=landing.at[block],
            send_sem=send_sem.at[sem],
            recv_sem=recv_sem.at[block],
            device_id=(dp, target),
            device_id_type=MESH,
        )

    def start():
        @pl.when(z < line - 1)
        def _():
            copy(source, z, line, z + 1).start()

        @pl.when(z > 0)
        def _():
            copy(source, z, line + 1, z - 1).start()

    def pass_on(apart):
        low = jnp.maximum(z - apart, 0)
        high = jnp.minimum(z + apart, line - 1)

        @pl.when(z - apart >= 0)
        def _():
            copy(source, low, low, z).wait_recv()

            @pl.when(z < line - 1)
            def _():
                copy(landing.at[low], low, low, z + 1).start()

        @pl.when(z + apart < line)
        def _():
            copy(source, high, high, z).wait_recv()

            @pl.when(z > 0)
            def _():
                copy(landing.at[high], high, high, z - 1).start()

    def finish():
        @pl.when(z < line - 1)
        def _():
            copy(source, z, line, z + 1).wait_send()

        @pl.when(z > 0)
        def _():
            copy(source, z, line + 1, z - 1).wait_send()

        for s in range(line):

            @pl.when(((s < z) & (z < line - 1)) | ((s > z) & (z > 0)))
            def _(s=s):
                copy(source, s, s, z).wait_send()

    return start, pass_on, finish


def pass_steps(line, experts):
    steps = []
    for z in range(line):
        order = visit_order(line)[z]
        for apart in range(1, line):
            met = [k for k in range(line) if abs(order[k] - z) == apart]
            if not met:
                continue
            forwards = (z - apart >= 0 and z < line - 1) or (z + apart < line and z > 0)
            early = experts // 2 if forwards and apart > 1 else 0
            steps.append((z, met[0] * experts - early, apart))
    return steps


def pick(table, row, column):
    value = jnp.int32(table[0][0])
    for r in range(len(table)):
        for c in range(len(table[0])):
            value = jnp.where((row == r) & (column == c), jnp.int32(table[r][c]), value)
    return value


def weight_grads_kernel(rows, cots, gated, inner, up_grad, down_grad):
    step = 256
    for at in range(0, rows.shape[1], step):
        up_grad[0, at : at + step] = contract(rows[:, at : at + step], inner[...], 0, 0).astype(BF16)
        down_grad[0, at : at + step] = contract(cots[:, at : at + step], gated[...], 0, 0).astype(
            BF16
        )


def weight_grads(rows, cots, gated, inner, experts):
    tokens, width = rows.shape
    ff_width = gated.shape[1] // experts
    whole = pl.BlockSpec((tokens, width), lambda e: (0, 0))
    return pl.pallas_call(
        weight_grads_kernel,
        grid=(experts,),
        out_shape=(
            jax.ShapeDtypeStruct((experts, width, 2 * ff_width), BF16),
            jax.ShapeDtypeStruct((experts, width, ff_width), BF16),
        ),
        in_specs=[
            whole,
            whole,
            pl.BlockSpec((tokens, ff_width), lambda e: (0, e)),
            pl.BlockSpec((tokens, 2 * ff_width), lambda e: (0, e)),
        ],
        out_specs=(
            pl.BlockSpec((1, width, 2 * ff_width), lambda e: (e, 0, 0)),
            pl.BlockSpec((1, width, ff_width), lambda e: (e, 0, 0)),
        ),
        compiler_params=pltpu.CompilerParams(vmem_limit_bytes=VMEM_MOST),
        cost_estimate=pl.CostEstimate(
            flops=6 * tokens * width * experts * ff_width,
            bytes_accessed=2 * tokens * (2 * width + 3 * experts * ff_width)
            + 6 * experts * width * ff_width,
            transcendentals=0,
        ),
    )(rows, cots, gated, inner)


def bank_grads_kernel(
    rows_hbm,
    cots_hbm,
    gated_hbm,
    inner_hbm,
    sum_hbm,
    rows,
    cots,
    gated,
    inner,
    grads,
    core_sum,
    first_sum,
    load_sem,
    send_sem,
    recv_sem,
    out_sem,
):
    experts = grads.shape[0]
    ff_width = gated.shape[2]
    block_rows = grads.shape[4]
    dp = lax.axis_index("dp")
    z = lax.axis_index("expert")
    y, x, core = dp // 4, lax.rem(dp // 2, 2), lax.rem(dp, 2)
    core_peer, x_peer, y_peer = dp + 1 - 2 * core, dp + 2 - 4 * x, dp + 4 - 8 * y

    def loads(e, slot):
        return (
            pltpu.make_async_copy(
                gated_hbm.at[:, pl.ds(pl.multiple_of(e * ff_width, ff_width), ff_width)],
                gated.at[slot],
                load_sem.at[slot, 0],
            ),
            pltpu.make_async_copy(
                inner_hbm.at[:, pl.ds(pl.multiple_of(2 * e * ff_width, ff_width), 2 * ff_width)],
                inner.at[slot],
                load_sem.at[slot, 1],
            ),
        )

    row_load = pltpu.make_async_copy(rows_hbm, rows, load_sem.at[0, 2])
    cot_load = pltpu.make_async_copy(cots_hbm, cots, load_sem.at[1, 2])
    row_load.start()
    for copy in loads(0, 0):
        copy.start()
    cot_load.start()
    barrier = pltpu.get_barrier_semaphore()
    for peer in (core_peer, x_peer, y_peer):
        pl.semaphore_signal(barrier, inc=1, device_id=(peer, z), device_id_type=MESH)
    pl.semaphore_wait(barrier, 3)
    row_load.wait()
    cot_load.wait()

    def send(stage, e, source, target, peer):
        return pltpu.make_async_remote_copy(
            src_ref=source,
            dst_ref=target,
            send_sem=send_sem.at[stage, e],
            recv_sem=recv_sem.at[stage, e],
            device_id=(peer, z),
            device_id_type=MESH,
        )

    def core_send(e):
        return send(0, e, grads.at[e, :, :, 1 - core], core_sum.at[e], core_peer)

    def first_send(e, along_x):
        if along_x:
            return send(1, e, core_sum.at[e, :, 1 - x], first_sum.at[e], x_peer)
        return send(1, e, core_sum.at[e, 1 - y], first_sum.at[e], y_peer)

    def by_parity(e, act):
        even = lax.rem(e, 2) == 0

        @pl.when(even)
        def _():
            act(True)

        @pl.when(jnp.logical_not(even))
        def _():
            act(False)

    def after_core(e):
        core_send(e).wait_recv()
        for yy in range(2):
            for xx in range(2):
                core_sum[e, yy, xx] = (
                    grads[e, yy, xx, core].astype(F32) + core_sum[e, yy, xx].astype(F32)
                ).astype(BF16)
        by_parity(e, lambda even: first_send(e, even).start())

    def after_first(e):
        def act(even):
            first_send(e, even).wait_recv()
            for other in range(2):
                kept = core_sum[e, other, x] if even else core_sum[e, y, other]
                first_sum[e, other] = (
                    kept.astype(F32) + first_sum[e, other].astype(F32)
                ).astype(BF16)

        by_parity(e, act)
        pltpu.make_async_copy(first_sum.at[e], sum_hbm.at[e], out_sem.at[e]).start()

    def step(e, _):
        slot = lax.rem(e, 2)
        for copy in loads(e, slot):
            copy.wait()

        @pl.when(e + 1 < experts)
        def _():
            for copy in loads(e + 1, 1 - slot):
                copy.start()

        def tile(at, _):
            columns = pl.ds(pl.multiple_of(at * 2 * block_rows, 2 * block_rows), 2 * block_rows)
            up_grad = contract(rows[:, columns], inner[slot], 0, 0).astype(BF16)
            down_grad = contract(cots[:, columns], gated[slot], 0, 0).astype(BF16)
            for side in range(2):
                part = slice(side * block_rows, (side + 1) * block_rows)
                grads[e, at // 2, lax.rem(at, 2), side, :, : 2 * ff_width] = up_grad[part]
                grads[e, at // 2, lax.rem(at, 2), side, :, 2 * ff_width :] = down_grad[part]
            return 0

        lax.fori_loop(0, 4, tile, 0)
        core_send(e).start()

        @pl.when(e >= 1)
        def _():
            after_core(e - 1)

        @pl.when(e >= 3)
        def _():
            after_first(e - 3)

        return 0

    lax.fori_loop(0, experts, step, 0)
    after_core(experts - 1)

    for e in range(max(experts - 3, 0), experts):
        after_first(e)
    for e in range(experts):
        core_send(e).wait_send()
        first_send(e, e % 2 == 0).wait_send()
        pltpu.make_async_copy(first_sum.at[e], sum_hbm.at[e], out_sem.at[e]).wait()


def bank_grads(rows, cots, gated, inner, experts):
    tokens, width = rows.shape
    ff_width = gated.shape[1] // experts
    lanes = 3 * ff_width
    block_rows = width // 8
    anywhere = pl.BlockSpec(memory_space=pl.ANY)
    return pl.pallas_call(
        bank_grads_kernel,
        out_shape=jax.ShapeDtypeStruct((experts, 2, block_rows, lanes), BF16),
        in_specs=[anywhere] * 4,
        out_specs=anywhere,
        scratch_shapes=[
            pltpu.VMEM((tokens, width), BF16),
            pltpu.VMEM((tokens, width), BF16),
            pltpu.VMEM((2, tokens, ff_width), BF16),
            pltpu.VMEM((2, tokens, 2 * ff_width), BF16),
            pltpu.VMEM((experts, 2, 2, 2, block_rows, lanes), BF16),
            pltpu.VMEM((experts, 2, 2, block_rows, lanes), BF16),
            pltpu.VMEM((experts, 2, block_rows, lanes), BF16),
            pltpu.SemaphoreType.DMA((2, 3)),
            pltpu.SemaphoreType.DMA((2, experts)),
            pltpu.SemaphoreType.DMA((2, experts)),
            pltpu.SemaphoreType.DMA((experts,)),
        ],
        compiler_params=pltpu.CompilerParams(
            collective_id=2, has_side_effects=True, vmem_limit_bytes=VMEM_MOST
        ),
        cost_estimate=pl.CostEstimate(
            flops=6 * tokens * width * experts * ff_width,
            bytes_accessed=2**27,
            transcendentals=0,
        ),
    )(rows, cots, gated, inner)


PAIR = 2 * HEAD_DIM
UNIT = 512
PIECES = 3


def swap_halves(value):
    lane = lax.broadcasted_iota(jnp.int32, value.shape, 1)
    half = HEAD_DIM // 2
    return jnp.where(
        lax.rem(lane, HEAD_DIM) < half,
        pltpu.roll(value, value.shape[1] - half, 1),
        pltpu.roll(value, half, 1),
    )


def sides(pair, side, scale):
    value = pair.astype(F32)
    if scale is not None:
        value = value * scale
    turned = pltpu.roll(value, HEAD_DIM, 1)
    lane = lax.broadcasted_iota(jnp.int32, value.shape, 1)
    left, right = (value, turned) if side == 0 else (turned, value)
    return (
        jnp.where(lane < HEAD_DIM, left, 0.0).astype(BF16),
        jnp.where(lane < HEAD_DIM, 0.0, right).astype(BF16),
    )


def lanes_at(start, size):
    return pl.ds(pl.multiple_of(start, 128), size)


def front_kernel(
    line,
    prompt,
    late,
    tokens,
    cots_hbm,
    gain_rows,
    heads_in_hbm,
    heads_out_hbm,
    router_rows,
    route_rows,
    label_row,
    frequencies,
    up_hbm,
    down_hbm,
    first_in_hbm,
    queries_hbm,
    keys_hbm,
    values_hbm,
    attended_hbm,
    hidden_hbm,
    second_in_hbm,
    gate_rows,
    log_totals,
    cosine_hbm,
    sine_hbm,
    bias_hbm,
    cots_all,
    mix_all,
    mix_late,
    back_hbm,
    gate_grads_hbm,
    gated_hbm,
    inner_hbm,
    rows_all_hbm,
    cots,
    rows,
    gates_own,
    gates,
    gate_grads,
    gate_grads_sent,
    up,
    down,
    projected,
    stage,
    mix_stage,
    gated,
    inner,
    columns,
    cot_send,
    cot_recv,
    row_send,
    row_recv,
    gate_send,
    gate_recv,
    weight_sem,
    local_sem,
    out_sem,
    grad_send,
    grad_recv,
    mix_send,
    mix_recv,
    heads_in,
    heads_out,
    first_in,
    queries,
    keys,
    values,
    attended,
    hidden,
    second_in,
    cosine,
    sine,
    bias,
    held_sem,
):
    dp = lax.axis_index("dp")
    z = lax.axis_index("expert")
    experts, _, ff_width = down_hbm.shape
    start_cots, pass_cots, finish_cots = line_gather(
        line, z, dp, cots_hbm, cots_all, cot_send, cot_recv
    )
    start_rows, pass_rows, finish_rows = line_gather(
        line, z, dp, second_in, rows, row_send, row_recv
    )

    heads_in_load = pltpu.make_async_copy(heads_in_hbm, heads_in, held_sem.at[0])
    heads_out_load = pltpu.make_async_copy(heads_out_hbm, heads_out, held_sem.at[1])
    held_out = [
        pltpu.make_async_copy(source, target, held_sem.at[2 + number])
        for number, (source, target) in enumerate(
            (
                (first_in, first_in_hbm),
                (queries, queries_hbm),
                (keys, keys_hbm),
                (values, values_hbm),
                (attended, attended_hbm),
                (hidden, hidden_hbm),
                (second_in, second_in_hbm),
                (cosine, cosine_hbm),
                (sine, sine_hbm),
                (bias, bias_hbm),
            )
        )
    ]

    def weight_copies(e):
        return (
            pltpu.make_async_copy(
                up_hbm.at[e],
                up.at[:, pl.ds(pl.multiple_of(e * 2 * ff_width, ff_width), 2 * ff_width)],
                weight_sem.at[0, e],
            ),
            pltpu.make_async_copy(
                down_hbm.at[e],
                down.at[:, pl.ds(pl.multiple_of(e * ff_width, ff_width), ff_width)],
                weight_sem.at[1, e],
            ),
        )

    barrier = pltpu.get_barrier_semaphore()
    for step in range(1, line):
        pl.semaphore_signal(
            barrier, inc=1, device_id=(dp, lax.rem(z + step, line)), device_id_type=MESH
        )
    pl.semaphore_wait(barrier, line - 1)
    start_cots()
    cots_in = pltpu.make_async_copy(cots_hbm, cots, local_sem.at[2])
    cots_in.start()
    heads_in_load.start()
    heads_out_load.start()
    for e in range(experts):
        for copy in weight_copies(e):
            copy.start()

    query_end = HEADS * HEAD_DIM
    key_end = query_end + KV_HEADS * HEAD_DIM
    token_rows = tokens[...].astype(F32)
    factor = lax.rsqrt(jnp.mean(token_rows * token_rows, axis=1, keepdims=True) + EPS)
    first_in[...] = (token_rows * factor * gain_rows[0:1]).astype(BF16)
    log_totals[...] = jnp.zeros_like(log_totals)
    cots_in.wait()
    own_cots = pltpu.make_async_copy(cots, cots_all.at[z], local_sem.at[0])
    own_cots.start()

    labels = label_row[...].astype(F32)
    size = labels.shape[1]
    square = jnp.broadcast_to(labels, (size, size))
    upright = square.T
    earlier = jnp.sum(jnp.where(square < upright, 1.0, 0.0), axis=1, keepdims=True)
    place = lax.broadcasted_iota(jnp.int32, (token_rows.shape[0], 128), 0).astype(F32)
    shift = jnp.concatenate([jnp.zeros((prompt, 1), F32), earlier], axis=0)
    angles = (place - shift) * frequencies[...]
    lane = lax.broadcasted_iota(jnp.int32, angles.shape, 1)
    sines = jnp.sin(angles)
    cosine[...] = jnp.cos(angles)
    sine[...] = jnp.where(lax.rem(lane, HEAD_DIM) < HEAD_DIM // 2, -sines, sines)
    own_label = jnp.concatenate([jnp.full((prompt, 1), -1.0, F32), upright[:, :1]], axis=0)
    seen_label = jnp.concatenate([jnp.full((1, prompt), -1.0, F32), labels], axis=1)
    row = lax.broadcasted_iota(jnp.int32, bias.shape, 0)
    column = lax.broadcasted_iota(jnp.int32, bias.shape, 1)
    allowed = (column <= row) & ((column < prompt) | (own_label == seen_label))
    bias[...] = jnp.where(allowed, 0.0, -1e30)
    heads_in_load.wait()

    def project(i, _):
        at = lanes_at(i * UNIT, UNIT)
        projected[:, at] = contract(first_in[...], heads_in[:, at], 1, 0)
        return 0

    lax.fori_loop(0, heads_in.shape[1] // UNIT, project, 0)

    def pair(j, _):
        for side in range(2):
            at = lanes_at((2 * j + side) * PAIR, PAIR)
            wide = projected[:, at]
            queries[:, at] = (wide * cosine[...] + swap_halves(wide) * sine[...]).astype(BF16)
        wide = projected[:, lanes_at(query_end + j * PAIR, PAIR)]
        keys[:, lanes_at(j * PAIR, PAIR)] = (
            wide * cosine[...] + swap_halves(wide) * sine[...]
        ).astype(BF16)
        values[:, lanes_at(j * PAIR, PAIR)] = projected[
            :, lanes_at(key_end + j * PAIR, PAIR)
        ].astype(BF16)
        heads = [(side, member) for side in range(2) for member in range(2)]
        groups = [queries[:, lanes_at((2 * j + side) * PAIR, PAIR)] for side in range(2)]
        key_sides = [sides(keys[:, lanes_at(j * PAIR, PAIR)], side, SCALE) for side in range(2)]
        value_sides = [sides(values[:, lanes_at(j * PAIR, PAIR)], side, None) for side in range(2)]
        parts = ((0, prompt, prompt), (prompt, groups[0].shape[0], groups[0].shape[0]))

        def scores_of(side, member):
            return [
                contract(groups[side][begin:end], key_sides[side][member][:seen], 1, 1)
                + bias[begin:end, :seen]
                for begin, end, seen in parts
            ]

        lane = lax.broadcasted_iota(jnp.int32, log_totals.shape, 1)
        added = jnp.zeros(log_totals.shape, F32)
        sums = [0.0, 0.0]
        scores = scores_of(*heads[0])
        for number, (side, member) in enumerate(heads):
            following = scores_of(*heads[number + 1]) if number + 1 < len(heads) else None
            mixed = []
            totals = []
            for part, (_, _, seen) in zip(scores, parts):
                peak = jnp.max(part, axis=1, keepdims=True)
                powers = jnp.exp(part - peak)
                amount = jnp.sum(powers, axis=1, keepdims=True)
                weights = (powers * (1.0 / amount)).astype(BF16)
                totals.append(peak + jnp.log(amount))
                mixed.append(contract(weights, value_sides[side][member][:seen], 1, 0))
            sums[side] = sums[side] + jnp.concatenate(mixed, axis=0)
            added = jnp.where(lane == 4 * j + number, jnp.concatenate(totals, axis=0), added)
            scores = following
        log_totals[...] += added
        for side in range(2):
            attended[:, lanes_at((2 * j + side) * PAIR, PAIR)] = sums[side].astype(BF16)
        return 0

    lax.fori_loop(0, KV_HEADS // 2, pair, 0)
    heads_out_load.wait()
    hidden_rows = token_rows + contract(attended[...], heads_out[...], 1, 1)
    hidden[...] = hidden_rows
    factor = lax.rsqrt(jnp.mean(hidden_rows * hidden_rows, axis=1, keepdims=True) + EPS)
    second = (hidden_rows * factor * gain_rows[1:2]).astype(BF16)
    second_in[...] = second
    start_rows()
    for copy in held_out:
        copy.start()
    own_rows = pltpu.make_async_copy(second_in, rows.at[z], local_sem.at[1])
    own_rows.start()
    logits = contract(router_rows[...], second, 1, 1)
    expert = lax.broadcasted_iota(jnp.int32, logits.shape, 0)
    named = expert == route_rows[0:1]
    for k in range(1, route_rows.shape[0]):
        named = named | (expert == route_rows[k : k + 1])
    peak = jnp.max(jnp.where(named, logits, -1e30), axis=0, keepdims=True)
    powers = jnp.where(named, jnp.exp(jnp.where(named, logits, peak) - peak), 0.0)
    gate_values = powers / jnp.sum(powers, axis=0, keepdims=True)
    gate_rows[...] = gate_values
    gates_own[...] = jnp.zeros_like(gates_own)
    for peer in range(line):
        gates_own[peer, :experts] = gate_values[peer * experts : (peer + 1) * experts]
    gates[z] = gates_own[z]
    def gate_copy(step):
        peer = lax.rem(z + step, line)
        return pltpu.make_async_remote_copy(
            src_ref=gates_own.at[peer],
            dst_ref=gates.at[z],
            send_sem=gate_send.at[step],
            recv_sem=gate_recv.at[step],
            device_id=(dp, peer),
            device_id_type=MESH,
        )

    for step in range(1, line):
        gate_copy(step).start()
    own_rows.wait()
    own_cots.wait()
    pass_cots(1)
    for step in range(1, line):
        gate_copy(step).wait()

    order = visit_order(line)

    def out_copies(slot, block):
        return (
            pltpu.make_async_copy(stage.at[slot], back_hbm.at[block], out_sem.at[slot, 0]),
            pltpu.make_async_copy(gated.at[slot], gated_hbm.at[block], out_sem.at[slot, 1]),
            pltpu.make_async_copy(inner.at[slot], inner_hbm.at[block], out_sem.at[slot, 2]),
        )

    def mix_copy(block, source, target):
        return pltpu.make_async_remote_copy(
            src_ref=mix_stage.at[block],
            dst_ref=mix_all.at[source],
            send_sem=mix_send.at[block],
            recv_sem=mix_recv.at[source],
            device_id=(dp, target),
            device_id_type=MESH,
        )

    def own_mix():
        return pltpu.make_async_copy(mix_stage.at[z], mix_all.at[z], local_sem.at[3])

    def late_mix(side):
        return pltpu.make_async_copy(
            mix_stage.at[side * (line - 1)], mix_late.at[side], local_sem.at[4 + side]
        )

    def at_end(block):
        return (block == 0) | (block == line - 1)

    def grad_copy(block, step):
        return pltpu.make_async_remote_copy(
            src_ref=gate_grads_sent.at[block],
            dst_ref=gate_grads.at[z],
            send_sem=grad_send.at[block],
            recv_sem=grad_recv.at[z],
            device_id=(dp, block),
            device_id_type=MESH,
        )

    def visit(k, _):
        block = pick(order, z, k)
        slot = lax.rem(k, 2)
        @pl.when(k >= 2)
        def _():
            for copy in out_copies(slot, pick(order, z, jnp.maximum(k - 2, 0))):
                copy.wait()

        cot_load = pltpu.make_async_copy(cots_all.at[block], cots, local_sem.at[2])
        gate_columns = gates[block].T
        tile = min(ff_width, 256)
        def arrive(e):
            step = k * experts + e
            apart = jnp.int32(0)
            for at_z, at_step, distance in pass_steps(line, experts):
                apart = jnp.where((z == at_z) & (step == at_step), distance, apart)

            @pl.when(apart > 0)
            def _():
                pass_rows(apart)

            if line > 2:

                @pl.when(apart == 1)
                def _():
                    pass_cots(2)

            @pl.when(apart > 2)
            def _():
                pass_cots(apart)

            @pl.when((k > 0) & (e == 0))
            def _():
                cot_load.start()
                cot_load.wait()

        def products(e, at):
            gate_at = pl.multiple_of(2 * e * ff_width + at, tile)
            up_at = pl.multiple_of((2 * e + 1) * ff_width + at, tile)
            down_at = pl.multiple_of(e * ff_width + at, tile)
            return (
                contract(rows[block], up[:, pl.ds(gate_at, tile)], 1, 0),
                contract(rows[block], up[:, pl.ds(up_at, tile)], 1, 0),
                contract(cots[...], down[:, pl.ds(down_at, tile)], 1, 0),
            )

        narrow_lane = lax.broadcasted_iota(jnp.int32, gate_columns.shape, 1)
        wide_lane = lax.broadcasted_iota(jnp.int32, columns.shape, 1)
        several = experts // 2
        columns[...] = jnp.zeros_like(columns)

        def half(part, _):
            begin = part * several
            arrive(begin)

            @pl.when(k == 0)
            def _():
                for e in range(several):
                    for copy in weight_copies(begin + e):
                        copy.wait()

            tiles = [(e, at) for e in range(several) for at in range(0, ff_width, tile)]
            ready = products(begin + tiles[0][0], tiles[0][1])
            sums = [0.0] * several
            for number, (near, at) in enumerate(tiles):
                following = None
                if number + 1 < len(tiles):
                    following = products(begin + tiles[number + 1][0], tiles[number + 1][1])
                e = begin + near
                gate_part, up_part, returned = ready
                gate_col = jnp.sum(
                    jnp.where(narrow_lane == e, gate_columns, 0.0), axis=1, keepdims=True
                )
                sigmoid_gate = jax.nn.sigmoid(gate_part)
                silu_gate = gate_part * sigmoid_gate
                active = silu_gate * up_part
                sums[near] = sums[near] + jnp.sum(active * returned, axis=1, keepdims=True)
                scaled = returned * gate_col
                grad_gate = scaled * up_part * (sigmoid_gate + silu_gate * (1.0 - sigmoid_gate))
                gate_at = pl.multiple_of(2 * e * ff_width + at, tile)
                up_at = pl.multiple_of((2 * e + 1) * ff_width + at, tile)
                down_at = pl.multiple_of(e * ff_width + at, tile)
                gated[slot, :, pl.ds(down_at, tile)] = (active * gate_col).astype(BF16)
                inner[slot, :, pl.ds(gate_at, tile)] = grad_gate.astype(BF16)
                inner[slot, :, pl.ds(up_at, tile)] = (scaled * silu_gate).astype(BF16)
                ready = following
            value = columns[...]
            for near in range(several):
                value = jnp.where(wide_lane == begin + near, sums[near], value)
            columns[...] = value
            return 0

        lax.fori_loop(0, 2, half, 0)
        mix_stage[block] = contract(gated[slot], down[...], 1, 1).astype(BF16)

        @pl.when(block == z)
        def _():
            own_mix().start()

        if late:
            for side in range(2):

                @pl.when((block != z) & (block == side * (line - 1)))
                def _(side=side):
                    late_mix(side).start()

            @pl.when((block != z) & jnp.logical_not(at_end(block)))
            def _():
                mix_copy(block, z, block).start()

        else:

            @pl.when(block != z)
            def _():
                mix_copy(block, z, block).start()

        stage[slot] = contract(inner[slot], up[...], 1, 1).astype(BF16)
        for copy in out_copies(slot, block):
            copy.start()
        gate_grads_sent[block] = columns[...].T[: gate_grads.shape[1]]

        @pl.when(block == z)
        def _():
            gate_grads[z] = gate_grads_sent[z]

        @pl.when(block != z)
        def _():
            grad_copy(block, 0).start()

        return 0

    lax.fori_loop(0, line, visit, 0)
    for k in range(max(line - 2, 0), line):
        for copy in out_copies(k % 2, pick(order, z, k)):
            copy.wait()

    finish_rows()
    finish_cots()
    for copy in held_out:
        copy.wait()
    own_mix().wait()
    if late:
        for side in range(2):

            @pl.when(z != side * (line - 1))
            def _(side=side):
                late_mix(side).wait()

    for s in range(line):
        send_ends = late and s in (0, line - 1)

        @pl.when(z != s)
        def _(s=s, send_ends=send_ends):
            if not send_ends:
                mix_copy(s, s, z).wait_send()
            if late:

                @pl.when(jnp.logical_not(at_end(z)))
                def _():
                    mix_copy(s, s, z).wait_recv()

            else:
                mix_copy(s, s, z).wait_recv()

    for s in range(line):

        @pl.when(s != z)
        def _(s=s):
            grad_copy(s, 0).wait_send()
            pltpu.make_async_remote_copy(
                src_ref=gate_grads_sent.at[s],
                dst_ref=gate_grads.at[s],
                send_sem=grad_send.at[s],
                recv_sem=grad_recv.at[s],
                device_id=(dp, z),
                device_id_type=MESH,
            ).wait_recv()

    last = (
        pltpu.make_async_copy(rows, rows_all_hbm, local_sem.at[0]),
        pltpu.make_async_copy(gate_grads, gate_grads_hbm, local_sem.at[1]),
    )
    for copy in last:
        copy.start()
    for copy in last:
        copy.wait()


def front(
    late,
    tokens,
    cots,
    gain_rows,
    heads_in,
    heads_out,
    router_rows,
    route_rows,
    label_row,
    frequencies,
    up,
    down,
    line,
    prompt,
):
    count, width = tokens.shape
    named = router_rows.shape[0]
    experts, _, ff_width = down.shape
    kv_width = KV_HEADS * HEAD_DIM
    shape = jax.ShapeDtypeStruct
    padded = experts + -experts % 8
    held = pl.BlockSpec(memory_space=pltpu.VMEM)
    anywhere = pl.BlockSpec(memory_space=pl.ANY)
    small = pltpu.VMEM((line, padded, count), F32)
    return pl.pallas_call(
        functools.partial(front_kernel, line, prompt, late),
        out_shape=(
            shape((count, width), BF16),
            shape((count, HEADS * HEAD_DIM), BF16),
            shape((count, kv_width), BF16),
            shape((count, kv_width), BF16),
            shape((count, HEADS * HEAD_DIM), BF16),
            shape((count, width), F32),
            shape((count, width), BF16),
            shape((named, count), F32),
            shape((count, 128), F32),
            shape((count, 128), F32),
            shape((count, 128), F32),
            shape((count, count), F32),
            shape((line, count, width), BF16),
            shape((line, count, width), BF16),
            shape((2, count, width), BF16),
            shape((line, count, width), BF16),
            shape((line, padded, count), F32),
            shape((line, count, experts * ff_width), BF16),
            shape((line, count, experts * 2 * ff_width), BF16),
            shape((line, count, width), BF16),
        ),
        in_specs=[held, anywhere, held, anywhere, anywhere] + [held] * 4 + [anywhere] * 2,
        out_specs=(anywhere,) * 7 + (held,) * 2 + (anywhere,) * 11,
        scratch_shapes=[
            pltpu.VMEM((count, width), BF16),
            pltpu.VMEM((line, count, width), BF16),
            small,
            small,
            small,
            small,
            pltpu.VMEM((width, experts * 2 * ff_width), BF16),
            pltpu.VMEM((width, experts * ff_width), BF16),
            pltpu.VMEM((count, heads_in.shape[1]), F32),
            pltpu.VMEM((2, count, width), BF16),
            pltpu.VMEM((line, count, width), BF16),
            pltpu.VMEM((2, count, experts * ff_width), BF16),
            pltpu.VMEM((2, count, experts * 2 * ff_width), BF16),
            pltpu.VMEM((count, 128), F32),
            pltpu.SemaphoreType.DMA((line + 2,)),
            pltpu.SemaphoreType.DMA((line,)),
            pltpu.SemaphoreType.DMA((line + 2,)),
            pltpu.SemaphoreType.DMA((line,)),
            pltpu.SemaphoreType.DMA((line,)),
            pltpu.SemaphoreType.DMA((line,)),
            pltpu.SemaphoreType.DMA((2, experts)),
            pltpu.SemaphoreType.DMA((6,)),
            pltpu.SemaphoreType.DMA((2, 3)),
            pltpu.SemaphoreType.DMA((line,)),
            pltpu.SemaphoreType.DMA((line,)),
            pltpu.SemaphoreType.DMA((line,)),
            pltpu.SemaphoreType.DMA((line,)),
            pltpu.VMEM(heads_in.shape, BF16),
            pltpu.VMEM(heads_out.shape, BF16),
            pltpu.VMEM((count, width), BF16),
            pltpu.VMEM((count, HEADS * HEAD_DIM), BF16),
            pltpu.VMEM((count, kv_width), BF16),
            pltpu.VMEM((count, kv_width), BF16),
            pltpu.VMEM((count, HEADS * HEAD_DIM), BF16),
            pltpu.VMEM((count, width), F32),
            pltpu.VMEM((count, width), BF16),
            pltpu.VMEM((count, 128), F32),
            pltpu.VMEM((count, 128), F32),
            pltpu.VMEM((count, count), F32),
            pltpu.SemaphoreType.DMA((12,)),
        ],
        compiler_params=pltpu.CompilerParams(
            collective_id=4, has_side_effects=True, vmem_limit_bytes=VMEM_MOST
        ),
        cost_estimate=pl.CostEstimate(flops=2**35, bytes_accessed=2**26, transcendentals=2**22),
    )(
        tokens,
        cots,
        gain_rows,
        heads_in,
        heads_out,
        router_rows,
        route_rows,
        label_row,
        frequencies,
        up,
        down,
    )


def attend_back_kernel(
    paired,
    line,
    back_rows,
    hidden,
    cots,
    second_in,
    gate_rows,
    gate_grads,
    router_rows,
    gain_rows,
    heads_out,
    queries,
    keys,
    values,
    attended,
    log_totals,
    cosine,
    sine,
    bias,
    tokens_hbm,
    first_hbm,
    in_hbm,
    mix_hbm,
    late_hbm,
    *others,
):
    bank_hbm, others = (others[0], others[1:]) if paired else (None, others)
    output, token_grad, sum_hbm, small_hbm, *others = others
    bank_sum_hbm, others = (others[0], others[1:]) if paired else (None, others)
    (
        tokens,
        first_in,
        heads_in,
        mixes,
        gate_grad_rows,
        grad_hidden,
        grad_attended,
        grad_projected,
        small_rows,
        own,
        own_small,
        *scratch,
    ) = others
    dp = lax.axis_index("dp")
    z = lax.axis_index("expert")
    units = own.shape[0]
    block_rows = own.shape[4]
    load_sem = scratch[0]
    loads = (
        pltpu.make_async_copy(first_hbm, first_in, load_sem.at[0]),
        pltpu.make_async_copy(tokens_hbm, tokens, load_sem.at[1]),
        pltpu.make_async_copy(in_hbm, heads_in, load_sem.at[2]),
    )
    for copy in loads:
        copy.start()

    def mix_load(b):
        return pltpu.make_async_copy(mix_hbm.at[b], mixes.at[b], load_sem.at[5 + b])

    def direct(b):
        ends = (z == 0) | (z == line - 1)
        return jnp.logical_not(ends) | (z == b) if paired else z == z

    for b in range(line):

        @pl.when(direct(b))
        def _(b=b):
            mix_load(b).start()

    if paired:
        (
            cores,
            firsts,
            lasts,
            sums,
            lines,
            totals,
            small_cores,
            small_firsts,
            small_lasts,
            small_sums,
            small_lines,
            small_totals,
            send_sem,
            recv_sem,
            line_send,
            line_recv,
            out_sem,
            bank_kept,
            bank_last,
            bank_total,
            bank_sem,
            small_columns,
            chain_own,
            chain_in,
            chain_out,
            chain_load_sem,
            chain_sem,
        ) = scratch[1:]
        rows = totals.shape[1]
        y, x, core = dp // 4, lax.rem(dp // 2, 2), lax.rem(dp, 2)
        core_peer, x_peer, y_peer = dp + 1 - 2 * core, dp + 2 - 4 * x, dp + 4 - 8 * y
        barrier = pltpu.get_barrier_semaphore()
        for peer in (core_peer, x_peer, y_peer):
            pl.semaphore_signal(barrier, inc=1, device_id=(peer, z), device_id_type=MESH)
        for step in range(1, line):
            pl.semaphore_signal(
                barrier, inc=1, device_id=(dp, lax.rem(z + step, line)), device_id_type=MESH
            )
        pl.semaphore_wait(barrier, 3 + line - 1)

        def bank_kept_copy(e):
            kept = y if e % 2 == 0 else x
            return pltpu.make_async_copy(
                bank_hbm.at[e, kept], bank_kept.at[e], bank_sem.at[0, e]
            )

        def bank_last_copy(e):
            sent, peer = (1 - y, y_peer) if e % 2 == 0 else (1 - x, x_peer)
            return pltpu.make_async_remote_copy(
                src_ref=bank_hbm.at[e, sent],
                dst_ref=bank_last.at[e],
                send_sem=bank_sem.at[1, e],
                recv_sem=bank_sem.at[2, e],
                device_id=(peer, z),
                device_id_type=MESH,
            )

        def bank_total_copy(e):
            return pltpu.make_async_copy(
                bank_total.at[e], bank_sum_hbm.at[e], bank_sem.at[3, e]
            )

        for e in range(bank_hbm.shape[0]):
            bank_kept_copy(e).start()
            bank_last_copy(e).start()

        piece = hidden.shape[0] // PIECES

        def part(p):
            return pl.ds(p * piece, piece)

        def chain_load(side):
            return pltpu.make_async_copy(
                late_hbm.at[side], chain_own.at[side], chain_load_sem.at[side]
            )

        def chain_send(side, p, source):
            return pltpu.make_async_remote_copy(
                src_ref=source.at[side, part(p)],
                dst_ref=chain_in.at[side, part(p)],
                send_sem=chain_sem.at[0, side, p],
                recv_sem=chain_sem.at[1, side, p],
                device_id=(dp, jnp.clip(z + 2 * side - 1, 0, line - 1)),
                device_id_type=MESH,
            )

        inside = (z > 0) & (z < line - 1)
        starts = (z == line - 1, z == 0)
        for side in range(2):

            @pl.when(inside)
            def _(side=side):
                chain_load(side).start()

            @pl.when(starts[side])
            def _(side=side):
                for p in range(PIECES):
                    chain_send(side, p, late_hbm).start()

        def relay(side, p):
            if p == 0:
                chain_load(side).wait()
            chain_send(side, p, chain_out).wait_recv()
            chain_out[side, part(p)] = (
                chain_own[side, part(p)].astype(F32) + chain_in[side, part(p)].astype(F32)
            ).astype(BF16)
            chain_send(side, p, chain_out).start()

        def relay_on(near, p):
            low_half = 2 * z < line - 1

            @pl.when(inside & low_half)
            def _():
                relay(1 if near else 0, p)

            @pl.when(inside & jnp.logical_not(low_half))
            def _():
                relay(0 if near else 1, p)

        buffers = (own, cores, firsts, lasts, sums, lines, totals)
        small_buffers = (
            own_small,
            small_cores,
            small_firsts,
            small_lasts,
            small_sums,
            small_lines,
            small_totals,
        )

        def send(stage, u, source, target, peer):
            return pltpu.make_async_remote_copy(
                src_ref=source,
                dst_ref=target,
                send_sem=send_sem.at[stage, u],
                recv_sem=recv_sem.at[stage, u],
                device_id=(peer, z),
                device_id_type=MESH,
            )

        class Sums:
            def __init__(self, held, shift):
                self.own, self.cores, self.firsts, self.lasts = held[:4]
                self.sums, self.lines, self.totals = held[4:]
                self.shift = shift

            def core_send(self, u):
                return send(
                    0,
                    u + self.shift,
                    self.own.at[u, :, :, 1 - core],
                    self.cores.at[u],
                    core_peer,
                )

            def first_send(self, u, along_x):
                if along_x:
                    source, peer = self.cores.at[u, :, 1 - x], x_peer
                else:
                    source, peer = self.cores.at[u, 1 - y], y_peer
                return send(1, u + self.shift, source, self.firsts.at[u], peer)

            def last_send(self, u, along_x):
                if along_x:
                    source, peer = self.firsts.at[u, 1 - x], x_peer
                else:
                    source, peer = self.firsts.at[u, 1 - y], y_peer
                return send(2, u + self.shift, source, self.lasts.at[u], peer)

            def line_copy(self, u, step):
                peer = lax.rem(z + step, line)
                return pltpu.make_async_remote_copy(
                    src_ref=self.sums.at[u, pl.ds(pl.multiple_of(peer * rows, rows), rows)],
                    dst_ref=self.lines.at[u, step],
                    send_sem=line_send.at[u + self.shift, step],
                    recv_sem=line_recv.at[u + self.shift, step],
                    device_id=(dp, peer),
                    device_id_type=MESH,
                )

            def by_parity(self, u, act):
                even = lax.rem(jnp.int32(u), 2) == 0

                @pl.when(even)
                def _():
                    act(True)

                @pl.when(jnp.logical_not(even))
                def _():
                    act(False)

            def after_core(self, u):
                self.core_send(u).wait_recv()
                for yy in range(2):
                    for xx in range(2):
                        self.cores[u, yy, xx] = (
                            self.own[u, yy, xx, core].astype(F32)
                            + self.cores[u, yy, xx].astype(F32)
                        ).astype(BF16)
                self.by_parity(u, lambda even: self.first_send(u, even).start())

            def after_first(self, u):
                def act(even):
                    self.first_send(u, even).wait_recv()
                    for other in range(2):
                        kept = self.cores[u, other, x] if even else self.cores[u, y, other]
                        self.firsts[u, other] = (
                            kept.astype(F32) + self.firsts[u, other].astype(F32)
                        ).astype(BF16)
                    self.last_send(u, not even).start()

                self.by_parity(u, act)

            def after_last(self, u):
                def act(even):
                    self.last_send(u, not even).wait_recv()
                    kept = self.firsts[u, y] if even else self.firsts[u, x]
                    self.sums[u] = (kept.astype(F32) + self.lasts[u].astype(F32)).astype(BF16)

                self.by_parity(u, act)
                for step in range(1, line):
                    self.line_copy(u, step).start()

            def after_line(self, u):
                value = self.sums[u, pl.ds(pl.multiple_of(z * rows, rows), rows)].astype(F32)
                for step in range(1, line):
                    self.line_copy(u, step).wait_recv()
                    value = value + self.lines[u, step].astype(F32)
                self.totals[u] = value

            def finish(self, u):
                self.core_send(u).wait_send()
                self.first_send(u, u % 2 == 0).wait_send()
                self.last_send(u, u % 2 == 1).wait_send()
                for step in range(1, line):
                    self.line_copy(u, step).wait_send()

        wide_sums = Sums(buffers, 0)
        small_sum = Sums(small_buffers, units)

    def keep(target, u, value):
        for block in range(8):
            target[u, block // 4, block // 2 % 2, block % 2] = value[
                block * block_rows : (block + 1) * block_rows
            ]

    gates = gate_rows[...]
    local = gates.shape[0] // line
    for b in range(line):
        gate_grad_rows[b * local : (b + 1) * local] = gate_grads[b, :local]
    gate_grad = gate_grad_rows[...]
    logit_grad = gates * (gate_grad - jnp.sum(gates * gate_grad, axis=0, keepdims=True))
    high = logit_grad.astype(BF16)
    low = (logit_grad - high.astype(F32)).astype(BF16)
    grad_second = (
        back_rows[...].astype(F32)
        + contract(high, router_rows[...], 0, 0)
        + contract(low, router_rows[...], 0, 0)
    )
    small_rows[...] = jnp.zeros_like(small_rows)
    experts = high.shape[0]
    small_rows[:experts] = contract(high, second_in[...], 1, 0) + contract(low, second_in[...], 1, 0)

    def norm_back(incoming, rows, gain):
        factor = lax.rsqrt(jnp.mean(rows * rows, axis=1, keepdims=True) + EPS)
        normed = rows * factor
        gain_grad = jnp.sum(incoming * normed, axis=0, keepdims=True)
        weighted = incoming * gain
        mean = jnp.mean(weighted * normed, axis=1, keepdims=True)
        return factor * (weighted - normed * mean), gain_grad

    norm_grad, gain_grad = norm_back(grad_second, hidden[...], gain_rows[1:2])
    small_rows[experts + 1 : experts + 2] = gain_grad
    grad_hidden[...] = cots[...].astype(F32) + norm_grad
    branch = grad_hidden[...].astype(BF16)
    for u in range(2):
        keep(
            own,
            u,
            contract(branch, attended[:, u * UNIT : (u + 1) * UNIT], 0, 0).astype(BF16),
        )
        if paired:
            wide_sums.core_send(u).start()
    grad_attended[...] = contract(branch, heads_out[...], 1, 0).astype(BF16)
    loads[0].wait()
    if paired:
        wide_sums.after_core(0)
        relay_on(True, 0)

    def pair(j, _):
        key_pair = keys[:, lanes_at(j * PAIR, PAIR)]
        value_pair = values[:, lanes_at(j * PAIR, PAIR)]
        key_grads = []
        value_grads = []
        for side in range(2):
            at = lanes_at((2 * j + side) * PAIR, PAIR)
            group = queries[:, at]
            group_grad = grad_attended[:, at]
            key_sides = sides(key_pair, side, SCALE)
            value_sides = sides(value_pair, side, None)
            product = group_grad.astype(F32) * attended[:, at].astype(F32)
            lane = lax.broadcasted_iota(jnp.int32, product.shape, 1)
            grad = jnp.zeros(group.shape, F32)
            key_grad = []
            value_grad = []
            for member in range(2):
                head = 4 * j + 2 * side + member
                log_total = jnp.sum(
                    jnp.where(lane == head, log_totals[...], 0.0), axis=1, keepdims=True
                )
                mine = (lane < HEAD_DIM) if member == 0 else (lane >= HEAD_DIM)
                spread = jnp.sum(jnp.where(mine, product, 0.0), axis=1, keepdims=True)
                scores = contract(group, key_sides[member], 1, 1) + bias[...]
                weights = jnp.exp(scores - log_total)
                weight_grads = contract(group_grad, value_sides[member], 1, 1)
                score_grads = (weights * (weight_grads - spread)).astype(BF16)
                grad = grad + contract(score_grads, key_sides[member], 1, 0)
                rows_of = slice(member * HEAD_DIM, (member + 1) * HEAD_DIM)
                key_grad.append(contract(group, score_grads, 0, 0)[rows_of])
                value_grad.append(contract(group_grad, weights.astype(BF16), 0, 0)[rows_of])
            grad_projected[j, :, side * PAIR : (side + 1) * PAIR] = (
                grad * cosine[...] - swap_halves(grad) * sine[...]
            ).astype(BF16)
            key_grads.append(key_grad[0] + key_grad[1])
            value_grads.append(value_grad[0] + value_grad[1])
        key_rows = jnp.concatenate(key_grads, axis=0).T * SCALE
        grad_projected[j, :, 2 * PAIR : 3 * PAIR] = (
            key_rows * cosine[...] - swap_halves(key_rows) * sine[...]
        ).astype(BF16)
        grad_projected[j, :, 3 * PAIR :] = jnp.concatenate(value_grads, axis=0).T.astype(BF16)
        keep(own, 2 + j, contract(first_in[...], grad_projected[j], 0, 0).astype(BF16))
        if paired:
            wide_sums.core_send(2 + j).start()
            wide_sums.after_core(1 + j)

            @pl.when(j >= 2)
            def _():
                wide_sums.after_first(j - 2)

            for at, near, p in ((0, True, 1), (1, True, 2), (2, False, 0), (3, False, 1)):

                @pl.when(j == at)
                def _(near=near, p=p):
                    relay_on(near, p)

        return 0

    pairs = KV_HEADS // 2
    lax.fori_loop(0, pairs, pair, 0)
    last = units - 1
    if paired:
        wide_sums.after_core(last)
        relay_on(False, 2)
        wide_sums.after_first(2)
        wide_sums.after_last(0)
    loads[1].wait()
    loads[2].wait()
    grad_first = jnp.zeros(grad_hidden.shape, F32)
    query_end = HEADS * HEAD_DIM
    key_end = query_end + KV_HEADS * HEAD_DIM
    for j in range(pairs):
        for at, begin, size in (
            (0, 2 * j * PAIR, 2 * PAIR),
            (2 * PAIR, query_end + j * PAIR, PAIR),
            (3 * PAIR, key_end + j * PAIR, PAIR),
        ):
            grad_first = grad_first + contract(
                grad_projected[j, :, at : at + size], heads_in[:, begin : begin + size], 1, 1
            )
    norm_grad, gain_grad = norm_back(grad_first, tokens[...].astype(F32), gain_rows[0:1])
    small_rows[experts : experts + 1] = gain_grad
    keep(own_small, 0, small_rows[...].T.astype(BF16))
    if paired:
        small_sum.core_send(0).start()
    token_grad[...] = grad_hidden[...] + norm_grad
    if paired:
        for e in range(bank_hbm.shape[0]):
            bank_kept_copy(e).wait()
            bank_last_copy(e).wait()
            bank_total[e] = bank_kept[e].astype(F32) + bank_last[e].astype(F32)
            bank_total_copy(e).start()

    @pl.when(direct(-1))
    def _():
        total = hidden[...]
        for b in range(line):
            mix_load(b).wait()
            total = total + mixes[b].astype(F32)
        output[...] = total.astype(BF16)

    if paired:
        small_sum.after_core(0)
        wide_sums.after_first(3)
        wide_sums.after_last(1)
        wide_sums.after_first(4)
        wide_sums.after_last(2)
        small_sum.after_first(0)
        wide_sums.after_first(5)
        wide_sums.after_last(3)
        small_sum.after_last(0)
        wide_sums.after_line(0)
        wide_sums.after_last(4)
        wide_sums.after_line(1)
        wide_sums.after_last(5)
        for u in range(2, units):
            wide_sums.after_line(u)
        small_sum.after_line(0)
        places = [(u, 0, UNIT, key_end + KV_HEADS * HEAD_DIM + u * UNIT) for u in range(2)]
        for j in range(pairs):
            places.append((2 + j, 0, 2 * PAIR, 2 * j * PAIR))
            places.append((2 + j, 2 * PAIR, PAIR, query_end + j * PAIR))
            places.append((2 + j, 3 * PAIR, PAIR, key_end + j * PAIR))
        small_columns[...] = small_totals[0].T
        gain_values = gain_rows[...]
        share = jnp.zeros((2, rows), F32)
        for i in range(gain_values.shape[1] // rows):
            share = jnp.where(
                dp * line + z == i, gain_values[:, i * rows : (i + 1) * rows], share
            )
        small_columns[experts + 2 : experts + 4] = share
        outs = [pltpu.make_async_copy(small_columns, small_hbm, out_sem.at[len(places)])]
        for number, (u, at, size, column) in enumerate(places):
            outs.append(
                pltpu.make_async_copy(
                    totals.at[u, :, at : at + size],
                    sum_hbm.at[:, column : column + size],
                    out_sem.at[number],
                )
            )
    else:
        outs = (
            pltpu.make_async_copy(own, sum_hbm, load_sem.at[3]),
            pltpu.make_async_copy(own_small, small_hbm, load_sem.at[4]),
        )
    for copy in outs:
        copy.start()
    if paired:
        for u in range(units):
            wide_sums.finish(u)
        small_sum.finish(0)
        for e in range(bank_hbm.shape[0]):
            bank_total_copy(e).wait()
        for side in range(2):

            @pl.when(starts[1 - side])
            def _(side=side):
                mix_load(z).wait()
                for p in range(PIECES):
                    chain_send(side, p, late_hbm).wait_recv()
                output[...] = (
                    hidden[...] + mixes[z].astype(F32) + chain_in[side].astype(F32)
                ).astype(BF16)

            @pl.when(jnp.logical_not(starts[1 - side]))
            def _(side=side):
                for p in range(PIECES):
                    chain_send(side, p, late_hbm).wait_send()

    for copy in outs:
        copy.wait()


def attend_back(held_args, far_args, paired, line):
    tokens, first_in, heads_in = far_args[:3]
    count, width = tokens.shape
    pairs = KV_HEADS // 2
    units = 2 + pairs
    block_rows = width // 8
    rows = block_rows // line
    shape = jax.ShapeDtypeStruct
    held = pl.BlockSpec(memory_space=pltpu.VMEM)
    anywhere = pl.BlockSpec(memory_space=pl.ANY)
    if paired:
        sum_shapes = (shape((rows, units * UNIT), F32), shape((128, rows), F32))
    else:
        sum_shapes = (
            shape((units, 2, 2, 2, block_rows, UNIT), BF16),
            shape((1, 2, 2, 2, block_rows, 128), BF16),
        )
    exchange = []
    if paired:
        for number, lanes in ((units, UNIT), (1, 128)):
            exchange += [
                pltpu.VMEM((number, 2, 2, block_rows, lanes), BF16),
                pltpu.VMEM((number, 2, block_rows, lanes), BF16),
                pltpu.VMEM((number, block_rows, lanes), BF16),
                pltpu.VMEM((number, block_rows, lanes), BF16),
                pltpu.VMEM((number, line, rows, lanes), BF16),
                pltpu.VMEM((number, rows, lanes), F32),
            ]
        exchange += [
            pltpu.SemaphoreType.DMA((3, units + 1)),
            pltpu.SemaphoreType.DMA((3, units + 1)),
            pltpu.SemaphoreType.DMA((units + 1, line)),
            pltpu.SemaphoreType.DMA((units + 1, line)),
            pltpu.SemaphoreType.DMA((3 + 3 * pairs,)),
        ]
        bank_shape = (far_args[5].shape[0],) + far_args[5].shape[2:]
        sum_shapes += (shape(bank_shape, F32),)
        exchange += [
            pltpu.VMEM(bank_shape, BF16),
            pltpu.VMEM(bank_shape, BF16),
            pltpu.VMEM(bank_shape, F32),
            pltpu.SemaphoreType.DMA((4, bank_shape[0])),
            pltpu.VMEM((128, rows), F32),
            pltpu.VMEM((2, count, width), BF16),
            pltpu.VMEM((2, count, width), BF16),
            pltpu.VMEM((2, count, width), BF16),
            pltpu.SemaphoreType.DMA((2,)),
            pltpu.SemaphoreType.DMA((2, 2, PIECES)),
        ]
    settings = dict(vmem_limit_bytes=VMEM_MOST)
    if paired:
        settings.update(collective_id=3, has_side_effects=True)
    return pl.pallas_call(
        functools.partial(attend_back_kernel, paired, line),
        out_shape=(shape((count, width), BF16), shape((count, width), F32)) + sum_shapes,
        in_specs=[held] * len(held_args) + [anywhere] * len(far_args),
        out_specs=(held, held) + (anywhere,) * len(sum_shapes),
        scratch_shapes=[
            pltpu.VMEM((count, width), BF16),
            pltpu.VMEM((count, width), BF16),
            pltpu.VMEM(heads_in.shape, BF16),
            pltpu.VMEM((line, count, width), BF16),
            pltpu.VMEM(held_args[4].shape, F32),
            pltpu.VMEM((count, width), F32),
            pltpu.VMEM((count, HEADS * HEAD_DIM), BF16),
            pltpu.VMEM((pairs, count, 4 * PAIR), BF16),
            pltpu.VMEM((128, width), F32),
            pltpu.VMEM((units, 2, 2, 2, block_rows, UNIT), BF16),
            pltpu.VMEM((1, 2, 2, 2, block_rows, 128), BF16),
            pltpu.SemaphoreType.DMA((5 + line,)),
            *exchange,
        ],
        compiler_params=pltpu.CompilerParams(**settings),
        cost_estimate=pl.CostEstimate(flops=2**34, bytes_accessed=2**25, transcendentals=2**21),
    )(*held_args, *far_args)


def unit_columns(sums):
    pairs = KV_HEADS // 2
    parts = sums[2 : 2 + pairs]
    rows = sums.shape[1]

    def side_by_side(value):
        return jnp.transpose(value, (1, 0, 2)).reshape(rows, -1)

    return (
        jnp.concatenate(
            [
                side_by_side(parts[:, :, : 2 * PAIR]),
                side_by_side(parts[:, :, 2 * PAIR : 3 * PAIR]),
                side_by_side(parts[:, :, 3 * PAIR :]),
            ],
            axis=1,
        ),
        side_by_side(sums[:2]),
    )


def update_kernel(width, experts, bank_sum, head_sum, small_rows, *refs):
    lanes = refs[0].shape[2]
    gradients = (
        bank_sum[0, :, :lanes],
        bank_sum[0, :, lanes:],
        head_sum[:, :width],
        head_sum[:, width:],
        small_rows[:experts],
        small_rows[experts : experts + 2],
    )
    count = len(gradients)
    for number, gradient in enumerate(gradients):
        held = refs[3 * number : 3 * number + 3]
        if number == count - 1:
            held = (small_rows.at[experts + 2 : experts + 4], *held[1:])
        results = refs[3 * (count + number) : 3 * (count + number) + 3]
        at = (0,) if held[0].ndim == 3 else (Ellipsis,)
        values = update(gradient, *(ref[at] for ref in held))
        for ref, value in zip(results, values):
            ref[at] = value


def update_all(bank_sum, head_sum, small_rows, states):
    experts, block_rows, _ = bank_sum.shape
    half = block_rows // 2
    rows = head_sum.shape[0] // experts

    def spec(value):
        if value.ndim == 3:
            return pl.BlockSpec((1, half, value.shape[2]), lambda i: (i // 2, i % 2, 0))
        if value.shape[0] == head_sum.shape[0] and value.shape[1] > 128:
            return pl.BlockSpec((rows, value.shape[1]), lambda i: (i // 2, 0))
        return pl.BlockSpec(value.shape, lambda i: (0, 0))

    flat = [value for state in states for value in state]
    results = pl.pallas_call(
        functools.partial(update_kernel, states[2][0].shape[1], states[4][0].shape[0]),
        grid=(2 * experts,),
        out_shape=tuple(jax.ShapeDtypeStruct(value.shape, F32) for value in flat),
        in_specs=[spec(value) for value in (bank_sum, head_sum, small_rows, *flat)],
        out_specs=tuple(spec(value) for value in flat),
        compiler_params=pltpu.CompilerParams(vmem_limit_bytes=VMEM_MOST),
        cost_estimate=pl.CostEstimate(flops=2**23, bytes_accessed=25 * 2**20, transcendentals=0),
    )(bank_sum, head_sum, small_rows, *flat)
    return [tuple(results[i : i + 3]) for i in range(0, len(flat), 3)]


def body(
    tokens,
    cotangent,
    routes,
    cont_ids,
    norm_gains,
    gains_moment,
    gains_average,
    heads_in,
    heads_in_master,
    heads_in_moment,
    heads_in_average,
    heads_out,
    heads_out_master,
    heads_out_moment,
    heads_out_average,
    router,
    router_master,
    router_moment,
    router_average,
    expert_in,
    expert_in_master,
    expert_in_moment,
    expert_in_average,
    expert_out,
    expert_out_master,
    expert_out_moment,
    expert_out_average,
):
    token_count, model_width = tokens.shape
    local_experts = expert_in.shape[0]
    peer_count = lax.axis_size("expert")
    experts = local_experts * peer_count
    paired = lax.axis_size("dp") == 8 and peer_count == 4
    half = HEAD_DIM // 2
    powers = [THETA ** (-2.0 * (lane % half) / HEAD_DIM) for lane in range(128)]
    frequencies = jnp.asarray(np.array(powers, np.float32)[None])
    gain_rows = norm_gains.T
    router_rows = router.T
    (
        first_in,
        queries,
        key_rows,
        value_rows,
        attended,
        hidden,
        second_in,
        gates,
        log_totals,
        cosine,
        sine,
        bias,
        cots_all,
        mix_all,
        mix_late,
        grad_part,
        gate_grads,
        gated,
        grad_gate_up,
        rows_all,
    ) = front(
        paired,
        tokens,
        cotangent,
        gain_rows,
        heads_in,
        heads_out,
        router_rows,
        routes.T,
        cont_ids,
        frequencies,
        expert_in,
        expert_out,
        peer_count,
        token_count - cont_ids.shape[1],
    )
    back_rows = lax.psum_scatter(
        grad_part.reshape(peer_count * token_count, model_width),
        "expert",
        scatter_dimension=0,
        tiled=True,
    )
    grad_sources = (
        rows_all.reshape(peer_count * token_count, model_width),
        cots_all.reshape(peer_count * token_count, model_width),
        gated.reshape(peer_count * token_count, -1),
        grad_gate_up.reshape(peer_count * token_count, -1),
    )
    if paired:
        expert_sums = (bank_grads(*grad_sources, local_experts),)
    else:
        expert_sums = tuple(
            lax.psum_scatter(part, "dp", scatter_dimension=1, tiled=True).astype(jnp.float32)
            for part in weight_grads(*grad_sources, local_experts)
        )
    output, token_grad, unit_sums, small_sum, *bank_sums = attend_back(
        (
            back_rows,
            hidden,
            cotangent,
            second_in,
            gates,
            gate_grads,
            router_rows,
            gain_rows,
            heads_out,
            queries,
            key_rows,
            value_rows,
            attended,
            log_totals,
            cosine,
            sine,
            bias,
        ),
        (tokens, first_in, heads_in, mix_all, mix_late, *(expert_sums if paired else ())),
        paired,
        peer_count,
    )
    if paired:
        gains_share = gains_moment.T
    else:
        shard_rows = model_width // lax.axis_size(("dp", "expert"))
        gains_share = lax.dynamic_slice_in_dim(
            gain_rows, lax.axis_index(("dp", "expert")) * shard_rows, shard_rows, 1
        )
    states = (
        (expert_in_master, expert_in_moment, expert_in_average),
        (expert_out_master, expert_out_moment, expert_out_average),
        (heads_in_master, heads_in_moment, heads_in_average),
        (heads_out_master, heads_out_moment, heads_out_average),
        (router_master.T, router_moment.T, router_average.T),
        (gains_share, gains_moment.T, gains_average.T),
    )
    if paired:
        news = update_all(bank_sums[0], unit_sums, small_sum, states)
    else:
        head_parts = unit_columns(unit_sums.reshape(unit_sums.shape[0], model_width, UNIT))
        packed = jnp.concatenate([*head_parts, small_sum.reshape(model_width, 128)], axis=1)
        head_total = lax.psum_scatter(
            packed, ("dp", "expert"), scatter_dimension=0, tiled=True
        ).astype(jnp.float32)
        cut_in = head_parts[0].shape[1]
        cut_out = cut_in + head_parts[1].shape[1]
        small_rows = head_total[:, cut_out:].T
        sums = (
            *expert_sums,
            head_total[:, :cut_in],
            head_total[:, cut_in:cut_out],
            small_rows[:experts],
            small_rows[experts : experts + 2],
        )
        news = [update(gradient, *state) for gradient, state in zip(sums, states)]
    upper_new, lower_new, inproj_new, outproj_new, router_new, gains_new = news
    router_new = tuple(value.T for value in router_new)
    gains_new = tuple(value.T for value in gains_new)
    return (
        output,
        token_grad,
        gains_new[0],
        gains_new[1],
        gains_new[2],
        inproj_new[0],
        inproj_new[1],
        inproj_new[2],
        outproj_new[0],
        outproj_new[1],
        outproj_new[2],
        router_new[0],
        router_new[1],
        router_new[2],
        upper_new[0],
        upper_new[1],
        upper_new[2],
        lower_new[0],
        lower_new[1],
        lower_new[2],
    )


def solution(mesh):
    return jax.shard_map(
        body,
        mesh=mesh,
        in_specs=(
            P(("dp", "expert"), None),
            P(("dp", "expert"), None),
            P(("dp", "expert"), None),
            P(("dp", "expert"), None),
            P(),
            P(("dp", "expert"), None),
            P(("dp", "expert"), None),
            P(),
            P(("dp", "expert"), None),
            P(("dp", "expert"), None),
            P(("dp", "expert"), None),
            P(),
            P(("dp", "expert"), None),
            P(("dp", "expert"), None),
            P(("dp", "expert"), None),
            P(),
            P(("dp", "expert"), None),
            P(("dp", "expert"), None),
            P(("dp", "expert"), None),
            P("expert", None, None),
            P("expert", "dp", None),
            P("expert", "dp", None),
            P("expert", "dp", None),
            P("expert", None, None),
            P("expert", "dp", None),
            P("expert", "dp", None),
            P("expert", "dp", None),
        ),
        out_specs=(
            P(("dp", "expert"), None),
            P(("dp", "expert"), None),
            P(("dp", "expert"), None),
            P(("dp", "expert"), None),
            P(("dp", "expert"), None),
            P(("dp", "expert"), None),
            P(("dp", "expert"), None),
            P(("dp", "expert"), None),
            P(("dp", "expert"), None),
            P(("dp", "expert"), None),
            P(("dp", "expert"), None),
            P(("dp", "expert"), None),
            P(("dp", "expert"), None),
            P(("dp", "expert"), None),
            P("expert", "dp", None),
            P("expert", "dp", None),
            P("expert", "dp", None),
            P("expert", "dp", None),
            P("expert", "dp", None),
            P("expert", "dp", None),
        ),
        check_vma=False,
    )
```

```python
import functools

import jax
import jax.numpy as jnp
import numpy as np
from jax import lax
from jax.experimental import pallas as pl
from jax.experimental.pallas import tpu as pltpu
from jax.sharding import PartitionSpec as P

HEADS = 16
KV_HEADS = 8
HEAD_DIM = 64


EPS = 1e-06
SCALE = 0.015625
THETA = 10000.0
MOMENTUM = 0.9
DECAY = 0.8
RATE = 0.001
HIGHEST = lax.Precision.HIGHEST


def update(gradient, master, moment, average):
    moment_next = MOMENTUM * moment + gradient
    master_next = master - RATE * (gradient + MOMENTUM * moment_next)
    return (master_next, moment_next, DECAY * average + (1.0 - DECAY) * master_next)


F32 = jnp.float32
BF16 = jnp.bfloat16
MESH = pl.DeviceIdType.MESH
VMEM_MOST = 61 * 2**20


def contract(left, right, left_axis, right_axis):
    return lax.dot_general(
        left, right, (((left_axis,), (right_axis,)), ((), ())), preferred_element_type=F32
    )


def visit_order(line):
    return [sorted(range(line), key=lambda s: (abs(s - z), s)) for z in range(line)]


def line_gather(line, z, dp, source, landing, send_sem, recv_sem):
    def copy(origin, block, sem, target):
        return pltpu.make_async_remote_copy(
            src_ref=origin,
            dst_ref=landing.at[block],
            send_sem=send_sem.at[sem],
            recv_sem=recv_sem.at[block],
            device_id=(dp, target),
            device_id_type=MESH,
        )

    def start():
        @pl.when(z < line - 1)
        def _():
            copy(source, z, line, z + 1).start()

        @pl.when(z > 0)
        def _():
            copy(source, z, line + 1, z - 1).start()

    def pass_on(apart):
        low = jnp.maximum(z - apart, 0)
        high = jnp.minimum(z + apart, line - 1)

        @pl.when(z - apart >= 0)
        def _():
            copy(source, low, low, z).wait_recv()

            @pl.when(z < line - 1)
            def _():
                copy(landing.at[low], low, low, z + 1).start()

        @pl.when(z + apart < line)
        def _():
            copy(source, high, high, z).wait_recv()

            @pl.when(z > 0)
            def _():
                copy(landing.at[high], high, high, z - 1).start()

    def finish():
        @pl.when(z < line - 1)
        def _():
            copy(source, z, line, z + 1).wait_send()

        @pl.when(z > 0)
        def _():
            copy(source, z, line + 1, z - 1).wait_send()

        for s in range(line):

            @pl.when(((s < z) & (z < line - 1)) | ((s > z) & (z > 0)))
            def _(s=s):
                copy(source, s, s, z).wait_send()

    return start, pass_on, finish


def pass_steps(line, experts):
    steps = []
    for z in range(line):
        order = visit_order(line)[z]
        for apart in range(1, line):
            met = [k for k in range(line) if abs(order[k] - z) == apart]
            if not met:
                continue
            forwards = (z - apart >= 0 and z < line - 1) or (z + apart < line and z > 0)
            early = experts // 2 if forwards and apart > 1 else 0
            steps.append((z, met[0] * experts - early, apart))
    return steps


def pick(table, row, column):
    value = jnp.int32(table[0][0])
    for r in range(len(table)):
        for c in range(len(table[0])):
            value = jnp.where((row == r) & (column == c), jnp.int32(table[r][c]), value)
    return value


def weight_grads_kernel(rows, cots, gated, inner, up_grad, down_grad):
    step = 256
    for at in range(0, rows.shape[1], step):
        up_grad[0, at : at + step] = contract(rows[:, at : at + step], inner[...], 0, 0).astype(BF16)
        down_grad[0, at : at + step] = contract(cots[:, at : at + step], gated[...], 0, 0).astype(
            BF16
        )


def weight_grads(rows, cots, gated, inner, experts):
    tokens, width = rows.shape
    ff_width = gated.shape[1] // experts
    whole = pl.BlockSpec((tokens, width), lambda e: (0, 0))
    return pl.pallas_call(
        weight_grads_kernel,
        grid=(experts,),
        out_shape=(
            jax.ShapeDtypeStruct((experts, width, 2 * ff_width), BF16),
            jax.ShapeDtypeStruct((experts, width, ff_width), BF16),
        ),
        in_specs=[
            whole,
            whole,
            pl.BlockSpec((tokens, ff_width), lambda e: (0, e)),
            pl.BlockSpec((tokens, 2 * ff_width), lambda e: (0, e)),
        ],
        out_specs=(
            pl.BlockSpec((1, width, 2 * ff_width), lambda e: (e, 0, 0)),
            pl.BlockSpec((1, width, ff_width), lambda e: (e, 0, 0)),
        ),
        compiler_params=pltpu.CompilerParams(vmem_limit_bytes=VMEM_MOST),
        cost_estimate=pl.CostEstimate(
            flops=6 * tokens * width * experts * ff_width,
            bytes_accessed=2 * tokens * (2 * width + 3 * experts * ff_width)
            + 6 * experts * width * ff_width,
            transcendentals=0,
        ),
    )(rows, cots, gated, inner)


def bank_grads_kernel(
    rows_hbm,
    cots_hbm,
    gated_hbm,
    inner_hbm,
    sum_hbm,
    rows,
    cots,
    gated,
    inner,
    grads,
    core_sum,
    first_sum,
    load_sem,
    send_sem,
    recv_sem,
    out_sem,
):
    experts = grads.shape[0]
    ff_width = gated.shape[2]
    block_rows = grads.shape[4]
    dp = lax.axis_index("dp")
    z = lax.axis_index("expert")
    y, x, core = dp // 4, lax.rem(dp // 2, 2), lax.rem(dp, 2)
    core_peer, x_peer, y_peer = dp + 1 - 2 * core, dp + 2 - 4 * x, dp + 4 - 8 * y

    def loads(e, slot):
        return (
            pltpu.make_async_copy(
                gated_hbm.at[:, pl.ds(pl.multiple_of(e * ff_width, ff_width), ff_width)],
                gated.at[slot],
                load_sem.at[slot, 0],
            ),
            pltpu.make_async_copy(
                inner_hbm.at[:, pl.ds(pl.multiple_of(2 * e * ff_width, ff_width), 2 * ff_width)],
                inner.at[slot],
                load_sem.at[slot, 1],
            ),
        )

    row_load = pltpu.make_async_copy(rows_hbm, rows, load_sem.at[0, 2])
    cot_load = pltpu.make_async_copy(cots_hbm, cots, load_sem.at[1, 2])
    row_load.start()
    for copy in loads(0, 0):
        copy.start()
    cot_load.start()
    barrier = pltpu.get_barrier_semaphore()
    for peer in (core_peer, x_peer, y_peer):
        pl.semaphore_signal(barrier, inc=1, device_id=(peer, z), device_id_type=MESH)
    pl.semaphore_wait(barrier, 3)
    row_load.wait()
    cot_load.wait()

    def send(stage, e, source, target, peer):
        return pltpu.make_async_remote_copy(
            src_ref=source,
            dst_ref=target,
            send_sem=send_sem.at[stage, e],
            recv_sem=recv_sem.at[stage, e],
            device_id=(peer, z),
            device_id_type=MESH,
        )

    def core_send(e):
        return send(0, e, grads.at[e, :, :, 1 - core], core_sum.at[e], core_peer)

    def first_send(e, along_x):
        if along_x:
            return send(1, e, core_sum.at[e, :, 1 - x], first_sum.at[e], x_peer)
        return send(1, e, core_sum.at[e, 1 - y], first_sum.at[e], y_peer)

    def by_parity(e, act):
        even = lax.rem(e, 2) == 0

        @pl.when(even)
        def _():
            act(True)

        @pl.when(jnp.logical_not(even))
        def _():
            act(False)

    def after_core(e):
        core_send(e).wait_recv()
        for yy in range(2):
            for xx in range(2):
                core_sum[e, yy, xx] = (
                    grads[e, yy, xx, core].astype(F32) + core_sum[e, yy, xx].astype(F32)
                ).astype(BF16)
        by_parity(e, lambda even: first_send(e, even).start())

    def after_first(e):
        def act(even):
            first_send(e, even).wait_recv()
            for other in range(2):
                kept = core_sum[e, other, x] if even else core_sum[e, y, other]
                first_sum[e, other] = (
                    kept.astype(F32) + first_sum[e, other].astype(F32)
                ).astype(BF16)

        by_parity(e, act)
        pltpu.make_async_copy(first_sum.at[e], sum_hbm.at[e], out_sem.at[e]).start()

    def step(e, _):
        slot = lax.rem(e, 2)
        for copy in loads(e, slot):
            copy.wait()

        @pl.when(e + 1 < experts)
        def _():
            for copy in loads(e + 1, 1 - slot):
                copy.start()

        def tile(at, _):
            columns = pl.ds(pl.multiple_of(at * 2 * block_rows, 2 * block_rows), 2 * block_rows)
            up_grad = contract(rows[:, columns], inner[slot], 0, 0).astype(BF16)
            down_grad = contract(cots[:, columns], gated[slot], 0, 0).astype(BF16)
            for side in range(2):
                part = slice(side * block_rows, (side + 1) * block_rows)
                grads[e, at // 2, lax.rem(at, 2), side, :, : 2 * ff_width] = up_grad[part]
                grads[e, at // 2, lax.rem(at, 2), side, :, 2 * ff_width :] = down_grad[part]
            return 0

        lax.fori_loop(0, 4, tile, 0)
        core_send(e).start()

        @pl.when(e >= 1)
        def _():
            after_core(e - 1)

        @pl.when(e >= 3)
        def _():
            after_first(e - 3)

        return 0

    lax.fori_loop(0, experts, step, 0)
    after_core(experts - 1)

    for e in range(max(experts - 3, 0), experts):
        after_first(e)
    for e in range(experts):
        core_send(e).wait_send()
        first_send(e, e % 2 == 0).wait_send()
        pltpu.make_async_copy(first_sum.at[e], sum_hbm.at[e], out_sem.at[e]).wait()


def bank_grads(rows, cots, gated, inner, experts):
    tokens, width = rows.shape
    ff_width = gated.shape[1] // experts
    lanes = 3 * ff_width
    block_rows = width // 8
    anywhere = pl.BlockSpec(memory_space=pl.ANY)
    return pl.pallas_call(
        bank_grads_kernel,
        out_shape=jax.ShapeDtypeStruct((experts, 2, block_rows, lanes), BF16),
        in_specs=[anywhere] * 4,
        out_specs=anywhere,
        scratch_shapes=[
            pltpu.VMEM((tokens, width), BF16),
            pltpu.VMEM((tokens, width), BF16),
            pltpu.VMEM((2, tokens, ff_width), BF16),
            pltpu.VMEM((2, tokens, 2 * ff_width), BF16),
            pltpu.VMEM((experts, 2, 2, 2, block_rows, lanes), BF16),
            pltpu.VMEM((experts, 2, 2, block_rows, lanes), BF16),
            pltpu.VMEM((experts, 2, block_rows, lanes), BF16),
            pltpu.SemaphoreType.DMA((2, 3)),
            pltpu.SemaphoreType.DMA((2, experts)),
            pltpu.SemaphoreType.DMA((2, experts)),
            pltpu.SemaphoreType.DMA((experts,)),
        ],
        compiler_params=pltpu.CompilerParams(
            collective_id=2, has_side_effects=True, vmem_limit_bytes=VMEM_MOST
        ),
        cost_estimate=pl.CostEstimate(
            flops=6 * tokens * width * experts * ff_width,
            bytes_accessed=2**27,
            transcendentals=0,
        ),
    )(rows, cots, gated, inner)


PAIR = 2 * HEAD_DIM
UNIT = 512
PIECES = 3


def swap_halves(value):
    lane = lax.broadcasted_iota(jnp.int32, value.shape, 1)
    half = HEAD_DIM // 2
    return jnp.where(
        lax.rem(lane, HEAD_DIM) < half,
        pltpu.roll(value, value.shape[1] - half, 1),
        pltpu.roll(value, half, 1),
    )


def sides(pair, side, scale):
    value = pair.astype(F32)
    if scale is not None:
        value = value * scale
    turned = pltpu.roll(value, HEAD_DIM, 1)
    lane = lax.broadcasted_iota(jnp.int32, value.shape, 1)
    left, right = (value, turned) if side == 0 else (turned, value)
    return (
        jnp.where(lane < HEAD_DIM, left, 0.0).astype(BF16),
        jnp.where(lane < HEAD_DIM, 0.0, right).astype(BF16),
    )


def lanes_at(start, size):
    return pl.ds(pl.multiple_of(start, 128), size)


def front_kernel(
    line,
    prompt,
    late,
    tokens,
    cots_hbm,
    gain_rows,
    heads_in_hbm,
    heads_out_hbm,
    router_rows,
    route_rows,
    label_row,
    frequencies,
    up_hbm,
    down_hbm,
    first_in_hbm,
    queries_hbm,
    keys_hbm,
    values_hbm,
    attended_hbm,
    hidden_hbm,
    second_in_hbm,
    gate_rows,
    log_totals,
    cosine_hbm,
    sine_hbm,
    bias_hbm,
    cots_all,
    mix_all,
    mix_late,
    back_hbm,
    gate_grads_hbm,
    gated_hbm,
    inner_hbm,
    rows_all_hbm,
    cots,
    rows,
    gates_own,
    gates,
    gate_grads,
    gate_grads_sent,
    up,
    down,
    projected,
    stage,
    mix_stage,
    gated,
    inner,
    columns,
    cot_send,
    cot_recv,
    row_send,
    row_recv,
    gate_send,
    gate_recv,
    weight_sem,
    local_sem,
    out_sem,
    grad_send,
    grad_recv,
    mix_send,
    mix_recv,
    heads_in,
    heads_out,
    first_in,
    queries,
    keys,
    values,
    attended,
    hidden,
    second_in,
    cosine,
    sine,
    bias,
    held_sem,
    row_out_sem,
):
    dp = lax.axis_index("dp")
    z = lax.axis_index("expert")
    experts, _, ff_width = down_hbm.shape
    start_cots, pass_cots, finish_cots = line_gather(
        line, z, dp, cots_hbm, cots_all, cot_send, cot_recv
    )
    start_rows, pass_rows, finish_rows = line_gather(
        line, z, dp, second_in, rows, row_send, row_recv
    )

    heads_in_load = pltpu.make_async_copy(heads_in_hbm, heads_in, held_sem.at[0])
    heads_out_load = pltpu.make_async_copy(heads_out_hbm, heads_out, held_sem.at[1])
    held_out = [
        pltpu.make_async_copy(source, target, held_sem.at[2 + number])
        for number, (source, target) in enumerate(
            (
                (first_in, first_in_hbm),
                (queries, queries_hbm),
                (keys, keys_hbm),
                (values, values_hbm),
                (attended, attended_hbm),
                (hidden, hidden_hbm),
                (second_in, second_in_hbm),
                (cosine, cosine_hbm),
                (sine, sine_hbm),
                (bias, bias_hbm),
            )
        )
    ]

    def weight_copies(e):
        return (
            pltpu.make_async_copy(
                up_hbm.at[e],
                up.at[:, pl.ds(pl.multiple_of(e * 2 * ff_width, ff_width), 2 * ff_width)],
                weight_sem.at[0, e],
            ),
            pltpu.make_async_copy(
                down_hbm.at[e],
                down.at[:, pl.ds(pl.multiple_of(e * ff_width, ff_width), ff_width)],
                weight_sem.at[1, e],
            ),
        )

    barrier = pltpu.get_barrier_semaphore()
    for step in range(1, line):
        pl.semaphore_signal(
            barrier, inc=1, device_id=(dp, lax.rem(z + step, line)), device_id_type=MESH
        )
    pl.semaphore_wait(barrier, line - 1)
    start_cots()
    cots_in = pltpu.make_async_copy(cots_hbm, cots, local_sem.at[2])
    cots_in.start()
    heads_in_load.start()
    heads_out_load.start()
    for e in range(experts):
        for copy in weight_copies(e):
            copy.start()

    query_end = HEADS * HEAD_DIM
    key_end = query_end + KV_HEADS * HEAD_DIM
    token_rows = tokens[...].astype(F32)
    factor = lax.rsqrt(jnp.mean(token_rows * token_rows, axis=1, keepdims=True) + EPS)
    first_in[...] = (token_rows * factor * gain_rows[0:1]).astype(BF16)
    log_totals[...] = jnp.zeros_like(log_totals)
    cots_in.wait()
    own_cots = pltpu.make_async_copy(cots, cots_all.at[z], local_sem.at[0])
    own_cots.start()

    labels = label_row[...].astype(F32)
    size = labels.shape[1]
    square = jnp.broadcast_to(labels, (size, size))
    upright = square.T
    earlier = jnp.sum(jnp.where(square < upright, 1.0, 0.0), axis=1, keepdims=True)
    place = lax.broadcasted_iota(jnp.int32, (token_rows.shape[0], 128), 0).astype(F32)
    shift = jnp.concatenate([jnp.zeros((prompt, 1), F32), earlier], axis=0)
    angles = (place - shift) * frequencies[...]
    lane = lax.broadcasted_iota(jnp.int32, angles.shape, 1)
    sines = jnp.sin(angles)
    cosine[...] = jnp.cos(angles)
    sine[...] = jnp.where(lax.rem(lane, HEAD_DIM) < HEAD_DIM // 2, -sines, sines)
    own_label = jnp.concatenate([jnp.full((prompt, 1), -1.0, F32), upright[:, :1]], axis=0)
    seen_label = jnp.concatenate([jnp.full((1, prompt), -1.0, F32), labels], axis=1)
    row = lax.broadcasted_iota(jnp.int32, bias.shape, 0)
    column = lax.broadcasted_iota(jnp.int32, bias.shape, 1)
    allowed = (column <= row) & ((column < prompt) | (own_label == seen_label))
    bias[...] = jnp.where(allowed, 0.0, -1e30)
    heads_in_load.wait()

    def project(i, _):
        at = lanes_at(i * UNIT, UNIT)
        projected[:, at] = contract(first_in[...], heads_in[:, at], 1, 0)
        return 0

    lax.fori_loop(0, heads_in.shape[1] // UNIT, project, 0)

    def pair(j, _):
        for side in range(2):
            at = lanes_at((2 * j + side) * PAIR, PAIR)
            wide = projected[:, at]
            queries[:, at] = (wide * cosine[...] + swap_halves(wide) * sine[...]).astype(BF16)
        wide = projected[:, lanes_at(query_end + j * PAIR, PAIR)]
        keys[:, lanes_at(j * PAIR, PAIR)] = (
            wide * cosine[...] + swap_halves(wide) * sine[...]
        ).astype(BF16)
        values[:, lanes_at(j * PAIR, PAIR)] = projected[
            :, lanes_at(key_end + j * PAIR, PAIR)
        ].astype(BF16)
        heads = [(side, member) for side in range(2) for member in range(2)]
        groups = [queries[:, lanes_at((2 * j + side) * PAIR, PAIR)] for side in range(2)]
        key_sides = [sides(keys[:, lanes_at(j * PAIR, PAIR)], side, SCALE) for side in range(2)]
        value_sides = [sides(values[:, lanes_at(j * PAIR, PAIR)], side, None) for side in range(2)]
        parts = ((0, prompt, prompt), (prompt, groups[0].shape[0], groups[0].shape[0]))

        def scores_of(side, member):
            return [
                contract(groups[side][begin:end], key_sides[side][member][:seen], 1, 1)
                + bias[begin:end, :seen]
                for begin, end, seen in parts
            ]

        lane = lax.broadcasted_iota(jnp.int32, log_totals.shape, 1)
        added = jnp.zeros(log_totals.shape, F32)
        sums = [0.0, 0.0]
        scores = scores_of(*heads[0])
        for number, (side, member) in enumerate(heads):
            following = scores_of(*heads[number + 1]) if number + 1 < len(heads) else None
            mixed = []
            totals = []
            for part, (_, _, seen) in zip(scores, parts):
                peak = jnp.max(part, axis=1, keepdims=True)
                powers = jnp.exp(part - peak)
                amount = jnp.sum(powers, axis=1, keepdims=True)
                weights = (powers * (1.0 / amount)).astype(BF16)
                totals.append(peak + jnp.log(amount))
                mixed.append(contract(weights, value_sides[side][member][:seen], 1, 0))
            sums[side] = sums[side] + jnp.concatenate(mixed, axis=0)
            added = jnp.where(lane == 4 * j + number, jnp.concatenate(totals, axis=0), added)
            scores = following
        log_totals[...] += added
        for side in range(2):
            attended[:, lanes_at((2 * j + side) * PAIR, PAIR)] = sums[side].astype(BF16)
        return 0

    lax.fori_loop(0, KV_HEADS // 2, pair, 0)
    heads_out_load.wait()
    hidden_rows = token_rows + contract(attended[...], heads_out[...], 1, 1)
    hidden[...] = hidden_rows
    factor = lax.rsqrt(jnp.mean(hidden_rows * hidden_rows, axis=1, keepdims=True) + EPS)
    second = (hidden_rows * factor * gain_rows[1:2]).astype(BF16)
    second_in[...] = second
    start_rows()
    for copy in held_out:
        copy.start()
    own_rows = pltpu.make_async_copy(second_in, rows.at[z], local_sem.at[1])
    own_rows.start()
    logits = contract(router_rows[...], second, 1, 1)
    expert = lax.broadcasted_iota(jnp.int32, logits.shape, 0)
    named = expert == route_rows[0:1]
    for k in range(1, route_rows.shape[0]):
        named = named | (expert == route_rows[k : k + 1])
    peak = jnp.max(jnp.where(named, logits, -1e30), axis=0, keepdims=True)
    powers = jnp.where(named, jnp.exp(jnp.where(named, logits, peak) - peak), 0.0)
    gate_values = powers / jnp.sum(powers, axis=0, keepdims=True)
    gate_rows[...] = gate_values
    gates_own[...] = jnp.zeros_like(gates_own)
    for peer in range(line):
        gates_own[peer, :experts] = gate_values[peer * experts : (peer + 1) * experts]
    gates[z] = gates_own[z]
    def gate_copy(step):
        peer = lax.rem(z + step, line)
        return pltpu.make_async_remote_copy(
            src_ref=gates_own.at[peer],
            dst_ref=gates.at[z],
            send_sem=gate_send.at[step],
            recv_sem=gate_recv.at[step],
            device_id=(dp, peer),
            device_id_type=MESH,
        )

    for step in range(1, line):
        gate_copy(step).start()
    own_rows.wait()
    own_cots.wait()
    pass_cots(1)
    for step in range(1, line):
        gate_copy(step).wait()

    order = visit_order(line)

    def out_copies(slot, block):
        return (
            pltpu.make_async_copy(stage.at[slot], back_hbm.at[block], out_sem.at[slot, 0]),
            pltpu.make_async_copy(gated.at[slot], gated_hbm.at[block], out_sem.at[slot, 1]),
            pltpu.make_async_copy(inner.at[slot], inner_hbm.at[block], out_sem.at[slot, 2]),
        )

    def mix_copy(block, source, target):
        return pltpu.make_async_remote_copy(
            src_ref=mix_stage.at[block],
            dst_ref=mix_all.at[source],
            send_sem=mix_send.at[block],
            recv_sem=mix_recv.at[source],
            device_id=(dp, target),
            device_id_type=MESH,
        )

    def row_out(block):
        return pltpu.make_async_copy(rows.at[block], rows_all_hbm.at[block], row_out_sem.at[block])

    def own_mix():
        return pltpu.make_async_copy(mix_stage.at[z], mix_all.at[z], local_sem.at[3])

    def late_mix(side):
        return pltpu.make_async_copy(
            mix_stage.at[side * (line - 1)], mix_late.at[side], local_sem.at[4 + side]
        )

    def at_end(block):
        return (block == 0) | (block == line - 1)

    def grad_copy(block, step):
        return pltpu.make_async_remote_copy(
            src_ref=gate_grads_sent.at[block],
            dst_ref=gate_grads.at[z],
            send_sem=grad_send.at[block],
            recv_sem=grad_recv.at[z],
            device_id=(dp, block),
            device_id_type=MESH,
        )

    def visit(k, _):
        block = pick(order, z, k)
        slot = lax.rem(k, 2)
        @pl.when(k >= 2)
        def _():
            for copy in out_copies(slot, pick(order, z, jnp.maximum(k - 2, 0))):
                copy.wait()

        cot_load = pltpu.make_async_copy(cots_all.at[block], cots, local_sem.at[2])
        gate_columns = gates[block].T
        tile = min(ff_width, 256)
        def arrive(e):
            step = k * experts + e
            apart = jnp.int32(0)
            for at_z, at_step, distance in pass_steps(line, experts):
                apart = jnp.where((z == at_z) & (step == at_step), distance, apart)

            @pl.when(apart > 0)
            def _():
                pass_rows(apart)

            if line > 2:

                @pl.when(apart == 1)
                def _():
                    pass_cots(2)

            @pl.when(apart > 2)
            def _():
                pass_cots(apart)

            @pl.when((k > 0) & (e == 0))
            def _():
                cot_load.start()
                cot_load.wait()

        def products(e, at):
            gate_at = pl.multiple_of(2 * e * ff_width + at, tile)
            up_at = pl.multiple_of((2 * e + 1) * ff_width + at, tile)
            down_at = pl.multiple_of(e * ff_width + at, tile)
            return (
                contract(rows[block], up[:, pl.ds(gate_at, tile)], 1, 0),
                contract(rows[block], up[:, pl.ds(up_at, tile)], 1, 0),
                contract(cots[...], down[:, pl.ds(down_at, tile)], 1, 0),
            )

        narrow_lane = lax.broadcasted_iota(jnp.int32, gate_columns.shape, 1)
        wide_lane = lax.broadcasted_iota(jnp.int32, columns.shape, 1)
        several = experts // 2
        columns[...] = jnp.zeros_like(columns)

        def half(part, _):
            begin = part * several
            arrive(begin)

            @pl.when(k == 0)
            def _():
                for e in range(several):
                    for copy in weight_copies(begin + e):
                        copy.wait()

            tiles = [(e, at) for e in range(several) for at in range(0, ff_width, tile)]
            ready = products(begin + tiles[0][0], tiles[0][1])
            sums = [0.0] * several
            for number, (near, at) in enumerate(tiles):
                following = None
                if number + 1 < len(tiles):
                    following = products(begin + tiles[number + 1][0], tiles[number + 1][1])
                e = begin + near
                gate_part, up_part, returned = ready
                gate_col = jnp.sum(
                    jnp.where(narrow_lane == e, gate_columns, 0.0), axis=1, keepdims=True
                )
                sigmoid_gate = jax.nn.sigmoid(gate_part)
                silu_gate = gate_part * sigmoid_gate
                active = silu_gate * up_part
                sums[near] = sums[near] + jnp.sum(active * returned, axis=1, keepdims=True)
                scaled = returned * gate_col
                grad_gate = scaled * up_part * (sigmoid_gate + silu_gate * (1.0 - sigmoid_gate))
                gate_at = pl.multiple_of(2 * e * ff_width + at, tile)
                up_at = pl.multiple_of((2 * e + 1) * ff_width + at, tile)
                down_at = pl.multiple_of(e * ff_width + at, tile)
                gated[slot, :, pl.ds(down_at, tile)] = (active * gate_col).astype(BF16)
                inner[slot, :, pl.ds(gate_at, tile)] = grad_gate.astype(BF16)
                inner[slot, :, pl.ds(up_at, tile)] = (scaled * silu_gate).astype(BF16)
                ready = following
            value = columns[...]
            for near in range(several):
                value = jnp.where(wide_lane == begin + near, sums[near], value)
            columns[...] = value
            return 0

        lax.fori_loop(0, 2, half, 0)
        row_out(block).start()
        mix_stage[block] = contract(gated[slot], down[...], 1, 1).astype(BF16)

        @pl.when(block == z)
        def _():
            own_mix().start()

        if late:
            for side in range(2):

                @pl.when((block != z) & (block == side * (line - 1)))
                def _(side=side):
                    late_mix(side).start()

            @pl.when((block != z) & jnp.logical_not(at_end(block)))
            def _():
                mix_copy(block, z, block).start()

        else:

            @pl.when(block != z)
            def _():
                mix_copy(block, z, block).start()

        stage[slot] = contract(inner[slot], up[...], 1, 1).astype(BF16)
        for copy in out_copies(slot, block):
            copy.start()
        gate_grads_sent[block] = columns[...].T[: gate_grads.shape[1]]

        @pl.when(block == z)
        def _():
            gate_grads[z] = gate_grads_sent[z]

        @pl.when(block != z)
        def _():
            grad_copy(block, 0).start()

        return 0

    lax.fori_loop(0, line, visit, 0)
    for k in range(max(line - 2, 0), line):
        for copy in out_copies(k % 2, pick(order, z, k)):
            copy.wait()

    finish_rows()
    finish_cots()
    for copy in held_out:
        copy.wait()
    own_mix().wait()
    if late:
        for side in range(2):

            @pl.when(z != side * (line - 1))
            def _(side=side):
                late_mix(side).wait()

    for s in range(line):
        send_ends = late and s in (0, line - 1)

        @pl.when(z != s)
        def _(s=s, send_ends=send_ends):
            if not send_ends:
                mix_copy(s, s, z).wait_send()
            if late:

                @pl.when(jnp.logical_not(at_end(z)))
                def _():
                    mix_copy(s, s, z).wait_recv()

            else:
                mix_copy(s, s, z).wait_recv()

    for s in range(line):

        @pl.when(s != z)
        def _(s=s):
            grad_copy(s, 0).wait_send()
            pltpu.make_async_remote_copy(
                src_ref=gate_grads_sent.at[s],
                dst_ref=gate_grads.at[s],
                send_sem=grad_send.at[s],
                recv_sem=grad_recv.at[s],
                device_id=(dp, z),
                device_id_type=MESH,
            ).wait_recv()

    last = pltpu.make_async_copy(gate_grads, gate_grads_hbm, local_sem.at[1])
    last.start()
    for s in range(line):
        row_out(s).wait()
    last.wait()


def front(
    late,
    tokens,
    cots,
    gain_rows,
    heads_in,
    heads_out,
    router_rows,
    route_rows,
    label_row,
    frequencies,
    up,
    down,
    line,
    prompt,
):
    count, width = tokens.shape
    named = router_rows.shape[0]
    experts, _, ff_width = down.shape
    kv_width = KV_HEADS * HEAD_DIM
    shape = jax.ShapeDtypeStruct
    padded = experts + -experts % 8
    held = pl.BlockSpec(memory_space=pltpu.VMEM)
    anywhere = pl.BlockSpec(memory_space=pl.ANY)
    small = pltpu.VMEM((line, padded, count), F32)
    return pl.pallas_call(
        functools.partial(front_kernel, line, prompt, late),
        out_shape=(
            shape((count, width), BF16),
            shape((count, HEADS * HEAD_DIM), BF16),
            shape((count, kv_width), BF16),
            shape((count, kv_width), BF16),
            shape((count, HEADS * HEAD_DIM), BF16),
            shape((count, width), F32),
            shape((count, width), BF16),
            shape((named, count), F32),
            shape((count, 128), F32),
            shape((count, 128), F32),
            shape((count, 128), F32),
            shape((count, count), F32),
            shape((line, count, width), BF16),
            shape((line, count, width), BF16),
            shape((2, count, width), BF16),
            shape((line, count, width), BF16),
            shape((line, padded, count), F32),
            shape((line, count, experts * ff_width), BF16),
            shape((line, count, experts * 2 * ff_width), BF16),
            shape((line, count, width), BF16),
        ),
        in_specs=[held, anywhere, held, anywhere, anywhere] + [held] * 4 + [anywhere] * 2,
        out_specs=(anywhere,) * 7 + (held,) * 2 + (anywhere,) * 11,
        scratch_shapes=[
            pltpu.VMEM((count, width), BF16),
            pltpu.VMEM((line, count, width), BF16),
            small,
            small,
            small,
            small,
            pltpu.VMEM((width, experts * 2 * ff_width), BF16),
            pltpu.VMEM((width, experts * ff_width), BF16),
            pltpu.VMEM((count, heads_in.shape[1]), F32),
            pltpu.VMEM((2, count, width), BF16),
            pltpu.VMEM((line, count, width), BF16),
            pltpu.VMEM((2, count, experts * ff_width), BF16),
            pltpu.VMEM((2, count, experts * 2 * ff_width), BF16),
            pltpu.VMEM((count, 128), F32),
            pltpu.SemaphoreType.DMA((line + 2,)),
            pltpu.SemaphoreType.DMA((line,)),
            pltpu.SemaphoreType.DMA((line + 2,)),
            pltpu.SemaphoreType.DMA((line,)),
            pltpu.SemaphoreType.DMA((line,)),
            pltpu.SemaphoreType.DMA((line,)),
            pltpu.SemaphoreType.DMA((2, experts)),
            pltpu.SemaphoreType.DMA((6,)),
            pltpu.SemaphoreType.DMA((2, 3)),
            pltpu.SemaphoreType.DMA((line,)),
            pltpu.SemaphoreType.DMA((line,)),
            pltpu.SemaphoreType.DMA((line,)),
            pltpu.SemaphoreType.DMA((line,)),
            pltpu.VMEM(heads_in.shape, BF16),
            pltpu.VMEM(heads_out.shape, BF16),
            pltpu.VMEM((count, width), BF16),
            pltpu.VMEM((count, HEADS * HEAD_DIM), BF16),
            pltpu.VMEM((count, kv_width), BF16),
            pltpu.VMEM((count, kv_width), BF16),
            pltpu.VMEM((count, HEADS * HEAD_DIM), BF16),
            pltpu.VMEM((count, width), F32),
            pltpu.VMEM((count, width), BF16),
            pltpu.VMEM((count, 128), F32),
            pltpu.VMEM((count, 128), F32),
            pltpu.VMEM((count, count), F32),
            pltpu.SemaphoreType.DMA((12,)),
            pltpu.SemaphoreType.DMA((line,)),
        ],
        compiler_params=pltpu.CompilerParams(
            collective_id=4, has_side_effects=True, vmem_limit_bytes=VMEM_MOST
        ),
        cost_estimate=pl.CostEstimate(flops=2**35, bytes_accessed=2**26, transcendentals=2**22),
    )(
        tokens,
        cots,
        gain_rows,
        heads_in,
        heads_out,
        router_rows,
        route_rows,
        label_row,
        frequencies,
        up,
        down,
    )


def attend_back_kernel(
    paired,
    line,
    back_rows,
    hidden,
    cots,
    second_in,
    gate_rows,
    gate_grads,
    router_rows,
    gain_rows,
    heads_out,
    queries,
    keys,
    values,
    attended,
    log_totals,
    cosine,
    sine,
    bias,
    tokens_hbm,
    first_hbm,
    in_hbm,
    mix_hbm,
    late_hbm,
    *others,
):
    bank_hbm, others = (others[0], others[1:]) if paired else (None, others)
    output, token_grad, sum_hbm, small_hbm, *others = others
    bank_sum_hbm, others = (others[0], others[1:]) if paired else (None, others)
    (
        tokens,
        first_in,
        heads_in,
        mixes,
        gate_grad_rows,
        grad_hidden,
        grad_attended,
        grad_projected,
        small_rows,
        own,
        own_small,
        *scratch,
    ) = others
    dp = lax.axis_index("dp")
    z = lax.axis_index("expert")
    units = own.shape[0]
    block_rows = own.shape[4]
    load_sem = scratch[0]
    loads = (
        pltpu.make_async_copy(first_hbm, first_in, load_sem.at[0]),
        pltpu.make_async_copy(tokens_hbm, tokens, load_sem.at[1]),
        pltpu.make_async_copy(in_hbm, heads_in, load_sem.at[2]),
    )
    for copy in loads:
        copy.start()

    def mix_load(b):
        return pltpu.make_async_copy(mix_hbm.at[b], mixes.at[b], load_sem.at[5 + b])

    def direct(b):
        ends = (z == 0) | (z == line - 1)
        return jnp.logical_not(ends) | (z == b) if paired else z == z

    for b in range(line):

        @pl.when(direct(b))
        def _(b=b):
            mix_load(b).start()

    if paired:
        (
            cores,
            firsts,
            lasts,
            sums,
            lines,
            totals,
            small_cores,
            small_firsts,
            small_lasts,
            small_sums,
            small_lines,
            small_totals,
            send_sem,
            recv_sem,
            line_send,
            line_recv,
            out_sem,
            bank_kept,
            bank_last,
            bank_total,
            bank_sem,
            small_columns,
            chain_own,
            chain_in,
            chain_out,
            chain_load_sem,
            chain_sem,
        ) = scratch[1:]
        rows = totals.shape[1]
        y, x, core = dp // 4, lax.rem(dp // 2, 2), lax.rem(dp, 2)
        core_peer, x_peer, y_peer = dp + 1 - 2 * core, dp + 2 - 4 * x, dp + 4 - 8 * y
        barrier = pltpu.get_barrier_semaphore()
        for peer in (core_peer, x_peer, y_peer):
            pl.semaphore_signal(barrier, inc=1, device_id=(peer, z), device_id_type=MESH)
        for step in range(1, line):
            pl.semaphore_signal(
                barrier, inc=1, device_id=(dp, lax.rem(z + step, line)), device_id_type=MESH
            )
        pl.semaphore_wait(barrier, 3 + line - 1)

        def bank_kept_copy(e):
            kept = y if e % 2 == 0 else x
            return pltpu.make_async_copy(
                bank_hbm.at[e, kept], bank_kept.at[e], bank_sem.at[0, e]
            )

        def bank_last_copy(e):
            sent, peer = (1 - y, y_peer) if e % 2 == 0 else (1 - x, x_peer)
            return pltpu.make_async_remote_copy(
                src_ref=bank_hbm.at[e, sent],
                dst_ref=bank_last.at[e],
                send_sem=bank_sem.at[1, e],
                recv_sem=bank_sem.at[2, e],
                device_id=(peer, z),
                device_id_type=MESH,
            )

        def bank_total_copy(e):
            return pltpu.make_async_copy(
                bank_total.at[e], bank_sum_hbm.at[e], bank_sem.at[3, e]
            )

        for e in range(bank_hbm.shape[0]):
            bank_kept_copy(e).start()
            bank_last_copy(e).start()

        piece = hidden.shape[0] // PIECES

        def part(p):
            return pl.ds(p * piece, piece)

        def chain_load(side):
            return pltpu.make_async_copy(
                late_hbm.at[side], chain_own.at[side], chain_load_sem.at[side]
            )

        def chain_send(side, p, source):
            return pltpu.make_async_remote_copy(
                src_ref=source.at[side, part(p)],
                dst_ref=chain_in.at[side, part(p)],
                send_sem=chain_sem.at[0, side, p],
                recv_sem=chain_sem.at[1, side, p],
                device_id=(dp, jnp.clip(z + 2 * side - 1, 0, line - 1)),
                device_id_type=MESH,
            )

        inside = (z > 0) & (z < line - 1)
        starts = (z == line - 1, z == 0)
        for side in range(2):

            @pl.when(inside)
            def _(side=side):
                chain_load(side).start()

            @pl.when(starts[side])
            def _(side=side):
                for p in range(PIECES):
                    chain_send(side, p, late_hbm).start()

        def relay(side, p):
            if p == 0:
                chain_load(side).wait()
            chain_send(side, p, chain_out).wait_recv()
            chain_out[side, part(p)] = (
                chain_own[side, part(p)].astype(F32) + chain_in[side, part(p)].astype(F32)
            ).astype(BF16)
            chain_send(side, p, chain_out).start()

        def relay_on(near, p):
            low_half = 2 * z < line - 1

            @pl.when(inside & low_half)
            def _():
                relay(1 if near else 0, p)

            @pl.when(inside & jnp.logical_not(low_half))
            def _():
                relay(0 if near else 1, p)

        buffers = (own, cores, firsts, lasts, sums, lines, totals)
        small_buffers = (
            own_small,
            small_cores,
            small_firsts,
            small_lasts,
            small_sums,
            small_lines,
            small_totals,
        )

        def send(stage, u, source, target, peer):
            return pltpu.make_async_remote_copy(
                src_ref=source,
                dst_ref=target,
                send_sem=send_sem.at[stage, u],
                recv_sem=recv_sem.at[stage, u],
                device_id=(peer, z),
                device_id_type=MESH,
            )

        class Sums:
            def __init__(self, held, shift):
                self.own, self.cores, self.firsts, self.lasts = held[:4]
                self.sums, self.lines, self.totals = held[4:]
                self.shift = shift

            def core_send(self, u):
                return send(
                    0,
                    u + self.shift,
                    self.own.at[u, :, :, 1 - core],
                    self.cores.at[u],
                    core_peer,
                )

            def first_send(self, u, along_x):
                if along_x:
                    source, peer = self.cores.at[u, :, 1 - x], x_peer
                else:
                    source, peer = self.cores.at[u, 1 - y], y_peer
                return send(1, u + self.shift, source, self.firsts.at[u], peer)

            def last_send(self, u, along_x):
                if along_x:
                    source, peer = self.firsts.at[u, 1 - x], x_peer
                else:
                    source, peer = self.firsts.at[u, 1 - y], y_peer
                return send(2, u + self.shift, source, self.lasts.at[u], peer)

            def line_copy(self, u, step):
                peer = lax.rem(z + step, line)
                return pltpu.make_async_remote_copy(
                    src_ref=self.sums.at[u, pl.ds(pl.multiple_of(peer * rows, rows), rows)],
                    dst_ref=self.lines.at[u, step],
                    send_sem=line_send.at[u + self.shift, step],
                    recv_sem=line_recv.at[u + self.shift, step],
                    device_id=(dp, peer),
                    device_id_type=MESH,
                )

            def by_parity(self, u, act):
                even = lax.rem(jnp.int32(u), 2) == 0

                @pl.when(even)
                def _():
                    act(True)

                @pl.when(jnp.logical_not(even))
                def _():
                    act(False)

            def after_core(self, u):
                self.core_send(u).wait_recv()
                for yy in range(2):
                    for xx in range(2):
                        self.cores[u, yy, xx] = (
                            self.own[u, yy, xx, core].astype(F32)
                            + self.cores[u, yy, xx].astype(F32)
                        ).astype(BF16)
                self.by_parity(u, lambda even: self.first_send(u, even).start())

            def after_first(self, u):
                def act(even):
                    self.first_send(u, even).wait_recv()
                    for other in range(2):
                        kept = self.cores[u, other, x] if even else self.cores[u, y, other]
                        self.firsts[u, other] = (
                            kept.astype(F32) + self.firsts[u, other].astype(F32)
                        ).astype(BF16)
                    self.last_send(u, not even).start()

                self.by_parity(u, act)

            def after_last(self, u):
                def act(even):
                    self.last_send(u, not even).wait_recv()
                    kept = self.firsts[u, y] if even else self.firsts[u, x]
                    self.sums[u] = (kept.astype(F32) + self.lasts[u].astype(F32)).astype(BF16)

                self.by_parity(u, act)
                for step in range(1, line):
                    self.line_copy(u, step).start()

            def after_line(self, u):
                value = self.sums[u, pl.ds(pl.multiple_of(z * rows, rows), rows)].astype(F32)
                for step in range(1, line):
                    self.line_copy(u, step).wait_recv()
                    value = value + self.lines[u, step].astype(F32)
                self.totals[u] = value

            def finish(self, u):
                self.core_send(u).wait_send()
                self.first_send(u, u % 2 == 0).wait_send()
                self.last_send(u, u % 2 == 1).wait_send()
                for step in range(1, line):
                    self.line_copy(u, step).wait_send()

        wide_sums = Sums(buffers, 0)
        small_sum = Sums(small_buffers, units)

    def keep(target, u, value):
        for block in range(8):
            target[u, block // 4, block // 2 % 2, block % 2] = value[
                block * block_rows : (block + 1) * block_rows
            ]

    gates = gate_rows[...]
    local = gates.shape[0] // line
    for b in range(line):
        gate_grad_rows[b * local : (b + 1) * local] = gate_grads[b, :local]
    gate_grad = gate_grad_rows[...]
    logit_grad = gates * (gate_grad - jnp.sum(gates * gate_grad, axis=0, keepdims=True))
    high = logit_grad.astype(BF16)
    low = (logit_grad - high.astype(F32)).astype(BF16)
    grad_second = (
        back_rows[...].astype(F32)
        + contract(high, router_rows[...], 0, 0)
        + contract(low, router_rows[...], 0, 0)
    )
    small_rows[...] = jnp.zeros_like(small_rows)
    experts = high.shape[0]
    small_rows[:experts] = contract(high, second_in[...], 1, 0) + contract(low, second_in[...], 1, 0)

    def norm_back(incoming, rows, gain):
        factor = lax.rsqrt(jnp.mean(rows * rows, axis=1, keepdims=True) + EPS)
        normed = rows * factor
        gain_grad = jnp.sum(incoming * normed, axis=0, keepdims=True)
        weighted = incoming * gain
        mean = jnp.mean(weighted * normed, axis=1, keepdims=True)
        return factor * (weighted - normed * mean), gain_grad

    norm_grad, gain_grad = norm_back(grad_second, hidden[...], gain_rows[1:2])
    small_rows[experts + 1 : experts + 2] = gain_grad
    grad_hidden[...] = cots[...].astype(F32) + norm_grad
    branch = grad_hidden[...].astype(BF16)
    for u in range(2):
        keep(
            own,
            u,
            contract(branch, attended[:, u * UNIT : (u + 1) * UNIT], 0, 0).astype(BF16),
        )
        if paired:
            wide_sums.core_send(u).start()
    grad_attended[...] = contract(branch, heads_out[...], 1, 0).astype(BF16)
    loads[0].wait()
    if paired:
        wide_sums.after_core(0)
        relay_on(True, 0)

    def pair(j, _):
        key_pair = keys[:, lanes_at(j * PAIR, PAIR)]
        value_pair = values[:, lanes_at(j * PAIR, PAIR)]
        key_grads = []
        value_grads = []
        for side in range(2):
            at = lanes_at((2 * j + side) * PAIR, PAIR)
            group = queries[:, at]
            group_grad = grad_attended[:, at]
            key_sides = sides(key_pair, side, SCALE)
            value_sides = sides(value_pair, side, None)
            product = group_grad.astype(F32) * attended[:, at].astype(F32)
            lane = lax.broadcasted_iota(jnp.int32, product.shape, 1)
            grad = jnp.zeros(group.shape, F32)
            key_grad = []
            value_grad = []
            for member in range(2):
                head = 4 * j + 2 * side + member
                log_total = jnp.sum(
                    jnp.where(lane == head, log_totals[...], 0.0), axis=1, keepdims=True
                )
                mine = (lane < HEAD_DIM) if member == 0 else (lane >= HEAD_DIM)
                spread = jnp.sum(jnp.where(mine, product, 0.0), axis=1, keepdims=True)
                scores = contract(group, key_sides[member], 1, 1) + bias[...]
                weights = jnp.exp(scores - log_total)
                weight_grads = contract(group_grad, value_sides[member], 1, 1)
                score_grads = (weights * (weight_grads - spread)).astype(BF16)
                grad = grad + contract(score_grads, key_sides[member], 1, 0)
                rows_of = slice(member * HEAD_DIM, (member + 1) * HEAD_DIM)
                key_grad.append(contract(group, score_grads, 0, 0)[rows_of])
                value_grad.append(contract(group_grad, weights.astype(BF16), 0, 0)[rows_of])
            grad_projected[j, :, side * PAIR : (side + 1) * PAIR] = (
                grad * cosine[...] - swap_halves(grad) * sine[...]
            ).astype(BF16)
            key_grads.append(key_grad[0] + key_grad[1])
            value_grads.append(value_grad[0] + value_grad[1])
        key_rows = jnp.concatenate(key_grads, axis=0).T * SCALE
        grad_projected[j, :, 2 * PAIR : 3 * PAIR] = (
            key_rows * cosine[...] - swap_halves(key_rows) * sine[...]
        ).astype(BF16)
        grad_projected[j, :, 3 * PAIR :] = jnp.concatenate(value_grads, axis=0).T.astype(BF16)
        keep(own, 2 + j, contract(first_in[...], grad_projected[j], 0, 0).astype(BF16))
        if paired:
            wide_sums.core_send(2 + j).start()
            wide_sums.after_core(1 + j)

            @pl.when(j >= 2)
            def _():
                wide_sums.after_first(j - 2)

            for at, near, p in ((0, True, 1), (1, True, 2), (2, False, 0), (3, False, 1)):

                @pl.when(j == at)
                def _(near=near, p=p):
                    relay_on(near, p)

        return 0

    pairs = KV_HEADS // 2
    lax.fori_loop(0, pairs, pair, 0)
    last = units - 1
    if paired:
        wide_sums.after_core(last)
        relay_on(False, 2)
        wide_sums.after_first(2)
        wide_sums.after_last(0)
        wide_sums.after_first(3)
        wide_sums.after_last(1)
    loads[1].wait()
    loads[2].wait()
    grad_first = jnp.zeros(grad_hidden.shape, F32)
    query_end = HEADS * HEAD_DIM
    key_end = query_end + KV_HEADS * HEAD_DIM
    for j in range(pairs):
        for at, begin, size in (
            (0, 2 * j * PAIR, 2 * PAIR),
            (2 * PAIR, query_end + j * PAIR, PAIR),
            (3 * PAIR, key_end + j * PAIR, PAIR),
        ):
            grad_first = grad_first + contract(
                grad_projected[j, :, at : at + size], heads_in[:, begin : begin + size], 1, 1
            )
    norm_grad, gain_grad = norm_back(grad_first, tokens[...].astype(F32), gain_rows[0:1])
    small_rows[experts : experts + 1] = gain_grad
    keep(own_small, 0, small_rows[...].T.astype(BF16))
    if paired:
        small_sum.core_send(0).start()
    if paired:
        wide_sums.after_first(4)
        wide_sums.after_last(2)
        small_sum.after_core(0)
        wide_sums.after_first(5)
        wide_sums.after_last(3)
        small_sum.after_first(0)
    token_grad[...] = grad_hidden[...] + norm_grad
    if paired:
        for e in range(bank_hbm.shape[0]):
            bank_kept_copy(e).wait()
            bank_last_copy(e).wait()
            bank_total[e] = bank_kept[e].astype(F32) + bank_last[e].astype(F32)
            bank_total_copy(e).start()

    @pl.when(direct(-1))
    def _():
        total = hidden[...]
        for b in range(line):
            mix_load(b).wait()
            total = total + mixes[b].astype(F32)
        output[...] = total.astype(BF16)

    if paired:
        wide_sums.after_last(4)
        small_sum.after_last(0)
        wide_sums.after_last(5)
        for u in range(units):
            wide_sums.after_line(u)
        small_sum.after_line(0)
        places = [(u, 0, UNIT, key_end + KV_HEADS * HEAD_DIM + u * UNIT) for u in range(2)]
        for j in range(pairs):
            places.append((2 + j, 0, 2 * PAIR, 2 * j * PAIR))
            places.append((2 + j, 2 * PAIR, PAIR, query_end + j * PAIR))
            places.append((2 + j, 3 * PAIR, PAIR, key_end + j * PAIR))
        small_columns[...] = small_totals[0].T
        gain_values = gain_rows[...]
        share = jnp.zeros((2, rows), F32)
        for i in range(gain_values.shape[1] // rows):
            share = jnp.where(
                dp * line + z == i, gain_values[:, i * rows : (i + 1) * rows], share
            )
        small_columns[experts + 2 : experts + 4] = share
        outs = [pltpu.make_async_copy(small_columns, small_hbm, out_sem.at[len(places)])]
        for number, (u, at, size, column) in enumerate(places):
            outs.append(
                pltpu.make_async_copy(
                    totals.at[u, :, at : at + size],
                    sum_hbm.at[:, column : column + size],
                    out_sem.at[number],
                )
            )
    else:
        outs = (
            pltpu.make_async_copy(own, sum_hbm, load_sem.at[3]),
            pltpu.make_async_copy(own_small, small_hbm, load_sem.at[4]),
        )
    for copy in outs:
        copy.start()
    if paired:
        for u in range(units):
            wide_sums.finish(u)
        small_sum.finish(0)
        for e in range(bank_hbm.shape[0]):
            bank_total_copy(e).wait()
        for side in range(2):

            @pl.when(starts[1 - side])
            def _(side=side):
                mix_load(z).wait()
                for p in range(PIECES):
                    chain_send(side, p, late_hbm).wait_recv()
                output[...] = (
                    hidden[...] + mixes[z].astype(F32) + chain_in[side].astype(F32)
                ).astype(BF16)

            @pl.when(jnp.logical_not(starts[1 - side]))
            def _(side=side):
                for p in range(PIECES):
                    chain_send(side, p, late_hbm).wait_send()

    for copy in outs:
        copy.wait()


def attend_back(held_args, far_args, paired, line):
    tokens, first_in, heads_in = far_args[:3]
    count, width = tokens.shape
    pairs = KV_HEADS // 2
    units = 2 + pairs
    block_rows = width // 8
    rows = block_rows // line
    shape = jax.ShapeDtypeStruct
    held = pl.BlockSpec(memory_space=pltpu.VMEM)
    anywhere = pl.BlockSpec(memory_space=pl.ANY)
    if paired:
        sum_shapes = (shape((rows, units * UNIT), F32), shape((128, rows), F32))
    else:
        sum_shapes = (
            shape((units, 2, 2, 2, block_rows, UNIT), BF16),
            shape((1, 2, 2, 2, block_rows, 128), BF16),
        )
    exchange = []
    if paired:
        for number, lanes in ((units, UNIT), (1, 128)):
            exchange += [
                pltpu.VMEM((number, 2, 2, block_rows, lanes), BF16),
                pltpu.VMEM((number, 2, block_rows, lanes), BF16),
                pltpu.VMEM((number, block_rows, lanes), BF16),
                pltpu.VMEM((number, block_rows, lanes), BF16),
                pltpu.VMEM((number, line, rows, lanes), BF16),
                pltpu.VMEM((number, rows, lanes), F32),
            ]
        exchange += [
            pltpu.SemaphoreType.DMA((3, units + 1)),
            pltpu.SemaphoreType.DMA((3, units + 1)),
            pltpu.SemaphoreType.DMA((units + 1, line)),
            pltpu.SemaphoreType.DMA((units + 1, line)),
            pltpu.SemaphoreType.DMA((3 + 3 * pairs,)),
        ]
        bank_shape = (far_args[5].shape[0],) + far_args[5].shape[2:]
        sum_shapes += (shape(bank_shape, F32),)
        exchange += [
            pltpu.VMEM(bank_shape, BF16),
            pltpu.VMEM(bank_shape, BF16),
            pltpu.VMEM(bank_shape, F32),
            pltpu.SemaphoreType.DMA((4, bank_shape[0])),
            pltpu.VMEM((128, rows), F32),
            pltpu.VMEM((2, count, width), BF16),
            pltpu.VMEM((2, count, width), BF16),
            pltpu.VMEM((2, count, width), BF16),
            pltpu.SemaphoreType.DMA((2,)),
            pltpu.SemaphoreType.DMA((2, 2, PIECES)),
        ]
    settings = dict(vmem_limit_bytes=VMEM_MOST)
    if paired:
        settings.update(collective_id=3, has_side_effects=True)
    return pl.pallas_call(
        functools.partial(attend_back_kernel, paired, line),
        out_shape=(shape((count, width), BF16), shape((count, width), F32)) + sum_shapes,
        in_specs=[held] * len(held_args) + [anywhere] * len(far_args),
        out_specs=(held, held) + (anywhere,) * len(sum_shapes),
        scratch_shapes=[
            pltpu.VMEM((count, width), BF16),
            pltpu.VMEM((count, width), BF16),
            pltpu.VMEM(heads_in.shape, BF16),
            pltpu.VMEM((line, count, width), BF16),
            pltpu.VMEM(held_args[4].shape, F32),
            pltpu.VMEM((count, width), F32),
            pltpu.VMEM((count, HEADS * HEAD_DIM), BF16),
            pltpu.VMEM((pairs, count, 4 * PAIR), BF16),
            pltpu.VMEM((128, width), F32),
            pltpu.VMEM((units, 2, 2, 2, block_rows, UNIT), BF16),
            pltpu.VMEM((1, 2, 2, 2, block_rows, 128), BF16),
            pltpu.SemaphoreType.DMA((5 + line,)),
            *exchange,
        ],
        compiler_params=pltpu.CompilerParams(**settings),
        cost_estimate=pl.CostEstimate(flops=2**34, bytes_accessed=2**25, transcendentals=2**21),
    )(*held_args, *far_args)


def unit_columns(sums):
    pairs = KV_HEADS // 2
    parts = sums[2 : 2 + pairs]
    rows = sums.shape[1]

    def side_by_side(value):
        return jnp.transpose(value, (1, 0, 2)).reshape(rows, -1)

    return (
        jnp.concatenate(
            [
                side_by_side(parts[:, :, : 2 * PAIR]),
                side_by_side(parts[:, :, 2 * PAIR : 3 * PAIR]),
                side_by_side(parts[:, :, 3 * PAIR :]),
            ],
            axis=1,
        ),
        side_by_side(sums[:2]),
    )


def update_kernel(width, experts, bank_sum, head_sum, small_rows, *refs):
    lanes = refs[0].shape[2]
    gradients = (
        bank_sum[0, :, :lanes],
        bank_sum[0, :, lanes:],
        head_sum[:, :width],
        head_sum[:, width:],
        small_rows[:experts],
        small_rows[experts : experts + 2],
    )
    count = len(gradients)
    for number, gradient in enumerate(gradients):
        held = refs[3 * number : 3 * number + 3]
        if number == count - 1:
            held = (small_rows.at[experts + 2 : experts + 4], *held[1:])
        results = refs[3 * (count + number) : 3 * (count + number) + 3]
        at = (0,) if held[0].ndim == 3 else (Ellipsis,)
        values = update(gradient, *(ref[at] for ref in held))
        for ref, value in zip(results, values):
            ref[at] = value


def update_all(bank_sum, head_sum, small_rows, states):
    experts, block_rows, _ = bank_sum.shape
    rows = head_sum.shape[0] // experts

    def spec(value):
        if value.ndim == 3:
            return pl.BlockSpec((1, block_rows, value.shape[2]), lambda i: (i, 0, 0))
        if value.shape[0] == head_sum.shape[0] and value.shape[1] > 128:
            return pl.BlockSpec((rows, value.shape[1]), lambda i: (i, 0))
        return pl.BlockSpec(value.shape, lambda i: (0, 0))

    flat = [value for state in states for value in state]
    results = pl.pallas_call(
        functools.partial(update_kernel, states[2][0].shape[1], states[4][0].shape[0]),
        grid=(experts,),
        out_shape=tuple(jax.ShapeDtypeStruct(value.shape, F32) for value in flat),
        in_specs=[spec(value) for value in (bank_sum, head_sum, small_rows, *flat)],
        out_specs=tuple(spec(value) for value in flat),
        compiler_params=pltpu.CompilerParams(vmem_limit_bytes=VMEM_MOST),
        cost_estimate=pl.CostEstimate(flops=2**23, bytes_accessed=25 * 2**20, transcendentals=0),
    )(bank_sum, head_sum, small_rows, *flat)
    return [tuple(results[i : i + 3]) for i in range(0, len(flat), 3)]


def body(
    tokens,
    cotangent,
    routes,
    cont_ids,
    norm_gains,
    gains_moment,
    gains_average,
    heads_in,
    heads_in_master,
    heads_in_moment,
    heads_in_average,
    heads_out,
    heads_out_master,
    heads_out_moment,
    heads_out_average,
    router,
    router_master,
    router_moment,
    router_average,
    expert_in,
    expert_in_master,
    expert_in_moment,
    expert_in_average,
    expert_out,
    expert_out_master,
    expert_out_moment,
    expert_out_average,
):
    token_count, model_width = tokens.shape
    local_experts = expert_in.shape[0]
    peer_count = lax.axis_size("expert")
    experts = local_experts * peer_count
    paired = lax.axis_size("dp") == 8 and peer_count == 4
    half = HEAD_DIM // 2
    powers = [THETA ** (-2.0 * (lane % half) / HEAD_DIM) for lane in range(128)]
    frequencies = jnp.asarray(np.array(powers, np.float32)[None])
    gain_rows = norm_gains.T
    router_rows = router.T
    (
        first_in,
        queries,
        key_rows,
        value_rows,
        attended,
        hidden,
        second_in,
        gates,
        log_totals,
        cosine,
        sine,
        bias,
        cots_all,
        mix_all,
        mix_late,
        grad_part,
        gate_grads,
        gated,
        grad_gate_up,
        rows_all,
    ) = front(
        paired,
        tokens,
        cotangent,
        gain_rows,
        heads_in,
        heads_out,
        router_rows,
        routes.T,
        cont_ids,
        frequencies,
        expert_in,
        expert_out,
        peer_count,
        token_count - cont_ids.shape[1],
    )
    back_rows = lax.psum_scatter(
        grad_part.reshape(peer_count * token_count, model_width),
        "expert",
        scatter_dimension=0,
        tiled=True,
    )
    grad_sources = (
        rows_all.reshape(peer_count * token_count, model_width),
        cots_all.reshape(peer_count * token_count, model_width),
        gated.reshape(peer_count * token_count, -1),
        grad_gate_up.reshape(peer_count * token_count, -1),
    )
    if paired:
        expert_sums = (bank_grads(*grad_sources, local_experts),)
    else:
        expert_sums = tuple(
            lax.psum_scatter(part, "dp", scatter_dimension=1, tiled=True).astype(jnp.float32)
            for part in weight_grads(*grad_sources, local_experts)
        )
    output, token_grad, unit_sums, small_sum, *bank_sums = attend_back(
        (
            back_rows,
            hidden,
            cotangent,
            second_in,
            gates,
            gate_grads,
            router_rows,
            gain_rows,
            heads_out,
            queries,
            key_rows,
            value_rows,
            attended,
            log_totals,
            cosine,
            sine,
            bias,
        ),
        (tokens, first_in, heads_in, mix_all, mix_late, *(expert_sums if paired else ())),
        paired,
        peer_count,
    )
    if paired:
        gains_share = gains_moment.T
    else:
        shard_rows = model_width // lax.axis_size(("dp", "expert"))
        gains_share = lax.dynamic_slice_in_dim(
            gain_rows, lax.axis_index(("dp", "expert")) * shard_rows, shard_rows, 1
        )
    states = (
        (expert_in_master, expert_in_moment, expert_in_average),
        (expert_out_master, expert_out_moment, expert_out_average),
        (heads_in_master, heads_in_moment, heads_in_average),
        (heads_out_master, heads_out_moment, heads_out_average),
        (router_master.T, router_moment.T, router_average.T),
        (gains_share, gains_moment.T, gains_average.T),
    )
    if paired:
        news = update_all(bank_sums[0], unit_sums, small_sum, states)
    else:
        head_parts = unit_columns(unit_sums.reshape(unit_sums.shape[0], model_width, UNIT))
        packed = jnp.concatenate([*head_parts, small_sum.reshape(model_width, 128)], axis=1)
        head_total = lax.psum_scatter(
            packed, ("dp", "expert"), scatter_dimension=0, tiled=True
        ).astype(jnp.float32)
        cut_in = head_parts[0].shape[1]
        cut_out = cut_in + head_parts[1].shape[1]
        small_rows = head_total[:, cut_out:].T
        sums = (
            *expert_sums,
            head_total[:, :cut_in],
            head_total[:, cut_in:cut_out],
            small_rows[:experts],
            small_rows[experts : experts + 2],
        )
        news = [update(gradient, *state) for gradient, state in zip(sums, states)]
    upper_new, lower_new, inproj_new, outproj_new, router_new, gains_new = news
    router_new = tuple(value.T for value in router_new)
    gains_new = tuple(value.T for value in gains_new)
    return (
        output,
        token_grad,
        gains_new[0],
        gains_new[1],
        gains_new[2],
        inproj_new[0],
        inproj_new[1],
        inproj_new[2],
        outproj_new[0],
        outproj_new[1],
        outproj_new[2],
        router_new[0],
        router_new[1],
        router_new[2],
        upper_new[0],
        upper_new[1],
        upper_new[2],
        lower_new[0],
        lower_new[1],
        lower_new[2],
    )


def solution(mesh):
    return jax.shard_map(
        body,
        mesh=mesh,
        in_specs=(
            P(("dp", "expert"), None),
            P(("dp", "expert"), None),
            P(("dp", "expert"), None),
            P(("dp", "expert"), None),
            P(),
            P(("dp", "expert"), None),
            P(("dp", "expert"), None),
            P(),
            P(("dp", "expert"), None),
            P(("dp", "expert"), None),
            P(("dp", "expert"), None),
            P(),
            P(("dp", "expert"), None),
            P(("dp", "expert"), None),
            P(("dp", "expert"), None),
            P(),
            P(("dp", "expert"), None),
            P(("dp", "expert"), None),
            P(("dp", "expert"), None),
            P("expert", None, None),
            P("expert", "dp", None),
            P("expert", "dp", None),
            P("expert", "dp", None),
            P("expert", None, None),
            P("expert", "dp", None),
            P("expert", "dp", None),
            P("expert", "dp", None),
        ),
        out_specs=(
            P(("dp", "expert"), None),
            P(("dp", "expert"), None),
            P(("dp", "expert"), None),
            P(("dp", "expert"), None),
            P(("dp", "expert"), None),
            P(("dp", "expert"), None),
            P(("dp", "expert"), None),
            P(("dp", "expert"), None),
            P(("dp", "expert"), None),
            P(("dp", "expert"), None),
            P(("dp", "expert"), None),
            P(("dp", "expert"), None),
            P(("dp", "expert"), None),
            P(("dp", "expert"), None),
            P("expert", "dp", None),
            P("expert", "dp", None),
            P("expert", "dp", None),
            P("expert", "dp", None),
            P("expert", "dp", None),
            P("expert", "dp", None),
        ),
        check_vma=False,
    )
```

```python
import functools

import jax
import jax.numpy as jnp
import numpy as np
from jax import lax
from jax.experimental import pallas as pl
from jax.experimental.pallas import tpu as pltpu
from jax.sharding import PartitionSpec as P

HEADS = 16
KV_HEADS = 8
HEAD_DIM = 64


EPS = 1e-06
SCALE = 0.015625
THETA = 10000.0
MOMENTUM = 0.9
DECAY = 0.8
RATE = 0.001
HIGHEST = lax.Precision.HIGHEST


def update(gradient, master, moment, average):
    moment_next = MOMENTUM * moment + gradient
    master_next = master - RATE * (gradient + MOMENTUM * moment_next)
    return (master_next, moment_next, DECAY * average + (1.0 - DECAY) * master_next)


F32 = jnp.float32
BF16 = jnp.bfloat16
MESH = pl.DeviceIdType.MESH
VMEM_MOST = 61 * 2**20


def contract(left, right, left_axis, right_axis):
    return lax.dot_general(
        left, right, (((left_axis,), (right_axis,)), ((), ())), preferred_element_type=F32
    )


def visit_order(line):
    return [sorted(range(line), key=lambda s: (abs(s - z), s)) for z in range(line)]


def line_gather(line, z, dp, source, landing, send_sem, recv_sem):
    def copy(origin, block, sem, target):
        return pltpu.make_async_remote_copy(
            src_ref=origin,
            dst_ref=landing.at[block],
            send_sem=send_sem.at[sem],
            recv_sem=recv_sem.at[block],
            device_id=(dp, target),
            device_id_type=MESH,
        )

    def start():
        @pl.when(z < line - 1)
        def _():
            copy(source, z, line, z + 1).start()

        @pl.when(z > 0)
        def _():
            copy(source, z, line + 1, z - 1).start()

    def pass_on(apart):
        low = jnp.maximum(z - apart, 0)
        high = jnp.minimum(z + apart, line - 1)

        @pl.when(z - apart >= 0)
        def _():
            copy(source, low, low, z).wait_recv()

            @pl.when(z < line - 1)
            def _():
                copy(landing.at[low], low, low, z + 1).start()

        @pl.when(z + apart < line)
        def _():
            copy(source, high, high, z).wait_recv()

            @pl.when(z > 0)
            def _():
                copy(landing.at[high], high, high, z - 1).start()

    def finish():
        @pl.when(z < line - 1)
        def _():
            copy(source, z, line, z + 1).wait_send()

        @pl.when(z > 0)
        def _():
            copy(source, z, line + 1, z - 1).wait_send()

        for s in range(line):

            @pl.when(((s < z) & (z < line - 1)) | ((s > z) & (z > 0)))
            def _(s=s):
                copy(source, s, s, z).wait_send()

    return start, pass_on, finish


def pass_steps(line, experts):
    steps = []
    for z in range(line):
        order = visit_order(line)[z]
        for apart in range(1, line):
            met = [k for k in range(line) if abs(order[k] - z) == apart]
            if not met:
                continue
            forwards = (z - apart >= 0 and z < line - 1) or (z + apart < line and z > 0)
            early = experts // 2 if forwards and apart > 1 else 0
            steps.append((z, met[0] * experts - early, apart))
    return steps


def pick(table, row, column):
    value = jnp.int32(table[0][0])
    for r in range(len(table)):
        for c in range(len(table[0])):
            value = jnp.where((row == r) & (column == c), jnp.int32(table[r][c]), value)
    return value


def weight_grads_kernel(rows, cots, gated, inner, up_grad, down_grad):
    step = 256
    for at in range(0, rows.shape[1], step):
        up_grad[0, at : at + step] = contract(rows[:, at : at + step], inner[...], 0, 0).astype(BF16)
        down_grad[0, at : at + step] = contract(cots[:, at : at + step], gated[...], 0, 0).astype(
            BF16
        )


def weight_grads(rows, cots, gated, inner, experts):
    tokens, width = rows.shape
    ff_width = gated.shape[1] // experts
    whole = pl.BlockSpec((tokens, width), lambda e: (0, 0))
    return pl.pallas_call(
        weight_grads_kernel,
        grid=(experts,),
        out_shape=(
            jax.ShapeDtypeStruct((experts, width, 2 * ff_width), BF16),
            jax.ShapeDtypeStruct((experts, width, ff_width), BF16),
        ),
        in_specs=[
            whole,
            whole,
            pl.BlockSpec((tokens, ff_width), lambda e: (0, e)),
            pl.BlockSpec((tokens, 2 * ff_width), lambda e: (0, e)),
        ],
        out_specs=(
            pl.BlockSpec((1, width, 2 * ff_width), lambda e: (e, 0, 0)),
            pl.BlockSpec((1, width, ff_width), lambda e: (e, 0, 0)),
        ),
        compiler_params=pltpu.CompilerParams(vmem_limit_bytes=VMEM_MOST),
        cost_estimate=pl.CostEstimate(
            flops=6 * tokens * width * experts * ff_width,
            bytes_accessed=2 * tokens * (2 * width + 3 * experts * ff_width)
            + 6 * experts * width * ff_width,
            transcendentals=0,
        ),
    )(rows, cots, gated, inner)


def bank_grads_kernel(
    rows_hbm,
    cots_hbm,
    gated_hbm,
    inner_hbm,
    sum_hbm,
    rows,
    cots,
    gated,
    inner,
    grads,
    core_sum,
    first_sum,
    load_sem,
    send_sem,
    recv_sem,
    out_sem,
):
    experts = grads.shape[0]
    ff_width = gated.shape[2]
    block_rows = grads.shape[4]
    dp = lax.axis_index("dp")
    z = lax.axis_index("expert")
    y, x, core = dp // 4, lax.rem(dp // 2, 2), lax.rem(dp, 2)
    core_peer, x_peer, y_peer = dp + 1 - 2 * core, dp + 2 - 4 * x, dp + 4 - 8 * y

    def loads(e, slot):
        return (
            pltpu.make_async_copy(
                gated_hbm.at[:, pl.ds(pl.multiple_of(e * ff_width, ff_width), ff_width)],
                gated.at[slot],
                load_sem.at[slot, 0],
            ),
            pltpu.make_async_copy(
                inner_hbm.at[:, pl.ds(pl.multiple_of(2 * e * ff_width, ff_width), 2 * ff_width)],
                inner.at[slot],
                load_sem.at[slot, 1],
            ),
        )

    row_load = pltpu.make_async_copy(rows_hbm, rows, load_sem.at[0, 2])
    cot_load = pltpu.make_async_copy(cots_hbm, cots, load_sem.at[1, 2])
    row_load.start()
    for copy in loads(0, 0):
        copy.start()
    cot_load.start()
    barrier = pltpu.get_barrier_semaphore()
    for peer in (core_peer, x_peer, y_peer):
        pl.semaphore_signal(barrier, inc=1, device_id=(peer, z), device_id_type=MESH)
    pl.semaphore_wait(barrier, 3)
    row_load.wait()
    cot_load.wait()

    def send(stage, e, source, target, peer):
        return pltpu.make_async_remote_copy(
            src_ref=source,
            dst_ref=target,
            send_sem=send_sem.at[stage, e],
            recv_sem=recv_sem.at[stage, e],
            device_id=(peer, z),
            device_id_type=MESH,
        )

    def core_send(e):
        return send(0, e, grads.at[e, :, :, 1 - core], core_sum.at[e], core_peer)

    def first_send(e, along_x):
        if along_x:
            return send(1, e, core_sum.at[e, :, 1 - x], first_sum.at[e], x_peer)
        return send(1, e, core_sum.at[e, 1 - y], first_sum.at[e], y_peer)

    def by_parity(e, act):
        even = lax.rem(e, 2) == 0

        @pl.when(even)
        def _():
            act(True)

        @pl.when(jnp.logical_not(even))
        def _():
            act(False)

    def after_core(e):
        core_send(e).wait_recv()
        for yy in range(2):
            for xx in range(2):
                core_sum[e, yy, xx] = (
                    grads[e, yy, xx, core].astype(F32) + core_sum[e, yy, xx].astype(F32)
                ).astype(BF16)
        by_parity(e, lambda even: first_send(e, even).start())

    def after_first(e):
        def act(even):
            first_send(e, even).wait_recv()
            for other in range(2):
                kept = core_sum[e, other, x] if even else core_sum[e, y, other]
                first_sum[e, other] = (
                    kept.astype(F32) + first_sum[e, other].astype(F32)
                ).astype(BF16)

        by_parity(e, act)
        pltpu.make_async_copy(first_sum.at[e], sum_hbm.at[e], out_sem.at[e]).start()

    def step(e, _):
        slot = lax.rem(e, 2)
        for copy in loads(e, slot):
            copy.wait()

        @pl.when(e + 1 < experts)
        def _():
            for copy in loads(e + 1, 1 - slot):
                copy.start()

        def tile(at, _):
            columns = pl.ds(pl.multiple_of(at * 2 * block_rows, 2 * block_rows), 2 * block_rows)
            up_grad = contract(rows[:, columns], inner[slot], 0, 0).astype(BF16)
            down_grad = contract(cots[:, columns], gated[slot], 0, 0).astype(BF16)
            for side in range(2):
                part = slice(side * block_rows, (side + 1) * block_rows)
                grads[e, at // 2, lax.rem(at, 2), side, :, : 2 * ff_width] = up_grad[part]
                grads[e, at // 2, lax.rem(at, 2), side, :, 2 * ff_width :] = down_grad[part]
            return 0

        lax.fori_loop(0, 4, tile, 0)
        core_send(e).start()

        @pl.when(e >= 1)
        def _():
            after_core(e - 1)

        @pl.when(e >= 3)
        def _():
            after_first(e - 3)

        return 0

    lax.fori_loop(0, experts, step, 0)
    after_core(experts - 1)

    for e in range(max(experts - 3, 0), experts):
        after_first(e)
    for e in range(experts):
        core_send(e).wait_send()
        first_send(e, e % 2 == 0).wait_send()
        pltpu.make_async_copy(first_sum.at[e], sum_hbm.at[e], out_sem.at[e]).wait()


def bank_grads(rows, cots, gated, inner, experts):
    tokens, width = rows.shape
    ff_width = gated.shape[1] // experts
    lanes = 3 * ff_width
    block_rows = width // 8
    anywhere = pl.BlockSpec(memory_space=pl.ANY)
    return pl.pallas_call(
        bank_grads_kernel,
        out_shape=jax.ShapeDtypeStruct((experts, 2, block_rows, lanes), BF16),
        in_specs=[anywhere] * 4,
        out_specs=anywhere,
        scratch_shapes=[
            pltpu.VMEM((tokens, width), BF16),
            pltpu.VMEM((tokens, width), BF16),
            pltpu.VMEM((2, tokens, ff_width), BF16),
            pltpu.VMEM((2, tokens, 2 * ff_width), BF16),
            pltpu.VMEM((experts, 2, 2, 2, block_rows, lanes), BF16),
            pltpu.VMEM((experts, 2, 2, block_rows, lanes), BF16),
            pltpu.VMEM((experts, 2, block_rows, lanes), BF16),
            pltpu.SemaphoreType.DMA((2, 3)),
            pltpu.SemaphoreType.DMA((2, experts)),
            pltpu.SemaphoreType.DMA((2, experts)),
            pltpu.SemaphoreType.DMA((experts,)),
        ],
        compiler_params=pltpu.CompilerParams(
            collective_id=2, has_side_effects=True, vmem_limit_bytes=VMEM_MOST
        ),
        cost_estimate=pl.CostEstimate(
            flops=6 * tokens * width * experts * ff_width,
            bytes_accessed=2**27,
            transcendentals=0,
        ),
    )(rows, cots, gated, inner)


PAIR = 2 * HEAD_DIM
UNIT = 512
PIECES = 3


def swap_halves(value):
    lane = lax.broadcasted_iota(jnp.int32, value.shape, 1)
    half = HEAD_DIM // 2
    return jnp.where(
        lax.rem(lane, HEAD_DIM) < half,
        pltpu.roll(value, value.shape[1] - half, 1),
        pltpu.roll(value, half, 1),
    )


def sides(pair, side, scale):
    value = pair.astype(F32)
    if scale is not None:
        value = value * scale
    turned = pltpu.roll(value, HEAD_DIM, 1)
    lane = lax.broadcasted_iota(jnp.int32, value.shape, 1)
    left, right = (value, turned) if side == 0 else (turned, value)
    return (
        jnp.where(lane < HEAD_DIM, left, 0.0).astype(BF16),
        jnp.where(lane < HEAD_DIM, 0.0, right).astype(BF16),
    )


def lanes_at(start, size):
    return pl.ds(pl.multiple_of(start, 128), size)


def front_kernel(
    line,
    prompt,
    late,
    tokens,
    cots_hbm,
    gain_rows,
    heads_in_hbm,
    heads_out_hbm,
    router_rows,
    route_rows,
    label_row,
    frequencies,
    up_hbm,
    down_hbm,
    first_in_hbm,
    queries_hbm,
    keys_hbm,
    values_hbm,
    attended_hbm,
    hidden_hbm,
    second_in_hbm,
    gate_rows,
    log_totals,
    cosine_hbm,
    sine_hbm,
    bias_hbm,
    cots_all,
    mix_all,
    mix_late,
    back_hbm,
    gate_grads_hbm,
    gated_hbm,
    inner_hbm,
    rows_all_hbm,
    cots,
    rows,
    gates_own,
    gates,
    gate_grads,
    gate_grads_sent,
    up,
    down,
    projected,
    stage,
    mix_stage,
    gated,
    inner,
    columns,
    cot_send,
    cot_recv,
    row_send,
    row_recv,
    gate_send,
    gate_recv,
    weight_sem,
    local_sem,
    out_sem,
    grad_send,
    grad_recv,
    mix_send,
    mix_recv,
    heads_in,
    heads_out,
    first_in,
    queries,
    keys,
    values,
    attended,
    hidden,
    second_in,
    cosine,
    sine,
    bias,
    held_sem,
    row_out_sem,
):
    dp = lax.axis_index("dp")
    z = lax.axis_index("expert")
    experts, _, ff_width = down_hbm.shape
    start_cots, pass_cots, finish_cots = line_gather(
        line, z, dp, cots_hbm, cots_all, cot_send, cot_recv
    )
    start_rows, pass_rows, finish_rows = line_gather(
        line, z, dp, second_in, rows, row_send, row_recv
    )

    heads_in_load = pltpu.make_async_copy(heads_in_hbm, heads_in, held_sem.at[0])
    heads_out_load = pltpu.make_async_copy(heads_out_hbm, heads_out, held_sem.at[1])
    held_out = [
        pltpu.make_async_copy(source, target, held_sem.at[2 + number])
        for number, (source, target) in enumerate(
            (
                (first_in, first_in_hbm),
                (queries, queries_hbm),
                (keys, keys_hbm),
                (values, values_hbm),
                (attended, attended_hbm),
                (hidden, hidden_hbm),
                (second_in, second_in_hbm),
                (cosine, cosine_hbm),
                (sine, sine_hbm),
                (bias, bias_hbm),
            )
        )
    ]

    def weight_copies(e):
        return (
            pltpu.make_async_copy(
                up_hbm.at[e],
                up.at[:, pl.ds(pl.multiple_of(e * 2 * ff_width, ff_width), 2 * ff_width)],
                weight_sem.at[0, e],
            ),
            pltpu.make_async_copy(
                down_hbm.at[e],
                down.at[:, pl.ds(pl.multiple_of(e * ff_width, ff_width), ff_width)],
                weight_sem.at[1, e],
            ),
        )

    barrier = pltpu.get_barrier_semaphore()
    for step in range(1, line):
        pl.semaphore_signal(
            barrier, inc=1, device_id=(dp, lax.rem(z + step, line)), device_id_type=MESH
        )
    pl.semaphore_wait(barrier, line - 1)
    start_cots()
    cots_in = pltpu.make_async_copy(cots_hbm, cots, local_sem.at[2])
    cots_in.start()
    heads_in_load.start()
    heads_out_load.start()
    for e in range(experts):
        for copy in weight_copies(e):
            copy.start()

    query_end = HEADS * HEAD_DIM
    key_end = query_end + KV_HEADS * HEAD_DIM
    token_rows = tokens[...].astype(F32)
    factor = lax.rsqrt(jnp.mean(token_rows * token_rows, axis=1, keepdims=True) + EPS)
    first_in[...] = (token_rows * factor * gain_rows[0:1]).astype(BF16)
    log_totals[...] = jnp.zeros_like(log_totals)
    cots_in.wait()
    own_cots = pltpu.make_async_copy(cots, cots_all.at[z], local_sem.at[0])
    own_cots.start()

    labels = label_row[...].astype(F32)
    size = labels.shape[1]
    square = jnp.broadcast_to(labels, (size, size))
    upright = square.T
    earlier = jnp.sum(jnp.where(square < upright, 1.0, 0.0), axis=1, keepdims=True)
    place = lax.broadcasted_iota(jnp.int32, (token_rows.shape[0], 128), 0).astype(F32)
    shift = jnp.concatenate([jnp.zeros((prompt, 1), F32), earlier], axis=0)
    angles = (place - shift) * frequencies[...]
    lane = lax.broadcasted_iota(jnp.int32, angles.shape, 1)
    sines = jnp.sin(angles)
    cosine[...] = jnp.cos(angles)
    sine[...] = jnp.where(lax.rem(lane, HEAD_DIM) < HEAD_DIM // 2, -sines, sines)
    own_label = jnp.concatenate([jnp.full((prompt, 1), -1.0, F32), upright[:, :1]], axis=0)
    seen_label = jnp.concatenate([jnp.full((1, prompt), -1.0, F32), labels], axis=1)
    row = lax.broadcasted_iota(jnp.int32, bias.shape, 0)
    column = lax.broadcasted_iota(jnp.int32, bias.shape, 1)
    allowed = (column <= row) & ((column < prompt) | (own_label == seen_label))
    bias[...] = jnp.where(allowed, 0.0, -1e30)
    heads_in_load.wait()

    def project(i, _):
        at = lanes_at(i * UNIT, UNIT)
        projected[:, at] = contract(first_in[...], heads_in[:, at], 1, 0)
        return 0

    lax.fori_loop(0, heads_in.shape[1] // UNIT, project, 0)

    def pair(j, _):
        for side in range(2):
            at = lanes_at((2 * j + side) * PAIR, PAIR)
            wide = projected[:, at]
            queries[:, at] = (wide * cosine[...] + swap_halves(wide) * sine[...]).astype(BF16)
        wide = projected[:, lanes_at(query_end + j * PAIR, PAIR)]
        keys[:, lanes_at(j * PAIR, PAIR)] = (
            wide * cosine[...] + swap_halves(wide) * sine[...]
        ).astype(BF16)
        values[:, lanes_at(j * PAIR, PAIR)] = projected[
            :, lanes_at(key_end + j * PAIR, PAIR)
        ].astype(BF16)
        heads = [(side, member) for side in range(2) for member in range(2)]
        groups = [queries[:, lanes_at((2 * j + side) * PAIR, PAIR)] for side in range(2)]
        key_sides = [sides(keys[:, lanes_at(j * PAIR, PAIR)], side, SCALE) for side in range(2)]
        value_sides = [sides(values[:, lanes_at(j * PAIR, PAIR)], side, None) for side in range(2)]
        parts = ((0, prompt, prompt), (prompt, groups[0].shape[0], groups[0].shape[0]))

        def scores_of(side, member):
            return [
                contract(groups[side][begin:end], key_sides[side][member][:seen], 1, 1)
                + bias[begin:end, :seen]
                for begin, end, seen in parts
            ]

        lane = lax.broadcasted_iota(jnp.int32, log_totals.shape, 1)
        added = jnp.zeros(log_totals.shape, F32)
        sums = [0.0, 0.0]
        scores = scores_of(*heads[0])
        for number, (side, member) in enumerate(heads):
            following = scores_of(*heads[number + 1]) if number + 1 < len(heads) else None
            mixed = []
            totals = []
            for part, (_, _, seen) in zip(scores, parts):
                peak = jnp.max(part, axis=1, keepdims=True)
                powers = jnp.exp(part - peak)
                amount = jnp.sum(powers, axis=1, keepdims=True)
                weights = (powers * (1.0 / amount)).astype(BF16)
                totals.append(peak + jnp.log(amount))
                mixed.append(contract(weights, value_sides[side][member][:seen], 1, 0))
            sums[side] = sums[side] + jnp.concatenate(mixed, axis=0)
            added = jnp.where(lane == 4 * j + number, jnp.concatenate(totals, axis=0), added)
            scores = following
        log_totals[...] += added
        for side in range(2):
            attended[:, lanes_at((2 * j + side) * PAIR, PAIR)] = sums[side].astype(BF16)
        return 0

    lax.fori_loop(0, KV_HEADS // 2, pair, 0)
    heads_out_load.wait()
    hidden_rows = token_rows + contract(attended[...], heads_out[...], 1, 1)
    hidden[...] = hidden_rows
    factor = lax.rsqrt(jnp.mean(hidden_rows * hidden_rows, axis=1, keepdims=True) + EPS)
    second = (hidden_rows * factor * gain_rows[1:2]).astype(BF16)
    second_in[...] = second
    start_rows()
    for copy in held_out:
        copy.start()
    own_rows = pltpu.make_async_copy(second_in, rows.at[z], local_sem.at[1])
    own_rows.start()
    logits = contract(router_rows[...], second, 1, 1)
    expert = lax.broadcasted_iota(jnp.int32, logits.shape, 0)
    named = expert == route_rows[0:1]
    for k in range(1, route_rows.shape[0]):
        named = named | (expert == route_rows[k : k + 1])
    peak = jnp.max(jnp.where(named, logits, -1e30), axis=0, keepdims=True)
    powers = jnp.where(named, jnp.exp(jnp.where(named, logits, peak) - peak), 0.0)
    gate_values = powers / jnp.sum(powers, axis=0, keepdims=True)
    gate_rows[...] = gate_values
    gates_own[...] = jnp.zeros_like(gates_own)
    for peer in range(line):
        gates_own[peer, :experts] = gate_values[peer * experts : (peer + 1) * experts]
    gates[z] = gates_own[z]
    def gate_copy(step):
        peer = lax.rem(z + step, line)
        return pltpu.make_async_remote_copy(
            src_ref=gates_own.at[peer],
            dst_ref=gates.at[z],
            send_sem=gate_send.at[step],
            recv_sem=gate_recv.at[step],
            device_id=(dp, peer),
            device_id_type=MESH,
        )

    for step in range(1, line):
        gate_copy(step).start()
    own_rows.wait()
    own_cots.wait()
    pass_cots(1)
    for step in range(1, line):
        gate_copy(step).wait()

    order = visit_order(line)

    def out_copies(slot, block):
        return (
            pltpu.make_async_copy(stage.at[slot], back_hbm.at[block], out_sem.at[slot, 0]),
            pltpu.make_async_copy(gated.at[slot], gated_hbm.at[block], out_sem.at[slot, 1]),
            pltpu.make_async_copy(inner.at[slot], inner_hbm.at[block], out_sem.at[slot, 2]),
        )

    def mix_copy(block, source, target):
        return pltpu.make_async_remote_copy(
            src_ref=mix_stage.at[block],
            dst_ref=mix_all.at[source],
            send_sem=mix_send.at[block],
            recv_sem=mix_recv.at[source],
            device_id=(dp, target),
            device_id_type=MESH,
        )

    def row_out(block):
        return pltpu.make_async_copy(rows.at[block], rows_all_hbm.at[block], row_out_sem.at[block])

    def own_mix():
        return pltpu.make_async_copy(mix_stage.at[z], mix_all.at[z], local_sem.at[3])

    def late_mix(side):
        return pltpu.make_async_copy(
            mix_stage.at[side * (line - 1)], mix_late.at[side], local_sem.at[4 + side]
        )

    def at_end(block):
        return (block == 0) | (block == line - 1)

    def grad_copy(block, step):
        return pltpu.make_async_remote_copy(
            src_ref=gate_grads_sent.at[block],
            dst_ref=gate_grads.at[z],
            send_sem=grad_send.at[block],
            recv_sem=grad_recv.at[z],
            device_id=(dp, block),
            device_id_type=MESH,
        )

    def visit(k, _):
        block = pick(order, z, k)
        slot = lax.rem(k, 2)
        @pl.when(k >= 2)
        def _():
            for copy in out_copies(slot, pick(order, z, jnp.maximum(k - 2, 0))):
                copy.wait()

        cot_load = pltpu.make_async_copy(cots_all.at[block], cots, local_sem.at[2])
        gate_columns = gates[block].T
        tile = min(ff_width, 256)
        def arrive(e):
            step = k * experts + e
            apart = jnp.int32(0)
            for at_z, at_step, distance in pass_steps(line, experts):
                apart = jnp.where((z == at_z) & (step == at_step), distance, apart)

            @pl.when(apart > 0)
            def _():
                pass_rows(apart)

            if line > 2:

                @pl.when(apart == 1)
                def _():
                    pass_cots(2)

            @pl.when(apart > 2)
            def _():
                pass_cots(apart)

            @pl.when((k > 0) & (e == 0))
            def _():
                cot_load.start()
                cot_load.wait()

        def products(e, at):
            gate_at = pl.multiple_of(2 * e * ff_width + at, tile)
            up_at = pl.multiple_of((2 * e + 1) * ff_width + at, tile)
            down_at = pl.multiple_of(e * ff_width + at, tile)
            return (
                contract(rows[block], up[:, pl.ds(gate_at, tile)], 1, 0),
                contract(rows[block], up[:, pl.ds(up_at, tile)], 1, 0),
                contract(cots[...], down[:, pl.ds(down_at, tile)], 1, 0),
            )

        narrow_lane = lax.broadcasted_iota(jnp.int32, gate_columns.shape, 1)
        wide_lane = lax.broadcasted_iota(jnp.int32, columns.shape, 1)
        several = experts // 2
        columns[...] = jnp.zeros_like(columns)

        def half(part, _):
            begin = part * several
            arrive(begin)

            @pl.when(k == 0)
            def _():
                for e in range(several):
                    for copy in weight_copies(begin + e):
                        copy.wait()

            tiles = [(e, at) for e in range(several) for at in range(0, ff_width, tile)]
            ready = products(begin + tiles[0][0], tiles[0][1])
            sums = [0.0] * several
            for number, (near, at) in enumerate(tiles):
                following = None
                if number + 1 < len(tiles):
                    following = products(begin + tiles[number + 1][0], tiles[number + 1][1])
                e = begin + near
                gate_part, up_part, returned = ready
                gate_col = jnp.sum(
                    jnp.where(narrow_lane == e, gate_columns, 0.0), axis=1, keepdims=True
                )
                sigmoid_gate = jax.nn.sigmoid(gate_part)
                silu_gate = gate_part * sigmoid_gate
                active = silu_gate * up_part
                sums[near] = sums[near] + jnp.sum(active * returned, axis=1, keepdims=True)
                scaled = returned * gate_col
                grad_gate = scaled * up_part * (sigmoid_gate + silu_gate * (1.0 - sigmoid_gate))
                gate_at = pl.multiple_of(2 * e * ff_width + at, tile)
                up_at = pl.multiple_of((2 * e + 1) * ff_width + at, tile)
                down_at = pl.multiple_of(e * ff_width + at, tile)
                gated[slot, :, pl.ds(down_at, tile)] = (active * gate_col).astype(BF16)
                inner[slot, :, pl.ds(gate_at, tile)] = grad_gate.astype(BF16)
                inner[slot, :, pl.ds(up_at, tile)] = (scaled * silu_gate).astype(BF16)
                ready = following
            value = columns[...]
            for near in range(several):
                value = jnp.where(wide_lane == begin + near, sums[near], value)
            columns[...] = value
            return 0

        lax.fori_loop(0, 2, half, 0)
        row_out(block).start()
        mix_stage[block] = contract(gated[slot], down[...], 1, 1).astype(BF16)

        @pl.when(block == z)
        def _():
            own_mix().start()

        if late:
            for side in range(2):

                @pl.when((block != z) & (block == side * (line - 1)))
                def _(side=side):
                    late_mix(side).start()

            @pl.when((block != z) & jnp.logical_not(at_end(block)))
            def _():
                mix_copy(block, z, block).start()

        else:

            @pl.when(block != z)
            def _():
                mix_copy(block, z, block).start()

        stage[slot] = contract(inner[slot], up[...], 1, 1).astype(BF16)
        for copy in out_copies(slot, block):
            copy.start()
        gate_grads_sent[block] = columns[...].T[: gate_grads.shape[1]]

        @pl.when(block == z)
        def _():
            gate_grads[z] = gate_grads_sent[z]

        @pl.when(block != z)
        def _():
            grad_copy(block, 0).start()

        return 0

    lax.fori_loop(0, line, visit, 0)
    for k in range(max(line - 2, 0), line):
        for copy in out_copies(k % 2, pick(order, z, k)):
            copy.wait()

    finish_rows()
    finish_cots()
    for copy in held_out:
        copy.wait()
    own_mix().wait()
    if late:
        for side in range(2):

            @pl.when(z != side * (line - 1))
            def _(side=side):
                late_mix(side).wait()

    for s in range(line):
        send_ends = late and s in (0, line - 1)

        @pl.when(z != s)
        def _(s=s, send_ends=send_ends):
            if not send_ends:
                mix_copy(s, s, z).wait_send()
            if late:

                @pl.when(jnp.logical_not(at_end(z)))
                def _():
                    mix_copy(s, s, z).wait_recv()

            else:
                mix_copy(s, s, z).wait_recv()

    for s in range(line):

        @pl.when(s != z)
        def _(s=s):
            grad_copy(s, 0).wait_send()
            pltpu.make_async_remote_copy(
                src_ref=gate_grads_sent.at[s],
                dst_ref=gate_grads.at[s],
                send_sem=grad_send.at[s],
                recv_sem=grad_recv.at[s],
                device_id=(dp, z),
                device_id_type=MESH,
            ).wait_recv()

    last = pltpu.make_async_copy(gate_grads, gate_grads_hbm, local_sem.at[1])
    last.start()
    for s in range(line):
        row_out(s).wait()
    last.wait()


def front(
    late,
    tokens,
    cots,
    gain_rows,
    heads_in,
    heads_out,
    router_rows,
    route_rows,
    label_row,
    frequencies,
    up,
    down,
    line,
    prompt,
):
    count, width = tokens.shape
    named = router_rows.shape[0]
    experts, _, ff_width = down.shape
    kv_width = KV_HEADS * HEAD_DIM
    shape = jax.ShapeDtypeStruct
    padded = experts + -experts % 8
    held = pl.BlockSpec(memory_space=pltpu.VMEM)
    anywhere = pl.BlockSpec(memory_space=pl.ANY)
    small = pltpu.VMEM((line, padded, count), F32)
    return pl.pallas_call(
        functools.partial(front_kernel, line, prompt, late),
        out_shape=(
            shape((count, width), BF16),
            shape((count, HEADS * HEAD_DIM), BF16),
            shape((count, kv_width), BF16),
            shape((count, kv_width), BF16),
            shape((count, HEADS * HEAD_DIM), BF16),
            shape((count, width), F32),
            shape((count, width), BF16),
            shape((named, count), F32),
            shape((count, 128), F32),
            shape((count, 128), F32),
            shape((count, 128), F32),
            shape((count, count), F32),
            shape((line, count, width), BF16),
            shape((line, count, width), BF16),
            shape((2, count, width), BF16),
            shape((line, count, width), BF16),
            shape((line, padded, count), F32),
            shape((line, count, experts * ff_width), BF16),
            shape((line, count, experts * 2 * ff_width), BF16),
            shape((line, count, width), BF16),
        ),
        in_specs=[held, anywhere, held, anywhere, anywhere] + [held] * 4 + [anywhere] * 2,
        out_specs=(anywhere,) * 7 + (held,) * 2 + (anywhere,) * 11,
        scratch_shapes=[
            pltpu.VMEM((count, width), BF16),
            pltpu.VMEM((line, count, width), BF16),
            small,
            small,
            small,
            small,
            pltpu.VMEM((width, experts * 2 * ff_width), BF16),
            pltpu.VMEM((width, experts * ff_width), BF16),
            pltpu.VMEM((count, heads_in.shape[1]), F32),
            pltpu.VMEM((2, count, width), BF16),
            pltpu.VMEM((line, count, width), BF16),
            pltpu.VMEM((2, count, experts * ff_width), BF16),
            pltpu.VMEM((2, count, experts * 2 * ff_width), BF16),
            pltpu.VMEM((count, 128), F32),
            pltpu.SemaphoreType.DMA((line + 2,)),
            pltpu.SemaphoreType.DMA((line,)),
            pltpu.SemaphoreType.DMA((line + 2,)),
            pltpu.SemaphoreType.DMA((line,)),
            pltpu.SemaphoreType.DMA((line,)),
            pltpu.SemaphoreType.DMA((line,)),
            pltpu.SemaphoreType.DMA((2, experts)),
            pltpu.SemaphoreType.DMA((6,)),
            pltpu.SemaphoreType.DMA((2, 3)),
            pltpu.SemaphoreType.DMA((line,)),
            pltpu.SemaphoreType.DMA((line,)),
            pltpu.SemaphoreType.DMA((line,)),
            pltpu.SemaphoreType.DMA((line,)),
            pltpu.VMEM(heads_in.shape, BF16),
            pltpu.VMEM(heads_out.shape, BF16),
            pltpu.VMEM((count, width), BF16),
            pltpu.VMEM((count, HEADS * HEAD_DIM), BF16),
            pltpu.VMEM((count, kv_width), BF16),
            pltpu.VMEM((count, kv_width), BF16),
            pltpu.VMEM((count, HEADS * HEAD_DIM), BF16),
            pltpu.VMEM((count, width), F32),
            pltpu.VMEM((count, width), BF16),
            pltpu.VMEM((count, 128), F32),
            pltpu.VMEM((count, 128), F32),
            pltpu.VMEM((count, count), F32),
            pltpu.SemaphoreType.DMA((12,)),
            pltpu.SemaphoreType.DMA((line,)),
        ],
        compiler_params=pltpu.CompilerParams(
            collective_id=4, has_side_effects=True, vmem_limit_bytes=VMEM_MOST
        ),
        cost_estimate=pl.CostEstimate(flops=2**35, bytes_accessed=2**26, transcendentals=2**22),
    )(
        tokens,
        cots,
        gain_rows,
        heads_in,
        heads_out,
        router_rows,
        route_rows,
        label_row,
        frequencies,
        up,
        down,
    )


def attend_back_kernel(
    paired,
    line,
    back_rows,
    hidden,
    cots,
    second_in,
    gate_rows,
    gate_grads,
    router_rows,
    gain_rows,
    heads_out_hbm,
    queries_hbm,
    keys_hbm,
    values_hbm,
    attended,
    log_totals,
    cosine,
    sine,
    bias,
    tokens_hbm,
    first_hbm,
    in_hbm,
    mix_hbm,
    late_hbm,
    *others,
):
    bank_hbm, others = (others[0], others[1:]) if paired else (None, others)
    output, token_grad, sum_hbm, small_hbm, *others = others
    bank_sum_hbm, others = (others[0], others[1:]) if paired else (None, others)
    (
        tokens,
        first_in,
        heads_in,
        mixes,
        gate_grad_rows,
        grad_hidden,
        grad_attended,
        grad_projected,
        small_rows,
        own,
        own_small,
        heads_out,
        queries,
        keys,
        values,
        held_sem,
        *scratch,
    ) = others
    dp = lax.axis_index("dp")
    z = lax.axis_index("expert")
    units = own.shape[0]
    block_rows = own.shape[4]
    load_sem = scratch[0]
    loads = (
        pltpu.make_async_copy(first_hbm, first_in, load_sem.at[0]),
        pltpu.make_async_copy(tokens_hbm, tokens, load_sem.at[1]),
        pltpu.make_async_copy(in_hbm, heads_in, load_sem.at[2]),
    )
    held_loads = [
        pltpu.make_async_copy(source, target, held_sem.at[number])
        for number, (source, target) in enumerate(
            (
                (heads_out_hbm, heads_out),
                (queries_hbm, queries),
                (keys_hbm, keys),
                (values_hbm, values),
            )
        )
    ]
    for copy in held_loads:
        copy.start()
    for copy in loads:
        copy.start()

    def mix_load(b):
        return pltpu.make_async_copy(mix_hbm.at[b], mixes.at[b], load_sem.at[5 + b])

    def direct(b):
        ends = (z == 0) | (z == line - 1)
        return jnp.logical_not(ends) | (z == b) if paired else z == z

    for b in range(line):

        @pl.when(direct(b))
        def _(b=b):
            mix_load(b).start()

    if paired:
        (
            cores,
            firsts,
            lasts,
            sums,
            lines,
            totals,
            small_cores,
            small_firsts,
            small_lasts,
            small_sums,
            small_lines,
            small_totals,
            send_sem,
            recv_sem,
            line_send,
            line_recv,
            out_sem,
            bank_kept,
            bank_last,
            bank_total,
            bank_sem,
            small_columns,
            chain_own,
            chain_in,
            chain_out,
            chain_load_sem,
            chain_sem,
        ) = scratch[1:]
        rows = totals.shape[1]
        y, x, core = dp // 4, lax.rem(dp // 2, 2), lax.rem(dp, 2)
        core_peer, x_peer, y_peer = dp + 1 - 2 * core, dp + 2 - 4 * x, dp + 4 - 8 * y
        barrier = pltpu.get_barrier_semaphore()
        for peer in (core_peer, x_peer, y_peer):
            pl.semaphore_signal(barrier, inc=1, device_id=(peer, z), device_id_type=MESH)
        for step in range(1, line):
            pl.semaphore_signal(
                barrier, inc=1, device_id=(dp, lax.rem(z + step, line)), device_id_type=MESH
            )
        pl.semaphore_wait(barrier, 3 + line - 1)

        def bank_kept_copy(e):
            kept = y if e % 2 == 0 else x
            return pltpu.make_async_copy(
                bank_hbm.at[e, kept], bank_kept.at[e], bank_sem.at[0, e]
            )

        def bank_last_copy(e):
            sent, peer = (1 - y, y_peer) if e % 2 == 0 else (1 - x, x_peer)
            return pltpu.make_async_remote_copy(
                src_ref=bank_hbm.at[e, sent],
                dst_ref=bank_last.at[e],
                send_sem=bank_sem.at[1, e],
                recv_sem=bank_sem.at[2, e],
                device_id=(peer, z),
                device_id_type=MESH,
            )

        def bank_total_copy(e):
            return pltpu.make_async_copy(
                bank_total.at[e], bank_sum_hbm.at[e], bank_sem.at[3, e]
            )

        for e in range(bank_hbm.shape[0]):
            bank_kept_copy(e).start()
            bank_last_copy(e).start()

        piece = hidden.shape[0] // PIECES

        def part(p):
            return pl.ds(p * piece, piece)

        def chain_load(side):
            return pltpu.make_async_copy(
                late_hbm.at[side], chain_own.at[side], chain_load_sem.at[side]
            )

        def chain_send(side, p, source):
            return pltpu.make_async_remote_copy(
                src_ref=source.at[side, part(p)],
                dst_ref=chain_in.at[side, part(p)],
                send_sem=chain_sem.at[0, side, p],
                recv_sem=chain_sem.at[1, side, p],
                device_id=(dp, jnp.clip(z + 2 * side - 1, 0, line - 1)),
                device_id_type=MESH,
            )

        inside = (z > 0) & (z < line - 1)
        starts = (z == line - 1, z == 0)
        for side in range(2):

            @pl.when(inside)
            def _(side=side):
                chain_load(side).start()

            @pl.when(starts[side])
            def _(side=side):
                for p in range(PIECES):
                    chain_send(side, p, late_hbm).start()

        def relay(side, p):
            if p == 0:
                chain_load(side).wait()
            chain_send(side, p, chain_out).wait_recv()
            chain_out[side, part(p)] = (
                chain_own[side, part(p)].astype(F32) + chain_in[side, part(p)].astype(F32)
            ).astype(BF16)
            chain_send(side, p, chain_out).start()

        def relay_on(near, p):
            low_half = 2 * z < line - 1

            @pl.when(inside & low_half)
            def _():
                relay(1 if near else 0, p)

            @pl.when(inside & jnp.logical_not(low_half))
            def _():
                relay(0 if near else 1, p)

        buffers = (own, cores, firsts, lasts, sums, lines, totals)
        small_buffers = (
            own_small,
            small_cores,
            small_firsts,
            small_lasts,
            small_sums,
            small_lines,
            small_totals,
        )

        def send(stage, u, source, target, peer):
            return pltpu.make_async_remote_copy(
                src_ref=source,
                dst_ref=target,
                send_sem=send_sem.at[stage, u],
                recv_sem=recv_sem.at[stage, u],
                device_id=(peer, z),
                device_id_type=MESH,
            )

        class Sums:
            def __init__(self, held, shift):
                self.own, self.cores, self.firsts, self.lasts = held[:4]
                self.sums, self.lines, self.totals = held[4:]
                self.shift = shift

            def core_send(self, u):
                return send(
                    0,
                    u + self.shift,
                    self.own.at[u, :, :, 1 - core],
                    self.cores.at[u],
                    core_peer,
                )

            def first_send(self, u, along_x):
                if along_x:
                    source, peer = self.cores.at[u, :, 1 - x], x_peer
                else:
                    source, peer = self.cores.at[u, 1 - y], y_peer
                return send(1, u + self.shift, source, self.firsts.at[u], peer)

            def last_send(self, u, along_x):
                if along_x:
                    source, peer = self.firsts.at[u, 1 - x], x_peer
                else:
                    source, peer = self.firsts.at[u, 1 - y], y_peer
                return send(2, u + self.shift, source, self.lasts.at[u], peer)

            def line_copy(self, u, step):
                peer = lax.rem(z + step, line)
                return pltpu.make_async_remote_copy(
                    src_ref=self.sums.at[u, pl.ds(pl.multiple_of(peer * rows, rows), rows)],
                    dst_ref=self.lines.at[u, step],
                    send_sem=line_send.at[u + self.shift, step],
                    recv_sem=line_recv.at[u + self.shift, step],
                    device_id=(dp, peer),
                    device_id_type=MESH,
                )

            def by_parity(self, u, act):
                even = lax.rem(jnp.int32(u), 2) == 0

                @pl.when(even)
                def _():
                    act(True)

                @pl.when(jnp.logical_not(even))
                def _():
                    act(False)

            def after_core(self, u):
                self.core_send(u).wait_recv()
                for yy in range(2):
                    for xx in range(2):
                        self.cores[u, yy, xx] = (
                            self.own[u, yy, xx, core].astype(F32)
                            + self.cores[u, yy, xx].astype(F32)
                        ).astype(BF16)
                self.by_parity(u, lambda even: self.first_send(u, even).start())

            def after_first(self, u):
                def act(even):
                    self.first_send(u, even).wait_recv()
                    for other in range(2):
                        kept = self.cores[u, other, x] if even else self.cores[u, y, other]
                        self.firsts[u, other] = (
                            kept.astype(F32) + self.firsts[u, other].astype(F32)
                        ).astype(BF16)
                    self.last_send(u, not even).start()

                self.by_parity(u, act)

            def after_last(self, u):
                def act(even):
                    self.last_send(u, not even).wait_recv()
                    kept = self.firsts[u, y] if even else self.firsts[u, x]
                    self.sums[u] = (kept.astype(F32) + self.lasts[u].astype(F32)).astype(BF16)

                self.by_parity(u, act)
                for step in range(1, line):
                    self.line_copy(u, step).start()

            def after_line(self, u):
                value = self.sums[u, pl.ds(pl.multiple_of(z * rows, rows), rows)].astype(F32)
                for step in range(1, line):
                    self.line_copy(u, step).wait_recv()
                    value = value + self.lines[u, step].astype(F32)
                self.totals[u] = value

            def finish(self, u):
                self.core_send(u).wait_send()
                self.first_send(u, u % 2 == 0).wait_send()
                self.last_send(u, u % 2 == 1).wait_send()
                for step in range(1, line):
                    self.line_copy(u, step).wait_send()

        wide_sums = Sums(buffers, 0)
        small_sum = Sums(small_buffers, units)

    def keep(target, u, value):
        for block in range(8):
            target[u, block // 4, block // 2 % 2, block % 2] = value[
                block * block_rows : (block + 1) * block_rows
            ]

    gates = gate_rows[...]
    local = gates.shape[0] // line
    for b in range(line):
        gate_grad_rows[b * local : (b + 1) * local] = gate_grads[b, :local]
    gate_grad = gate_grad_rows[...]
    logit_grad = gates * (gate_grad - jnp.sum(gates * gate_grad, axis=0, keepdims=True))
    high = logit_grad.astype(BF16)
    low = (logit_grad - high.astype(F32)).astype(BF16)
    grad_second = (
        back_rows[...].astype(F32)
        + contract(high, router_rows[...], 0, 0)
        + contract(low, router_rows[...], 0, 0)
    )
    small_rows[...] = jnp.zeros_like(small_rows)
    experts = high.shape[0]
    small_rows[:experts] = contract(high, second_in[...], 1, 0) + contract(low, second_in[...], 1, 0)

    def norm_back(incoming, rows, gain):
        factor = lax.rsqrt(jnp.mean(rows * rows, axis=1, keepdims=True) + EPS)
        normed = rows * factor
        gain_grad = jnp.sum(incoming * normed, axis=0, keepdims=True)
        weighted = incoming * gain
        mean = jnp.mean(weighted * normed, axis=1, keepdims=True)
        return factor * (weighted - normed * mean), gain_grad

    norm_grad, gain_grad = norm_back(grad_second, hidden[...], gain_rows[1:2])
    small_rows[experts + 1 : experts + 2] = gain_grad
    grad_hidden[...] = cots[...].astype(F32) + norm_grad
    branch = grad_hidden[...].astype(BF16)
    for u in range(2):
        keep(
            own,
            u,
            contract(branch, attended[:, u * UNIT : (u + 1) * UNIT], 0, 0).astype(BF16),
        )
        if paired:
            wide_sums.core_send(u).start()
    for copy in held_loads:
        copy.wait()
    grad_attended[...] = contract(branch, heads_out[...], 1, 0).astype(BF16)
    loads[0].wait()
    if paired:
        wide_sums.after_core(0)
        relay_on(True, 0)

    def pair(j, _):
        key_pair = keys[:, lanes_at(j * PAIR, PAIR)]
        value_pair = values[:, lanes_at(j * PAIR, PAIR)]
        key_grads = []
        value_grads = []
        for side in range(2):
            at = lanes_at((2 * j + side) * PAIR, PAIR)
            group = queries[:, at]
            group_grad = grad_attended[:, at]
            key_sides = sides(key_pair, side, SCALE)
            value_sides = sides(value_pair, side, None)
            product = group_grad.astype(F32) * attended[:, at].astype(F32)
            lane = lax.broadcasted_iota(jnp.int32, product.shape, 1)
            grad = jnp.zeros(group.shape, F32)
            key_grad = []
            value_grad = []
            for member in range(2):
                head = 4 * j + 2 * side + member
                log_total = jnp.sum(
                    jnp.where(lane == head, log_totals[...], 0.0), axis=1, keepdims=True
                )
                mine = (lane < HEAD_DIM) if member == 0 else (lane >= HEAD_DIM)
                spread = jnp.sum(jnp.where(mine, product, 0.0), axis=1, keepdims=True)
                scores = contract(group, key_sides[member], 1, 1) + bias[...]
                weights = jnp.exp(scores - log_total)
                weight_grads = contract(group_grad, value_sides[member], 1, 1)
                score_grads = (weights * (weight_grads - spread)).astype(BF16)
                grad = grad + contract(score_grads, key_sides[member], 1, 0)
                rows_of = slice(member * HEAD_DIM, (member + 1) * HEAD_DIM)
                key_grad.append(contract(group, score_grads, 0, 0)[rows_of])
                value_grad.append(contract(group_grad, weights.astype(BF16), 0, 0)[rows_of])
            grad_projected[j, :, side * PAIR : (side + 1) * PAIR] = (
                grad * cosine[...] - swap_halves(grad) * sine[...]
            ).astype(BF16)
            key_grads.append(key_grad[0] + key_grad[1])
            value_grads.append(value_grad[0] + value_grad[1])
        key_rows = jnp.concatenate(key_grads, axis=0).T * SCALE
        grad_projected[j, :, 2 * PAIR : 3 * PAIR] = (
            key_rows * cosine[...] - swap_halves(key_rows) * sine[...]
        ).astype(BF16)
        grad_projected[j, :, 3 * PAIR :] = jnp.concatenate(value_grads, axis=0).T.astype(BF16)
        keep(own, 2 + j, contract(first_in[...], grad_projected[j], 0, 0).astype(BF16))
        if paired:
            wide_sums.core_send(2 + j).start()
            wide_sums.after_core(1 + j)

            @pl.when(j >= 2)
            def _():
                wide_sums.after_first(j - 2)

            for at, near, p in ((0, True, 1), (1, True, 2), (2, False, 0), (3, False, 1)):

                @pl.when(j == at)
                def _(near=near, p=p):
                    relay_on(near, p)

        return 0

    pairs = KV_HEADS // 2
    lax.fori_loop(0, pairs, pair, 0)
    last = units - 1
    if paired:
        wide_sums.after_core(last)
        relay_on(False, 2)
        wide_sums.after_first(2)
        wide_sums.after_last(0)
        wide_sums.after_first(3)
        wide_sums.after_last(1)
    loads[1].wait()
    loads[2].wait()
    grad_first = jnp.zeros(grad_hidden.shape, F32)
    query_end = HEADS * HEAD_DIM
    key_end = query_end + KV_HEADS * HEAD_DIM
    for j in range(pairs):
        for at, begin, size in (
            (0, 2 * j * PAIR, 2 * PAIR),
            (2 * PAIR, query_end + j * PAIR, PAIR),
            (3 * PAIR, key_end + j * PAIR, PAIR),
        ):
            grad_first = grad_first + contract(
                grad_projected[j, :, at : at + size], heads_in[:, begin : begin + size], 1, 1
            )
    norm_grad, gain_grad = norm_back(grad_first, tokens[...].astype(F32), gain_rows[0:1])
    small_rows[experts : experts + 1] = gain_grad
    keep(own_small, 0, small_rows[...].T.astype(BF16))
    if paired:
        small_sum.core_send(0).start()
    if paired:
        wide_sums.after_first(4)
        wide_sums.after_last(2)
        small_sum.after_core(0)
        wide_sums.after_first(5)
        wide_sums.after_last(3)
        small_sum.after_first(0)
    token_grad[...] = grad_hidden[...] + norm_grad
    if paired:
        for e in range(bank_hbm.shape[0]):
            bank_kept_copy(e).wait()
            bank_last_copy(e).wait()
            bank_total[e] = bank_kept[e].astype(F32) + bank_last[e].astype(F32)
            bank_total_copy(e).start()

    @pl.when(direct(-1))
    def _():
        total = hidden[...]
        for b in range(line):
            mix_load(b).wait()
            total = total + mixes[b].astype(F32)
        output[...] = total.astype(BF16)

    if paired:
        wide_sums.after_last(4)
        small_sum.after_last(0)
        wide_sums.after_last(5)
        for u in range(units):
            wide_sums.after_line(u)
        small_sum.after_line(0)
        places = [(u, 0, UNIT, key_end + KV_HEADS * HEAD_DIM + u * UNIT) for u in range(2)]
        for j in range(pairs):
            places.append((2 + j, 0, 2 * PAIR, 2 * j * PAIR))
            places.append((2 + j, 2 * PAIR, PAIR, query_end + j * PAIR))
            places.append((2 + j, 3 * PAIR, PAIR, key_end + j * PAIR))
        small_columns[...] = small_totals[0].T
        gain_values = gain_rows[...]
        share = jnp.zeros((2, rows), F32)
        for i in range(gain_values.shape[1] // rows):
            share = jnp.where(
                dp * line + z == i, gain_values[:, i * rows : (i + 1) * rows], share
            )
        small_columns[experts + 2 : experts + 4] = share
        outs = [pltpu.make_async_copy(small_columns, small_hbm, out_sem.at[len(places)])]
        for number, (u, at, size, column) in enumerate(places):
            outs.append(
                pltpu.make_async_copy(
                    totals.at[u, :, at : at + size],
                    sum_hbm.at[:, column : column + size],
                    out_sem.at[number],
                )
            )
    else:
        outs = (
            pltpu.make_async_copy(own, sum_hbm, load_sem.at[3]),
            pltpu.make_async_copy(own_small, small_hbm, load_sem.at[4]),
        )
    for copy in outs:
        copy.start()
    if paired:
        for u in range(units):
            wide_sums.finish(u)
        small_sum.finish(0)
        for e in range(bank_hbm.shape[0]):
            bank_total_copy(e).wait()
        for side in range(2):

            @pl.when(starts[1 - side])
            def _(side=side):
                mix_load(z).wait()
                for p in range(PIECES):
                    chain_send(side, p, late_hbm).wait_recv()
                output[...] = (
                    hidden[...] + mixes[z].astype(F32) + chain_in[side].astype(F32)
                ).astype(BF16)

            @pl.when(jnp.logical_not(starts[1 - side]))
            def _(side=side):
                for p in range(PIECES):
                    chain_send(side, p, late_hbm).wait_send()

    for copy in outs:
        copy.wait()


def attend_back(held_args, far_args, paired, line):
    tokens, first_in, heads_in = far_args[:3]
    count, width = tokens.shape
    pairs = KV_HEADS // 2
    units = 2 + pairs
    block_rows = width // 8
    rows = block_rows // line
    shape = jax.ShapeDtypeStruct
    held = pl.BlockSpec(memory_space=pltpu.VMEM)
    anywhere = pl.BlockSpec(memory_space=pl.ANY)
    if paired:
        sum_shapes = (shape((rows, units * UNIT), F32), shape((128, rows), F32))
    else:
        sum_shapes = (
            shape((units, 2, 2, 2, block_rows, UNIT), BF16),
            shape((1, 2, 2, 2, block_rows, 128), BF16),
        )
    exchange = []
    if paired:
        for number, lanes in ((units, UNIT), (1, 128)):
            exchange += [
                pltpu.VMEM((number, 2, 2, block_rows, lanes), BF16),
                pltpu.VMEM((number, 2, block_rows, lanes), BF16),
                pltpu.VMEM((number, block_rows, lanes), BF16),
                pltpu.VMEM((number, block_rows, lanes), BF16),
                pltpu.VMEM((number, line, rows, lanes), BF16),
                pltpu.VMEM((number, rows, lanes), F32),
            ]
        exchange += [
            pltpu.SemaphoreType.DMA((3, units + 1)),
            pltpu.SemaphoreType.DMA((3, units + 1)),
            pltpu.SemaphoreType.DMA((units + 1, line)),
            pltpu.SemaphoreType.DMA((units + 1, line)),
            pltpu.SemaphoreType.DMA((3 + 3 * pairs,)),
        ]
        bank_shape = (far_args[5].shape[0],) + far_args[5].shape[2:]
        sum_shapes += (shape(bank_shape, F32),)
        exchange += [
            pltpu.VMEM(bank_shape, BF16),
            pltpu.VMEM(bank_shape, BF16),
            pltpu.VMEM(bank_shape, F32),
            pltpu.SemaphoreType.DMA((4, bank_shape[0])),
            pltpu.VMEM((128, rows), F32),
            pltpu.VMEM((2, count, width), BF16),
            pltpu.VMEM((2, count, width), BF16),
            pltpu.VMEM((2, count, width), BF16),
            pltpu.SemaphoreType.DMA((2,)),
            pltpu.SemaphoreType.DMA((2, 2, PIECES)),
        ]
    settings = dict(vmem_limit_bytes=VMEM_MOST)
    if paired:
        settings.update(collective_id=3, has_side_effects=True)
    return pl.pallas_call(
        functools.partial(attend_back_kernel, paired, line),
        out_shape=(shape((count, width), BF16), shape((count, width), F32)) + sum_shapes,
        in_specs=[anywhere if 8 <= i < 12 else held for i in range(len(held_args))]
        + [anywhere] * len(far_args),
        out_specs=(held, held) + (anywhere,) * len(sum_shapes),
        scratch_shapes=[
            pltpu.VMEM((count, width), BF16),
            pltpu.VMEM((count, width), BF16),
            pltpu.VMEM(heads_in.shape, BF16),
            pltpu.VMEM((line, count, width), BF16),
            pltpu.VMEM(held_args[4].shape, F32),
            pltpu.VMEM((count, width), F32),
            pltpu.VMEM((count, HEADS * HEAD_DIM), BF16),
            pltpu.VMEM((pairs, count, 4 * PAIR), BF16),
            pltpu.VMEM((128, width), F32),
            pltpu.VMEM((units, 2, 2, 2, block_rows, UNIT), BF16),
            pltpu.VMEM((1, 2, 2, 2, block_rows, 128), BF16),
            *[pltpu.VMEM(value.shape, BF16) for value in held_args[8:12]],
            pltpu.SemaphoreType.DMA((4,)),
            pltpu.SemaphoreType.DMA((5 + line,)),
            *exchange,
        ],
        compiler_params=pltpu.CompilerParams(**settings),
        cost_estimate=pl.CostEstimate(flops=2**34, bytes_accessed=2**25, transcendentals=2**21),
    )(*held_args, *far_args)


def unit_columns(sums):
    pairs = KV_HEADS // 2
    parts = sums[2 : 2 + pairs]
    rows = sums.shape[1]

    def side_by_side(value):
        return jnp.transpose(value, (1, 0, 2)).reshape(rows, -1)

    return (
        jnp.concatenate(
            [
                side_by_side(parts[:, :, : 2 * PAIR]),
                side_by_side(parts[:, :, 2 * PAIR : 3 * PAIR]),
                side_by_side(parts[:, :, 3 * PAIR :]),
            ],
            axis=1,
        ),
        side_by_side(sums[:2]),
    )


def update_kernel(width, experts, bank_sum, head_sum, small_rows, *refs):
    lanes = refs[0].shape[2]
    gradients = (
        bank_sum[0, :, :lanes],
        bank_sum[0, :, lanes:],
        head_sum[:, :width],
        head_sum[:, width:],
        small_rows[:experts],
        small_rows[experts : experts + 2],
    )
    count = len(gradients)
    for number, gradient in enumerate(gradients):
        held = refs[3 * number : 3 * number + 3]
        if number == count - 1:
            held = (small_rows.at[experts + 2 : experts + 4], *held[1:])
        results = refs[3 * (count + number) : 3 * (count + number) + 3]
        at = (0,) if held[0].ndim == 3 else (Ellipsis,)
        values = update(gradient, *(ref[at] for ref in held))
        for ref, value in zip(results, values):
            ref[at] = value


def update_all(bank_sum, head_sum, small_rows, states):
    experts, block_rows, _ = bank_sum.shape
    rows = head_sum.shape[0] // experts

    def spec(value):
        if value.ndim == 3:
            return pl.BlockSpec((1, block_rows, value.shape[2]), lambda i: (i, 0, 0))
        if value.shape[0] == head_sum.shape[0] and value.shape[1] > 128:
            return pl.BlockSpec((rows, value.shape[1]), lambda i: (i, 0))
        return pl.BlockSpec(value.shape, lambda i: (0, 0))

    flat = [value for state in states for value in state]
    results = pl.pallas_call(
        functools.partial(update_kernel, states[2][0].shape[1], states[4][0].shape[0]),
        grid=(experts,),
        out_shape=tuple(jax.ShapeDtypeStruct(value.shape, F32) for value in flat),
        in_specs=[spec(value) for value in (bank_sum, head_sum, small_rows, *flat)],
        out_specs=tuple(spec(value) for value in flat),
        compiler_params=pltpu.CompilerParams(vmem_limit_bytes=VMEM_MOST),
        cost_estimate=pl.CostEstimate(flops=2**23, bytes_accessed=25 * 2**20, transcendentals=0),
    )(bank_sum, head_sum, small_rows, *flat)
    return [tuple(results[i : i + 3]) for i in range(0, len(flat), 3)]


def body(
    tokens,
    cotangent,
    routes,
    cont_ids,
    norm_gains,
    gains_moment,
    gains_average,
    heads_in,
    heads_in_master,
    heads_in_moment,
    heads_in_average,
    heads_out,
    heads_out_master,
    heads_out_moment,
    heads_out_average,
    router,
    router_master,
    router_moment,
    router_average,
    expert_in,
    expert_in_master,
    expert_in_moment,
    expert_in_average,
    expert_out,
    expert_out_master,
    expert_out_moment,
    expert_out_average,
):
    token_count, model_width = tokens.shape
    local_experts = expert_in.shape[0]
    peer_count = lax.axis_size("expert")
    experts = local_experts * peer_count
    paired = lax.axis_size("dp") == 8 and peer_count == 4
    half = HEAD_DIM // 2
    powers = [THETA ** (-2.0 * (lane % half) / HEAD_DIM) for lane in range(128)]
    frequencies = jnp.asarray(np.array(powers, np.float32)[None])
    gain_rows = norm_gains.T
    router_rows = router.T
    (
        first_in,
        queries,
        key_rows,
        value_rows,
        attended,
        hidden,
        second_in,
        gates,
        log_totals,
        cosine,
        sine,
        bias,
        cots_all,
        mix_all,
        mix_late,
        grad_part,
        gate_grads,
        gated,
        grad_gate_up,
        rows_all,
    ) = front(
        paired,
        tokens,
        cotangent,
        gain_rows,
        heads_in,
        heads_out,
        router_rows,
        routes.T,
        cont_ids,
        frequencies,
        expert_in,
        expert_out,
        peer_count,
        token_count - cont_ids.shape[1],
    )
    back_rows = lax.psum_scatter(
        grad_part.reshape(peer_count * token_count, model_width),
        "expert",
        scatter_dimension=0,
        tiled=True,
    )
    grad_sources = (
        rows_all.reshape(peer_count * token_count, model_width),
        cots_all.reshape(peer_count * token_count, model_width),
        gated.reshape(peer_count * token_count, -1),
        grad_gate_up.reshape(peer_count * token_count, -1),
    )
    if paired:
        expert_sums = (bank_grads(*grad_sources, local_experts),)
    else:
        expert_sums = tuple(
            lax.psum_scatter(part, "dp", scatter_dimension=1, tiled=True).astype(jnp.float32)
            for part in weight_grads(*grad_sources, local_experts)
        )
    output, token_grad, unit_sums, small_sum, *bank_sums = attend_back(
        (
            back_rows,
            hidden,
            cotangent,
            second_in,
            gates,
            gate_grads,
            router_rows,
            gain_rows,
            heads_out,
            queries,
            key_rows,
            value_rows,
            attended,
            log_totals,
            cosine,
            sine,
            bias,
        ),
        (tokens, first_in, heads_in, mix_all, mix_late, *(expert_sums if paired else ())),
        paired,
        peer_count,
    )
    if paired:
        gains_share = gains_moment.T
    else:
        shard_rows = model_width // lax.axis_size(("dp", "expert"))
        gains_share = lax.dynamic_slice_in_dim(
            gain_rows, lax.axis_index(("dp", "expert")) * shard_rows, shard_rows, 1
        )
    states = (
        (expert_in_master, expert_in_moment, expert_in_average),
        (expert_out_master, expert_out_moment, expert_out_average),
        (heads_in_master, heads_in_moment, heads_in_average),
        (heads_out_master, heads_out_moment, heads_out_average),
        (router_master.T, router_moment.T, router_average.T),
        (gains_share, gains_moment.T, gains_average.T),
    )
    if paired:
        news = update_all(bank_sums[0], unit_sums, small_sum, states)
    else:
        head_parts = unit_columns(unit_sums.reshape(unit_sums.shape[0], model_width, UNIT))
        packed = jnp.concatenate([*head_parts, small_sum.reshape(model_width, 128)], axis=1)
        head_total = lax.psum_scatter(
            packed, ("dp", "expert"), scatter_dimension=0, tiled=True
        ).astype(jnp.float32)
        cut_in = head_parts[0].shape[1]
        cut_out = cut_in + head_parts[1].shape[1]
        small_rows = head_total[:, cut_out:].T
        sums = (
            *expert_sums,
            head_total[:, :cut_in],
            head_total[:, cut_in:cut_out],
            small_rows[:experts],
            small_rows[experts : experts + 2],
        )
        news = [update(gradient, *state) for gradient, state in zip(sums, states)]
    upper_new, lower_new, inproj_new, outproj_new, router_new, gains_new = news
    router_new = tuple(value.T for value in router_new)
    gains_new = tuple(value.T for value in gains_new)
    return (
        output,
        token_grad,
        gains_new[0],
        gains_new[1],
        gains_new[2],
        inproj_new[0],
        inproj_new[1],
        inproj_new[2],
        outproj_new[0],
        outproj_new[1],
        outproj_new[2],
        router_new[0],
        router_new[1],
        router_new[2],
        upper_new[0],
        upper_new[1],
        upper_new[2],
        lower_new[0],
        lower_new[1],
        lower_new[2],
    )


def solution(mesh):
    return jax.shard_map(
        body,
        mesh=mesh,
        in_specs=(
            P(("dp", "expert"), None),
            P(("dp", "expert"), None),
            P(("dp", "expert"), None),
            P(("dp", "expert"), None),
            P(),
            P(("dp", "expert"), None),
            P(("dp", "expert"), None),
            P(),
            P(("dp", "expert"), None),
            P(("dp", "expert"), None),
            P(("dp", "expert"), None),
            P(),
            P(("dp", "expert"), None),
            P(("dp", "expert"), None),
            P(("dp", "expert"), None),
            P(),
            P(("dp", "expert"), None),
            P(("dp", "expert"), None),
            P(("dp", "expert"), None),
            P("expert", None, None),
            P("expert", "dp", None),
            P("expert", "dp", None),
            P("expert", "dp", None),
            P("expert", None, None),
            P("expert", "dp", None),
            P("expert", "dp", None),
            P("expert", "dp", None),
        ),
        out_specs=(
            P(("dp", "expert"), None),
            P(("dp", "expert"), None),
            P(("dp", "expert"), None),
            P(("dp", "expert"), None),
            P(("dp", "expert"), None),
            P(("dp", "expert"), None),
            P(("dp", "expert"), None),
            P(("dp", "expert"), None),
            P(("dp", "expert"), None),
            P(("dp", "expert"), None),
            P(("dp", "expert"), None),
            P(("dp", "expert"), None),
            P(("dp", "expert"), None),
            P(("dp", "expert"), None),
            P("expert", "dp", None),
            P("expert", "dp", None),
            P("expert", "dp", None),
            P("expert", "dp", None),
            P("expert", "dp", None),
            P("expert", "dp", None),
        ),
        check_vma=False,
    )
```
